32 devices in a mesh: seq: 8 (over y, x, core), tensor: 4 (over z).
Axes of the slice: x: 2, y: 2, z: 4, core: 2. Of those that a mesh axis runs over, the one named last changes fastest.
Arguments:
- tokens: bfloat16 [8192, 1024], P('seq', 'tensor'), may hold values from -6 to 6
- segment_ids: int32 [8192], P('seq'), may hold values from 0 to 4, as said below
- out_grad: bfloat16 [8192, 1024], P('seq', 'tensor'), may hold values from -6 to 6
- ln1_gain: bfloat16 [1024], P('tensor'), may hold values from 0.099609375 to 1.8984375
- ln1_bias: bfloat16 [1024], P('tensor'), may hold values from -3 to 3
- w_qkv: bfloat16 [1024, 16, 192], P(None, 'tensor'), may hold values from -0.1875 to 0.1875
- b_qv: bfloat16 [16, 128], P('tensor'), may hold values from -3 to 3
- w_out: bfloat16 [16, 64, 1024], P('tensor'), may hold values from -2 to 2
- b_out: bfloat16 [1024], P('tensor'), may hold values from -3 to 3
- ln2_gain: bfloat16 [1024], P('tensor'), may hold values from 0.099609375 to 1.8984375
- ln2_bias: bfloat16 [1024], P('tensor'), may hold values from -3 to 3
- w_up: bfloat16 [1024, 4096], P(None, 'tensor'), may hold values from -0.1875 to 0.1875
- b_up: bfloat16 [4096], P('tensor'), may hold values from -3 to 3
- w_down: bfloat16 [4096, 1024], P('tensor'), may hold values from -0.09375 to 0.09375
- b_down: bfloat16 [1024], P('tensor'), may hold values from -3 to 3
- prefix_embed: bfloat16 [10, 1024], replicated, may hold values from -6 to 6
- reparam_in: bfloat16 [1024, 512], replicated, may hold values from -0.1875 to 0.1875
- reparam_in_bias: bfloat16 [512], replicated, may hold values from -3 to 3
- reparam_out: bfloat16 [512, 16, 128], P(None, 'tensor'), may hold values from -0.25 to 0.25
- reparam_out_bias: bfloat16 [16, 128], P('tensor'), may hold values from -3 to 3
Outputs:
- output_act: bfloat16 [8192, 1024], P('seq', 'tensor')
- input_grad: bfloat16 [8192, 1024], P('seq', 'tensor')
- grad_ln1_gain: float32 [1024], P('tensor')
- grad_ln1_bias: float32 [1024], P('tensor')
- grad_w_qkv: float32 [1024, 16, 192], P(None, 'tensor')
- grad_b_qv: float32 [16, 128], P('tensor')
- grad_w_out: float32 [16, 64, 1024], P('tensor')
- grad_b_out: float32 [1024], P('tensor')
- grad_ln2_gain: float32 [1024], P('tensor')
- grad_ln2_bias: float32 [1024], P('tensor')
- grad_w_up: float32 [1024, 4096], P(None, 'tensor')
- grad_b_up: float32 [4096], P('tensor')
- grad_w_down: float32 [4096, 1024], P('tensor')
- grad_b_down: float32 [1024], P('tensor')
- grad_prefix_embed: float32 [10, 1024], replicated
- grad_reparam_in: float32 [1024, 512], replicated
- grad_reparam_in_bias: float32 [512], replicated
- grad_reparam_out: float32 [512, 16, 128], P(None, 'tensor')
- grad_reparam_out_bias: float32 [16, 128], P('tensor')
The draws below stay inside these ranges and needn't reach their ends.
Inputs may be any that keep to these rules, and one draw needn't show every extreme that they name: `segment_ids`: never falling along the tokens; every document has 1 or more tokens; document 2 has exactly 7168 tokens and starts within the first 1024 tokens.
All inputs are finite; a program needn't handle non-finite values.
Results may differ from the reference program's by a relative error of at most 0.024.
Values may be sent and summed in bfloat16 or wider, within the bound.
No kernel may reach another device: no remote copies, remote signals or barrier semaphores. Data moves between devices by JAX's collectives and lax.ppermute only.
A program may use at most 128 MiB of HBM per device.

```python
import functools
import math
import jax
import jax.numpy as jnp
from jax import lax

D = 1024
H = 16
HD = 64
FF = 4096
PRE = 10
PH = 512
TOK_DEV = 1024
TOKENS = 8192
DOC_MOST = 7168


def draw_segment_ids(key, part):
    first_key, second_key, third_key = jax.random.split(jax.random.fold_in(key, 7), 3)
    long_start = jax.random.randint(first_key, (), 2, TOK_DEV - 1)
    first_cut = jax.random.randint(second_key, (), 1, long_start)
    long_end = long_start + DOC_MOST
    last_cut = long_end + jax.random.randint(third_key, (), 1, TOK_DEV - long_start)
    places = jnp.arange(TOKENS, dtype=jnp.int32)
    return (places >= first_cut).astype(jnp.int32) + (places >= long_start).astype(jnp.int32) + (places >= long_end).astype(jnp.int32) + (places >= last_cut).astype(jnp.int32)


def block_levels(stream_key, shape, cuts, low, high):
    level = 1.0
    for dim, parts in cuts:
        heights = jax.random.uniform(jax.random.fold_in(jax.random.fold_in(stream_key, 6), dim), (parts,), jnp.float32, low / len(cuts), high / len(cuts))
        level = level * jnp.repeat(jnp.exp(heights), shape[dim] // parts).reshape((-1,) + (1,) * (len(shape) - 1 - dim))
    return level


def noise(own_key, extent, scale, reach, cuts=(), kind=jnp.bfloat16):
    level = block_levels(own_key, extent, cuts, -0.22, 0.18) if cuts else 1.0
    array = jax.random.normal(own_key, extent, jnp.float32) * scale * level
    return jnp.minimum(jnp.maximum(array, -reach), reach).astype(kind)


def setup_inputs(seed: int = 0) -> dict:
    key_list = jax.random.split(jax.random.key(seed), 21)
    return {
        "tokens": noise(key_list[0], (TOKENS, D), 1.0, 6.0, ((0, 8), (1, 4))),
        "segment_ids": draw_segment_ids(jax.random.fold_in(key_list[20], 71), 0),
        "out_grad": noise(key_list[2], (TOKENS, D), 1.0, 6.0, ((0, 8), (1, 4))),
        "ln1_gain": jnp.clip(1.0 + 0.18 * jax.random.normal(key_list[3], (D,), jnp.float32), 0.099609375, 1.8984375).astype(jnp.bfloat16),
        "ln1_bias": noise(key_list[4], (D,), 0.5, 3.0, ((0, 4),)),
        "w_qkv": noise(key_list[5], (D, H, 3 * HD), D ** -0.5, 0.1875, ((1, 4),)),
        "b_qv": noise(key_list[6], (H, 2 * HD), 0.5, 3.0, ((0, 4),)),
        "w_out": noise(key_list[7], (H, HD, D), (max(8, D // 128)) ** -0.5, 2.0, ((0, 4),)),
        "b_out": noise(key_list[8], (D,), 0.5, 3.0, ((0, 4),)),
        "ln2_gain": jnp.clip(1.0 + 0.18 * jax.random.normal(key_list[9], (D,), jnp.float32), 0.099609375, 1.8984375).astype(jnp.bfloat16),
        "ln2_bias": noise(key_list[10], (D,), 0.5, 3.0, ((0, 4),)),
        "w_up": noise(key_list[11], (D, FF), D ** -0.5, 0.1875, ((1, 4),)),
        "b_up": noise(key_list[12], (FF,), 0.5, 3.0, ((0, 4),)),
        "w_down": noise(key_list[13], (FF, D), FF ** -0.5, 0.09375, ((0, 4),)),
        "b_down": noise(key_list[14], (D,), 0.5, 3.0, ((0, 4),)),
        "prefix_embed": noise(key_list[15], (PRE, D), 1.0, 6.0),
        "reparam_in": noise(key_list[16], (D, PH), D ** -0.5, 0.1875),
        "reparam_in_bias": noise(key_list[17], (PH,), 0.5, 3.0),
        "reparam_out": noise(key_list[18], (PH, H, 2 * HD), PH ** -0.5, 0.25, ((1, 4),)),
        "reparam_out_bias": noise(key_list[19], (H, 2 * HD), 0.5, 3.0, ((0, 4),)),
    }


@jax.custom_vjp
def low(v):
    return lax.optimization_barrier(v.astype(jnp.bfloat16)).astype(jnp.float32)

@jax.custom_vjp
def low_back(v):
    return v

def low_keep(v):
    return (low(v), None)

def low_pass(kept, grad):
    return (grad,)

def back_keep(v):
    return (v, None)

def back_low(kept, grad):
    return (low(grad),)
low.defvjp(low_keep, low_pass)
low_back.defvjp(back_keep, back_low)
HIGHEST = lax.Precision.HIGHEST
EPS = 1e-05
NEGATIVE = -1e+30

def layer_norm(values, gain, shift):
    mean = lax.optimization_barrier(jnp.mean(values, -1, keepdims=True))
    centered = values - mean
    spread = lax.optimization_barrier(jnp.mean(centered * centered, -1, keepdims=True))
    return centered * lax.rsqrt(spread + EPS) * gain + shift

def attend_rows(query_block, doc_block, place_block, key_all, value_all, documents, places):
    prefix_count = key_all.shape[0] - documents.shape[0]
    scores = jnp.einsum('qhd,khd->hqk', query_block, key_all, precision=HIGHEST) * HD ** (-0.5)
    scores = low_back(scores)
    token_mask = (doc_block[:, None] == documents[None, :]) & (places[None, :] <= place_block[:, None])
    mask = jnp.concatenate([jnp.ones((doc_block.shape[0], prefix_count), bool), token_mask], 1)
    scores = jnp.where(mask[None], scores, NEGATIVE)
    probs = low(jax.nn.softmax(scores, -1))
    return jnp.einsum('hqk,khd->qhd', probs, value_all, precision=HIGHEST)

def forward(segment_ids, tokens, ln1_gain, ln1_bias, w_qkv, b_qv, w_out, b_out, ln2_gain, ln2_bias, w_up, b_up, w_down, b_down, prefix_embed, reparam_in, reparam_in_bias, reparam_out, reparam_out_bias):
    count = tokens.shape[0]
    normed1 = low(layer_norm(tokens, ln1_gain, ln1_bias))
    mixed = jnp.einsum('td,dhe->the', normed1, w_qkv, precision=HIGHEST)
    query = low(low_back(mixed[..., :HD] + b_qv[:, :HD]))
    key_rows = low(low_back(mixed[..., HD:2 * HD]))
    value_rows = low(low_back(mixed[..., 2 * HD:] + b_qv[:, HD:]))
    prefix_hidden = jnp.tanh(jnp.dot(prefix_embed, reparam_in, precision=HIGHEST) + reparam_in_bias)
    prefix_pair = jnp.einsum('pa,ahe->phe', prefix_hidden, reparam_out, precision=HIGHEST) + reparam_out_bias
    prefix_pair = low(low_back(prefix_pair))
    key_all = jnp.concatenate([prefix_pair[..., :HD], key_rows], 0)
    value_all = jnp.concatenate([prefix_pair[..., HD:], value_rows], 0)
    places = jnp.arange(count, dtype=jnp.int32)
    block = math.gcd(count, 512)
    groups = count // block

    def one_block(inputs):
        return attend_rows(inputs[0], inputs[1], inputs[2], key_all, value_all, segment_ids, places)
    attended = lax.map(jax.checkpoint(one_block), (query.reshape(groups, block, H, HD), segment_ids.reshape(groups, block), places.reshape(groups, block)))
    attended = low(low_back(attended.reshape(count, H, HD)))
    branch = low_back(jnp.einsum('the,hed->td', attended, w_out, precision=HIGHEST))
    middle = tokens + branch + b_out
    normed2 = low(layer_norm(middle, ln2_gain, ln2_bias))
    hidden_pre = low_back(jnp.dot(normed2, w_up, precision=HIGHEST) + b_up)
    hidden_act = low(jax.nn.gelu(hidden_pre, approximate=True))
    return middle + jnp.dot(hidden_act, w_down, precision=HIGHEST) + b_down

def reference(tokens, segment_ids, out_grad, ln1_gain, ln1_bias, w_qkv, b_qv, w_out, b_out, ln2_gain, ln2_bias, w_up, b_up, w_down, b_down, prefix_embed, reparam_in, reparam_in_bias, reparam_out, reparam_out_bias):
    floats = [a.astype(jnp.float32) for a in (tokens, ln1_gain, ln1_bias, w_qkv, b_qv, w_out, b_out, ln2_gain, ln2_bias, w_up, b_up, w_down, b_down, prefix_embed, reparam_in, reparam_in_bias, reparam_out, reparam_out_bias)]
    result, pullback = jax.vjp(functools.partial(forward, segment_ids), *floats)
    grads = pullback(out_grad.astype(jnp.float32))
    return (result.astype(jnp.bfloat16), grads[0].astype(jnp.bfloat16), grads[1], grads[2], grads[3], grads[4], grads[5], grads[6], grads[7], grads[8], grads[9], grads[10], grads[11], grads[12], grads[13], grads[14], grads[15], grads[16], grads[17])
```

```python
import functools

import jax
import jax.numpy as jnp
from jax import lax
from jax.experimental import pallas as pl
from jax.experimental.pallas import tpu as pltpu
from jax.sharding import PartitionSpec as P

EPS = 1e-05
NEGATIVE = -1e30
HIGHEST = lax.Precision.HIGHEST
F32 = jnp.float32
BF16 = jnp.bfloat16
LANES = 128
PAD = 16
WEAK = 1e-24
DOCS = 5

VM = pl.BlockSpec(memory_space=pltpu.VMEM)
SM = pl.BlockSpec(memory_space=pltpu.SMEM)


def gelu_tanh(values):
    return jax.nn.gelu(values, approximate=True)


def contract(first, second, first_dim, second_dim):
    return lax.dot_general(
        first, second, (((first_dim,), (second_dim,)), ((), ())), preferred_element_type=F32
    )


def work(queries, keys, products):
    pairs = queries * keys // 2
    return pl.CostEstimate(
        flops=2 * 256 * products * pairs, bytes_accessed=8 * 2**20, transcendentals=pairs
    )


def after(values, other):
    return lax.optimization_barrier((values, other))[0]


def document_start(meta, place):
    found = jnp.zeros_like(place) if getattr(place, "shape", ()) else jnp.int32(0)
    for number in range(DOCS - 1):
        begin = meta[number]
        found = jnp.where(place >= begin, jnp.maximum(found, begin), found)
    return found


def query_places(meta, index, base, chunk, group):
    return base + (index // chunk) * (chunk * group) + meta[DOCS - 1] * chunk + index % chunk


def tile_bounds(meta, base, count, chunk, group):
    rank = meta[DOCS - 1]
    first = base + rank * chunk
    last = base + (count // chunk - 1) * (chunk * group) + rank * chunk + chunk - 1
    return first, last, document_start(meta, first), document_start(meta, last)


def one_row(rows, columns):
    return lax.broadcasted_iota(jnp.int32, (rows, columns), 0) == 0


def over_keys(bounds, keys, block):
    first, last, low, low_last = bounds

    def step(number, _):
        clear = (number * keys >= low_last) & ((number + 1) * keys - 1 <= first)

        @pl.when(clear)
        def _():
            block(number, False)

        @pl.when(jnp.logical_not(clear))
        def _():
            block(number, True)

        return 0

    lax.fori_loop(low // keys, last // keys + 1, step, 0)


def allowed(meta, number, keys, places):
    key = number * keys + lax.broadcasted_iota(jnp.int32, (keys, 1), 0)
    return (key <= places) & (key >= document_start(meta, places))


def forward_kernel(
    meta, query, key, value, pre_key, pre_value,
    out_low, out_full, log_total,
    key_rows, value_ones, accum, peak,
    *, tile, keys, prefix, chunk, group,
):
    sources, size, length = key.shape
    blocks, _, width = query.shape
    per, parts = width // tile, length // keys
    scale = size**-0.5
    padded = pre_key.shape[1]

    def extended(values, count, total):
        ones = jnp.where(one_row(PAD, count), 1.0, 0.0).astype(BF16)
        rest = total - size - PAD
        tail = [jnp.zeros((rest, count), BF16)] if rest else []
        return jnp.concatenate([values, ones] + tail, 0)

    def longest(values):
        wide = values.astype(F32)
        return jnp.max(jnp.sum(wide * wide, 0, keepdims=True), 1, keepdims=True)

    def prepare(source, most):
        rows = pl.ds(pl.multiple_of(source * length, length), length)
        key_rows[rows, :] = extended(key[source], length, LANES).astype(F32).T.astype(BF16)
        value_ones[source] = extended(value[source], length, size + PAD)
        return jnp.maximum(most, longest(key[source]))

    most = jnp.sqrt(lax.fori_loop(0, sources, prepare, longest(pre_key[...])))
    pre_key_ones = extended(pre_key[...], padded, LANES)
    pre_value_ones = extended(pre_value[...], padded, size + PAD)
    pre_row = lax.broadcasted_iota(jnp.int32, (padded, tile), 0)

    def query_tile(number, _):
        source, part = number // per, number % per
        base = number * tile * group
        columns = pl.ds(pl.multiple_of(part * tile, tile), tile)
        scaled = query[source, :, columns].astype(F32) * scale
        limit = jnp.sqrt(jnp.sum(scaled * scaled, 0, keepdims=True)) * most
        limit = limit.astype(BF16).astype(F32)
        shifted = jnp.concatenate(
            [
                scaled,
                jnp.where(one_row(PAD, tile), -limit, 0.0),
                jnp.zeros((LANES - size - PAD, tile), F32),
            ],
            0,
        ).astype(BF16)
        index = lax.broadcasted_iota(jnp.int32, (1, tile), 1)
        places = query_places(meta, index, base, chunk, group)
        bounds = tile_bounds(meta, base, tile, chunk, group)

        weights = jnp.where(pre_row < prefix, jnp.exp(contract(pre_key_ones, shifted, 0, 0)), 0.0)
        accum[...] = contract(pre_value_ones, weights.astype(BF16), 1, 0)

        def block(number, masked):
            rows = pl.ds(pl.multiple_of(number * keys, keys), keys)
            lanes = pl.ds(pl.multiple_of((number % parts) * keys, keys), keys)
            weights = jnp.exp(contract(key_rows[rows, :], shifted, 1, 0))
            if masked:
                weights = jnp.where(allowed(meta, number, keys, places), weights, 0.0)
            accum[...] += contract(value_ones[number // parts, :, lanes], weights.astype(BF16), 1, 0)

        over_keys(bounds, keys, block)
        peak[...] = limit

        @pl.when(jnp.min(accum[size : size + 1, :]) < WEAK)
        def _():
            plain = scaled.astype(BF16)

            def fold(scores, mask, values):
                scores = jnp.where(mask, scores, NEGATIVE)
                new = jnp.maximum(peak[...], jnp.max(scores, 0, keepdims=True))
                weights = jnp.where(mask, jnp.exp(scores - new), 0.0).astype(BF16)
                accum[...] = accum[...] * jnp.exp(peak[...] - new) + contract(values, weights, 1, 0)
                peak[...] = new

            peak[...] = jnp.full(peak.shape, NEGATIVE, F32)
            accum[...] = jnp.zeros(accum.shape, F32)
            fold(contract(pre_key[...], plain, 0, 0), pre_row < prefix, pre_value_ones)

            def slow(number, masked):
                rows = pl.ds(pl.multiple_of(number * keys, keys), keys)
                lanes = pl.ds(pl.multiple_of((number % parts) * keys, keys), keys)
                scores = contract(key_rows[rows, :][:, :size], plain, 1, 0)
                fold(
                    scores,
                    allowed(meta, number, keys, places),
                    value_ones[number // parts, :, lanes],
                )

            def step(number, _):
                slow(number, True)
                return 0

            lax.fori_loop(bounds[2] // keys, bounds[1] // keys + 1, step, 0)

        total = accum[size : size + 1, :]
        result = accum[:size, :] / total
        log_total[number] = peak[...] + jnp.log(total)
        for part in range(tile // LANES):
            piece = result[:, part * LANES : (part + 1) * LANES]
            out_full[number * (tile // LANES) + part] = piece
            out_low[number * (tile // LANES) + part] = piece.astype(BF16)
        return 0

    lax.fori_loop(0, blocks * per, query_tile, 0)


def attend_forward(meta, query, key, value, pre_key, pre_value, tile, keys, prefix, chunk, group):
    sources, size, length = key.shape
    count = query.shape[0] * query.shape[2]
    return pl.pallas_call(
        functools.partial(
            forward_kernel, tile=tile, keys=keys, prefix=prefix, chunk=chunk, group=group
        ),
        out_shape=(
            jax.ShapeDtypeStruct((count // LANES, size, LANES), BF16),
            jax.ShapeDtypeStruct((count // LANES, size, LANES), F32),
            jax.ShapeDtypeStruct((count // tile, 1, tile), F32),
        ),
        in_specs=[SM] + [VM] * 5,
        out_specs=(VM, VM, VM),
        scratch_shapes=[
            pltpu.VMEM((sources * length, LANES), BF16),
            pltpu.VMEM((sources, size + PAD, length), BF16),
            pltpu.VMEM((size + PAD, tile), F32),
            pltpu.VMEM((1, tile), F32),
        ],
        compiler_params=pltpu.CompilerParams(vmem_limit_bytes=48 * 2**20),
        cost_estimate=work(count, sources * length, 2),
        name="attend_forward",
    )(meta, query, key, value, pre_key, pre_value)


def backward_kernel(
    meta, query, key, value, pre_key, pre_value, grad_out, out_full, log_total,
    grad_query, grad_keep, grad_prefix,
    key_rows, value_rows, key_sum, value_sum, query_sum,
    *, tile, keys, prefix, chunk, group,
):
    sources, size, length = key.shape
    blocks, _, width = query.shape
    per, parts = width // tile, length // keys
    scale = size**-0.5
    count = tile // LANES
    rank = meta[DOCS - 1]

    def prepare(source, _):
        rows = pl.ds(pl.multiple_of(source * length, length), length)
        key_rows[rows, :] = key[source].astype(F32).T.astype(BF16)
        value_rows[rows, :] = value[source].astype(F32).T.astype(BF16)
        key_sum[rows, :] = jnp.zeros((length, size), F32)
        value_sum[rows, :] = jnp.zeros((length, size), F32)
        return 0

    lax.fori_loop(0, sources, prepare, 0)
    grad_prefix[...] = jnp.zeros(grad_prefix.shape, F32)
    pre_row = lax.broadcasted_iota(jnp.int32, (pre_key.shape[0], tile), 0)

    def query_tile(number, _):
        source, part = number // per, number % per
        base = number * tile * group
        columns = pl.ds(pl.multiple_of(part * tile, tile), tile)
        scaled = (query[source, :, columns].astype(F32) * scale).astype(BF16)
        pieces = [number * count + piece for piece in range(count)]
        grad = jnp.concatenate([grad_out[piece] for piece in pieces], 1)
        full = jnp.concatenate([out_full[piece] for piece in pieces], 1)
        delta = jnp.sum(grad.astype(F32) * full, 0, keepdims=True)
        level = log_total[number]
        index = lax.broadcasted_iota(jnp.int32, (1, tile), 1)
        places = query_places(meta, index, base, chunk, group)
        bounds = tile_bounds(meta, base, tile, chunk, group)

        probs = jnp.exp(contract(pre_key[...], scaled, 1, 0) - level)
        probs = jnp.where(pre_row < prefix, probs, 0.0)
        slope = (probs * (contract(pre_value[...], grad, 1, 0) - delta)).astype(BF16)
        grad_prefix[0] += contract(slope, scaled, 1, 1)
        grad_prefix[1] += contract(probs.astype(BF16), grad, 1, 1)
        query_sum[...] = contract(pre_key[...], slope, 0, 0)

        def block(number, masked):
            rows = pl.ds(pl.multiple_of(number * keys, keys), keys)
            lanes = pl.ds(pl.multiple_of((number % parts) * keys, keys), keys)
            probs = jnp.exp(contract(key_rows[rows, :], scaled, 1, 0) - level)
            if masked:
                probs = jnp.where(allowed(meta, number, keys, places), probs, 0.0)
            slope = contract(value_rows[rows, :], grad, 1, 0)
            slope = (probs * (slope - delta)).astype(BF16)
            value_sum[rows, :] += contract(probs.astype(BF16), grad, 1, 1)
            key_sum[rows, :] += contract(slope, scaled, 1, 1)
            query_sum[...] += contract(key[number // parts, :, lanes], slope, 1, 0)

        over_keys(bounds, keys, block)
        grad_query[source, :, columns] = (query_sum[...] * scale).astype(BF16)
        return 0

    lax.fori_loop(0, blocks * per, query_tile, 0)
    key_slot = rank if group == 2 else 0
    value_slot = 1 - rank if group == 2 else 1

    def flush(source, _):
        rows = pl.ds(pl.multiple_of(source * length, length), length)
        grad_keep[key_slot, source] = key_sum[rows, :].T.astype(BF16)
        grad_keep[value_slot, source] = value_sum[rows, :].T.astype(BF16)
        return 0

    lax.fori_loop(0, sources, flush, 0)


def attend_backward(
    meta, query, key, value, pre_key, pre_value, grad_out, out_full, log_total,
    tile, keys, prefix, chunk, group,
):
    sources, size, length = key.shape
    return pl.pallas_call(
        functools.partial(
            backward_kernel, tile=tile, keys=keys, prefix=prefix, chunk=chunk, group=group
        ),
        out_shape=(
            jax.ShapeDtypeStruct(query.shape, BF16),
            jax.ShapeDtypeStruct((2,) + key.shape, BF16),
            jax.ShapeDtypeStruct((2,) + pre_key.shape, F32),
        ),
        in_specs=[SM] + [VM] * 8,
        out_specs=(VM, VM, VM),
        scratch_shapes=[
            pltpu.VMEM((sources * length, size), BF16),
            pltpu.VMEM((sources * length, size), BF16),
            pltpu.VMEM((sources * length, size), F32),
            pltpu.VMEM((sources * length, size), F32),
            pltpu.VMEM((size, tile), F32),
        ],
        compiler_params=pltpu.CompilerParams(vmem_limit_bytes=56 * 2**20),
        cost_estimate=work(query.shape[0] * query.shape[2], sources * length, 5),
        name="attend_backward",
    )(meta, query, key, value, pre_key, pre_value, grad_out, out_full, log_total)


def turn_kernel(*refs):
    count = len(refs) // 2
    for source, target in zip(refs[:count], refs[count:]):
        target[...] = source[...].astype(F32).T.astype(BF16)


def turned(*arrays):
    return pl.pallas_call(
        turn_kernel,
        out_shape=tuple(jax.ShapeDtypeStruct(a.shape[::-1], BF16) for a in arrays),
        in_specs=[VM] * len(arrays),
        out_specs=(VM,) * len(arrays),
        compiler_params=pltpu.CompilerParams(vmem_limit_bytes=32 * 2**20),
        name="turned",
    )(*arrays)


def project_kernel(rows, columns, weight, bias, full, sent, stats, *, heads, size, step):
    length = rows.shape[1]
    pieces = length // step
    half = step // 2
    width = length // 2
    for piece in range(pieces):
        lanes = slice(piece * step, (piece + 1) * step)
        values = rows[:, lanes].astype(F32)
        mean = jnp.mean(values, 0, keepdims=True)
        centered = values - mean
        inverse = lax.rsqrt(jnp.mean(centered * centered, 0, keepdims=True) + EPS)
        stats[0:1, lanes] = mean
        stats[1:2, lanes] = inverse
        low = (centered * inverse * columns[:, 0:1] + columns[:, 1:2]).astype(BF16)
        full[:, lanes] = low
        mixed = (contract(weight[...], low, 1, 0) + bias[...]).astype(BF16)
        for head in range(heads):
            part = mixed[head * 3 * size : (head + 1) * 3 * size]
            spot = slice(piece * half, (piece + 1) * half)
            sent[2 * head, :, spot] = part[:size, :half]
            sent[2 * head + 1, :, spot] = part[:size, half:]
            spot = slice(width + piece * step, width + (piece + 1) * step)
            sent[2 * head, :, spot] = part[size : 2 * size]
            sent[2 * head + 1, :, spot] = part[2 * size :]


def project(rows, columns, weight, bias, heads, size, step):
    width, length = rows.shape
    return pl.pallas_call(
        functools.partial(project_kernel, heads=heads, size=size, step=step),
        out_shape=(
            jax.ShapeDtypeStruct((width, length), BF16),
            jax.ShapeDtypeStruct((2 * heads, size, length // 2 * 3), BF16),
            jax.ShapeDtypeStruct((2, length), F32),
        ),
        in_specs=[VM] * 4,
        out_specs=(VM, VM, VM),
        compiler_params=pltpu.CompilerParams(vmem_limit_bytes=40 * 2**20),
        name="project",
    )(rows, columns, weight, bias)


def unproject_kernel(
    slot, came, weight, rows, stats, columns, own_grad,
    flat, part, row_sums, sums, head_sums,
    *, heads, size, step,
):
    length = rows.shape[1]
    half = step // 2
    width = length // 2
    gain = columns[:, 0:1]
    sums[...] = jnp.zeros(sums.shape, F32)
    head_sums[...] = jnp.zeros(head_sums.shape, F32)
    for piece in range(length // step):
        lanes = slice(piece * step, (piece + 1) * step)
        spot = slice(piece * half, (piece + 1) * half)
        pair = slice(width + piece * step, width + (piece + 1) * step)
        pieces = []
        for head in range(heads):
            first, second = came[2 * head], came[2 * head + 1]
            pieces.append(jnp.concatenate([first[:, spot], second[:, spot]], 1))
            pieces += [first[:, pair], second[:, pair]]
        grads = jnp.concatenate(pieces, 0)
        flat[:, lanes] = grads
        head_sums[...] += jnp.sum(grads.astype(F32), 1, keepdims=True)
        back = contract(weight[...], grads, 1, 0)
        part[:, lanes] = back.astype(BF16)

        @pl.when(slot[0] == piece)
        def _():
            part[:, lanes] = (back + own_grad[...] / (stats[1:2, lanes] * gain)).astype(BF16)

        normed = (rows[:, lanes].astype(F32) - stats[0:1, lanes]) * stats[1:2, lanes]
        scaled = back * gain
        row_sums[0:1, lanes] = jnp.sum(scaled, 0, keepdims=True)
        row_sums[1:2, lanes] = jnp.sum(scaled * normed, 0, keepdims=True)
        sums[:, 0:1] += jnp.sum(back * normed, 1, keepdims=True)
        sums[:, 1:2] += jnp.sum(back, 1, keepdims=True)


def unproject(slot, came, weight, rows, stats, columns, own_grad, heads, size, step):
    width, length = rows.shape
    return pl.pallas_call(
        functools.partial(unproject_kernel, heads=heads, size=size, step=step),
        out_shape=(
            jax.ShapeDtypeStruct((3 * heads * size, length), BF16),
            jax.ShapeDtypeStruct((width, length), BF16),
            jax.ShapeDtypeStruct((2, length), F32),
            jax.ShapeDtypeStruct((width, 2), F32),
            jax.ShapeDtypeStruct((3 * heads * size, 1), F32),
        ),
        in_specs=[SM] + [VM] * 6,
        out_specs=(VM,) * 5,
        compiler_params=pltpu.CompilerParams(vmem_limit_bytes=40 * 2**20),
        name="unproject",
    )(slot, came, weight, rows, stats, columns, own_grad)


def finish_kernel(up, down, own_up, own_down, rows, gain, stats, row_sums, grad):
    half = up.shape[0]
    mean, inverse = stats[0:1], stats[1:2]
    first, second = row_sums[0:1], row_sums[1:2]
    for start, came, own in ((0, up, own_up), (half, down, own_down)):
        spot = slice(start, start + half)
        total = came[...].astype(F32) + own[...].astype(F32)
        normed = (rows[spot].astype(F32) - mean) * inverse
        back = inverse * (gain[spot] * total - first - normed * second)
        grad[:, spot] = back.T.astype(BF16)


def finish(up, down, own_up, own_down, rows, gain, stats, row_sums):
    return pl.pallas_call(
        finish_kernel,
        out_shape=jax.ShapeDtypeStruct(rows.shape[::-1], BF16),
        in_specs=[VM] * 8,
        out_specs=VM,
        compiler_params=pltpu.CompilerParams(vmem_limit_bytes=32 * 2**20),
        name="finish",
    )(up, down, own_up, own_down, rows, gain, stats, row_sums)


def feed_kernel(rows, grads, up_turned, up, down, bias, hidden, grad_pre, part):
    pre = contract(up_turned[...], rows[0], 1, 0) + bias[...]
    act, pull = jax.vjp(gelu_tanh, pre)
    hidden[0] = act.astype(BF16)
    low = pull(contract(down[...], grads[0], 1, 0))[0].astype(BF16)
    grad_pre[0] = low
    part[0] = contract(up[...], low, 1, 0).astype(BF16)


def feed(rows, grads, up_turned, up, down, bias):
    blocks, width, count = rows.shape
    inner = down.shape[0]

    def whole(shape):
        return pl.BlockSpec(shape, lambda i: (0,) * len(shape), pipeline_mode=pl.Buffered(1))

    def block(size):
        return pl.BlockSpec((1, size, count), lambda i: (i, 0, 0))

    return pl.pallas_call(
        feed_kernel,
        grid=(blocks,),
        out_shape=(
            jax.ShapeDtypeStruct((blocks, inner, count), BF16),
            jax.ShapeDtypeStruct((blocks, inner, count), BF16),
            jax.ShapeDtypeStruct((blocks, width, count), BF16),
        ),
        in_specs=[
            block(width),
            block(width),
            whole((inner, width)),
            whole((width, inner)),
            whole((inner, width)),
            whole((inner, 1)),
        ],
        out_specs=(block(inner), block(inner), block(width)),
        compiler_params=pltpu.CompilerParams(vmem_limit_bytes=32 * 2**20),
        cost_estimate=pl.CostEstimate(
            flops=6 * blocks * width * inner * count, bytes_accessed=2**24, transcendentals=0
        ),
        name="feed",
    )(rows, grads, up_turned, up, down, bias)


def feed_rest_kernel(
    slot, rows, grads, hidden, grad_pre, down_turned, middle, columns,
    weights, bias, out, *, square,
):
    blocks, width, _ = rows.shape
    inner = hidden.shape[1]
    features = out.shape[2]
    step = min(256, inner)
    pairs = [(hidden, grads), (rows, grad_pre) if square else (grad_pre, rows)]
    for which, (first, second) in enumerate(pairs):
        for start in range(0, inner, step):
            spot = slice(start, start + step)
            weights[which, spot] = sum(
                contract(first[n, spot], second[n], 1, 1) for n in range(blocks)
            ).astype(BF16)
    bias[...] = sum(jnp.sum(grad_pre[n].astype(F32), 1, keepdims=True) for n in range(blocks))
    for n in range(blocks):
        result = contract(down_turned[...], hidden[n], 1, 0)

        def put(values):
            for block in range(out.shape[0]):
                out[block, n] = values[block * features : (block + 1) * features].astype(BF16)

        put(result)

        @pl.when(slot[0] == n)
        def _():
            put(result + middle[...] + columns[:, 5:6])


def feed_rest(slot, rows, grads, hidden, grad_pre, down_turned, middle, columns):
    blocks, width, count = rows.shape
    inner = hidden.shape[1]
    return pl.pallas_call(
        functools.partial(feed_rest_kernel, square=inner == width),
        out_shape=(
            jax.ShapeDtypeStruct((2, inner, width), BF16),
            jax.ShapeDtypeStruct((inner, 1), F32),
            jax.ShapeDtypeStruct((blocks, blocks, width // blocks, count), BF16),
        ),
        in_specs=[SM] + [VM] * 7,
        out_specs=(VM,) * 3,
        compiler_params=pltpu.CompilerParams(vmem_limit_bytes=48 * 2**20),
        cost_estimate=pl.CostEstimate(
            flops=6 * blocks * width * inner * count, bytes_accessed=2**24, transcendentals=0
        ),
        name="feed_rest",
    )(slot, rows, grads, hidden, grad_pre, down_turned, middle, columns)


def spread(values, axis):
    count = lax.axis_size(axis)
    copies = jnp.broadcast_to(values[None], (count,) + values.shape)
    return lax.all_to_all(copies, axis, 0, 0, tiled=True)


def small_sum(values, axis):
    return jnp.sum(spread(values, axis), 0)


def ring(axis, by):
    count = lax.axis_size(axis)
    return [(source, (source + by) % count) for source in range(count)]


def ring_gather(values, axis):
    count, place = lax.axis_size(axis), lax.axis_index(axis)
    half = values.shape[0] // 2
    up, down = values[:half], values[half:]
    out = jnp.zeros((count,) + values.shape, values.dtype)
    out = lax.dynamic_update_slice_in_dim(out, values[None], place, 0)
    zeros = (0,) * (values.ndim - 1)
    for step in range(1, count):
        up = lax.ppermute(up, axis, ring(axis, 1))
        down = lax.ppermute(down, axis, ring(axis, -1))
        out = lax.dynamic_update_slice(out, up[None], ((place - step) % count, 0) + zeros)
        out = lax.dynamic_update_slice(out, down[None], ((place + step) % count, half) + zeros)
    return out


def ring_terms(blocks, axis):
    count, place = lax.axis_size(axis), lax.axis_index(axis)
    half = blocks.shape[1] // 2

    def own(offset, upper):
        block = lax.dynamic_index_in_dim(blocks, (place + offset) % count, 0, keepdims=False)
        return block[half:] if upper else block[:half]

    up, down = own(-1, False), own(1, True)
    for step in range(1, count):
        up = lax.ppermute(up, axis, ring(axis, 1))
        down = lax.ppermute(down, axis, ring(axis, -1))
        if step < count - 1:
            up = (up.astype(F32) + own(-1 - step, False).astype(F32)).astype(BF16)
            down = (down.astype(F32) + own(1 + step, True).astype(F32)).astype(BF16)
    return up, down, own(0, False), own(0, True)


def ring_sum(blocks, axis):
    up, down, own_up, own_down = [a.astype(F32) for a in ring_terms(blocks, axis)]
    return jnp.concatenate([up + own_up, down + own_down], 0)


def swapped(values):
    pairs = [(source, source ^ 1) for source in range(lax.axis_size("seq"))]
    return lax.ppermute(values, "seq", pairs)


def chip_groups():
    chips = lax.axis_size("seq") // 2
    return [[2 * chip + core for chip in range(chips)] for core in range(2)]


def core_halves(values):
    core = lax.axis_index("seq") % 2
    halves = values.reshape(2, values.shape[0] // 2, values.shape[1])
    mine = lax.dynamic_index_in_dim(halves, core, 0, keepdims=False)
    other = lax.dynamic_index_in_dim(halves, 1 - core, 0, keepdims=False)
    return (mine.astype(F32) + swapped(other).astype(F32)).astype(BF16)


def chip_parts(half):
    chips = lax.axis_size("seq") // 2
    blocks = half.reshape(chips, half.shape[0] // chips, half.shape[1])
    return lax.all_to_all(blocks, "seq", 0, 0, axis_index_groups=chip_groups(), tiled=True)


def chip_gather(parts):
    part = jnp.sum(parts.astype(F32), 0).astype(BF16)
    copies = jnp.broadcast_to(part[None], parts.shape)
    half = lax.all_to_all(copies, "seq", 0, 0, axis_index_groups=chip_groups(), tiled=True)
    return half.reshape(-1, half.shape[2])


def core_gather(half):
    core = lax.axis_index("seq") % 2
    other = swapped(half)
    first = jnp.where(core == 0, half, other)
    second = jnp.where(core == 0, other, half)
    return first, second


def regrouped(values, width):
    count, size, columns = values.shape
    if width == columns:
        return values
    if width > columns:
        merged = values.reshape(-1, width // columns, size, columns).transpose(0, 2, 1, 3)
        return merged.reshape(-1, size, width)
    cut = values.reshape(count, size, columns // width, width).transpose(0, 2, 1, 3)
    return cut.reshape(-1, size, width)


def group_gather(pieces, group):
    if group == 2:
        rank = lax.axis_index("seq") % 2
        other = swapped(pieces)
        return jnp.stack([jnp.where(rank == 0, pieces, other), jnp.where(rank == 0, other, pieces)])
    count = lax.axis_size("seq")
    groups = [[first + i for i in range(group)] for first in range(0, count, group)]
    return lax.all_gather(pieces, "seq", axis_index_groups=groups)


def on_device(
    tokens,
    segment_ids,
    out_grad,
    ln1_gain,
    ln1_bias,
    w_qkv,
    b_qv,
    w_out,
    b_out,
    ln2_gain,
    ln2_bias,
    w_up,
    b_up,
    w_down,
    b_down,
    prefix_embed,
    reparam_in,
    reparam_in_bias,
    reparam_out,
    reparam_out_bias,
):
    rows, features = tokens.shape
    heads = w_qkv.shape[1]
    size = w_qkv.shape[2] // 3
    inner = w_up.shape[1]
    seqs, tensors = lax.axis_size("seq"), lax.axis_size("tensor")
    width = features * tensors
    own_rows = rows // tensors
    group = seqs // heads
    chunk = own_rows // group
    place, slot = lax.axis_index("seq"), lax.axis_index("tensor")
    head, rank = place // group, place % group
    prefix = prefix_embed.shape[0]
    tokens_head = rows // group
    query_width = max(tokens_head, LANES)
    forward_tile = min(512, query_width)
    backward_tile = min(256, query_width)
    forward_keys, backward_keys = 512, 1024
    both = ("seq", "tensor")
    paired = group == 2 and chunk == LANES

    own_tokens, own_grads = turned(tokens, out_grad)
    full_tokens = ring_gather(own_tokens, "tensor").reshape(width, rows)
    numbers = jnp.arange(1, DOCS, dtype=jnp.int32)
    before = jnp.sum((segment_ids[None, :] < numbers[:, None]).astype(jnp.int32), 1)
    starts = small_sum(jnp.broadcast_to(before[:, None], (DOCS - 1, LANES)), "seq")[:, 0]
    meta = jnp.concatenate([starts, rank[None].astype(jnp.int32)])
    vectors = jnp.stack([ln1_gain, ln1_bias, ln2_gain, ln2_bias, b_out, b_down])
    share_rows = heads * size // seqs
    out_share = w_out.reshape(seqs, share_rows, width)
    out_share = lax.dynamic_index_in_dim(out_share, place, 0, keepdims=False)
    extra = -(-vectors.size // width)
    vectors = jnp.pad(vectors.reshape(-1), (0, extra * width - vectors.size))
    out_share = jnp.concatenate([out_share, vectors.reshape(extra, width)], 0)
    out_share = spread(out_share, "tensor")
    vectors = out_share[:, share_rows:].reshape(tensors, -1)[:, : 6 * features]
    columns = vectors.reshape(tensors, 6, features).transpose(0, 2, 1).reshape(width, 6).astype(F32)
    full_tokens, columns, meta, out_share = lax.optimization_barrier(
        (full_tokens, columns, meta, out_share[:, :share_rows])
    )
    out_share = spread(out_share, "seq")
    w_out_full = out_share.transpose(1, 0, 2, 3).reshape(width, width)
    gain2, shift2, bias_out = [columns[:, i : i + 1] for i in (2, 3, 4)]
    where_slot = slot[None].astype(jnp.int32)

    embed_float = prefix_embed.astype(F32)
    prefix_hidden = jnp.tanh(
        jnp.dot(prefix_embed, reparam_in, preferred_element_type=F32)
        + reparam_in_bias.astype(F32)
    )
    prefix_pair = jnp.einsum(
        "pa,ahe->phe", prefix_hidden, reparam_out.astype(F32), precision=HIGHEST
    )
    prefix_pair = (prefix_pair + reparam_out_bias.astype(F32)).astype(BF16)
    own_pair = lax.dynamic_index_in_dim(prefix_pair, head, 1, keepdims=False)
    own_pair = jnp.pad(own_pair, ((0, LANES - prefix), (0, 0)))
    pre_key, pre_value = own_pair[:, :size], own_pair[:, size:]

    w_flat = w_qkv.reshape(width, heads * 3 * size)
    bias_pair = b_qv.astype(F32)
    bias_three = jnp.stack(
        [bias_pair[:, :size], jnp.zeros((heads, size), F32), bias_pair[:, size:]], 1
    ).reshape(-1, 1)
    if paired:
        full1, sent, stats = project(
            full_tokens, columns, w_flat.T, bias_three, heads, size, own_rows
        )
    else:
        wide = full_tokens.astype(F32)
        mean = jnp.mean(wide, 0, keepdims=True)
        inverse = lax.rsqrt(jnp.mean((wide - mean) ** 2, 0, keepdims=True) + EPS)
        stats = jnp.concatenate([mean, inverse], 0)
        full1 = ((wide - mean) * inverse * columns[:, 0:1] + columns[:, 1:2]).astype(BF16)
        mixed = (contract(w_flat, full1, 0, 0) + bias_three).astype(BF16)
        mixed = mixed.reshape(heads, 3, size, rows)
        query_part = mixed[:, 0].reshape(heads, size, tensors, group, chunk)
        query_part = query_part.transpose(0, 3, 1, 2, 4).reshape(seqs, size, tokens_head)
        pair_part = mixed[:, 1:].transpose(0, 2, 1, 3).reshape(heads, size, group, 2 * tokens_head)
        pair_part = pair_part.transpose(0, 2, 1, 3).reshape(seqs, size, 2 * tokens_head)
        sent = jnp.concatenate([query_part, pair_part], 2)
    came = lax.all_to_all(sent, "seq", 0, 0, tiled=True)
    query, pair = came[:, :, :tokens_head], came[:, :, tokens_head:]
    query = regrouped(query, query_width)
    pair = group_gather(pair, group)
    if group == 2:
        key, value = pair[0], pair[1]
    else:
        pair = pair.transpose(1, 2, 0, 3).reshape(seqs, size, 2, rows)
        key, value = pair[:, :, 0], pair[:, :, 1]
    full_grad = lax.all_gather(after(own_grads, full_tokens), "tensor", axis=0, tiled=True)
    out_low, out_full, log_total = attend_forward(
        meta, query, key, value, pre_key.T, pre_value.T,
        forward_tile, forward_keys, prefix, chunk, group,
    )
    out_low, full_grad = lax.optimization_barrier((out_low, full_grad))

    came = lax.all_to_all(regrouped(out_low, chunk), both, 0, 0, tiled=True)
    came = came.reshape(heads, group, tensors, size, chunk).transpose(2, 0, 3, 1, 4)
    attended = came.reshape(width, own_rows)
    branch = contract(w_out_full, attended, 0, 0)
    own_block = lax.dynamic_slice_in_dim(full_tokens, slot * own_rows, own_rows, 1)
    middle = own_block.astype(F32) + branch + bias_out
    mean2 = jnp.mean(middle, 0, keepdims=True)
    centered = middle - mean2
    inverse2 = lax.rsqrt(jnp.mean(centered * centered, 0, keepdims=True) + EPS)
    normed2 = centered * inverse2
    out2 = (normed2 * gain2 + shift2).astype(BF16)

    full2 = ring_gather(out2, "tensor")
    grads = full_grad.reshape(width, tensors, own_rows).transpose(1, 0, 2)
    hidden, grad_pre, part = feed(
        full2, grads, w_up.T, w_up, w_down, b_up.astype(F32)[:, None]
    )
    feed_weights, grad_b_up, mlp_out = feed_rest(
        where_slot, full2, grads, hidden, grad_pre, w_down.T, middle, columns
    )
    core = place % 2
    feed_mine = lax.dynamic_index_in_dim(feed_weights, core, 0, keepdims=False)
    feed_other = lax.dynamic_index_in_dim(feed_weights, 1 - core, 0, keepdims=False)
    feed_half = (feed_mine.astype(F32) + swapped(feed_other).astype(F32)).astype(BF16)
    feed_parts = chip_parts(feed_half)
    grad_normed2 = ring_sum(part, "tensor")
    grad_normed2, feed_parts = lax.optimization_barrier((grad_normed2, feed_parts))

    scaled = grad_normed2 * gain2
    first = jnp.mean(scaled, 0, keepdims=True)
    second = jnp.mean(scaled * normed2, 0, keepdims=True)
    own_grad = lax.dynamic_index_in_dim(grads, slot, 0, keepdims=False)
    grad_middle = own_grad.astype(F32) + inverse2 * (scaled - first - normed2 * second)
    grad_branch = grad_middle.astype(BF16)
    grad_attended = contract(w_out_full, grad_branch, 1, 0).astype(BF16)
    sent = grad_attended.reshape(tensors, heads, size, group, chunk).transpose(1, 3, 0, 2, 4)
    came = lax.all_to_all(sent.reshape(seqs * tensors, size, chunk), both, 0, 0, tiled=True)
    grad_out = regrouped(came, LANES)

    token_sums = jnp.stack(
        [
            jnp.sum(grad_normed2 * normed2, 1),
            jnp.sum(grad_normed2, 1),
            jnp.sum(grad_middle, 1),
        ]
    )
    grad_w_out = contract(attended, grad_branch, 1, 1).astype(BF16)
    grad_out, mlp_out, grad_w_out, feed_parts = lax.optimization_barrier(
        (grad_out, mlp_out, grad_w_out, feed_parts)
    )
    feed_half = chip_gather(feed_parts)
    output_act = lax.psum_scatter(mlp_out, "tensor", scatter_dimension=0, tiled=True)
    grad_w_out = lax.psum_scatter(grad_w_out, "tensor", scatter_dimension=0, tiled=True)

    levels = log_total.reshape(-1, 1, backward_tile)
    grad_query, grad_pair, grad_prefix = attend_backward(
        meta, query, key, value, pre_key[:PAD], pre_value[:PAD], grad_out, out_full, levels,
        backward_tile, backward_keys, prefix, chunk, group,
    )
    grad_pair, output_act, grad_w_out, feed_half = lax.optimization_barrier(
        (grad_pair, output_act, grad_w_out, feed_half)
    )
    if group == 2:
        grad_share = (grad_pair[0].astype(F32) + swapped(grad_pair[1]).astype(F32)).astype(BF16)
    else:
        groups = [[first + i for i in range(group)] for first in range(0, seqs, group)]
        shares = grad_pair.transpose(1, 2, 0, 3).reshape(seqs, size, group, 2 * tokens_head)
        grad_share = lax.psum_scatter(
            shares.transpose(2, 0, 1, 3), "seq", axis_index_groups=groups
        )
    prefix_part = grad_prefix.transpose(2, 0, 1).reshape(size, 2 * PAD).astype(BF16)
    prefix_part = jnp.pad(prefix_part, ((0, 0), (0, LANES - 2 * PAD)))
    prefix_part = jnp.broadcast_to(prefix_part[None], (seqs, size, LANES))
    sent = jnp.concatenate([regrouped(grad_query, tokens_head), grad_share, prefix_part], 2)
    came = lax.all_to_all(sent, "seq", 0, 0, tiled=True)
    if paired:
        grad_flat, grad_part, row_sums, sums1, head_sums = unproject(
            where_slot, came, w_flat, full_tokens, stats, columns, grad_middle, heads, size, own_rows
        )
    else:
        query_part = came[:, :, :tokens_head].reshape(heads, group, size, tensors, chunk)
        query_part = query_part.transpose(0, 2, 3, 1, 4).reshape(heads, 1, size, rows)
        pair_part = came[:, :, tokens_head : 3 * tokens_head]
        pair_part = pair_part.reshape(heads, group, size, 2 * tokens_head).transpose(0, 2, 1, 3)
        pair_part = pair_part.reshape(heads, size, 2, rows).transpose(0, 2, 1, 3)
        grad_flat = jnp.concatenate([query_part, pair_part], 1).reshape(heads * 3 * size, rows)
        back = contract(w_flat, grad_flat, 1, 0)
        normed1 = (full_tokens.astype(F32) - stats[0]) * stats[1]
        scaled = back * columns[:, 0:1]
        row_sums = jnp.stack([jnp.sum(scaled, 0), jnp.sum(scaled * normed1, 0)])
        sums1 = jnp.stack([jnp.sum(back * normed1, 1), jnp.sum(back, 1)], 1)
        head_sums = jnp.sum(grad_flat.astype(F32), 1)
        own_inverse = lax.dynamic_slice_in_dim(stats[1:2], slot * own_rows, own_rows, 1)
        own_part = lax.dynamic_slice_in_dim(back, slot * own_rows, own_rows, 1)
        own_part = own_part + grad_middle / (own_inverse * columns[:, 0:1])
        back = lax.dynamic_update_slice_in_dim(back, own_part, slot * own_rows, 1)
        grad_part = back.astype(BF16)
    last_terms = ring_terms(grad_part.reshape(tensors, features, rows), "tensor")

    prefix_low = came[:, :, 3 * tokens_head : 3 * tokens_head + 2 * PAD].astype(F32)
    prefix_low = jnp.sum(prefix_low.reshape(heads, group, size, 2, PAD), 1)[..., :prefix]
    prefix_low = prefix_low.transpose(3, 0, 2, 1).reshape(prefix, heads, 2 * size).astype(BF16)
    prefix_grad = prefix_low.astype(F32)
    hidden_part = jnp.einsum("phe,ahe->pa", prefix_low, reparam_out, preferred_element_type=F32)
    owned = jnp.concatenate([sums1.T, token_sums], 0)
    owned = owned.reshape(-1, tensors, features).transpose(1, 0, 2).reshape(tensors, -1)
    shared = jnp.concatenate([row_sums.reshape(-1), hidden_part.reshape(-1)])
    shared = jnp.broadcast_to(shared[None], (tensors, shared.shape[0]))
    small = jnp.concatenate([owned, shared], 1)[:, None, :]
    small = jnp.sum(lax.all_to_all(small, "tensor", 0, 0, tiled=True), 0)[0]
    owned, row_sums = small[: 5 * features], small[5 * features : 5 * features + 2 * rows]
    hidden_grad = small[5 * features + 2 * rows :].reshape(prefix_hidden.shape)
    input_grad = finish(
        *last_terms, own_tokens, ln1_gain.astype(F32)[:, None], stats,
        row_sums.reshape(2, rows) / width,
    )
    output_act = output_act[0].transpose(0, 2, 1).reshape(rows, features)

    first_half, second_half = core_gather(feed_half)
    out_w_down = first_half.astype(F32)
    out_w_up = (second_half if inner == width else second_half.T).astype(F32)
    grad_w_qkv = contract(grad_flat, full1, 1, 1).astype(BF16)
    rest = jnp.concatenate([grad_w_qkv, grad_w_out], 0)
    rest_half = chip_gather(chip_parts(core_halves(rest)))
    rest = jnp.concatenate(core_gather(rest_half), 0).astype(F32)
    mixed_rows = heads * 3 * size
    out_w_qkv = rest[:mixed_rows].reshape(heads, 3 * size, width).transpose(2, 0, 1)
    out_w_out = rest[mixed_rows:].reshape(heads, size, width)

    grad_b_down = jnp.sum(out_grad.astype(F32), 0)
    head_sums = head_sums.reshape(heads, 3, size)
    late = jnp.concatenate(
        [
            owned,
            grad_b_down,
            grad_b_up.reshape(-1),
            head_sums[:, 0].reshape(-1),
            head_sums[:, 2].reshape(-1),
        ]
    )
    late = small_sum(late[None], "seq")[0]
    out_ln1_gain, out_ln1_bias, out_ln2_gain, out_ln2_bias, out_b_out, out_b_down = [
        late[i * features : (i + 1) * features] for i in range(6)
    ]
    late = late[6 * features :]
    out_b_up = late[:inner]
    pair_sums = late[inner:].reshape(2, heads, size)
    out_b_qv = jnp.concatenate([pair_sums[0], pair_sums[1]], 1)

    grad_reparam_out = jnp.einsum("pa,phe->ahe", prefix_hidden, prefix_grad, precision=HIGHEST)
    grad_reparam_out_bias = jnp.sum(prefix_grad, 0)
    grad_prefix_pre = hidden_grad * (1.0 - prefix_hidden * prefix_hidden)
    grad_reparam_in_bias = jnp.sum(grad_prefix_pre, 0)
    grad_reparam_in = jnp.einsum("pd,pa->da", embed_float, grad_prefix_pre, precision=HIGHEST)
    grad_prefix_embed = jnp.einsum(
        "pa,da->pd", grad_prefix_pre, reparam_in.astype(F32), precision=HIGHEST
    )
    return (
        output_act,
        input_grad,
        out_ln1_gain,
        out_ln1_bias,
        out_w_qkv,
        out_b_qv,
        out_w_out,
        out_b_out,
        out_ln2_gain,
        out_ln2_bias,
        out_w_up,
        out_b_up,
        out_w_down,
        out_b_down,
        grad_prefix_embed,
        grad_reparam_in,
        grad_reparam_in_bias,
        grad_reparam_out,
        grad_reparam_out_bias,
    )


def solution(mesh):
    placed = (
        P("seq", "tensor"),
        P("seq"),
        P("seq", "tensor"),
        P("tensor"),
        P("tensor"),
        P(None, "tensor", None),
        P("tensor", None),
        P("tensor", None, None),
        P("tensor"),
        P("tensor"),
        P("tensor"),
        P(None, "tensor"),
        P("tensor"),
        P("tensor", None),
        P("tensor"),
        P(),
        P(),
        P(),
        P(None, "tensor", None),
        P("tensor", None),
    )
    return jax.shard_map(
        on_device,
        mesh=mesh,
        in_specs=placed,
        out_specs=(
            P("seq", "tensor"),
            P("seq", "tensor"),
            P("tensor"),
            P("tensor"),
            P(None, "tensor", None),
            P("tensor", None),
            P("tensor", None, None),
            P("tensor"),
            P("tensor"),
            P("tensor"),
            P(None, "tensor"),
            P("tensor"),
            P("tensor", None),
            P("tensor"),
            P(),
            P(),
            P(),
            P(None, "tensor", None),
            P("tensor", None),
        ),
        check_vma=False,
    )
```

```python
import functools

import jax
import jax.numpy as jnp
from jax import lax
from jax.experimental import pallas as pl
from jax.experimental.pallas import tpu as pltpu
from jax.sharding import PartitionSpec as P

EPS = 1e-05
NEGATIVE = -1e30
HIGHEST = lax.Precision.HIGHEST
F32 = jnp.float32
BF16 = jnp.bfloat16
LANES = 128
PAD = 16
WEAK = 1e-24
DOCS = 5

VM = pl.BlockSpec(memory_space=pltpu.VMEM)
SM = pl.BlockSpec(memory_space=pltpu.SMEM)


def gelu_tanh(values):
    return jax.nn.gelu(values, approximate=True)


def contract(first, second, first_dim, second_dim):
    return lax.dot_general(
        first, second, (((first_dim,), (second_dim,)), ((), ())), preferred_element_type=F32
    )


def work(queries, keys, products):
    pairs = queries * keys // 2
    return pl.CostEstimate(
        flops=2 * 256 * products * pairs, bytes_accessed=8 * 2**20, transcendentals=pairs
    )


def after(values, other):
    return lax.optimization_barrier((values, other))[0]


def document_start(meta, place):
    found = jnp.zeros_like(place) if getattr(place, "shape", ()) else jnp.int32(0)
    for number in range(DOCS - 1):
        begin = meta[number]
        found = jnp.where(place >= begin, jnp.maximum(found, begin), found)
    return found


def query_places(meta, index, base, chunk, group):
    return base + (index // chunk) * (chunk * group) + meta[DOCS - 1] * chunk + index % chunk


def tile_bounds(meta, base, count, chunk, group):
    rank = meta[DOCS - 1]
    first = base + rank * chunk
    last = base + (count // chunk - 1) * (chunk * group) + rank * chunk + chunk - 1
    return first, last, document_start(meta, first), document_start(meta, last)


def one_row(rows, columns):
    return lax.broadcasted_iota(jnp.int32, (rows, columns), 0) == 0


def over_keys(bounds, keys, block):
    first, last, low, low_last = bounds

    def step(number, _):
        clear = (number * keys >= low_last) & ((number + 1) * keys - 1 <= first)

        @pl.when(clear)
        def _():
            block(number, False)

        @pl.when(jnp.logical_not(clear))
        def _():
            block(number, True)

        return 0

    lax.fori_loop(low // keys, last // keys + 1, step, 0)


def allowed(meta, number, keys, places):
    key = number * keys + lax.broadcasted_iota(jnp.int32, (keys, 1), 0)
    return (key <= places) & (key >= document_start(meta, places))


def forward_kernel(
    meta, query, key, value, pre_key, pre_value,
    out_low, out_full, log_total,
    key_rows, value_ones, accum, peak,
    *, tile, keys, prefix, chunk, group,
):
    sources, size, length = key.shape
    blocks, _, width = query.shape
    per = width // tile
    scale = size**-0.5
    padded = pre_key.shape[1]

    def extended(values, count, total):
        ones = jnp.where(one_row(PAD, count), 1.0, 0.0).astype(BF16)
        rest = total - size - PAD
        tail = [jnp.zeros((rest, count), BF16)] if rest else []
        return jnp.concatenate([values, ones] + tail, 0)

    def longest(values):
        wide = values.astype(F32)
        return jnp.max(jnp.sum(wide * wide, 0, keepdims=True), 1, keepdims=True)

    def prepare(source, most):
        rows = pl.ds(pl.multiple_of(source * length, length), length)
        key_rows[rows, :] = extended(key[source], length, LANES).astype(F32).T.astype(BF16)
        value_ones[:, rows] = extended(value[source], length, size + PAD)
        return jnp.maximum(most, longest(key[source]))

    most = jnp.sqrt(lax.fori_loop(0, sources, prepare, longest(pre_key[...])))
    pre_key_ones = extended(pre_key[...], padded, LANES)
    pre_value_ones = extended(pre_value[...], padded, size + PAD)
    pre_row = lax.broadcasted_iota(jnp.int32, (padded, tile), 0)

    def query_tile(number, _):
        source, part = number // per, number % per
        base = number * tile * group
        columns = pl.ds(pl.multiple_of(part * tile, tile), tile)
        scaled = query[source, :, columns].astype(F32) * scale
        limit = jnp.sqrt(jnp.sum(scaled * scaled, 0, keepdims=True)) * most
        limit = limit.astype(BF16).astype(F32)
        shifted = jnp.concatenate(
            [
                scaled,
                jnp.where(one_row(PAD, tile), -limit, 0.0),
                jnp.zeros((LANES - size - PAD, tile), F32),
            ],
            0,
        ).astype(BF16)
        index = lax.broadcasted_iota(jnp.int32, (1, tile), 1)
        places = query_places(meta, index, base, chunk, group)
        bounds = tile_bounds(meta, base, tile, chunk, group)

        weights = jnp.where(pre_row < prefix, jnp.exp(contract(pre_key_ones, shifted, 0, 0)), 0.0)
        accum[...] = contract(pre_value_ones, weights.astype(BF16), 1, 0)

        def block(number, masked):
            rows = pl.ds(pl.multiple_of(number * keys, keys), keys)
            weights = jnp.exp(contract(key_rows[rows, :], shifted, 1, 0))
            if masked:
                weights = jnp.where(allowed(meta, number, keys, places), weights, 0.0)
            accum[...] += contract(value_ones[:, rows], weights.astype(BF16), 1, 0)

        over_keys(bounds, keys, block)
        peak[...] = limit

        @pl.when(jnp.min(accum[size : size + 1, :]) < WEAK)
        def _():
            plain = scaled.astype(BF16)

            def fold(scores, mask, values):
                scores = jnp.where(mask, scores, NEGATIVE)
                new = jnp.maximum(peak[...], jnp.max(scores, 0, keepdims=True))
                weights = jnp.where(mask, jnp.exp(scores - new), 0.0).astype(BF16)
                accum[...] = accum[...] * jnp.exp(peak[...] - new) + contract(values, weights, 1, 0)
                peak[...] = new

            peak[...] = jnp.full(peak.shape, NEGATIVE, F32)
            accum[...] = jnp.zeros(accum.shape, F32)
            fold(contract(pre_key[...], plain, 0, 0), pre_row < prefix, pre_value_ones)

            def slow(number, masked):
                rows = pl.ds(pl.multiple_of(number * keys, keys), keys)
                scores = contract(key_rows[rows, :][:, :size], plain, 1, 0)
                fold(scores, allowed(meta, number, keys, places), value_ones[:, rows])

            def step(number, _):
                slow(number, True)
                return 0

            lax.fori_loop(bounds[2] // keys, bounds[1] // keys + 1, step, 0)

        total = accum[size : size + 1, :]
        result = accum[:size, :] / total
        log_total[number] = peak[...] + jnp.log(total)
        for part in range(tile // LANES):
            piece = result[:, part * LANES : (part + 1) * LANES]
            out_full[number * (tile // LANES) + part] = piece
            out_low[number * (tile // LANES) + part] = piece.astype(BF16)
        return 0

    lax.fori_loop(0, blocks * per, query_tile, 0)


def attend_forward(meta, query, key, value, pre_key, pre_value, tile, keys, prefix, chunk, group):
    sources, size, length = key.shape
    count = query.shape[0] * query.shape[2]
    return pl.pallas_call(
        functools.partial(
            forward_kernel, tile=tile, keys=keys, prefix=prefix, chunk=chunk, group=group
        ),
        out_shape=(
            jax.ShapeDtypeStruct((count // LANES, size, LANES), BF16),
            jax.ShapeDtypeStruct((count // LANES, size, LANES), F32),
            jax.ShapeDtypeStruct((count // tile, 1, tile), F32),
        ),
        in_specs=[SM] + [VM] * 5,
        out_specs=(VM, VM, VM),
        scratch_shapes=[
            pltpu.VMEM((sources * length, LANES), BF16),
            pltpu.VMEM((size + PAD, sources * length), BF16),
            pltpu.VMEM((size + PAD, tile), F32),
            pltpu.VMEM((1, tile), F32),
        ],
        compiler_params=pltpu.CompilerParams(vmem_limit_bytes=48 * 2**20),
        cost_estimate=work(count, sources * length, 2),
        name="attend_forward",
    )(meta, query, key, value, pre_key, pre_value)


def in_three(values):
    high = values.astype(BF16).astype(F32)
    middle = (values - high).astype(BF16).astype(F32)
    low = values - high - middle
    row = lax.broadcasted_iota(jnp.int32, (PAD, values.shape[1]), 0)
    return jnp.where(row == 0, high, jnp.where(row == 1, middle, jnp.where(row == 2, low, 0.0)))


def backward_kernel(
    meta, query, key, value, pre_key, pre_value, grad_out, out_full, log_total,
    grad_query, grad_keep, grad_send, grad_prefix,
    key_rows, value_rows, key_columns, sums, query_sum,
    *, tile, keys, prefix, chunk, group,
):
    sources, size, length = key.shape
    blocks, _, width = query.shape
    per = width // tile
    scale = size**-0.5
    count = tile // LANES
    rank = meta[DOCS - 1]

    def extended(values):
        ones = jnp.where(
            lax.broadcasted_iota(jnp.int32, (LANES - size, values.shape[1]), 0) < 3, 1.0, 0.0
        )
        return jnp.concatenate([values.astype(F32), ones], 0)

    def prepare(source, _):
        rows = pl.ds(pl.multiple_of(source * length, length), length)
        key_rows[rows, :] = extended(key[source]).T.astype(BF16)
        value_rows[rows, :] = extended(value[source]).T.astype(BF16)
        key_columns[:, rows] = key[source]
        sums[rows, :] = jnp.zeros((length, LANES), F32)
        return 0

    lax.fori_loop(0, sources, prepare, 0)
    grad_prefix[...] = jnp.zeros(grad_prefix.shape, F32)
    pre_row = lax.broadcasted_iota(jnp.int32, (pre_key.shape[0], tile), 0)

    def query_tile(number, _):
        source, part = number // per, number % per
        base = number * tile * group
        columns = pl.ds(pl.multiple_of(part * tile, tile), tile)
        scaled = (query[source, :, columns].astype(F32) * scale).astype(BF16)
        pieces = [number * count + piece for piece in range(count)]
        grad = jnp.concatenate([grad_out[piece] for piece in pieces], 1)
        full = jnp.concatenate([out_full[piece] for piece in pieces], 1)
        delta = jnp.sum(grad.astype(F32) * full, 0, keepdims=True)
        level = log_total[number]
        index = lax.broadcasted_iota(jnp.int32, (1, tile), 1)
        places = query_places(meta, index, base, chunk, group)
        bounds = tile_bounds(meta, base, tile, chunk, group)
        rest = jnp.zeros((LANES - size - PAD, tile), BF16)
        scaled_less = jnp.concatenate([scaled, in_three(-level).astype(BF16), rest], 0)
        grad_less = jnp.concatenate([grad, in_three(-delta).astype(BF16), rest], 0)
        none = jnp.zeros((size, tile), BF16)
        pair = jnp.concatenate(
            [jnp.concatenate([grad, none], 1), jnp.concatenate([none, scaled], 1)], 0
        )

        probs = jnp.exp(contract(pre_key[...], scaled, 1, 0) - level)
        probs = jnp.where(pre_row < prefix, probs, 0.0)
        slope = (probs * (contract(pre_value[...], grad, 1, 0) - delta)).astype(BF16)
        grad_prefix[0] += contract(slope, scaled, 1, 1)
        grad_prefix[1] += contract(probs.astype(BF16), grad, 1, 1)
        query_sum[...] = contract(pre_key[...], slope, 0, 0)

        def block(number, masked):
            rows = pl.ds(pl.multiple_of(number * keys, keys), keys)
            probs = jnp.exp(contract(key_rows[rows, :], scaled_less, 1, 0))
            if masked:
                probs = jnp.where(allowed(meta, number, keys, places), probs, 0.0)
            slope = (probs * contract(value_rows[rows, :], grad_less, 1, 0)).astype(BF16)
            both = jnp.concatenate([probs.astype(BF16), slope], 1)
            sums[rows, :] += contract(both, pair, 1, 1)
            query_sum[...] += contract(key_columns[:, rows], slope, 1, 0)

        over_keys(bounds, keys, block)
        grad_query[source, :, columns] = (query_sum[...] * scale).astype(BF16)
        return 0

    lax.fori_loop(0, blocks * per, query_tile, 0)

    def flush(keys_target, values_target):
        def step(source, _):
            rows = pl.ds(pl.multiple_of(source * length, length), length)
            turned = sums[rows, :].T.astype(BF16)
            values_target[source] = turned[:size]
            keys_target[source] = turned[size:]
            return 0

        lax.fori_loop(0, sources, step, 0)

    if group == 2:

        @pl.when(rank == 0)
        def _():
            flush(grad_keep, grad_send)

        @pl.when(rank == 1)
        def _():
            flush(grad_send, grad_keep)

    else:
        flush(grad_keep, grad_send)


def attend_backward(
    meta, query, key, value, pre_key, pre_value, grad_out, out_full, log_total,
    tile, keys, prefix, chunk, group,
):
    sources, size, length = key.shape
    return pl.pallas_call(
        functools.partial(
            backward_kernel, tile=tile, keys=keys, prefix=prefix, chunk=chunk, group=group
        ),
        out_shape=(
            jax.ShapeDtypeStruct(query.shape, BF16),
            jax.ShapeDtypeStruct(key.shape, BF16),
            jax.ShapeDtypeStruct(key.shape, BF16),
            jax.ShapeDtypeStruct((2,) + pre_key.shape, F32),
        ),
        in_specs=[SM] + [VM] * 8,
        out_specs=(VM,) * 4,
        scratch_shapes=[
            pltpu.VMEM((sources * length, LANES), BF16),
            pltpu.VMEM((sources * length, LANES), BF16),
            pltpu.VMEM((size, sources * length), BF16),
            pltpu.VMEM((sources * length, LANES), F32),
            pltpu.VMEM((size, tile), F32),
        ],
        compiler_params=pltpu.CompilerParams(vmem_limit_bytes=56 * 2**20),
        cost_estimate=work(query.shape[0] * query.shape[2], sources * length, 5),
        name="attend_backward",
    )(meta, query, key, value, pre_key, pre_value, grad_out, out_full, log_total)


def turn_kernel(*refs):
    count = len(refs) // 2
    for source, target in zip(refs[:count], refs[count:]):
        target[...] = source[...].astype(F32).T.astype(BF16)


def turned(*arrays):
    return pl.pallas_call(
        turn_kernel,
        out_shape=tuple(jax.ShapeDtypeStruct(a.shape[::-1], BF16) for a in arrays),
        in_specs=[VM] * len(arrays),
        out_specs=(VM,) * len(arrays),
        compiler_params=pltpu.CompilerParams(vmem_limit_bytes=32 * 2**20),
        name="turned",
    )(*arrays)


def project_kernel(rows, columns, weight, bias, full, sent, stats, *, heads, size, step):
    length = rows.shape[1]
    pieces = length // step
    half = step // 2
    width = length // 2
    for piece in range(pieces):
        lanes = slice(piece * step, (piece + 1) * step)
        values = rows[:, lanes].astype(F32)
        mean = jnp.mean(values, 0, keepdims=True)
        centered = values - mean
        inverse = lax.rsqrt(jnp.mean(centered * centered, 0, keepdims=True) + EPS)
        stats[0:1, lanes] = mean
        stats[1:2, lanes] = inverse
        low = (centered * inverse * columns[:, 0:1] + columns[:, 1:2]).astype(BF16)
        full[:, lanes] = low
        mixed = (contract(weight[...], low, 1, 0) + bias[...]).astype(BF16)
        for head in range(heads):
            part = mixed[head * 3 * size : (head + 1) * 3 * size]
            spot = slice(piece * half, (piece + 1) * half)
            sent[2 * head, :, spot] = part[:size, :half]
            sent[2 * head + 1, :, spot] = part[:size, half:]
            spot = slice(width + piece * step, width + (piece + 1) * step)
            sent[2 * head, :, spot] = part[size : 2 * size]
            sent[2 * head + 1, :, spot] = part[2 * size :]


def project(rows, columns, weight, bias, heads, size, step):
    width, length = rows.shape
    return pl.pallas_call(
        functools.partial(project_kernel, heads=heads, size=size, step=step),
        out_shape=(
            jax.ShapeDtypeStruct((width, length), BF16),
            jax.ShapeDtypeStruct((2 * heads, size, length // 2 * 3), BF16),
            jax.ShapeDtypeStruct((2, length), F32),
        ),
        in_specs=[VM] * 4,
        out_specs=(VM, VM, VM),
        compiler_params=pltpu.CompilerParams(vmem_limit_bytes=40 * 2**20),
        name="project",
    )(rows, columns, weight, bias)


def unproject_kernel(
    spot, flat, weight, rows, stats, columns, own_grad,
    part, row_sums, sums, head_sums,
    *, step,
):
    gain = columns[:, 0:1]
    sums[...] = jnp.zeros(sums.shape, F32)
    head_sums[...] = jnp.zeros(head_sums.shape, F32)
    for piece in range(rows.shape[1] // step):
        lanes = slice(piece * step, (piece + 1) * step)
        grads = flat[:, lanes]
        head_sums[...] += jnp.sum(grads.astype(F32), 1, keepdims=True)
        back = contract(weight[...], grads, 1, 0)
        part[:, lanes] = back.astype(BF16)

        @pl.when(spot[0] == piece)
        def _():
            part[:, lanes] = (back + own_grad[...] / (stats[1:2, lanes] * gain)).astype(BF16)

        normed = (rows[:, lanes].astype(F32) - stats[0:1, lanes]) * stats[1:2, lanes]
        scaled = back * gain
        row_sums[0:1, lanes] = jnp.sum(scaled, 0, keepdims=True)
        row_sums[1:2, lanes] = jnp.sum(scaled * normed, 0, keepdims=True)
        sums[:, 0:1] += jnp.sum(back * normed, 1, keepdims=True)
        sums[:, 1:2] += jnp.sum(back, 1, keepdims=True)


def unproject(spot, flat, weight, rows, stats, columns, own_grad, step):
    width, length = rows.shape
    return pl.pallas_call(
        functools.partial(unproject_kernel, step=step),
        out_shape=(
            jax.ShapeDtypeStruct((width, length), BF16),
            jax.ShapeDtypeStruct((2, length), F32),
            jax.ShapeDtypeStruct((width, 2), F32),
            jax.ShapeDtypeStruct((flat.shape[0], 1), F32),
        ),
        in_specs=[SM] + [VM] * 6,
        out_specs=(VM,) * 4,
        compiler_params=pltpu.CompilerParams(vmem_limit_bytes=40 * 2**20),
        cost_estimate=pl.CostEstimate(
            flops=4 * flat.shape[0] * width * length, bytes_accessed=2**23, transcendentals=0
        ),
        name="unproject",
    )(spot, flat, weight, rows, stats, columns, own_grad)


def finish_kernel(up, down, own_up, own_down, rows, gain, stats, row_sums, grad):
    half = up.shape[0]
    mean, inverse = stats[0:1], stats[1:2]
    first, second = row_sums[0:1], row_sums[1:2]
    for start, came, own in ((0, up, own_up), (half, down, own_down)):
        spot = slice(start, start + half)
        total = came[...].astype(F32) + own[...].astype(F32)
        normed = (rows[spot].astype(F32) - mean) * inverse
        back = inverse * (gain[spot] * total - first - normed * second)
        grad[:, spot] = back.T.astype(BF16)


def finish(up, down, own_up, own_down, rows, gain, stats, row_sums):
    return pl.pallas_call(
        finish_kernel,
        out_shape=jax.ShapeDtypeStruct(rows.shape[::-1], BF16),
        in_specs=[VM] * 8,
        out_specs=VM,
        compiler_params=pltpu.CompilerParams(vmem_limit_bytes=32 * 2**20),
        name="finish",
    )(up, down, own_up, own_down, rows, gain, stats, row_sums)


def feed_kernel(rows, grads, up_turned, up, down, bias, hidden, grad_pre, part):
    pre = contract(up_turned[...], rows[0], 1, 0) + bias[...]
    act, pull = jax.vjp(gelu_tanh, pre)
    hidden[0] = act.astype(BF16)
    given = grads[...] if len(grads.shape) == 2 else grads[0]
    low = pull(contract(down[...], given, 1, 0))[0].astype(BF16)
    grad_pre[0] = low
    part[0] = contract(up[...], low, 1, 0).astype(BF16)


def feed(rows, grads, up_turned, up, down, bias):
    blocks, width, count = rows.shape
    inner = down.shape[0]

    def whole(shape):
        return pl.BlockSpec(shape, lambda i: (0,) * len(shape), pipeline_mode=pl.Buffered(1))

    def block(size):
        return pl.BlockSpec((1, size, count), lambda i: (i, 0, 0))

    if count % LANES:
        grads = grads.reshape(width, blocks, count).transpose(1, 0, 2)

    return pl.pallas_call(
        feed_kernel,
        grid=(blocks,),
        out_shape=(
            jax.ShapeDtypeStruct((blocks, inner, count), BF16),
            jax.ShapeDtypeStruct((blocks, inner, count), BF16),
            jax.ShapeDtypeStruct((blocks, width, count), BF16),
        ),
        in_specs=[
            block(width),
            block(width) if count % LANES else pl.BlockSpec((width, count), lambda i: (0, i)),
            whole((inner, width)),
            whole((width, inner)),
            whole((inner, width)),
            whole((inner, 1)),
        ],
        out_specs=(block(inner), block(inner), block(width)),
        compiler_params=pltpu.CompilerParams(vmem_limit_bytes=32 * 2**20),
        cost_estimate=pl.CostEstimate(
            flops=6 * blocks * width * inner * count, bytes_accessed=2**24, transcendentals=0
        ),
        name="feed",
    )(rows, grads, up_turned, up, down, bias)


def feed_rest_kernel(
    spot, rows, grads, hidden, grad_pre, down_turned, middle, columns,
    mine, other, bias, out,
    *, square,
):
    blocks, width, count = rows.shape
    inner = hidden.shape[1]
    features = out.shape[2]

    def lanes(n):
        return slice(n * count, (n + 1) * count)

    def weights(target, first, second, columns):
        step = min(256, columns)
        whole = jnp.concatenate([first(n) for n in range(blocks)], 1)
        for start in range(0, columns, step):
            tile = slice(start, start + step)
            turned = jnp.concatenate([second(n, tile) for n in range(blocks)], 1)
            target[:, tile] = contract(whole, turned, 1, 1).astype(BF16)

    def down(target):
        weights(target, lambda n: hidden[n], lambda n, tile: grads[tile, lanes(n)], width)

    def up(target):
        if square:
            weights(target, lambda n: rows[n], lambda n, tile: grad_pre[n, tile], inner)
        else:
            weights(target, lambda n: grad_pre[n], lambda n, tile: rows[n, tile], width)

    down(mine)
    up(other)
    bias[...] = sum(jnp.sum(grad_pre[n].astype(F32), 1, keepdims=True) for n in range(blocks))
    for n in range(blocks):
        result = contract(down_turned[...], hidden[n], 1, 0)

        def put(values):
            for block in range(out.shape[0]):
                out[block, n] = values[block * features : (block + 1) * features].astype(BF16)

        put(result)

        @pl.when(spot[0] == n)
        def _():
            put(result + middle[...] + columns[:, 5:6])


def feed_rest(spot, rows, grads, hidden, grad_pre, down_turned, middle, columns):
    blocks, width, count = rows.shape
    inner = hidden.shape[1]
    return pl.pallas_call(
        functools.partial(feed_rest_kernel, square=inner == width),
        out_shape=(
            jax.ShapeDtypeStruct((inner, width), BF16),
            jax.ShapeDtypeStruct((inner, width), BF16),
            jax.ShapeDtypeStruct((inner, 1), F32),
            jax.ShapeDtypeStruct((blocks, blocks, width // blocks, count), BF16),
        ),
        in_specs=[SM] + [VM] * 7,
        out_specs=(VM,) * 4,
        compiler_params=pltpu.CompilerParams(vmem_limit_bytes=48 * 2**20),
        cost_estimate=pl.CostEstimate(
            flops=6 * blocks * width * inner * count, bytes_accessed=2**24, transcendentals=0
        ),
        name="feed_rest",
    )(spot, rows, grads, hidden, grad_pre, down_turned, middle, columns)


def rest_kernel(spot, came, full, out, flat, mine, other, *, heads, size, step):
    width, length = full.shape
    half = step // 2
    past = length // 2
    for piece in range(length // step):
        lanes = slice(piece * step, (piece + 1) * step)
        place = slice(piece * half, (piece + 1) * half)
        pair = slice(past + piece * step, past + (piece + 1) * step)
        for head in range(heads):
            first, second = 2 * head, 2 * head + 1
            row = 3 * size * head
            flat[row : row + size, lanes] = jnp.concatenate(
                [came[first, :, place], came[second, :, place]], 1
            )
            flat[row + size : row + 2 * size, lanes] = came[first, :, pair]
            flat[row + 2 * size : row + 3 * size, lanes] = came[second, :, pair]
    split = mine.shape[0]
    step = min(256, width)
    for start in range(0, width, step):
        tile = slice(start, start + step)
        result = contract(flat[...], full[tile], 1, 1).astype(BF16)
        first = result[:split]
        second = jnp.concatenate([result[split:], out[:, tile]], 0)

        @pl.when(spot[1] == 0)
        def _():
            mine[:, tile] = first
            other[:, tile] = second

        @pl.when(spot[1] == 1)
        def _():
            mine[:, tile] = second
            other[:, tile] = first


def rest_halves(spot, came, full, out, heads, size, step):
    width, length = full.shape
    rows = 3 * heads * size
    half = (rows + out.shape[0]) // 2
    return pl.pallas_call(
        functools.partial(rest_kernel, heads=heads, size=size, step=step),
        out_shape=(
            jax.ShapeDtypeStruct((rows, length), BF16),
            jax.ShapeDtypeStruct((half, width), BF16),
            jax.ShapeDtypeStruct((half, width), BF16),
        ),
        in_specs=[SM] + [VM] * 3,
        out_specs=(VM,) * 3,
        compiler_params=pltpu.CompilerParams(vmem_limit_bytes=32 * 2**20),
        name="rest_halves",
    )(spot, came, full, out)


def rest_whole_kernel(spot, half, other, mixed, out):
    rows = half.shape[0]
    extra = mixed.shape[0] - rows

    def write(first, second):
        mixed[:rows] = first[...].astype(F32)
        mixed[rows:] = second[:extra].astype(F32)
        out[...] = second[extra:].astype(F32)

    @pl.when(spot[1] == 0)
    def _():
        write(half, other)

    @pl.when(spot[1] == 1)
    def _():
        write(other, half)


def rest_whole(spot, half, other, rows):
    width = half.shape[1]
    return pl.pallas_call(
        rest_whole_kernel,
        out_shape=(
            jax.ShapeDtypeStruct((rows, width), F32),
            jax.ShapeDtypeStruct((2 * half.shape[0] - rows, width), F32),
        ),
        in_specs=[SM, VM, VM],
        out_specs=(VM, VM),
        compiler_params=pltpu.CompilerParams(vmem_limit_bytes=32 * 2**20),
        name="rest_whole",
    )(spot, half, other)


def spread(values, axis):
    count = lax.axis_size(axis)
    copies = jnp.broadcast_to(values[None], (count,) + values.shape)
    return lax.all_to_all(copies, axis, 0, 0, tiled=True)


def small_sum(values, axis):
    return jnp.sum(spread(values, axis), 0)


def ring(axis, by):
    count = lax.axis_size(axis)
    return [(source, (source + by) % count) for source in range(count)]


def ring_gather(values, axis, beside=()):
    count, place = lax.axis_size(axis), lax.axis_index(axis)
    half = values.shape[0] // 2
    up, down = values[:half], values[half:]
    out = jnp.zeros((count,) + values.shape, values.dtype)
    out = lax.dynamic_update_slice_in_dim(out, values[None], place, 0)
    zeros = (0,) * (values.ndim - 1)
    results = []
    for step in range(1, count):
        up = lax.ppermute(up, axis, ring(axis, 1))
        down = lax.ppermute(down, axis, ring(axis, -1))
        if step <= len(beside) and beside[step - 1]:
            up, down, result = lax.optimization_barrier((up, down, beside[step - 1]()))
            results.append(result)
        out = lax.dynamic_update_slice(out, up[None], ((place - step) % count, 0) + zeros)
        out = lax.dynamic_update_slice(out, down[None], ((place + step) % count, half) + zeros)
    return (out, results) if beside else out


def ring_terms(blocks, axis, beside=()):
    count, place = lax.axis_size(axis), lax.axis_index(axis)
    half = blocks.shape[1] // 2

    def own(offset, upper):
        block = lax.dynamic_index_in_dim(blocks, (place + offset) % count, 0, keepdims=False)
        return block[half:] if upper else block[:half]

    up, down = own(-1, False), own(1, True)
    state = None
    for step in range(1, count):
        up = lax.ppermute(up, axis, ring(axis, 1))
        down = lax.ppermute(down, axis, ring(axis, -1))
        if step <= len(beside):
            state = beside[step - 1](state)
            up, down, state = lax.optimization_barrier((up, down, state))
        if step < count - 1:
            up = (up.astype(F32) + own(-1 - step, False).astype(F32)).astype(BF16)
            down = (down.astype(F32) + own(1 + step, True).astype(F32)).astype(BF16)
    for other in beside[count - 1 :]:
        state = other(state)
    return (up, down, own(0, False), own(0, True)), state


def swapped(values):
    pairs = [(source, source ^ 1) for source in range(lax.axis_size("seq"))]
    return lax.ppermute(values, "seq", pairs)


def chip_groups():
    chips = lax.axis_size("seq") // 2
    return [[2 * chip + core for chip in range(chips)] for core in range(2)]


def core_sum(mine, other):
    return (mine.astype(F32) + swapped(other).astype(F32)).astype(BF16)


def chip_parts(half):
    chips = lax.axis_size("seq") // 2
    blocks = half.reshape(chips, half.shape[0] // chips, half.shape[1])
    return lax.all_to_all(blocks, "seq", 0, 0, axis_index_groups=chip_groups(), tiled=True)


def chip_copies(parts):
    part = jnp.sum(parts.astype(F32), 0).astype(BF16)
    return jnp.broadcast_to(part[None], parts.shape)


def chip_gather(copies):
    half = lax.all_to_all(copies, "seq", 0, 0, axis_index_groups=chip_groups(), tiled=True)
    return half.reshape(-1, half.shape[2])


def spread_direct(values, axis):
    count, place = lax.axis_size(axis), lax.axis_index(axis)
    out = jnp.zeros((count,) + values.shape, values.dtype)
    out = lax.dynamic_update_slice_in_dim(out, values[None], place, 0)
    for step in range(1, count):
        came = lax.ppermute(values, axis, ring(axis, step))
        out = lax.dynamic_update_slice_in_dim(out, came[None], (place - step) % count, 0)
    return out


def core_gather(half):
    core = lax.axis_index("seq") % 2
    other = swapped(half)
    first = jnp.where(core == 0, half, other)
    second = jnp.where(core == 0, other, half)
    return first, second


def regrouped(values, width):
    count, size, columns = values.shape
    if width == columns:
        return values
    if width > columns:
        merged = values.reshape(-1, width // columns, size, columns).transpose(0, 2, 1, 3)
        return merged.reshape(-1, size, width)
    cut = values.reshape(count, size, columns // width, width).transpose(0, 2, 1, 3)
    return cut.reshape(-1, size, width)


def group_gather(pieces, group):
    if group == 2:
        rank = lax.axis_index("seq") % 2
        other = swapped(pieces)
        return jnp.stack([jnp.where(rank == 0, pieces, other), jnp.where(rank == 0, other, pieces)])
    count = lax.axis_size("seq")
    groups = [[first + i for i in range(group)] for first in range(0, count, group)]
    return lax.all_gather(pieces, "seq", axis_index_groups=groups)


def on_device(
    tokens,
    segment_ids,
    out_grad,
    ln1_gain,
    ln1_bias,
    w_qkv,
    b_qv,
    w_out,
    b_out,
    ln2_gain,
    ln2_bias,
    w_up,
    b_up,
    w_down,
    b_down,
    prefix_embed,
    reparam_in,
    reparam_in_bias,
    reparam_out,
    reparam_out_bias,
):
    rows, features = tokens.shape
    heads = w_qkv.shape[1]
    size = w_qkv.shape[2] // 3
    inner = w_up.shape[1]
    seqs, tensors = lax.axis_size("seq"), lax.axis_size("tensor")
    width = features * tensors
    own_rows = rows // tensors
    group = seqs // heads
    chunk = own_rows // group
    place, slot = lax.axis_index("seq"), lax.axis_index("tensor")
    head, rank = place // group, place % group
    prefix = prefix_embed.shape[0]
    tokens_head = rows // group
    query_width = max(tokens_head, LANES)
    forward_tile = min(512, query_width)
    backward_tile = min(256, query_width)
    forward_keys, backward_keys = 1024, 1024
    both = ("seq", "tensor")
    paired = group == 2 and chunk == LANES

    own_tokens, own_grads = turned(tokens, out_grad)
    numbers = jnp.arange(1, DOCS, dtype=jnp.int32)

    def document_starts():
        before = jnp.sum((segment_ids[None, :] < numbers[:, None]).astype(jnp.int32), 1)
        return spread(jnp.broadcast_to(before[:, None], (DOCS - 1, LANES)), "seq")

    def whole_vectors():
        return spread(
            jnp.stack([ln1_gain, ln1_bias, ln2_gain, ln2_bias, b_out, b_down]), "tensor"
        )

    full_tokens, (vectors, starts) = ring_gather(
        own_tokens, "tensor", (None, whole_vectors, document_starts)
    )
    full_tokens = full_tokens.reshape(width, rows)
    meta = jnp.concatenate([jnp.sum(starts, 0)[:, 0], rank[None].astype(jnp.int32)])
    columns = vectors.transpose(0, 2, 1).reshape(width, 6).astype(F32)
    out_share = w_out.reshape(seqs, heads * size // seqs, width)
    out_share = lax.dynamic_index_in_dim(out_share, place, 0, keepdims=False)
    gain2, shift2, bias_out = [columns[:, i : i + 1] for i in (2, 3, 4)]
    core = place % 2
    spot = jnp.stack([slot, core]).astype(jnp.int32)

    embed_float = prefix_embed.astype(F32)
    prefix_hidden = jnp.tanh(
        jnp.dot(prefix_embed, reparam_in, preferred_element_type=F32)
        + reparam_in_bias.astype(F32)
    )
    prefix_pair = jnp.einsum(
        "pa,ahe->phe", prefix_hidden, reparam_out.astype(F32), precision=HIGHEST
    )
    prefix_pair = (prefix_pair + reparam_out_bias.astype(F32)).astype(BF16)
    own_pair = lax.dynamic_index_in_dim(prefix_pair, head, 1, keepdims=False)
    own_pair = jnp.pad(own_pair, ((0, LANES - prefix), (0, 0)))
    pre_key, pre_value = own_pair[:, :size], own_pair[:, size:]

    w_flat = w_qkv.reshape(width, heads * 3 * size)
    bias_pair = b_qv.astype(F32)
    bias_three = jnp.stack(
        [bias_pair[:, :size], jnp.zeros((heads, size), F32), bias_pair[:, size:]], 1
    ).reshape(-1, 1)
    if paired:
        full1, sent, stats = project(
            full_tokens, columns, w_flat.T, bias_three, heads, size, own_rows
        )
    else:
        wide = full_tokens.astype(F32)
        mean = jnp.mean(wide, 0, keepdims=True)
        inverse = lax.rsqrt(jnp.mean((wide - mean) ** 2, 0, keepdims=True) + EPS)
        stats = jnp.concatenate([mean, inverse], 0)
        full1 = ((wide - mean) * inverse * columns[:, 0:1] + columns[:, 1:2]).astype(BF16)
        mixed = (contract(w_flat, full1, 0, 0) + bias_three).astype(BF16)
        mixed = mixed.reshape(heads, 3, size, rows)
        query_part = mixed[:, 0].reshape(heads, size, tensors, group, chunk)
        query_part = query_part.transpose(0, 3, 1, 2, 4).reshape(seqs, size, tokens_head)
        pair_part = mixed[:, 1:].transpose(0, 2, 1, 3).reshape(heads, size, group, 2 * tokens_head)
        pair_part = pair_part.transpose(0, 2, 1, 3).reshape(seqs, size, 2 * tokens_head)
        sent = jnp.concatenate([query_part, pair_part], 2)
    out_share = spread_direct(after(out_share, sent), "tensor")
    came = lax.all_to_all(sent, "seq", 0, 0, tiled=True)
    out_share = jnp.broadcast_to(out_share[None], (seqs,) + out_share.shape)
    came, out_share = lax.optimization_barrier((came, out_share))
    out_share = lax.all_to_all(out_share, "seq", 0, 0, tiled=True)
    w_out_full = out_share.transpose(1, 0, 2, 3).reshape(width, width)
    query, pair = came[:, :, :tokens_head], came[:, :, tokens_head:]
    query = regrouped(query, query_width)
    pair = group_gather(pair, group)
    if group == 2:
        key, value = pair[0], pair[1]
    else:
        pair = pair.transpose(1, 2, 0, 3).reshape(seqs, size, 2, rows)
        key, value = pair[:, :, 0], pair[:, :, 1]
    full_grad = lax.all_gather(after(own_grads, full_tokens), "tensor", axis=0, tiled=True)
    out_low, out_full, log_total = attend_forward(
        meta, query, key, value, pre_key.T, pre_value.T,
        forward_tile, forward_keys, prefix, chunk, group,
    )
    out_low, full_grad, late_up, late_down = lax.optimization_barrier(
        (out_low, full_grad, w_up, w_down)
    )

    came = lax.all_to_all(regrouped(out_low, chunk), both, 0, 0, tiled=True)
    came, up_turned, down_turned, w_out_full = lax.optimization_barrier(
        (came, late_up.T, late_down.T, w_out_full)
    )
    came = came.reshape(heads, group, tensors, size, chunk).transpose(2, 0, 3, 1, 4)
    attended = came.reshape(width, own_rows)
    branch = contract(w_out_full, attended, 0, 0)
    own_block = lax.dynamic_slice_in_dim(full_tokens, slot * own_rows, own_rows, 1)
    middle = own_block.astype(F32) + branch + bias_out
    mean2 = jnp.mean(middle, 0, keepdims=True)
    centered = middle - mean2
    inverse2 = lax.rsqrt(jnp.mean(centered * centered, 0, keepdims=True) + EPS)
    normed2 = centered * inverse2
    out2 = (normed2 * gain2 + shift2).astype(BF16)

    full2 = ring_gather(out2, "tensor")
    hidden, grad_pre, part = feed(
        full2, full_grad, up_turned, w_up, w_down, b_up.astype(F32)[:, None]
    )

    def weights_here(_):
        return feed_rest(
            spot, full2, full_grad, hidden, grad_pre, down_turned, middle, columns
        )

    terms, (grad_w_down, grad_w_up, grad_b_up, mlp_out) = ring_terms(
        part, "tensor", (weights_here,)
    )
    feed_sums = lax.psum((grad_w_down, grad_w_up), "seq")
    up, down, own_up, own_down = [a.astype(F32) for a in terms]
    grad_normed2 = jnp.concatenate([up + own_up, down + own_down], 0)

    scaled = grad_normed2 * gain2
    first = jnp.mean(scaled, 0, keepdims=True)
    second = jnp.mean(scaled * normed2, 0, keepdims=True)
    own_grad = lax.dynamic_slice_in_dim(full_grad, slot * own_rows, own_rows, 1)
    grad_middle = own_grad.astype(F32) + inverse2 * (scaled - first - normed2 * second)
    grad_branch = grad_middle.astype(BF16)
    grad_attended = contract(w_out_full, grad_branch, 1, 0).astype(BF16)
    sent = grad_attended.reshape(tensors, heads, size, group, chunk).transpose(1, 3, 0, 2, 4)
    came = lax.all_to_all(sent.reshape(seqs * tensors, size, chunk), both, 0, 0, tiled=True)
    grad_out = regrouped(came, LANES)

    token_sums = jnp.stack(
        [
            jnp.sum(grad_normed2 * normed2, 1),
            jnp.sum(grad_normed2, 1),
            jnp.sum(grad_middle, 1),
        ]
    )
    grad_w_out = contract(attended, grad_branch, 1, 1).astype(BF16)
    grad_out, mlp_out, grad_w_out = lax.optimization_barrier((grad_out, mlp_out, grad_w_out))
    output_act = lax.all_to_all(mlp_out, "tensor", 0, 0, tiled=True)
    grad_w_out = lax.psum_scatter(grad_w_out, "tensor", scatter_dimension=0, tiled=True)

    levels = log_total.reshape(-1, 1, backward_tile)
    grad_query, grad_keep, grad_send, grad_prefix = attend_backward(
        meta, query, key, value, pre_key[:PAD], pre_value[:PAD], grad_out, out_full, levels,
        backward_tile, backward_keys, prefix, chunk, group,
    )
    if group == 2:
        grad_share = (grad_keep.astype(F32) + swapped(grad_send).astype(F32)).astype(BF16)
    else:
        grad_pair = jnp.stack([grad_keep, grad_send])
        groups = [[first + i for i in range(group)] for first in range(0, seqs, group)]
        shares = grad_pair.transpose(1, 2, 0, 3).reshape(seqs, size, group, 2 * tokens_head)
        grad_share = lax.psum_scatter(
            shares.transpose(2, 0, 1, 3), "seq", axis_index_groups=groups
        )
    prefix_part = grad_prefix.transpose(2, 0, 1).reshape(size, 2 * PAD).astype(BF16)
    prefix_part = jnp.pad(prefix_part, ((0, 0), (0, LANES - 2 * PAD)))
    prefix_part = jnp.broadcast_to(prefix_part[None], (seqs, size, LANES))
    sent = jnp.concatenate([regrouped(grad_query, tokens_head), grad_share, prefix_part], 2)
    sent, output_act, feed_sums = lax.optimization_barrier((sent, output_act, feed_sums))
    came = lax.all_to_all(sent, "seq", 0, 0, tiled=True)
    output_act = jnp.sum(output_act.astype(F32), 0).astype(BF16)
    output_act = output_act.transpose(0, 2, 1).reshape(rows, features)
    came, output_act, grad_w_out = lax.optimization_barrier((came, output_act, grad_w_out))
    if paired:
        grad_flat, mine, other = rest_halves(spot, came, full1, grad_w_out, heads, size, own_rows)
        grad_part, row_sums, sums1, head_sums = unproject(
            spot, grad_flat, w_flat, full_tokens, stats, columns, grad_middle, own_rows
        )
    else:
        query_part = came[:, :, :tokens_head].reshape(heads, group, size, tensors, chunk)
        query_part = query_part.transpose(0, 2, 3, 1, 4).reshape(heads, 1, size, rows)
        pair_part = came[:, :, tokens_head : 3 * tokens_head]
        pair_part = pair_part.reshape(heads, group, size, 2 * tokens_head).transpose(0, 2, 1, 3)
        pair_part = pair_part.reshape(heads, size, 2, rows).transpose(0, 2, 1, 3)
        grad_flat = jnp.concatenate([query_part, pair_part], 1).reshape(heads * 3 * size, rows)
        grad_w_qkv = contract(grad_flat, full1, 1, 1).astype(BF16)
        rest = jnp.concatenate([grad_w_qkv, grad_w_out], 0)
        halves = rest.reshape(2, rest.shape[0] // 2, width)
        mine = lax.dynamic_index_in_dim(halves, core, 0, keepdims=False)
        other = lax.dynamic_index_in_dim(halves, 1 - core, 0, keepdims=False)
        back = contract(w_flat, grad_flat, 1, 0)
        normed1 = (full_tokens.astype(F32) - stats[0]) * stats[1]
        scaled = back * columns[:, 0:1]
        row_sums = jnp.stack([jnp.sum(scaled, 0), jnp.sum(scaled * normed1, 0)])
        sums1 = jnp.stack([jnp.sum(back * normed1, 1), jnp.sum(back, 1)], 1)
        head_sums = jnp.sum(grad_flat.astype(F32), 1)
        own_inverse = lax.dynamic_slice_in_dim(stats[1:2], slot * own_rows, own_rows, 1)
        own_part = lax.dynamic_slice_in_dim(back, slot * own_rows, own_rows, 1)
        own_part = own_part + grad_middle / (own_inverse * columns[:, 0:1])
        back = lax.dynamic_update_slice_in_dim(back, own_part, slot * own_rows, 1)
        grad_part = back.astype(BF16)
    rest_half = core_sum(mine, other)
    grad_part, rest_half = lax.optimization_barrier((grad_part, rest_half))

    prefix_low = came[:, :, 3 * tokens_head : 3 * tokens_head + 2 * PAD].astype(F32)
    prefix_low = jnp.sum(prefix_low.reshape(heads, group, size, 2, PAD), 1)[..., :prefix]
    prefix_low = prefix_low.transpose(3, 0, 2, 1).reshape(prefix, heads, 2 * size).astype(BF16)
    prefix_grad = prefix_low.astype(F32)
    hidden_part = jnp.einsum("phe,ahe->pa", prefix_low, reparam_out, preferred_element_type=F32)
    owned = jnp.concatenate([sums1.T, token_sums], 0)
    owned = owned.reshape(-1, tensors, features).transpose(1, 0, 2).reshape(tensors, -1)
    shared = jnp.concatenate([row_sums.reshape(-1), hidden_part.reshape(-1)])
    shared = jnp.broadcast_to(shared[None], (tensors, shared.shape[0]))
    small = jnp.concatenate([owned, shared], 1)[:, None, :]

    grad_b_down = jnp.sum(out_grad.astype(F32), 0)
    head_sums = head_sums.reshape(heads, 3, size)

    def rest_parts(_):
        return chip_parts(rest_half)

    def small_here(parts):
        return chip_copies(parts), lax.all_to_all(small, "tensor", 0, 0, tiled=True)

    def rest_back(state):
        return chip_gather(state[0]), state[1]

    last_terms, (rest_half, small) = ring_terms(
        grad_part.reshape(tensors, features, rows),
        "tensor",
        (rest_parts, small_here) + (lambda state: state,) * (tensors - 4) + (rest_back,),
    )
    small = jnp.sum(small, 0)[0]
    late = jnp.concatenate(
        [
            small[: 5 * features],
            grad_b_down,
            grad_b_up.reshape(-1),
            head_sums[:, 0].reshape(-1),
            head_sums[:, 2].reshape(-1),
        ]
    )
    late = small_sum(late[None], "seq")[0]
    row_sums = small[5 * features : 5 * features + 2 * rows]
    hidden_grad = small[5 * features + 2 * rows :].reshape(prefix_hidden.shape)
    input_grad = finish(
        *last_terms, own_tokens, ln1_gain.astype(F32)[:, None], stats,
        row_sums.reshape(2, rows) / width,
    )
    mixed_rows = heads * 3 * size
    if paired:
        out_w_qkv, out_w_out = rest_whole(spot, rest_half, swapped(rest_half), mixed_rows)
    else:
        rest = jnp.concatenate(core_gather(rest_half), 0).astype(F32)
        out_w_qkv, out_w_out = rest[:mixed_rows], rest[mixed_rows:]
    out_w_qkv = out_w_qkv.reshape(heads, 3 * size, width).transpose(2, 0, 1)
    out_w_out = out_w_out.reshape(heads, size, width)
    out_w_down = feed_sums[0].astype(F32)
    out_w_up = (feed_sums[1] if inner == width else feed_sums[1].T).astype(F32)

    out_ln1_gain, out_ln1_bias, out_ln2_gain, out_ln2_bias, out_b_out, out_b_down = [
        late[i * features : (i + 1) * features] for i in range(6)
    ]
    late = late[6 * features :]
    out_b_up = late[:inner]
    pair_sums = late[inner:].reshape(2, heads, size)
    out_b_qv = jnp.concatenate([pair_sums[0], pair_sums[1]], 1)

    grad_reparam_out = jnp.einsum("pa,phe->ahe", prefix_hidden, prefix_grad, precision=HIGHEST)
    grad_reparam_out_bias = jnp.sum(prefix_grad, 0)
    grad_prefix_pre = hidden_grad * (1.0 - prefix_hidden * prefix_hidden)
    grad_reparam_in_bias = jnp.sum(grad_prefix_pre, 0)
    grad_reparam_in = jnp.einsum("pd,pa->da", embed_float, grad_prefix_pre, precision=HIGHEST)
    grad_prefix_embed = jnp.einsum(
        "pa,da->pd", grad_prefix_pre, reparam_in.astype(F32), precision=HIGHEST
    )
    return (
        output_act,
        input_grad,
        out_ln1_gain,
        out_ln1_bias,
        out_w_qkv,
        out_b_qv,
        out_w_out,
        out_b_out,
        out_ln2_gain,
        out_ln2_bias,
        out_w_up,
        out_b_up,
        out_w_down,
        out_b_down,
        grad_prefix_embed,
        grad_reparam_in,
        grad_reparam_in_bias,
        grad_reparam_out,
        grad_reparam_out_bias,
    )


def solution(mesh):
    placed = (
        P("seq", "tensor"),
        P("seq"),
        P("seq", "tensor"),
        P("tensor"),
        P("tensor"),
        P(None, "tensor", None),
        P("tensor", None),
        P("tensor", None, None),
        P("tensor"),
        P("tensor"),
        P("tensor"),
        P(None, "tensor"),
        P("tensor"),
        P("tensor", None),
        P("tensor"),
        P(),
        P(),
        P(),
        P(None, "tensor", None),
        P("tensor", None),
    )
    return jax.shard_map(
        on_device,
        mesh=mesh,
        in_specs=placed,
        out_specs=(
            P("seq", "tensor"),
            P("seq", "tensor"),
            P("tensor"),
            P("tensor"),
            P(None, "tensor", None),
            P("tensor", None),
            P("tensor", None, None),
            P("tensor"),
            P("tensor"),
            P("tensor"),
            P(None, "tensor"),
            P("tensor"),
            P("tensor", None),
            P("tensor"),
            P(),
            P(),
            P(),
            P(None, "tensor", None),
            P("tensor", None),
        ),
        check_vma=False,
    )
```

```python
import functools

import jax
import jax.numpy as jnp
from jax import lax
from jax.experimental import pallas as pl
from jax.experimental.pallas import tpu as pltpu
from jax.sharding import PartitionSpec as P

EPS = 1e-05
NEGATIVE = -1e30
HIGHEST = lax.Precision.HIGHEST
F32 = jnp.float32
BF16 = jnp.bfloat16
LANES = 128
PAD = 16
WEAK = 1e-24
DOCS = 5

VM = pl.BlockSpec(memory_space=pltpu.VMEM)
SM = pl.BlockSpec(memory_space=pltpu.SMEM)


def gelu_tanh(values):
    return jax.nn.gelu(values, approximate=True)


def contract(first, second, first_dim, second_dim):
    return lax.dot_general(
        first, second, (((first_dim,), (second_dim,)), ((), ())), preferred_element_type=F32
    )


def work(queries, keys, products):
    pairs = queries * keys // 2
    return pl.CostEstimate(
        flops=2 * 256 * products * pairs, bytes_accessed=8 * 2**20, transcendentals=pairs
    )


def after(values, other):
    return lax.optimization_barrier((values, other))[0]


def document_start(meta, place):
    found = jnp.zeros_like(place) if getattr(place, "shape", ()) else jnp.int32(0)
    for number in range(DOCS - 1):
        begin = meta[number]
        found = jnp.where(place >= begin, jnp.maximum(found, begin), found)
    return found


def query_places(meta, index, base, chunk, group):
    return base + (index // chunk) * (chunk * group) + meta[DOCS - 1] * chunk + index % chunk


def tile_bounds(meta, base, count, chunk, group):
    rank = meta[DOCS - 1]
    first = base + rank * chunk
    last = base + (count // chunk - 1) * (chunk * group) + rank * chunk + chunk - 1
    return document_start(meta, first), document_start(meta, last)


def one_row(rows, columns):
    return lax.broadcasted_iota(jnp.int32, (rows, columns), 0) == 0


def by_rank(meta, group, first, second, work):
    if group != 2:
        work(first, second)
        return

    @pl.when(meta[DOCS - 1] == 0)
    def _():
        work(first, second)

    @pl.when(meta[DOCS - 1] == 1)
    def _():
        work(second, first)


def over_keys(bounds, base, tile, group, keys, block):
    low, low_last = bounds

    def step(number, _):
        clear = number * keys >= low_last

        @pl.when(clear)
        def _():
            block(number * keys, keys, 0, False)

        @pl.when(jnp.logical_not(clear))
        def _():
            block(number * keys, keys, 0, True)

        return 0

    lax.fori_loop(low // keys, base // keys, step, 0)
    for stair in range(tile // LANES):
        block(base + stair * LANES * group, LANES * group, stair * LANES, True)


def allowed(meta, start, count, places):
    key = start + lax.broadcasted_iota(jnp.int32, (count, 1), 0)
    return (key <= places) & (key >= document_start(meta, places))


def forward_kernel(
    meta, query, own, other, pre_key, pre_value,
    out_low, out_full, log_total,
    key_rows, value_ones, accum, peak, norm,
    *, tile, keys, prefix, chunk, group, length, width,
):
    sources, size, whole = own.shape
    blocks = query.shape[0]
    per = width // tile
    scale = size**-0.5
    padded = pre_key.shape[1]
    kept = slice(whole - length, whole)

    def extended(values, count, total):
        ones = jnp.where(one_row(PAD, count), 1.0, 0.0).astype(BF16)
        rest = total - size - PAD
        tail = [jnp.zeros((rest, count), BF16)] if rest else []
        return jnp.concatenate([values, ones] + tail, 0)

    def longest(values):
        wide = values.astype(F32)
        return jnp.max(jnp.sum(wide * wide, 0, keepdims=True), 1, keepdims=True)

    norm[...] = jnp.broadcast_to(longest(pre_key[...]), norm.shape)

    def fill(key, value):
        def prepare(source, _):
            rows = pl.ds(pl.multiple_of(source * length, length), length)
            found = key[source, :, kept]
            key_rows[rows, :] = extended(found, length, LANES).astype(F32).T.astype(BF16)
            value_ones[:, rows] = extended(value[source, :, kept], length, size + PAD)
            norm[...] = jnp.maximum(norm[...], longest(found))
            return 0

        lax.fori_loop(0, sources, prepare, 0)

    by_rank(meta, group, own, other, fill)
    most = jnp.sqrt(norm[0:1, 0:1])
    pre_key_ones = extended(pre_key[...], padded, LANES)
    pre_value_ones = extended(pre_value[...], padded, size + PAD)
    pre_row = lax.broadcasted_iota(jnp.int32, (padded, tile), 0)

    def query_tile(number, _):
        source, part = number // per, number % per
        base = number * tile * group
        columns = pl.ds(pl.multiple_of(part * tile, tile), tile)
        scaled = query[source, :, columns].astype(F32) * scale
        limit = jnp.sqrt(jnp.sum(scaled * scaled, 0, keepdims=True)) * most
        limit = limit.astype(BF16).astype(F32)
        shifted = jnp.concatenate(
            [
                scaled,
                jnp.where(one_row(PAD, tile), -limit, 0.0),
                jnp.zeros((LANES - size - PAD, tile), F32),
            ],
            0,
        ).astype(BF16)
        index = lax.broadcasted_iota(jnp.int32, (1, tile), 1)
        places = query_places(meta, index, base, chunk, group)
        bounds = tile_bounds(meta, base, tile, chunk, group)

        weights = jnp.where(pre_row < prefix, jnp.exp(contract(pre_key_ones, shifted, 0, 0)), 0.0)
        accum[...] = contract(pre_value_ones, weights.astype(BF16), 1, 0)

        def block(start, count, lane, masked):
            rows = pl.ds(pl.multiple_of(start, LANES), count)
            weights = jnp.exp(contract(key_rows[rows, :], shifted[:, lane:], 1, 0))
            if masked:
                weights = jnp.where(allowed(meta, start, count, places[:, lane:]), weights, 0.0)
            accum[:, lane:] += contract(value_ones[:, rows], weights.astype(BF16), 1, 0)

        over_keys(bounds, base, tile, group, keys, block)
        peak[...] = limit

        @pl.when(jnp.min(accum[size : size + 1, :]) < WEAK)
        def _():
            plain = scaled.astype(BF16)

            def fold(scores, mask, values):
                scores = jnp.where(mask, scores, NEGATIVE)
                new = jnp.maximum(peak[...], jnp.max(scores, 0, keepdims=True))
                weights = jnp.where(mask, jnp.exp(scores - new), 0.0).astype(BF16)
                accum[...] = accum[...] * jnp.exp(peak[...] - new) + contract(values, weights, 1, 0)
                peak[...] = new

            peak[...] = jnp.full(peak.shape, NEGATIVE, F32)
            accum[...] = jnp.zeros(accum.shape, F32)
            fold(contract(pre_key[...], plain, 0, 0), pre_row < prefix, pre_value_ones)

            def step(number, _):
                rows = pl.ds(pl.multiple_of(number * keys, keys), keys)
                scores = contract(key_rows[rows, :][:, :size], plain, 1, 0)
                mask = allowed(meta, number * keys, keys, places)
                fold(scores, mask, value_ones[:, rows])
                return 0

            lax.fori_loop(bounds[0] // keys, (base + tile * group - 1) // keys + 1, step, 0)

        total = accum[size : size + 1, :]
        result = accum[:size, :] / total
        log_total[number] = peak[...] + jnp.log(total)
        for part in range(tile // LANES):
            piece = result[:, part * LANES : (part + 1) * LANES]
            out_full[number * (tile // LANES) + part] = piece
            out_low[number * (tile // LANES) + part] = piece.astype(BF16)
        return 0

    lax.fori_loop(0, blocks * per, query_tile, 0)


def attend_forward(
    meta, query, own, other, pre_key, pre_value,
    tile, keys, prefix, chunk, group, length, width,
):
    sources, size, _ = own.shape
    count = query.shape[0] * width
    return pl.pallas_call(
        functools.partial(
            forward_kernel, tile=tile, keys=keys, prefix=prefix, chunk=chunk, group=group,
            length=length, width=width,
        ),
        out_shape=(
            jax.ShapeDtypeStruct((count // LANES, size, LANES), BF16),
            jax.ShapeDtypeStruct((count // LANES, size, LANES), F32),
            jax.ShapeDtypeStruct((count // tile, 1, tile), F32),
        ),
        in_specs=[SM] + [VM] * 5,
        out_specs=(VM, VM, VM),
        scratch_shapes=[
            pltpu.VMEM((sources * length, LANES), BF16),
            pltpu.VMEM((size + PAD, sources * length), BF16),
            pltpu.VMEM((size + PAD, tile), F32),
            pltpu.VMEM((1, tile), F32),
            pltpu.VMEM((8, LANES), F32),
        ],
        compiler_params=pltpu.CompilerParams(vmem_limit_bytes=48 * 2**20),
        cost_estimate=work(count, sources * length, 2),
        name="attend_forward",
    )(meta, query, own, other, pre_key, pre_value)


def in_three(values):
    high = values.astype(BF16).astype(F32)
    middle = (values - high).astype(BF16).astype(F32)
    low = values - high - middle
    row = lax.broadcasted_iota(jnp.int32, (PAD, values.shape[1]), 0)
    return jnp.where(row == 0, high, jnp.where(row == 1, middle, jnp.where(row == 2, low, 0.0)))


def backward_kernel(
    meta, query, own, other, pre_key, pre_value, grad_out, out_full, log_total,
    grad_query, grad_keep, grad_send, grad_prefix,
    key_rows, value_rows, key_columns, sums, query_sum,
    *, tile, keys, prefix, chunk, group, length, width,
):
    sources, size, whole = own.shape
    blocks = query.shape[0]
    kept = slice(whole - length, whole)
    per = width // tile
    scale = size**-0.5
    count = tile // LANES
    rank = meta[DOCS - 1]

    def extended(values):
        ones = jnp.where(
            lax.broadcasted_iota(jnp.int32, (LANES - size, values.shape[1]), 0) < 3, 1.0, 0.0
        )
        return jnp.concatenate([values.astype(F32), ones], 0)

    def fill(key, value):
        def prepare(source, _):
            rows = pl.ds(pl.multiple_of(source * length, length), length)
            found = key[source, :, kept]
            key_rows[rows, :] = extended(found).T.astype(BF16)
            value_rows[rows, :] = extended(value[source, :, kept]).T.astype(BF16)
            key_columns[:, rows] = found
            sums[rows, :] = jnp.zeros((length, LANES), F32)
            return 0

        lax.fori_loop(0, sources, prepare, 0)

    by_rank(meta, group, own, other, fill)
    grad_prefix[...] = jnp.zeros(grad_prefix.shape, F32)
    pre_row = lax.broadcasted_iota(jnp.int32, (pre_key.shape[0], tile), 0)

    def query_tile(number, _):
        source, part = number // per, number % per
        base = number * tile * group
        columns = pl.ds(pl.multiple_of(part * tile, tile), tile)
        scaled = (query[source, :, columns].astype(F32) * scale).astype(BF16)
        pieces = [number * count + piece for piece in range(count)]
        grad = jnp.concatenate([grad_out[piece] for piece in pieces], 1)
        full = jnp.concatenate([out_full[piece] for piece in pieces], 1)
        delta = jnp.sum(grad.astype(F32) * full, 0, keepdims=True)
        level = log_total[number]
        index = lax.broadcasted_iota(jnp.int32, (1, tile), 1)
        places = query_places(meta, index, base, chunk, group)
        bounds = tile_bounds(meta, base, tile, chunk, group)
        rest = jnp.zeros((LANES - size - PAD, tile), BF16)
        scaled_less = jnp.concatenate([scaled, in_three(-level).astype(BF16), rest], 0)
        grad_less = jnp.concatenate([grad, in_three(-delta).astype(BF16), rest], 0)
        none = jnp.zeros((size, tile), BF16)
        pair = jnp.concatenate(
            [jnp.concatenate([grad, none], 1), jnp.concatenate([none, scaled], 1)], 0
        )

        probs = jnp.exp(contract(pre_key[...], scaled, 1, 0) - level)
        probs = jnp.where(pre_row < prefix, probs, 0.0)
        slope = (probs * (contract(pre_value[...], grad, 1, 0) - delta)).astype(BF16)
        grad_prefix[0] += contract(slope, scaled, 1, 1)
        grad_prefix[1] += contract(probs.astype(BF16), grad, 1, 1)
        query_sum[...] = contract(pre_key[...], slope, 0, 0)

        def block(start, count, lane, masked):
            rows = pl.ds(pl.multiple_of(start, LANES), count)
            probs = jnp.exp(contract(key_rows[rows, :], scaled_less[:, lane:], 1, 0))
            if masked:
                probs = jnp.where(allowed(meta, start, count, places[:, lane:]), probs, 0.0)
            slope = probs * contract(value_rows[rows, :], grad_less[:, lane:], 1, 0)
            slope = slope.astype(BF16)
            both = jnp.concatenate([probs.astype(BF16), slope], 1)
            ends = jnp.concatenate([pair[:, lane:tile], pair[:, tile + lane :]], 1) if lane else pair
            sums[rows, :] += contract(both, ends, 1, 1)
            query_sum[:, lane:] += contract(key_columns[:, rows], slope, 1, 0)

        over_keys(bounds, base, tile, group, keys, block)
        grad_query[source, :, columns] = (query_sum[...] * scale).astype(BF16)
        return 0

    lax.fori_loop(0, blocks * per, query_tile, 0)

    def flush(keys_target, values_target):
        def step(source, _):
            rows = pl.ds(pl.multiple_of(source * length, length), length)
            turned = sums[rows, :].T.astype(BF16)
            values_target[source] = turned[:size]
            keys_target[source] = turned[size:]
            return 0

        lax.fori_loop(0, sources, step, 0)

    if group == 2:

        @pl.when(rank == 0)
        def _():
            flush(grad_keep, grad_send)

        @pl.when(rank == 1)
        def _():
            flush(grad_send, grad_keep)

    else:
        flush(grad_keep, grad_send)


def attend_backward(
    meta, query, own, other, pre_key, pre_value, grad_out, out_full, log_total,
    tile, keys, prefix, chunk, group, length, width,
):
    sources, size, _ = own.shape
    pair = jax.ShapeDtypeStruct((sources, size, length), BF16)
    return pl.pallas_call(
        functools.partial(
            backward_kernel, tile=tile, keys=keys, prefix=prefix, chunk=chunk, group=group,
            length=length, width=width,
        ),
        out_shape=(
            jax.ShapeDtypeStruct((query.shape[0], size, width), BF16),
            pair,
            pair,
            jax.ShapeDtypeStruct((2,) + pre_key.shape, F32),
        ),
        in_specs=[SM] + [VM] * 8,
        out_specs=(VM,) * 4,
        scratch_shapes=[
            pltpu.VMEM((sources * length, LANES), BF16),
            pltpu.VMEM((sources * length, LANES), BF16),
            pltpu.VMEM((size, sources * length), BF16),
            pltpu.VMEM((sources * length, LANES), F32),
            pltpu.VMEM((size, tile), F32),
        ],
        compiler_params=pltpu.CompilerParams(vmem_limit_bytes=56 * 2**20),
        cost_estimate=work(query.shape[0] * width, sources * length, 5),
        name="attend_backward",
    )(meta, query, own, other, pre_key, pre_value, grad_out, out_full, log_total)


def turn_kernel(*refs):
    count = len(refs) // 2
    for source, target in zip(refs[:count], refs[count:]):
        target[...] = source[...].astype(F32).T.astype(BF16)


def turned(*arrays):
    return pl.pallas_call(
        turn_kernel,
        out_shape=tuple(jax.ShapeDtypeStruct(a.shape[::-1], BF16) for a in arrays),
        in_specs=[VM] * len(arrays),
        out_specs=(VM,) * len(arrays),
        compiler_params=pltpu.CompilerParams(vmem_limit_bytes=8 * 2**20),
        name="turned",
    )(*arrays)


def project_kernel(rows, columns, weight, bias, full, sent, stats, *, heads, size, step):
    length = rows.shape[1]
    pieces = length // step
    half = step // 2
    width = length // 2
    for piece in range(pieces):
        lanes = slice(piece * step, (piece + 1) * step)
        values = rows[:, lanes].astype(F32)
        mean = jnp.mean(values, 0, keepdims=True)
        centered = values - mean
        inverse = lax.rsqrt(jnp.mean(centered * centered, 0, keepdims=True) + EPS)
        stats[0:1, lanes] = mean
        stats[1:2, lanes] = inverse
        low = (centered * inverse * columns[:, 0:1] + columns[:, 1:2]).astype(BF16)
        full[:, lanes] = low
        mixed = (contract(weight[...], low, 1, 0) + bias[...]).astype(BF16)
        for head in range(heads):
            part = mixed[head * 3 * size : (head + 1) * 3 * size]
            spot = slice(piece * half, (piece + 1) * half)
            sent[2 * head, :, spot] = part[:size, :half]
            sent[2 * head + 1, :, spot] = part[:size, half:]
            spot = slice(width + piece * step, width + (piece + 1) * step)
            sent[2 * head, :, spot] = part[size : 2 * size]
            sent[2 * head + 1, :, spot] = part[2 * size :]


def project(rows, columns, weight, bias, heads, size, step):
    width, length = rows.shape
    return pl.pallas_call(
        functools.partial(project_kernel, heads=heads, size=size, step=step),
        out_shape=(
            jax.ShapeDtypeStruct((width, length), BF16),
            jax.ShapeDtypeStruct((2 * heads, size, length // 2 * 3), BF16),
            jax.ShapeDtypeStruct((2, length), F32),
        ),
        in_specs=[VM] * 4,
        out_specs=(VM, VM, VM),
        compiler_params=pltpu.CompilerParams(vmem_limit_bytes=20 * 2**20),
        name="project",
    )(rows, columns, weight, bias)


def unproject_kernel(
    spot, came, weight, rows, stats, columns, own_grad,
    flat, part, row_sums, sums, head_sums,
    *, heads, size, step,
):
    length = rows.shape[1]
    half = step // 2
    past = length // 2
    gain = columns[:, 0:1]
    sums[...] = jnp.zeros(sums.shape, F32)
    head_sums[...] = jnp.zeros(head_sums.shape, F32)
    for piece in range(length // step):
        lanes = slice(piece * step, (piece + 1) * step)
        place = slice(piece * half, (piece + 1) * half)
        pair = slice(past + piece * step, past + (piece + 1) * step)
        pieces = []
        for head in range(heads):
            first, second = 2 * head, 2 * head + 1
            pieces.append(jnp.concatenate([came[first, :, place], came[second, :, place]], 1))
            pieces += [came[first, :, pair], came[second, :, pair]]
        grads = jnp.concatenate(pieces, 0)
        flat[:, lanes] = grads
        head_sums[...] += jnp.sum(grads.astype(F32), 1, keepdims=True)
        back = contract(weight[...], grads, 1, 0)
        part[:, lanes] = back.astype(BF16)

        @pl.when(spot[0] == piece)
        def _():
            part[:, lanes] = (back + own_grad[...] / (stats[1:2, lanes] * gain)).astype(BF16)

        normed = (rows[:, lanes].astype(F32) - stats[0:1, lanes]) * stats[1:2, lanes]
        scaled = back * gain
        row_sums[0:1, lanes] = jnp.sum(scaled, 0, keepdims=True)
        row_sums[1:2, lanes] = jnp.sum(scaled * normed, 0, keepdims=True)
        sums[:, 0:1] += jnp.sum(back * normed, 1, keepdims=True)
        sums[:, 1:2] += jnp.sum(back, 1, keepdims=True)


def unproject(spot, came, weight, rows, stats, columns, own_grad, heads, size, step):
    width, length = rows.shape
    mixed = 3 * heads * size
    return pl.pallas_call(
        functools.partial(unproject_kernel, heads=heads, size=size, step=step),
        out_shape=(
            jax.ShapeDtypeStruct((mixed, length), BF16),
            jax.ShapeDtypeStruct((width, length), BF16),
            jax.ShapeDtypeStruct((2, length), F32),
            jax.ShapeDtypeStruct((width, 2), F32),
            jax.ShapeDtypeStruct((mixed, 1), F32),
        ),
        in_specs=[SM] + [VM] * 6,
        out_specs=(VM,) * 5,
        compiler_params=pltpu.CompilerParams(vmem_limit_bytes=20 * 2**20),
        cost_estimate=pl.CostEstimate(
            flops=4 * mixed * width * length, bytes_accessed=2**23, transcendentals=0
        ),
        name="unproject",
    )(spot, came, weight, rows, stats, columns, own_grad)


def finish_kernel(up, down, own_up, own_down, rows, gain, stats, row_sums, grad):
    half = up.shape[0]
    mean, inverse = stats[0:1], stats[1:2]
    first, second = row_sums[0:1], row_sums[1:2]
    for start, came, own in ((0, up, own_up), (half, down, own_down)):
        spot = slice(start, start + half)
        total = came[...].astype(F32) + own[...].astype(F32)
        normed = (rows[spot].astype(F32) - mean) * inverse
        back = inverse * (gain[spot] * total - first - normed * second)
        grad[:, spot] = back.T.astype(BF16)


def finish(up, down, own_up, own_down, rows, gain, stats, row_sums):
    return pl.pallas_call(
        finish_kernel,
        out_shape=jax.ShapeDtypeStruct(rows.shape[::-1], BF16),
        in_specs=[VM] * 8,
        out_specs=VM,
        compiler_params=pltpu.CompilerParams(vmem_limit_bytes=8 * 2**20),
        name="finish",
    )(up, down, own_up, own_down, rows, gain, stats, row_sums)


def feed_kernel(rows, grads, up_turned, up, down, bias, hidden, grad_pre, part):
    pre = contract(up_turned[...], rows[0], 1, 0) + bias[...]
    act, pull = jax.vjp(gelu_tanh, pre)
    hidden[0] = act.astype(BF16)
    given = grads[...] if len(grads.shape) == 2 else grads[0]
    low = pull(contract(down[...], given, 1, 0))[0].astype(BF16)
    grad_pre[0] = low
    part[0] = contract(up[...], low, 1, 0).astype(BF16)


def feed(rows, grads, up_turned, up, down, bias):
    blocks, width, count = rows.shape
    inner = down.shape[0]

    def whole(shape):
        return pl.BlockSpec(shape, lambda i: (0,) * len(shape), pipeline_mode=pl.Buffered(1))

    def block(size):
        return pl.BlockSpec((1, size, count), lambda i: (i, 0, 0))

    if count % LANES:
        grads = grads.reshape(width, blocks, count).transpose(1, 0, 2)

    return pl.pallas_call(
        feed_kernel,
        grid=(blocks,),
        out_shape=(
            jax.ShapeDtypeStruct((blocks, inner, count), BF16),
            jax.ShapeDtypeStruct((blocks, inner, count), BF16),
            jax.ShapeDtypeStruct((blocks, width, count), BF16),
        ),
        in_specs=[
            block(width),
            block(width) if count % LANES else pl.BlockSpec((width, count), lambda i: (0, i)),
            whole((inner, width)),
            whole((width, inner)),
            whole((inner, width)),
            whole((inner, 1)),
        ],
        out_specs=(block(inner), block(inner), block(width)),
        compiler_params=pltpu.CompilerParams(vmem_limit_bytes=28 * 2**20),
        cost_estimate=pl.CostEstimate(
            flops=6 * blocks * width * inner * count, bytes_accessed=2**24, transcendentals=0
        ),
        name="feed",
    )(rows, grads, up_turned, up, down, bias)


def feed_weights_kernel(rows, grads, hidden, grad_pre, grad_down, grad_up, bias, *, square):
    blocks, width, count = rows.shape
    inner = hidden.shape[1]

    def lanes(n):
        return slice(n * count, (n + 1) * count)

    def weights(target, first, second, columns):
        step = min(256, columns)
        whole = jnp.concatenate([first(n) for n in range(blocks)], 1)
        for start in range(0, columns, step):
            tile = slice(start, start + step)
            turned = jnp.concatenate([second(n, tile) for n in range(blocks)], 1)
            target[:, tile] = contract(whole, turned, 1, 1).astype(BF16)

    weights(grad_down, lambda n: hidden[n], lambda n, tile: grads[tile, lanes(n)], width)
    if square:
        weights(grad_up, lambda n: rows[n], lambda n, tile: grad_pre[n, tile], inner)
    else:
        weights(grad_up, lambda n: grad_pre[n], lambda n, tile: rows[n, tile], width)
    bias[...] = sum(jnp.sum(grad_pre[n].astype(F32), 1, keepdims=True) for n in range(blocks))


def feed_weights(rows, grads, hidden, grad_pre):
    blocks, width, count = rows.shape
    inner = hidden.shape[1]
    return pl.pallas_call(
        functools.partial(feed_weights_kernel, square=inner == width),
        out_shape=(
            jax.ShapeDtypeStruct((inner, width), BF16),
            jax.ShapeDtypeStruct((inner, width), BF16),
            jax.ShapeDtypeStruct((inner, 1), F32),
        ),
        in_specs=[VM] * 4,
        out_specs=(VM,) * 3,
        compiler_params=pltpu.CompilerParams(vmem_limit_bytes=14 * 2**20),
        cost_estimate=pl.CostEstimate(
            flops=4 * blocks * width * inner * count, bytes_accessed=2**24, transcendentals=0
        ),
        name="feed_weights",
    )(rows, grads, hidden, grad_pre)


def feed_out_kernel(spot, hidden, down_turned, middle, columns, out):
    features = out.shape[2]
    for n in range(hidden.shape[0]):
        result = contract(down_turned[...], hidden[n], 1, 0)

        def put(values):
            for block in range(out.shape[0]):
                out[block, n] = values[block * features : (block + 1) * features].astype(BF16)

        put(result)

        @pl.when(spot[0] == n)
        def _():
            put(result + middle[...] + columns[:, 5:6])


def feed_out(spot, hidden, down_turned, middle, columns):
    blocks, inner, count = hidden.shape
    width = middle.shape[0]
    return pl.pallas_call(
        feed_out_kernel,
        out_shape=jax.ShapeDtypeStruct((blocks, blocks, width // blocks, count), BF16),
        in_specs=[SM] + [VM] * 4,
        out_specs=VM,
        compiler_params=pltpu.CompilerParams(vmem_limit_bytes=8 * 2**20),
        cost_estimate=pl.CostEstimate(
            flops=2 * blocks * width * inner * count, bytes_accessed=2**23, transcendentals=0
        ),
        name="feed_out",
    )(spot, hidden, down_turned, middle, columns)


def enter_kernel(
    spot, came, weight, tokens, columns, attended, middle, normed, inverse, low, *, heads
):
    size, half = came.shape[1:]
    count = 2 * half
    tensors = came.shape[0] // (2 * heads)
    for block in range(tensors):
        for head in range(heads):
            row = (block * heads + head) * size
            for rank in range(2):
                attended[row : row + size, rank * half : (rank + 1) * half] = came[
                    (2 * head + rank) * tensors + block
                ]
    branch = contract(attended[...], weight[...], 0, 0).T
    lanes = pl.ds(pl.multiple_of(spot[0] * count, count), count)
    values = tokens[:, lanes].astype(F32) + branch + columns[:, 4:5]
    middle[...] = values
    centered = values - jnp.mean(values, 0, keepdims=True)
    scale = lax.rsqrt(jnp.mean(centered * centered, 0, keepdims=True) + EPS)
    inverse[...] = scale
    centered = centered * scale
    normed[...] = centered
    low[...] = (centered * columns[:, 2:3] + columns[:, 3:4]).astype(BF16)


def enter(spot, came, weight, tokens, columns, heads):
    width, count = tokens.shape[0], 2 * came.shape[2]
    return pl.pallas_call(
        functools.partial(enter_kernel, heads=heads),
        out_shape=(
            jax.ShapeDtypeStruct((width, count), BF16),
            jax.ShapeDtypeStruct((width, count), F32),
            jax.ShapeDtypeStruct((width, count), F32),
            jax.ShapeDtypeStruct((1, count), F32),
            jax.ShapeDtypeStruct((width, count), BF16),
        ),
        in_specs=[SM] + [VM] * 4,
        out_specs=(VM,) * 5,
        compiler_params=pltpu.CompilerParams(vmem_limit_bytes=12 * 2**20),
        name="enter",
    )(spot, came, weight, tokens, columns)


def leave_kernel(
    spot, up, down, own_up, own_down, normed, inverse, grads, weight, columns,
    middle, branch, sums, sent,
    *, heads,
):
    size, half = sent.shape[1:]
    count = 2 * half
    tensors = sent.shape[0] // (2 * heads)
    total = jnp.concatenate(
        [
            up[...].astype(F32) + own_up[...].astype(F32),
            down[...].astype(F32) + own_down[...].astype(F32),
        ],
        0,
    )
    scaled = total * columns[:, 2:3]
    first = jnp.mean(scaled, 0, keepdims=True)
    second = jnp.mean(scaled * normed[...], 0, keepdims=True)
    lanes = pl.ds(pl.multiple_of(spot[0] * count, count), count)
    result = grads[:, lanes].astype(F32) + inverse[...] * (
        scaled - first - normed[...] * second
    )
    middle[...] = result
    low = result.astype(BF16)
    branch[...] = low
    back = contract(weight[...], low, 1, 0).astype(BF16)
    for block in range(tensors):
        for head in range(heads):
            row = (block * heads + head) * size
            for rank in range(2):
                sent[(2 * head + rank) * tensors + block] = back[
                    row : row + size, rank * half : (rank + 1) * half
                ]
    sums[:, 0:1] = jnp.sum(total * normed[...], 1, keepdims=True)
    sums[:, 1:2] = jnp.sum(total, 1, keepdims=True)
    sums[:, 2:3] = jnp.sum(result, 1, keepdims=True)


def leave(spot, terms, normed, inverse, grads, weight, columns, heads, size):
    width, count = normed.shape
    blocks = width // size
    return pl.pallas_call(
        functools.partial(leave_kernel, heads=heads),
        out_shape=(
            jax.ShapeDtypeStruct((width, count), F32),
            jax.ShapeDtypeStruct((width, count), BF16),
            jax.ShapeDtypeStruct((width, 3), F32),
            jax.ShapeDtypeStruct((2 * blocks, size, count // 2), BF16),
        ),
        in_specs=[SM] + [VM] * 9,
        out_specs=(VM,) * 4,
        compiler_params=pltpu.CompilerParams(vmem_limit_bytes=12 * 2**20),
        name="leave",
    )(spot, *terms, normed, inverse, grads, weight, columns)


def rest_kernel(spot, flat, full, out, mine, other):
    width = full.shape[0]
    split = mine.shape[0]
    step = min(256, width)
    for start in range(0, width, step):
        tile = slice(start, start + step)
        result = contract(flat[...], full[tile], 1, 1).astype(BF16)
        first = result[:split]
        second = jnp.concatenate([result[split:], out[:, tile]], 0)

        @pl.when(spot[1] == 0)
        def _():
            mine[:, tile] = first
            other[:, tile] = second

        @pl.when(spot[1] == 1)
        def _():
            mine[:, tile] = second
            other[:, tile] = first


def rest_halves(spot, flat, full, out):
    half = (flat.shape[0] + out.shape[0]) // 2
    return pl.pallas_call(
        rest_kernel,
        out_shape=(jax.ShapeDtypeStruct((half, full.shape[0]), BF16),) * 2,
        in_specs=[SM] + [VM] * 3,
        out_specs=(VM, VM),
        compiler_params=pltpu.CompilerParams(vmem_limit_bytes=8 * 2**20),
        cost_estimate=pl.CostEstimate(
            flops=2 * flat.shape[0] * full.size, bytes_accessed=2**23, transcendentals=0
        ),
        name="rest_halves",
    )(spot, flat, full, out)


def rest_whole_kernel(spot, half, other, mixed, out):
    rows = half.shape[0]
    extra = mixed.shape[0] - rows

    def write(first, second):
        mixed[:rows] = first[...].astype(F32)
        mixed[rows:] = second[:extra].astype(F32)
        out[...] = second[extra:].astype(F32)

    @pl.when(spot[1] == 0)
    def _():
        write(half, other)

    @pl.when(spot[1] == 1)
    def _():
        write(other, half)


def rest_whole(spot, half, other, rows):
    width = half.shape[1]
    return pl.pallas_call(
        rest_whole_kernel,
        out_shape=(
            jax.ShapeDtypeStruct((rows, width), F32),
            jax.ShapeDtypeStruct((2 * half.shape[0] - rows, width), F32),
        ),
        in_specs=[SM, VM, VM],
        out_specs=(VM, VM),
        compiler_params=pltpu.CompilerParams(vmem_limit_bytes=8 * 2**20),
        name="rest_whole",
    )(spot, half, other)


def prefix_kernel(total, hidden, embed, weight, grad_embed, grad_weight, grad_bias):
    rows = hidden.shape[0]
    pre = total[...] * (1.0 - hidden[...] * hidden[...])
    grad_bias[...] = jnp.sum(pre, 0, keepdims=True)

    def exact(first, second, dims):
        return lax.dot_general(
            first, second, ((dims[:1], dims[1:]), ((), ())),
            preferred_element_type=F32, precision=HIGHEST,
        )

    wide = embed[...].astype(F32)
    grad_weight[...] = exact(wide, pre, (0, 0))
    grad_embed[...] = exact(pre, weight[...].astype(F32), (1, 1))[:rows]


def prefix_back(total, hidden, embed, weight):
    rows, width = embed.shape
    extra = -rows % 8
    total, hidden = [jnp.pad(a, ((0, extra), (0, 0))) for a in (total, hidden)]
    embed = jnp.pad(embed, ((0, extra), (0, 0)))
    grad_embed, grad_weight, grad_bias = pl.pallas_call(
        prefix_kernel,
        out_shape=(
            jax.ShapeDtypeStruct((rows + extra, width), F32),
            jax.ShapeDtypeStruct(weight.shape, F32),
            jax.ShapeDtypeStruct((1, weight.shape[1]), F32),
        ),
        in_specs=[VM] * 4,
        out_specs=(VM,) * 3,
        compiler_params=pltpu.CompilerParams(vmem_limit_bytes=12 * 2**20),
        name="prefix_back",
    )(total, hidden, embed, weight)
    return grad_embed[:rows], grad_weight, grad_bias[0]


def spread(values, axis):
    count = lax.axis_size(axis)
    copies = jnp.broadcast_to(values[None], (count,) + values.shape)
    return lax.all_to_all(copies, axis, 0, 0, tiled=True)


def small_sum(values, axis):
    return jnp.sum(spread(values, axis), 0)


def ring(axis, by):
    count = lax.axis_size(axis)
    return [(source, (source + by) % count) for source in range(count)]


def ring_gather(values, axis, beside=()):
    count, place = lax.axis_size(axis), lax.axis_index(axis)
    half = values.shape[0] // 2
    up, down = values[:half], values[half:]
    out = jnp.zeros((count,) + values.shape, values.dtype)
    out = lax.dynamic_update_slice_in_dim(out, values[None], place, 0)
    zeros = (0,) * (values.ndim - 1)
    results = []
    for step in range(1, count):
        up = lax.ppermute(up, axis, ring(axis, 1))
        down = lax.ppermute(down, axis, ring(axis, -1))
        if step <= len(beside) and beside[step - 1]:
            up, down, result = lax.optimization_barrier((up, down, beside[step - 1]()))
            results.append(result)
        out = lax.dynamic_update_slice(out, up[None], ((place - step) % count, 0) + zeros)
        out = lax.dynamic_update_slice(out, down[None], ((place + step) % count, half) + zeros)
    return (out, results) if beside else out


def ring_terms(blocks, axis, beside=()):
    count, place = lax.axis_size(axis), lax.axis_index(axis)
    half = blocks.shape[1] // 2

    def own(offset, upper):
        block = lax.dynamic_index_in_dim(blocks, (place + offset) % count, 0, keepdims=False)
        return block[half:] if upper else block[:half]

    up, down = own(-1, False), own(1, True)
    state = None
    for step in range(1, count):
        up = lax.ppermute(up, axis, ring(axis, 1))
        down = lax.ppermute(down, axis, ring(axis, -1))
        if step <= len(beside):
            state = beside[step - 1](state)
            up, down, state = lax.optimization_barrier((up, down, state))
        if step < count - 1:
            up = (up.astype(F32) + own(-1 - step, False).astype(F32)).astype(BF16)
            down = (down.astype(F32) + own(1 + step, True).astype(F32)).astype(BF16)
    for other in beside[count - 1 :]:
        state = other(state)
    return (up, down, own(0, False), own(0, True)), state


def swapped(values):
    pairs = [(source, source ^ 1) for source in range(lax.axis_size("seq"))]
    return lax.ppermute(values, "seq", pairs)


def chip_groups():
    chips = lax.axis_size("seq") // 2
    return [[2 * chip + core for chip in range(chips)] for core in range(2)]


def chip_parts_direct(half):
    count = lax.axis_size("seq")
    chips = count // 2
    chip = lax.axis_index("seq") // 2
    blocks = half.reshape(chips, half.shape[0] // chips, half.shape[1])
    total = lax.dynamic_index_in_dim(blocks, chip, 0, keepdims=False)
    parts = [total]
    for step in range(1, chips):
        block = lax.dynamic_index_in_dim(blocks, (chip + step) % chips, 0, keepdims=False)
        parts.append(lax.ppermute(block, "seq", ring("seq", 2 * step)))
    return parts


def owned_direct(values, axis):
    count, place = lax.axis_size(axis), lax.axis_index(axis)
    parts = [lax.dynamic_index_in_dim(values, place, 0, keepdims=False)]
    for step in range(1, count):
        block = lax.dynamic_index_in_dim(values, (place + step) % count, 0, keepdims=False)
        parts.append(lax.ppermute(block, axis, ring(axis, step)))
    return parts


def chip_copies(parts):
    part = sum(part.astype(F32) for part in parts).astype(BF16)
    return jnp.broadcast_to(part[None], (len(parts),) + part.shape)


def chip_gather(copies):
    half = lax.all_to_all(copies, "seq", 0, 0, axis_index_groups=chip_groups(), tiled=True)
    return half.reshape(-1, half.shape[2])


def spread_direct(values, axis):
    count, place = lax.axis_size(axis), lax.axis_index(axis)
    out = jnp.zeros((count,) + values.shape, values.dtype)
    out = lax.dynamic_update_slice_in_dim(out, values[None], place, 0)
    for step in range(1, count):
        came = lax.ppermute(values, axis, ring(axis, step))
        out = lax.dynamic_update_slice_in_dim(out, came[None], (place - step) % count, 0)
    return out


def core_gather(half):
    core = lax.axis_index("seq") % 2
    other = swapped(half)
    first = jnp.where(core == 0, half, other)
    second = jnp.where(core == 0, other, half)
    return first, second


def regrouped(values, width):
    count, size, columns = values.shape
    if width == columns:
        return values
    if width > columns:
        merged = values.reshape(-1, width // columns, size, columns).transpose(0, 2, 1, 3)
        return merged.reshape(-1, size, width)
    cut = values.reshape(count, size, columns // width, width).transpose(0, 2, 1, 3)
    return cut.reshape(-1, size, width)


def group_gather(pieces, group):
    if group == 2:
        rank = lax.axis_index("seq") % 2
        other = swapped(pieces)
        return jnp.stack([jnp.where(rank == 0, pieces, other), jnp.where(rank == 0, other, pieces)])
    count = lax.axis_size("seq")
    groups = [[first + i for i in range(group)] for first in range(0, count, group)]
    return lax.all_gather(pieces, "seq", axis_index_groups=groups)


def on_device(
    tokens,
    segment_ids,
    out_grad,
    ln1_gain,
    ln1_bias,
    w_qkv,
    b_qv,
    w_out,
    b_out,
    ln2_gain,
    ln2_bias,
    w_up,
    b_up,
    w_down,
    b_down,
    prefix_embed,
    reparam_in,
    reparam_in_bias,
    reparam_out,
    reparam_out_bias,
):
    rows, features = tokens.shape
    heads = w_qkv.shape[1]
    size = w_qkv.shape[2] // 3
    inner = w_up.shape[1]
    seqs, tensors = lax.axis_size("seq"), lax.axis_size("tensor")
    width = features * tensors
    own_rows = rows // tensors
    group = seqs // heads
    chunk = own_rows // group
    place, slot = lax.axis_index("seq"), lax.axis_index("tensor")
    head, rank = place // group, place % group
    prefix = prefix_embed.shape[0]
    tokens_head = rows // group
    query_width = max(tokens_head, LANES)
    forward_tile = min(512, query_width)
    backward_tile = min(512, query_width)
    forward_keys, backward_keys = 1024, 1024
    both = ("seq", "tensor")
    paired = group == 2 and chunk == LANES

    own_tokens, own_grads = turned(tokens, out_grad)
    numbers = jnp.arange(1, DOCS, dtype=jnp.int32)

    def document_starts():
        before = jnp.sum((segment_ids[None, :] < numbers[:, None]).astype(jnp.int32), 1)
        return spread(jnp.broadcast_to(before[:, None], (DOCS - 1, LANES)), "seq")

    def whole_vectors():
        return spread(
            jnp.stack([ln1_gain, ln1_bias, ln2_gain, ln2_bias, b_out, b_down]), "tensor"
        )

    full_tokens, (vectors, starts) = ring_gather(
        own_tokens, "tensor", (None, whole_vectors, document_starts)
    )
    full_tokens = full_tokens.reshape(width, rows)
    meta = jnp.concatenate([jnp.sum(starts, 0)[:, 0], rank[None].astype(jnp.int32)])
    columns = vectors.transpose(0, 2, 1).reshape(width, 6).astype(F32)
    out_share = w_out.reshape(seqs, heads * size // seqs, width)
    out_share = lax.dynamic_index_in_dim(out_share, place, 0, keepdims=False)
    core = place % 2
    spot = jnp.stack([slot, core]).astype(jnp.int32)

    prefix_hidden = jnp.tanh(
        jnp.dot(prefix_embed, reparam_in, preferred_element_type=F32)
        + reparam_in_bias.astype(F32)
    )
    prefix_pair = jnp.einsum(
        "pa,ahe->phe", prefix_hidden, reparam_out.astype(F32), precision=HIGHEST
    )
    prefix_pair = (prefix_pair + reparam_out_bias.astype(F32)).astype(BF16)
    own_pair = lax.dynamic_index_in_dim(prefix_pair, head, 1, keepdims=False)
    own_pair = jnp.pad(own_pair, ((0, LANES - prefix), (0, 0)))
    pre_key, pre_value = own_pair[:, :size], own_pair[:, size:]

    w_flat = w_qkv.reshape(width, heads * 3 * size)
    bias_pair = b_qv.astype(F32)
    bias_three = jnp.stack(
        [bias_pair[:, :size], jnp.zeros((heads, size), F32), bias_pair[:, size:]], 1
    ).reshape(-1, 1)
    if paired:
        full1, sent, stats = project(
            full_tokens, columns, w_flat.T, bias_three, heads, size, own_rows
        )
    else:
        wide = full_tokens.astype(F32)
        mean = jnp.mean(wide, 0, keepdims=True)
        inverse = lax.rsqrt(jnp.mean((wide - mean) ** 2, 0, keepdims=True) + EPS)
        stats = jnp.concatenate([mean, inverse], 0)
        full1 = ((wide - mean) * inverse * columns[:, 0:1] + columns[:, 1:2]).astype(BF16)
        mixed = (contract(w_flat, full1, 0, 0) + bias_three).astype(BF16)
        mixed = mixed.reshape(heads, 3, size, rows)
        query_part = mixed[:, 0].reshape(heads, size, tensors, group, chunk)
        query_part = query_part.transpose(0, 3, 1, 2, 4).reshape(seqs, size, tokens_head)
        pair_part = mixed[:, 1:].transpose(0, 2, 1, 3).reshape(heads, size, group, 2 * tokens_head)
        pair_part = pair_part.transpose(0, 2, 1, 3).reshape(seqs, size, 2 * tokens_head)
        sent = jnp.concatenate([query_part, pair_part], 2)
    out_share = spread_direct(after(out_share, sent), "tensor")
    came = lax.all_to_all(sent, "seq", 0, 0, tiled=True)
    came, out_share = lax.optimization_barrier((came, out_share))
    w_out_full = lax.all_gather(out_share, "seq")
    w_out_full = w_out_full.transpose(1, 0, 2, 3).reshape(width, width)
    if group == 2:
        query, own, other = came, came, swapped(came)
    else:
        query, pair = came[:, :, :tokens_head], came[:, :, tokens_head:]
        query = regrouped(query, query_width)
        pair = group_gather(pair, group).transpose(1, 2, 0, 3).reshape(seqs, size, 2, rows)
        own, other = pair[:, :, 0], pair[:, :, 1]
    full_grad = lax.all_gather(after(own_grads, full_tokens), "tensor", axis=0, tiled=True)
    out_low, out_full, log_total = attend_forward(
        meta, query, own, other, pre_key.T, pre_value.T,
        forward_tile, forward_keys, prefix, chunk, group, rows, query_width,
    )
    out_low, full_grad, late_up, late_down, late_qkv = lax.optimization_barrier(
        (out_low, full_grad, w_up, w_down, w_qkv)
    )
    late_flat = late_qkv.reshape(width, heads * 3 * size)

    came = lax.all_to_all(regrouped(out_low, chunk), both, 0, 0, tiled=True)
    came, up_turned, down_turned, late_flat, w_out_full = lax.optimization_barrier(
        (came, late_up.T, late_down.T, late_flat, w_out_full)
    )
    if paired:
        attended, middle, normed2, inverse2, out2 = enter(
            spot, came, w_out_full, full_tokens, columns, heads
        )
    else:
        came = came.reshape(heads, group, tensors, size, chunk).transpose(2, 0, 3, 1, 4)
        attended = came.reshape(width, own_rows)
        branch = contract(w_out_full, attended, 0, 0)
        own_block = lax.dynamic_slice_in_dim(full_tokens, slot * own_rows, own_rows, 1)
        middle = own_block.astype(F32) + branch + columns[:, 4:5]
        centered = middle - jnp.mean(middle, 0, keepdims=True)
        inverse2 = lax.rsqrt(jnp.mean(centered * centered, 0, keepdims=True) + EPS)
        normed2 = centered * inverse2
        out2 = (normed2 * columns[:, 2:3] + columns[:, 3:4]).astype(BF16)

    full2 = ring_gather(out2, "tensor")
    hidden, grad_pre, part = feed(
        full2, full_grad, up_turned, w_up, w_down, b_up.astype(F32)[:, None]
    )

    def weights_here(_):
        return feed_weights(full2, full_grad, hidden, grad_pre)

    def out_here(state):
        return state, feed_out(spot, hidden, down_turned, middle, columns)

    terms, (weights, mlp_out) = ring_terms(part, "tensor", (weights_here, out_here))
    grad_w_down, grad_w_up, grad_b_up = weights
    feed_sums = lax.psum((grad_w_down, grad_w_up), "seq")

    if paired:
        grad_middle, grad_branch, token_sums, sent = leave(
            spot, terms, normed2, inverse2, full_grad, w_out_full, columns, heads, size
        )
    else:
        up, down, own_up, own_down = [a.astype(F32) for a in terms]
        grad_normed2 = jnp.concatenate([up + own_up, down + own_down], 0)
        scaled = grad_normed2 * columns[:, 2:3]
        first = jnp.mean(scaled, 0, keepdims=True)
        second = jnp.mean(scaled * normed2, 0, keepdims=True)
        own_grad = lax.dynamic_slice_in_dim(full_grad, slot * own_rows, own_rows, 1)
        grad_middle = own_grad.astype(F32) + inverse2 * (scaled - first - normed2 * second)
        grad_branch = grad_middle.astype(BF16)
        token_sums = [grad_normed2 * normed2, grad_normed2, grad_middle]
        token_sums = jnp.stack([jnp.sum(a, 1) for a in token_sums], 1)
        sent = contract(w_out_full, grad_branch, 1, 0).astype(BF16)
        sent = sent.reshape(tensors, heads, size, group, chunk).transpose(1, 3, 0, 2, 4)
        sent = sent.reshape(seqs * tensors, size, chunk)
    came = lax.all_to_all(sent, both, 0, 0, tiled=True)
    grad_out = regrouped(came, LANES)

    grad_w_out = contract(attended, grad_branch, 1, 1).astype(BF16)
    grad_out, mlp_out, grad_w_out = lax.optimization_barrier((grad_out, mlp_out, grad_w_out))
    output_act = lax.all_to_all(mlp_out, "tensor", 0, 0, tiled=True)
    grad_w_out = lax.psum_scatter(grad_w_out, "tensor", scatter_dimension=0, tiled=True)

    levels = log_total.reshape(-1, 1, backward_tile)
    grad_query, grad_keep, grad_send, grad_prefix = attend_backward(
        meta, query, own, other, pre_key[:PAD], pre_value[:PAD], grad_out, out_full, levels,
        backward_tile, backward_keys, prefix, chunk, group, rows, query_width,
    )
    if group == 2:
        grad_share = (grad_keep.astype(F32) + swapped(grad_send).astype(F32)).astype(BF16)
    else:
        grad_pair = jnp.stack([grad_keep, grad_send])
        groups = [[first + i for i in range(group)] for first in range(0, seqs, group)]
        shares = grad_pair.transpose(1, 2, 0, 3).reshape(seqs, size, group, 2 * tokens_head)
        grad_share = lax.psum_scatter(
            shares.transpose(2, 0, 1, 3), "seq", axis_index_groups=groups
        )
    prefix_part = grad_prefix.transpose(2, 0, 1).reshape(size, 2 * PAD).astype(BF16)
    prefix_part = jnp.pad(prefix_part, ((0, 0), (0, LANES - 2 * PAD)))
    prefix_part = jnp.broadcast_to(prefix_part[None], (seqs, size, LANES))
    sent = jnp.concatenate([regrouped(grad_query, tokens_head), grad_share, prefix_part], 2)
    sent, output_act, feed_sums = lax.optimization_barrier((sent, output_act, feed_sums))
    came = lax.all_to_all(sent, "seq", 0, 0, tiled=True)
    output_act = jnp.sum(output_act.astype(F32), 0).astype(BF16)
    output_act = output_act.transpose(0, 2, 1).reshape(rows, features)
    out_w_down = feed_sums[0].astype(F32)
    out_w_up = (feed_sums[1] if inner == width else feed_sums[1].T).astype(F32)
    came, output_act, grad_w_out, out_w_down, out_w_up = lax.optimization_barrier(
        (came, output_act, grad_w_out, out_w_down, out_w_up)
    )
    if paired:
        grad_flat, grad_part, row_sums, sums1, head_sums = unproject(
            spot, came, late_flat, full_tokens, stats, columns, grad_middle, heads, size, own_rows
        )
    else:
        query_part = came[:, :, :tokens_head].reshape(heads, group, size, tensors, chunk)
        query_part = query_part.transpose(0, 2, 3, 1, 4).reshape(heads, 1, size, rows)
        pair_part = came[:, :, tokens_head : 3 * tokens_head]
        pair_part = pair_part.reshape(heads, group, size, 2 * tokens_head).transpose(0, 2, 1, 3)
        pair_part = pair_part.reshape(heads, size, 2, rows).transpose(0, 2, 1, 3)
        grad_flat = jnp.concatenate([query_part, pair_part], 1).reshape(heads * 3 * size, rows)
        back = contract(late_flat, grad_flat, 1, 0)
        normed1 = (full_tokens.astype(F32) - stats[0]) * stats[1]
        scaled = back * columns[:, 0:1]
        row_sums = jnp.stack([jnp.sum(scaled, 0), jnp.sum(scaled * normed1, 0)])
        sums1 = jnp.stack([jnp.sum(back * normed1, 1), jnp.sum(back, 1)], 1)
        head_sums = jnp.sum(grad_flat.astype(F32), 1)
        own_inverse = lax.dynamic_slice_in_dim(stats[1:2], slot * own_rows, own_rows, 1)
        own_part = lax.dynamic_slice_in_dim(back, slot * own_rows, own_rows, 1)
        own_part = own_part + grad_middle / (own_inverse * columns[:, 0:1])
        back = lax.dynamic_update_slice_in_dim(back, own_part, slot * own_rows, 1)
        grad_part = back.astype(BF16)
    prefix_low = came[:, :, 3 * tokens_head : 3 * tokens_head + 2 * PAD].astype(F32)
    prefix_low = jnp.sum(prefix_low.reshape(heads, group, size, 2, PAD), 1)[..., :prefix]
    prefix_low = prefix_low.transpose(3, 0, 2, 1).reshape(prefix, heads, 2 * size).astype(BF16)
    prefix_grad = prefix_low.astype(F32)
    hidden_part = jnp.einsum("phe,ahe->pa", prefix_low, reparam_out, preferred_element_type=F32)
    owned = jnp.concatenate([sums1, token_sums], 1).T
    owned = owned.reshape(-1, tensors, features).transpose(1, 0, 2).reshape(tensors, -1)
    shared = jnp.concatenate([row_sums.reshape(-1), hidden_part.reshape(-1)])
    shared = jnp.broadcast_to(shared[None], (tensors, shared.shape[0]))
    small = jnp.concatenate([owned, shared], 1)[:, None, :]

    grad_b_down = jnp.sum(out_grad.astype(F32), 0)
    head_sums = head_sums.reshape(heads, 3, size)

    def halves_here(_):
        if paired:
            return rest_halves(spot, grad_flat, full1, grad_w_out)
        grad_w_qkv = contract(grad_flat, full1, 1, 1).astype(BF16)
        rest = jnp.concatenate([grad_w_qkv, grad_w_out], 0)
        halves = rest.reshape(2, rest.shape[0] // 2, width)
        mine = lax.dynamic_index_in_dim(halves, core, 0, keepdims=False)
        other = lax.dynamic_index_in_dim(halves, 1 - core, 0, keepdims=False)
        return mine, other

    def small_here(state):
        return state[0], swapped(state[1]), owned_direct(small, "tensor")

    def parts_here(state):
        half = (state[0].astype(F32) + state[1].astype(F32)).astype(BF16)
        sums = sum(state[2])[0]
        late = jnp.concatenate(
            [
                sums[: 5 * features],
                grad_b_down,
                grad_b_up.reshape(-1),
                head_sums[:, 0].reshape(-1),
                head_sums[:, 2].reshape(-1),
            ]
        )
        return chip_parts_direct(half), sums, spread(late[None], "seq")

    last_terms, (rest_parts, small, late) = ring_terms(
        grad_part.reshape(tensors, features, rows),
        "tensor",
        (halves_here, small_here) + (lambda state: state,) * (tensors - 4) + (parts_here,),
    )
    rest_half = chip_gather(chip_copies(rest_parts))
    late = jnp.sum(late, 0)[0]
    row_sums = small[5 * features : 5 * features + 2 * rows]
    hidden_grad = small[5 * features + 2 * rows :].reshape(prefix_hidden.shape)
    input_grad = finish(
        *last_terms, own_tokens, ln1_gain.astype(F32)[:, None], stats,
        row_sums.reshape(2, rows) / width,
    )
    mixed_rows = heads * 3 * size
    if paired:
        out_w_qkv, out_w_out = rest_whole(spot, rest_half, swapped(rest_half), mixed_rows)
    else:
        rest = jnp.concatenate(core_gather(rest_half), 0).astype(F32)
        out_w_qkv, out_w_out = rest[:mixed_rows], rest[mixed_rows:]
    out_w_qkv = out_w_qkv.reshape(heads, 3 * size, width).transpose(2, 0, 1)
    out_w_out = out_w_out.reshape(heads, size, width)
    out_ln1_gain, out_ln1_bias, out_ln2_gain, out_ln2_bias, out_b_out, out_b_down = [
        late[i * features : (i + 1) * features] for i in range(6)
    ]
    late = late[6 * features :]
    out_b_up = late[:inner]
    pair_sums = late[inner:].reshape(2, heads, size)
    out_b_qv = jnp.concatenate([pair_sums[0], pair_sums[1]], 1)

    grad_reparam_out = jnp.einsum("pa,phe->ahe", prefix_hidden, prefix_grad, precision=HIGHEST)
    grad_reparam_out_bias = jnp.sum(prefix_grad, 0)
    grad_prefix_embed, grad_reparam_in, grad_reparam_in_bias = prefix_back(
        hidden_grad, prefix_hidden, prefix_embed, reparam_in
    )
    return (
        output_act,
        input_grad,
        out_ln1_gain,
        out_ln1_bias,
        out_w_qkv,
        out_b_qv,
        out_w_out,
        out_b_out,
        out_ln2_gain,
        out_ln2_bias,
        out_w_up,
        out_b_up,
        out_w_down,
        out_b_down,
        grad_prefix_embed,
        grad_reparam_in,
        grad_reparam_in_bias,
        grad_reparam_out,
        grad_reparam_out_bias,
    )


def solution(mesh):
    placed = (
        P("seq", "tensor"),
        P("seq"),
        P("seq", "tensor"),
        P("tensor"),
        P("tensor"),
        P(None, "tensor", None),
        P("tensor", None),
        P("tensor", None, None),
        P("tensor"),
        P("tensor"),
        P("tensor"),
        P(None, "tensor"),
        P("tensor"),
        P("tensor", None),
        P("tensor"),
        P(),
        P(),
        P(),
        P(None, "tensor", None),
        P("tensor", None),
    )
    return jax.shard_map(
        on_device,
        mesh=mesh,
        in_specs=placed,
        out_specs=(
            P("seq", "tensor"),
            P("seq", "tensor"),
            P("tensor"),
            P("tensor"),
            P(None, "tensor", None),
            P("tensor", None),
            P("tensor", None, None),
            P("tensor"),
            P("tensor"),
            P("tensor"),
            P(None, "tensor"),
            P("tensor"),
            P("tensor", None),
            P("tensor"),
            P(),
            P(),
            P(),
            P(None, "tensor", None),
            P("tensor", None),
        ),
        check_vma=False,
    )
```

```python
import functools

import jax
import jax.numpy as jnp
from jax import lax
from jax.experimental import pallas as pl
from jax.experimental.pallas import tpu as pltpu
from jax.sharding import PartitionSpec as P

EPS = 1e-05
NEGATIVE = -1e30
HIGHEST = lax.Precision.HIGHEST
F32 = jnp.float32
BF16 = jnp.bfloat16
LANES = 128
PAD = 16
WEAK = 1e-24
DOCS = 5

VM = pl.BlockSpec(memory_space=pltpu.VMEM)
SM = pl.BlockSpec(memory_space=pltpu.SMEM)


def gelu_tanh(values):
    return jax.nn.gelu(values, approximate=True)


def contract(first, second, first_dim, second_dim):
    return lax.dot_general(
        first, second, (((first_dim,), (second_dim,)), ((), ())), preferred_element_type=F32
    )


def work(queries, keys, products):
    pairs = queries * keys // 2
    return pl.CostEstimate(
        flops=2 * 256 * products * pairs, bytes_accessed=8 * 2**20, transcendentals=pairs
    )


def after(values, other):
    return lax.optimization_barrier((values, other))[0]


def document_start(meta, place):
    found = jnp.zeros_like(place) if getattr(place, "shape", ()) else jnp.int32(0)
    for number in range(DOCS - 1):
        begin = meta[number]
        found = jnp.where(place >= begin, jnp.maximum(found, begin), found)
    return found


def query_places(meta, index, base, chunk, group):
    return base + (index // chunk) * (chunk * group) + meta[DOCS - 1] * chunk + index % chunk


def tile_bounds(meta, base, count, chunk, group):
    rank = meta[DOCS - 1]
    first = base + rank * chunk
    last = base + (count // chunk - 1) * (chunk * group) + rank * chunk + chunk - 1
    return document_start(meta, first), document_start(meta, last)


def one_row(rows, columns):
    return lax.broadcasted_iota(jnp.int32, (rows, columns), 0) == 0


def by_rank(meta, group, first, second, work):
    if group != 2:
        work(first, second)
        return

    @pl.when(meta[DOCS - 1] == 0)
    def _():
        work(first, second)

    @pl.when(meta[DOCS - 1] == 1)
    def _():
        work(second, first)


def over_keys(bounds, base, tile, group, keys, block):
    low, low_last = bounds

    def step(number, _):
        clear = number * keys >= low_last

        @pl.when(clear)
        def _():
            block(number * keys, keys, 0, False)

        @pl.when(jnp.logical_not(clear))
        def _():
            block(number * keys, keys, 0, True)

        return 0

    lax.fori_loop(low // keys, base // keys, step, 0)
    for stair in range(tile // LANES):
        block(base + stair * LANES * group, LANES * group, stair * LANES, True)


def allowed(meta, start, count, places):
    key = start + lax.broadcasted_iota(jnp.int32, (count, 1), 0)
    return (key <= places) & (key >= document_start(meta, places))


def forward_kernel(
    meta, query, own, other, pre_key, pre_value,
    out_low, out_full, log_total,
    key_rows, value_ones, accum, peak, norm,
    *, tile, keys, prefix, chunk, group, length, width,
):
    sources, size, whole = own.shape
    blocks = query.shape[0]
    per = width // tile
    scale = size**-0.5
    padded = pre_key.shape[1]
    kept = slice(whole - length, whole)

    def extended(values, count, total):
        ones = jnp.where(one_row(PAD, count), 1.0, 0.0).astype(BF16)
        rest = total - size - PAD
        tail = [jnp.zeros((rest, count), BF16)] if rest else []
        return jnp.concatenate([values, ones] + tail, 0)

    def longest(values):
        wide = values.astype(F32)
        return jnp.max(jnp.sum(wide * wide, 0, keepdims=True), 1, keepdims=True)

    norm[...] = jnp.broadcast_to(longest(pre_key[...]), norm.shape)

    def fill(key, value):
        def prepare(source, _):
            rows = pl.ds(pl.multiple_of(source * length, length), length)
            found = key[source, :, kept]
            key_rows[rows, :] = extended(found, length, LANES).astype(F32).T.astype(BF16)
            value_ones[:, rows] = extended(value[source, :, kept], length, size + PAD)
            norm[...] = jnp.maximum(norm[...], longest(found))
            return 0

        lax.fori_loop(0, sources, prepare, 0)

    by_rank(meta, group, own, other, fill)
    most = jnp.sqrt(norm[0:1, 0:1])
    pre_key_ones = extended(pre_key[...], padded, LANES)
    pre_value_ones = extended(pre_value[...], padded, size + PAD)
    pre_row = lax.broadcasted_iota(jnp.int32, (padded, tile), 0)

    def query_tile(number, _):
        source, part = number // per, number % per
        base = number * tile * group
        columns = pl.ds(pl.multiple_of(part * tile, tile), tile)
        scaled = query[source, :, columns].astype(F32) * scale
        limit = jnp.sqrt(jnp.sum(scaled * scaled, 0, keepdims=True)) * most
        limit = limit.astype(BF16).astype(F32)
        shifted = jnp.concatenate(
            [
                scaled,
                jnp.where(one_row(PAD, tile), -limit, 0.0),
                jnp.zeros((LANES - size - PAD, tile), F32),
            ],
            0,
        ).astype(BF16)
        index = lax.broadcasted_iota(jnp.int32, (1, tile), 1)
        places = query_places(meta, index, base, chunk, group)
        bounds = tile_bounds(meta, base, tile, chunk, group)

        weights = jnp.where(pre_row < prefix, jnp.exp(contract(pre_key_ones, shifted, 0, 0)), 0.0)
        accum[...] = contract(pre_value_ones, weights.astype(BF16), 1, 0)

        def block(start, count, lane, masked):
            rows = pl.ds(pl.multiple_of(start, LANES), count)
            weights = jnp.exp(contract(key_rows[rows, :], shifted[:, lane:], 1, 0))
            if masked:
                weights = jnp.where(allowed(meta, start, count, places[:, lane:]), weights, 0.0)
            accum[:, lane:] += contract(value_ones[:, rows], weights.astype(BF16), 1, 0)

        over_keys(bounds, base, tile, group, keys, block)
        peak[...] = limit

        @pl.when(jnp.min(accum[size : size + 1, :]) < WEAK)
        def _():
            plain = scaled.astype(BF16)

            def fold(scores, mask, values):
                scores = jnp.where(mask, scores, NEGATIVE)
                new = jnp.maximum(peak[...], jnp.max(scores, 0, keepdims=True))
                weights = jnp.where(mask, jnp.exp(scores - new), 0.0).astype(BF16)
                accum[...] = accum[...] * jnp.exp(peak[...] - new) + contract(values, weights, 1, 0)
                peak[...] = new

            peak[...] = jnp.full(peak.shape, NEGATIVE, F32)
            accum[...] = jnp.zeros(accum.shape, F32)
            fold(contract(pre_key[...], plain, 0, 0), pre_row < prefix, pre_value_ones)

            def step(number, _):
                rows = pl.ds(pl.multiple_of(number * keys, keys), keys)
                scores = contract(key_rows[rows, :][:, :size], plain, 1, 0)
                mask = allowed(meta, number * keys, keys, places)
                fold(scores, mask, value_ones[:, rows])
                return 0

            lax.fori_loop(bounds[0] // keys, (base + tile * group - 1) // keys + 1, step, 0)

        total = accum[size : size + 1, :]
        result = accum[:size, :] / total
        log_total[number] = peak[...] + jnp.log(total)
        for part in range(tile // LANES):
            piece = result[:, part * LANES : (part + 1) * LANES]
            out_full[number * (tile // LANES) + part] = piece
            out_low[number * (tile // LANES) + part] = piece.astype(BF16)
        return 0

    lax.fori_loop(0, blocks * per, query_tile, 0)


def attend_forward(
    meta, query, own, other, pre_key, pre_value,
    tile, keys, prefix, chunk, group, length, width,
):
    sources, size, _ = own.shape
    count = query.shape[0] * width
    return pl.pallas_call(
        functools.partial(
            forward_kernel, tile=tile, keys=keys, prefix=prefix, chunk=chunk, group=group,
            length=length, width=width,
        ),
        out_shape=(
            jax.ShapeDtypeStruct((count // LANES, size, LANES), BF16),
            jax.ShapeDtypeStruct((count // LANES, size, LANES), F32),
            jax.ShapeDtypeStruct((count // tile, 1, tile), F32),
        ),
        in_specs=[SM] + [VM] * 5,
        out_specs=(VM, VM, VM),
        scratch_shapes=[
            pltpu.VMEM((sources * length, LANES), BF16),
            pltpu.VMEM((size + PAD, sources * length), BF16),
            pltpu.VMEM((size + PAD, tile), F32),
            pltpu.VMEM((1, tile), F32),
            pltpu.VMEM((8, LANES), F32),
        ],
        compiler_params=pltpu.CompilerParams(vmem_limit_bytes=26 * 2**20),
        cost_estimate=work(count, sources * length, 2),
        name="attend_forward",
    )(meta, query, own, other, pre_key, pre_value)


def in_three(values):
    high = values.astype(BF16).astype(F32)
    middle = (values - high).astype(BF16).astype(F32)
    low = values - high - middle
    row = lax.broadcasted_iota(jnp.int32, (PAD, values.shape[1]), 0)
    return jnp.where(row == 0, high, jnp.where(row == 1, middle, jnp.where(row == 2, low, 0.0)))


def backward_kernel(
    meta, query, own, other, pre_key, pre_value, grad_out, out_full, log_total,
    grad_query, grad_keep, grad_send, grad_prefix,
    key_rows, value_rows, key_columns, sums, query_sum,
    *, tile, keys, prefix, chunk, group, length, width,
):
    sources, size, whole = own.shape
    blocks = query.shape[0]
    kept = slice(whole - length, whole)
    per = width // tile
    scale = size**-0.5
    count = tile // LANES
    rank = meta[DOCS - 1]

    def extended(values):
        ones = jnp.where(
            lax.broadcasted_iota(jnp.int32, (LANES - size, values.shape[1]), 0) < 3, 1.0, 0.0
        )
        return jnp.concatenate([values.astype(F32), ones], 0)

    def fill(key, value):
        def prepare(source, _):
            rows = pl.ds(pl.multiple_of(source * length, length), length)
            found = key[source, :, kept]
            key_rows[rows, :] = extended(found).T.astype(BF16)
            value_rows[rows, :] = extended(value[source, :, kept]).T.astype(BF16)
            key_columns[:, rows] = found
            sums[rows, :] = jnp.zeros((length, LANES), F32)
            return 0

        lax.fori_loop(0, sources, prepare, 0)

    by_rank(meta, group, own, other, fill)
    grad_prefix[...] = jnp.zeros(grad_prefix.shape, F32)
    pre_row = lax.broadcasted_iota(jnp.int32, (pre_key.shape[0], tile), 0)

    def query_tile(number, _):
        source, part = number // per, number % per
        base = number * tile * group
        columns = pl.ds(pl.multiple_of(part * tile, tile), tile)
        scaled = (query[source, :, columns].astype(F32) * scale).astype(BF16)
        pieces = [number * count + piece for piece in range(count)]
        grad = jnp.concatenate([grad_out[piece] for piece in pieces], 1)
        full = jnp.concatenate([out_full[piece] for piece in pieces], 1)
        delta = jnp.sum(grad.astype(F32) * full, 0, keepdims=True)
        level = log_total[number]
        index = lax.broadcasted_iota(jnp.int32, (1, tile), 1)
        places = query_places(meta, index, base, chunk, group)
        bounds = tile_bounds(meta, base, tile, chunk, group)
        rest = jnp.zeros((LANES - size - PAD, tile), BF16)
        scaled_less = jnp.concatenate([scaled, in_three(-level).astype(BF16), rest], 0)
        grad_less = jnp.concatenate([grad, in_three(-delta).astype(BF16), rest], 0)
        none = jnp.zeros((size, tile), BF16)
        pair = jnp.concatenate(
            [jnp.concatenate([grad, none], 1), jnp.concatenate([none, scaled], 1)], 0
        )

        probs = jnp.exp(contract(pre_key[...], scaled, 1, 0) - level)
        probs = jnp.where(pre_row < prefix, probs, 0.0)
        slope = (probs * (contract(pre_value[...], grad, 1, 0) - delta)).astype(BF16)
        grad_prefix[0] += contract(slope, scaled, 1, 1)
        grad_prefix[1] += contract(probs.astype(BF16), grad, 1, 1)
        query_sum[...] = contract(pre_key[...], slope, 0, 0)

        def block(start, count, lane, masked):
            rows = pl.ds(pl.multiple_of(start, LANES), count)
            probs = jnp.exp(contract(key_rows[rows, :], scaled_less[:, lane:], 1, 0))
            if masked:
                probs = jnp.where(allowed(meta, start, count, places[:, lane:]), probs, 0.0)
            slope = probs * contract(value_rows[rows, :], grad_less[:, lane:], 1, 0)
            slope = slope.astype(BF16)
            both = jnp.concatenate([probs.astype(BF16), slope], 1)
            ends = jnp.concatenate([pair[:, lane:tile], pair[:, tile + lane :]], 1) if lane else pair
            sums[rows, :] += contract(both, ends, 1, 1)
            query_sum[:, lane:] += contract(key_columns[:, rows], slope, 1, 0)

        over_keys(bounds, base, tile, group, keys, block)
        grad_query[source, :, columns] = (query_sum[...] * scale).astype(BF16)
        return 0

    lax.fori_loop(0, blocks * per, query_tile, 0)

    def flush(keys_target, values_target):
        def step(source, _):
            rows = pl.ds(pl.multiple_of(source * length, length), length)
            turned = sums[rows, :].T.astype(BF16)
            values_target[source] = turned[:size]
            keys_target[source] = turned[size:]
            return 0

        lax.fori_loop(0, sources, step, 0)

    if group == 2:

        @pl.when(rank == 0)
        def _():
            flush(grad_keep, grad_send)

        @pl.when(rank == 1)
        def _():
            flush(grad_send, grad_keep)

    else:
        flush(grad_keep, grad_send)


def attend_backward(
    meta, query, own, other, pre_key, pre_value, grad_out, out_full, log_total,
    tile, keys, prefix, chunk, group, length, width,
):
    sources, size, _ = own.shape
    pair = jax.ShapeDtypeStruct((sources, size, length), BF16)
    return pl.pallas_call(
        functools.partial(
            backward_kernel, tile=tile, keys=keys, prefix=prefix, chunk=chunk, group=group,
            length=length, width=width,
        ),
        out_shape=(
            jax.ShapeDtypeStruct((query.shape[0], size, width), BF16),
            pair,
            pair,
            jax.ShapeDtypeStruct((2,) + pre_key.shape, F32),
        ),
        in_specs=[SM] + [VM] * 8,
        out_specs=(VM,) * 4,
        scratch_shapes=[
            pltpu.VMEM((sources * length, LANES), BF16),
            pltpu.VMEM((sources * length, LANES), BF16),
            pltpu.VMEM((size, sources * length), BF16),
            pltpu.VMEM((sources * length, LANES), F32),
            pltpu.VMEM((size, tile), F32),
        ],
        compiler_params=pltpu.CompilerParams(vmem_limit_bytes=34 * 2**20),
        cost_estimate=work(query.shape[0] * width, sources * length, 5),
        name="attend_backward",
    )(meta, query, own, other, pre_key, pre_value, grad_out, out_full, log_total)


def as_rows(columns):
    lane = lax.broadcasted_iota(jnp.int32, (columns[0].shape[0], LANES), 1)
    wide = jnp.zeros(lane.shape, F32)
    for number, column in enumerate(columns):
        wide = jnp.where(lane == number, column, wide)
    return wide.T[:8]


def turn_kernel(*refs):
    count = len(refs) // 2
    for source, target in zip(refs[:count], refs[count:]):
        target[...] = source[...].astype(F32).T.astype(BF16)


def turned(*arrays):
    return pl.pallas_call(
        turn_kernel,
        out_shape=tuple(jax.ShapeDtypeStruct(a.shape[::-1], BF16) for a in arrays),
        in_specs=[VM] * len(arrays),
        out_specs=(VM,) * len(arrays),
        compiler_params=pltpu.CompilerParams(vmem_limit_bytes=8 * 2**20),
        name="turned",
    )(*arrays)


def project_kernel(rows, columns, weight, bias, full, sent, stats, *, heads, size, step):
    length = rows.shape[1]
    pieces = length // step
    half = step // 2
    width = length // 2
    for piece in range(pieces):
        lanes = slice(piece * step, (piece + 1) * step)
        values = rows[:, lanes].astype(F32)
        mean = jnp.mean(values, 0, keepdims=True)
        centered = values - mean
        inverse = lax.rsqrt(jnp.mean(centered * centered, 0, keepdims=True) + EPS)
        stats[0:1, lanes] = mean
        stats[1:2, lanes] = inverse
        low = (centered * inverse * columns[:, 0:1] + columns[:, 1:2]).astype(BF16)
        full[:, lanes] = low
        mixed = (contract(weight[...], low, 1, 0) + bias[...]).astype(BF16)
        for head in range(heads):
            part = mixed[head * 3 * size : (head + 1) * 3 * size]
            spot = slice(piece * half, (piece + 1) * half)
            sent[2 * head, :, spot] = part[:size, :half]
            sent[2 * head + 1, :, spot] = part[:size, half:]
            spot = slice(width + piece * step, width + (piece + 1) * step)
            sent[2 * head, :, spot] = part[size : 2 * size]
            sent[2 * head + 1, :, spot] = part[2 * size :]


def project(rows, columns, weight, bias, heads, size, step):
    width, length = rows.shape
    return pl.pallas_call(
        functools.partial(project_kernel, heads=heads, size=size, step=step),
        out_shape=(
            jax.ShapeDtypeStruct((width, length), BF16),
            jax.ShapeDtypeStruct((2 * heads, size, length // 2 * 3), BF16),
            jax.ShapeDtypeStruct((2, length), F32),
        ),
        in_specs=[VM] * 4,
        out_specs=(VM, VM, VM),
        compiler_params=pltpu.CompilerParams(vmem_limit_bytes=20 * 2**20),
        name="project",
    )(rows, columns, weight, bias)


def unproject_kernel(
    spot, came, weight, rows, stats, columns, own_grad, token_rows, reparam,
    flat, part, first_up, first_down, head_row, prefix_low, *rest,
    heads, size, step,
):
    *small, totals = rest
    width, length = rows.shape
    half = step // 2
    past = length // 2
    gain = columns[:, 0:1]
    row_sums = []
    sums = [0.0, 0.0, 0.0]
    for piece in range(length // step):
        lanes = slice(piece * step, (piece + 1) * step)
        place = slice(piece * half, (piece + 1) * half)
        pair = slice(past + piece * step, past + (piece + 1) * step)
        pieces = []
        for head in range(heads):
            first, second = 2 * head, 2 * head + 1
            pieces.append(jnp.concatenate([came[first, :, place], came[second, :, place]], 1))
            pieces += [came[first, :, pair], came[second, :, pair]]
        grads = jnp.concatenate(pieces, 0)
        flat[:, lanes] = grads
        back = contract(weight[...], grads, 1, 0)
        part[:, lanes] = back.astype(BF16)

        @pl.when(spot[0] == piece)
        def _():
            part[:, lanes] = (back + own_grad[...] / (stats[1:2, lanes] * gain)).astype(BF16)

        normed = (rows[:, lanes].astype(F32) - stats[0:1, lanes]) * stats[1:2, lanes]
        scaled = back * gain
        row_sums.append(
            [jnp.sum(values, 0, keepdims=True) for values in (scaled, scaled * normed)]
        )
        for number, values in enumerate((back * normed, back, grads.astype(F32))):
            sums[number] += jnp.sum(values, 1, keepdims=True)
    count = first_up.shape[0]
    blocks = width // (2 * count)
    for block in range(blocks):
        row = 2 * count * block

        @pl.when(lax.rem(spot[0] + blocks - 1, blocks) == block)
        def _():
            first_up[...] = part[row : row + count]

        @pl.when(lax.rem(spot[0] + 1, blocks) == block)
        def _():
            first_down[...] = part[row + count : row + 2 * count]

    head_row[...] = as_rows(sums[2:])[:1]
    totals[...] = as_rows(sums[:2])
    found = []
    for head in range(heads):
        both = came[2 * head, :, 3 * past :].astype(F32) + came[2 * head + 1, :, 3 * past :].astype(F32)
        both = both.T
        found += [both[:PAD], both[PAD : 2 * PAD]]
    low = jnp.concatenate(found, 1).astype(BF16)
    prefix_low[...] = low
    hidden = contract(low, reparam[...], 1, 1)
    features = 2 * count
    for number, target in enumerate(small):
        start = pl.multiple_of(lax.rem(spot[0] + number, blocks) * features, features)
        target[0:2] = totals[0:2, pl.ds(start, features)]
        target[2:5] = token_rows[0:3, pl.ds(start, features)]
        target[5:8] = jnp.zeros((3, features), F32)
        for which in range(2):
            for piece in range(blocks):
                row = 8 + which * blocks + piece
                target[row : row + 1] = row_sums[piece][which]
        for piece in range(hidden.shape[1] // features):
            row = 8 + 2 * blocks + piece * PAD
            target[row : row + PAD] = hidden[:, piece * features : (piece + 1) * features]


def unproject(spot, came, weight, rows, stats, columns, own_grad, token_rows, reparam, heads, size, step):
    width, length = rows.shape
    blocks = length // step
    features = width // blocks
    mixed = 3 * heads * size
    small = 8 + 2 * blocks + reparam.shape[0] // features * PAD
    first = jax.ShapeDtypeStruct((features // 2, length), BF16)
    return pl.pallas_call(
        functools.partial(unproject_kernel, heads=heads, size=size, step=step),
        out_shape=(
            jax.ShapeDtypeStruct((mixed, length), BF16),
            jax.ShapeDtypeStruct((width, length), BF16),
            first,
            first,
            jax.ShapeDtypeStruct((1, mixed), F32),
            jax.ShapeDtypeStruct((PAD, 2 * heads * size), BF16),
        )
        + (jax.ShapeDtypeStruct((small, features), F32),) * blocks,
        in_specs=[SM] + [VM] * 8,
        out_specs=(VM,) * (6 + blocks),
        scratch_shapes=[pltpu.VMEM((8, width), F32)],
        compiler_params=pltpu.CompilerParams(vmem_limit_bytes=20 * 2**20),
        cost_estimate=pl.CostEstimate(
            flops=4 * mixed * width * length, bytes_accessed=2**23, transcendentals=0
        ),
        name="unproject",
    )(spot, came, weight, rows, stats, columns, own_grad, token_rows, reparam)


def small_kernel(*refs, blocks, width, hidden_rows):
    pieces = refs[:blocks]
    down_row, up_row, head_row, row_sums, hidden, late = refs[blocks:]
    total = sum(piece[...] for piece in pieces)
    features = total.shape[1]
    for which in range(2):
        for piece in range(blocks):
            row = 8 + which * blocks + piece
            lanes = slice(piece * features, (piece + 1) * features)
            row_sums[which : which + 1, lanes] = total[row : row + 1] / width
    for piece in range(hidden.shape[1] // features):
        row = 8 + 2 * blocks + piece * PAD
        hidden[:, piece * features : (piece + 1) * features] = total[row : row + PAD]
    late[...] = jnp.zeros(late.shape, F32)
    late[0:5] = total[0:5]
    late[5:6] = down_row[...]
    row = 6
    for source in (up_row, head_row):
        for piece in range(source.shape[1] // features):
            late[row : row + 1] = source[:, piece * features : (piece + 1) * features]
            row += 1


def small_totals(pieces, down_row, up_row, head_row, rows, hidden_width, width):
    features = pieces[0].shape[1]
    late = 6 + (up_row.shape[1] + head_row.shape[1]) // features
    return pl.pallas_call(
        functools.partial(
            small_kernel, blocks=len(pieces), width=width, hidden_rows=hidden_width
        ),
        out_shape=(
            jax.ShapeDtypeStruct((2, rows), F32),
            jax.ShapeDtypeStruct((PAD, hidden_width), F32),
            jax.ShapeDtypeStruct((-(-late // 8) * 8, features), F32),
        ),
        in_specs=[VM] * (len(pieces) + 3),
        out_specs=(VM,) * 3,
        compiler_params=pltpu.CompilerParams(vmem_limit_bytes=8 * 2**20),
        name="small_totals",
    )(*pieces, down_row, up_row, head_row)


def late_kernel(parts, vectors, up, pairs, *, heads, size):
    total = sum(parts[n] for n in range(parts.shape[0]))
    features = total.shape[1]
    vectors[...] = total[:8]
    count = up.shape[1] // features
    up[...] = jnp.concatenate([total[6 + n : 7 + n] for n in range(count)], 1)
    mixed = 3 * heads * size
    row = jnp.concatenate(
        [total[6 + count + n : 7 + count + n] for n in range(mixed // features)], 1
    )
    for head in range(heads):
        start = 3 * size * head
        pairs[head : head + 1] = jnp.concatenate(
            [row[:, start : start + size], row[:, start + 2 * size : start + 3 * size]], 1
        )


def late_totals(parts, inner, heads, size):
    return pl.pallas_call(
        functools.partial(late_kernel, heads=heads, size=size),
        out_shape=(
            jax.ShapeDtypeStruct((8, parts.shape[2]), F32),
            jax.ShapeDtypeStruct((1, inner), F32),
            jax.ShapeDtypeStruct((heads, 2 * size), F32),
        ),
        in_specs=[VM],
        out_specs=(VM,) * 3,
        compiler_params=pltpu.CompilerParams(vmem_limit_bytes=8 * 2**20),
        name="late_totals",
    )(parts)


def finish_kernel(up, down, own_up, own_down, rows, gain, stats, row_sums, grad):
    half = up.shape[0]
    mean, inverse = stats[0:1], stats[1:2]
    first, second = row_sums[0:1], row_sums[1:2]
    for start, came, own in ((0, up, own_up), (half, down, own_down)):
        spot = slice(start, start + half)
        total = came[...].astype(F32) + own[...].astype(F32)
        normed = (rows[spot].astype(F32) - mean) * inverse
        back = inverse * (gain[spot] * total - first - normed * second)
        grad[:, spot] = back.T.astype(BF16)


def finish(up, down, own_up, own_down, rows, gain, stats, row_sums):
    return pl.pallas_call(
        finish_kernel,
        out_shape=jax.ShapeDtypeStruct(rows.shape[::-1], BF16),
        in_specs=[VM] * 8,
        out_specs=VM,
        compiler_params=pltpu.CompilerParams(vmem_limit_bytes=8 * 2**20),
        name="finish",
    )(up, down, own_up, own_down, rows, gain, stats, row_sums)


def feed_kernel(rows, grads, up_turned, up, down, bias, hidden, grad_pre, part):
    pre = contract(up_turned[...], rows[0], 1, 0) + bias[...]
    act, pull = jax.vjp(gelu_tanh, pre)
    hidden[0] = act.astype(BF16)
    given = grads[...] if len(grads.shape) == 2 else grads[0]
    low = pull(contract(down[...], given, 1, 0))[0].astype(BF16)
    grad_pre[0] = low
    part[0] = contract(up[...], low, 1, 0).astype(BF16)


def feed(rows, grads, up_turned, up, down, bias):
    blocks, width, count = rows.shape
    inner = down.shape[0]

    def whole(shape):
        return pl.BlockSpec(shape, lambda i: (0,) * len(shape), pipeline_mode=pl.Buffered(1))

    def block(size):
        return pl.BlockSpec((1, size, count), lambda i: (i, 0, 0))

    if count % LANES:
        grads = grads.reshape(width, blocks, count).transpose(1, 0, 2)

    return pl.pallas_call(
        feed_kernel,
        grid=(blocks,),
        out_shape=(
            jax.ShapeDtypeStruct((blocks, inner, count), BF16),
            jax.ShapeDtypeStruct((blocks, inner, count), BF16),
            jax.ShapeDtypeStruct((blocks, width, count), BF16),
        ),
        in_specs=[
            block(width),
            block(width) if count % LANES else pl.BlockSpec((width, count), lambda i: (0, i)),
            whole((inner, width)),
            whole((width, inner)),
            whole((inner, width)),
            whole((inner, 1)),
        ],
        out_specs=(block(inner), block(inner), block(width)),
        compiler_params=pltpu.CompilerParams(vmem_limit_bytes=28 * 2**20),
        cost_estimate=pl.CostEstimate(
            flops=6 * blocks * width * inner * count, bytes_accessed=2**24, transcendentals=0
        ),
        name="feed",
    )(rows, grads, up_turned, up, down, bias)


def feed_weights_kernel(rows, grads, hidden, grad_pre, grad_down, grad_up, bias, *, square):
    blocks, width, count = rows.shape
    inner = hidden.shape[1]

    def lanes(n):
        return slice(n * count, (n + 1) * count)

    def weights(target, first, second, columns):
        step = min(256, columns)
        whole = jnp.concatenate([first(n) for n in range(blocks)], 1)
        for start in range(0, columns, step):
            tile = slice(start, start + step)
            turned = jnp.concatenate([second(n, tile) for n in range(blocks)], 1)
            target[:, tile] = contract(whole, turned, 1, 1).astype(BF16)

    weights(grad_down, lambda n: hidden[n], lambda n, tile: grads[tile, lanes(n)], width)
    if square:
        weights(grad_up, lambda n: rows[n], lambda n, tile: grad_pre[n, tile], inner)
    else:
        weights(grad_up, lambda n: grad_pre[n], lambda n, tile: rows[n, tile], width)
    total = sum(jnp.sum(grad_pre[n].astype(F32), 1, keepdims=True) for n in range(blocks))
    bias[...] = as_rows([total])[:1]


def feed_weights(rows, grads, hidden, grad_pre):
    blocks, width, count = rows.shape
    inner = hidden.shape[1]
    return pl.pallas_call(
        functools.partial(feed_weights_kernel, square=inner == width),
        out_shape=(
            jax.ShapeDtypeStruct((inner, width), BF16),
            jax.ShapeDtypeStruct((inner, width), BF16),
            jax.ShapeDtypeStruct((1, inner), F32),
        ),
        in_specs=[VM] * 4,
        out_specs=(VM,) * 3,
        compiler_params=pltpu.CompilerParams(vmem_limit_bytes=14 * 2**20),
        cost_estimate=pl.CostEstimate(
            flops=4 * blocks * width * inner * count, bytes_accessed=2**24, transcendentals=0
        ),
        name="feed_weights",
    )(rows, grads, hidden, grad_pre)


def feed_out_kernel(spot, hidden, down_turned, middle, columns, out):
    features = out.shape[2]
    for n in range(hidden.shape[0]):
        result = contract(down_turned[...], hidden[n], 1, 0)

        def put(values):
            for block in range(out.shape[0]):
                out[block, n] = values[block * features : (block + 1) * features].astype(BF16)

        put(result)

        @pl.when(spot[0] == n)
        def _():
            put(result + middle[...] + columns[:, 5:6])


def feed_out(spot, hidden, down_turned, middle, columns):
    blocks, inner, count = hidden.shape
    width = middle.shape[0]
    return pl.pallas_call(
        feed_out_kernel,
        out_shape=jax.ShapeDtypeStruct((blocks, blocks, width // blocks, count), BF16),
        in_specs=[SM] + [VM] * 4,
        out_specs=VM,
        compiler_params=pltpu.CompilerParams(vmem_limit_bytes=8 * 2**20),
        cost_estimate=pl.CostEstimate(
            flops=2 * blocks * width * inner * count, bytes_accessed=2**23, transcendentals=0
        ),
        name="feed_out",
    )(spot, hidden, down_turned, middle, columns)


def enter_kernel(
    spot, came, weight, tokens, columns, attended, middle, normed, inverse, low, *, heads
):
    size, half = came.shape[1:]
    count = 2 * half
    tensors = came.shape[0] // (2 * heads)
    for block in range(tensors):
        for head in range(heads):
            row = (block * heads + head) * size
            for rank in range(2):
                attended[row : row + size, rank * half : (rank + 1) * half] = came[
                    (2 * head + rank) * tensors + block
                ]
    branch = contract(attended[...], weight[...], 0, 0).T
    lanes = pl.ds(pl.multiple_of(spot[0] * count, count), count)
    values = tokens[:, lanes].astype(F32) + branch + columns[:, 4:5]
    middle[...] = values
    centered = values - jnp.mean(values, 0, keepdims=True)
    scale = lax.rsqrt(jnp.mean(centered * centered, 0, keepdims=True) + EPS)
    inverse[...] = scale
    centered = centered * scale
    normed[...] = centered
    low[...] = (centered * columns[:, 2:3] + columns[:, 3:4]).astype(BF16)


def enter(spot, came, weight, tokens, columns, heads):
    width, count = tokens.shape[0], 2 * came.shape[2]
    return pl.pallas_call(
        functools.partial(enter_kernel, heads=heads),
        out_shape=(
            jax.ShapeDtypeStruct((width, count), BF16),
            jax.ShapeDtypeStruct((width, count), F32),
            jax.ShapeDtypeStruct((width, count), F32),
            jax.ShapeDtypeStruct((1, count), F32),
            jax.ShapeDtypeStruct((width, count), BF16),
        ),
        in_specs=[SM] + [VM] * 4,
        out_specs=(VM,) * 5,
        compiler_params=pltpu.CompilerParams(vmem_limit_bytes=12 * 2**20),
        name="enter",
    )(spot, came, weight, tokens, columns)


def leave_kernel(
    spot, up, down, own_up, own_down, normed, inverse, grads, weight, columns,
    middle, branch, sums, sent,
    *, heads,
):
    size, half = sent.shape[1:]
    count = 2 * half
    tensors = sent.shape[0] // (2 * heads)
    total = jnp.concatenate(
        [
            up[...].astype(F32) + own_up[...].astype(F32),
            down[...].astype(F32) + own_down[...].astype(F32),
        ],
        0,
    )
    scaled = total * columns[:, 2:3]
    first = jnp.mean(scaled, 0, keepdims=True)
    second = jnp.mean(scaled * normed[...], 0, keepdims=True)
    lanes = pl.ds(pl.multiple_of(spot[0] * count, count), count)
    result = grads[:, lanes].astype(F32) + inverse[...] * (
        scaled - first - normed[...] * second
    )
    middle[...] = result
    low = result.astype(BF16)
    branch[...] = low
    back = contract(weight[...], low, 1, 0).astype(BF16)
    for block in range(tensors):
        for head in range(heads):
            row = (block * heads + head) * size
            for rank in range(2):
                sent[(2 * head + rank) * tensors + block] = back[
                    row : row + size, rank * half : (rank + 1) * half
                ]
    sums[...] = as_rows(
        [jnp.sum(values, 1, keepdims=True) for values in (total * normed[...], total, result)]
    )


def leave(spot, terms, normed, inverse, grads, weight, columns, heads, size):
    width, count = normed.shape
    blocks = width // size
    return pl.pallas_call(
        functools.partial(leave_kernel, heads=heads),
        out_shape=(
            jax.ShapeDtypeStruct((width, count), F32),
            jax.ShapeDtypeStruct((width, count), BF16),
            jax.ShapeDtypeStruct((8, width), F32),
            jax.ShapeDtypeStruct((2 * blocks, size, count // 2), BF16),
        ),
        in_specs=[SM] + [VM] * 9,
        out_specs=(VM,) * 4,
        compiler_params=pltpu.CompilerParams(vmem_limit_bytes=12 * 2**20),
        name="leave",
    )(spot, *terms, normed, inverse, grads, weight, columns)


def rest_kernel(spot, flat, full, out, mine, other):
    width = full.shape[0]
    split = mine.shape[0]
    step = min(256, width)
    for start in range(0, width, step):
        tile = slice(start, start + step)
        result = contract(flat[...], full[tile], 1, 1).astype(BF16)
        first = result[:split]
        second = jnp.concatenate([result[split:], out[:, tile]], 0)

        @pl.when(spot[1] == 0)
        def _():
            mine[:, tile] = first
            other[:, tile] = second

        @pl.when(spot[1] == 1)
        def _():
            mine[:, tile] = second
            other[:, tile] = first


def rest_halves(spot, flat, full, out):
    half = (flat.shape[0] + out.shape[0]) // 2
    return pl.pallas_call(
        rest_kernel,
        out_shape=(jax.ShapeDtypeStruct((half, full.shape[0]), BF16),) * 2,
        in_specs=[SM] + [VM] * 3,
        out_specs=(VM, VM),
        compiler_params=pltpu.CompilerParams(vmem_limit_bytes=8 * 2**20),
        cost_estimate=pl.CostEstimate(
            flops=2 * flat.shape[0] * full.size, bytes_accessed=2**23, transcendentals=0
        ),
        name="rest_halves",
    )(spot, flat, full, out)


def rest_whole_kernel(spot, half, other, mixed, out, *, chips):
    step = half.shape[0] // chips
    edge = mixed.shape[0] // step
    for piece in range(chips):
        owner = lax.rem(spot[2] + chips - piece, chips)
        rows = slice(piece * step, (piece + 1) * step)
        for source, core in ((half, spot[1]), (other, 1 - spot[1])):
            block = core * chips + owner
            values = source[rows].astype(F32)

            @pl.when(block < edge)
            def _():
                mixed[pl.ds(pl.multiple_of(jnp.minimum(block, edge - 1) * step, step), step)] = values

            @pl.when(block >= edge)
            def _():
                out[pl.ds(pl.multiple_of(jnp.maximum(block - edge, 0) * step, step), step)] = values


def rest_whole(spot, half, other, rows, chips):
    width = half.shape[1]
    return pl.pallas_call(
        functools.partial(rest_whole_kernel, chips=chips),
        out_shape=(
            jax.ShapeDtypeStruct((rows, width), F32),
            jax.ShapeDtypeStruct((2 * half.shape[0] - rows, width), F32),
        ),
        in_specs=[SM, VM, VM],
        out_specs=(VM, VM),
        compiler_params=pltpu.CompilerParams(vmem_limit_bytes=8 * 2**20),
        name="rest_whole",
    )(spot, half, other)


def prefix_kernel(
    total, hidden, embed, weight, low, grad_embed, grad_weight, grad_bias, grad_out, grad_out_bias
):
    pre = total[...] * (1.0 - hidden[...] * hidden[...])
    grad_bias[...] = jnp.sum(pre, 0, keepdims=True)

    def exact(first, second, dims):
        return lax.dot_general(
            first, second, ((dims[:1], dims[1:]), ((), ())),
            preferred_element_type=F32, precision=HIGHEST,
        )

    grad_weight[...] = exact(embed[...].astype(F32), pre, (0, 0))
    grad_embed[...] = exact(pre, weight[...].astype(F32), (1, 1))
    wide = low[...].astype(F32)
    result = exact(hidden[...], wide, (0, 0))
    sums = jnp.sum(wide, 0, keepdims=True)
    each = grad_out.shape[2]
    for head in range(grad_out.shape[1]):
        lanes = slice(head * each, (head + 1) * each)
        grad_out[:, head, :] = result[:, lanes]
        grad_out_bias[head : head + 1] = sums[:, lanes]


def prefix_back(total, hidden, embed, weight, low, heads):
    rows, width = embed.shape
    extra = PAD - rows
    hidden = jnp.pad(hidden, ((0, extra), (0, 0)))
    embed = jnp.pad(embed, ((0, extra), (0, 0)))
    inner = weight.shape[1]
    each = low.shape[1] // heads
    grad_embed, grad_weight, grad_bias, grad_out, grad_out_bias = pl.pallas_call(
        prefix_kernel,
        out_shape=(
            jax.ShapeDtypeStruct((PAD, width), F32),
            jax.ShapeDtypeStruct(weight.shape, F32),
            jax.ShapeDtypeStruct((1, inner), F32),
            jax.ShapeDtypeStruct((inner, heads, each), F32),
            jax.ShapeDtypeStruct((heads, each), F32),
        ),
        in_specs=[VM] * 5,
        out_specs=(VM,) * 5,
        compiler_params=pltpu.CompilerParams(vmem_limit_bytes=16 * 2**20),
        name="prefix_back",
    )(total, hidden, embed, weight, low)
    return grad_embed[:rows], grad_weight, grad_bias[0], grad_out, grad_out_bias


def spread(values, axis):
    count = lax.axis_size(axis)
    copies = jnp.broadcast_to(values[None], (count,) + values.shape)
    return lax.all_to_all(copies, axis, 0, 0, tiled=True)


def small_sum(values, axis):
    return jnp.sum(spread(values, axis), 0)


def ring(axis, by):
    count = lax.axis_size(axis)
    return [(source, (source + by) % count) for source in range(count)]


def ring_gather(values, axis, beside=()):
    count, place = lax.axis_size(axis), lax.axis_index(axis)
    half = values.shape[0] // 2
    up, down = values[:half], values[half:]
    out = jnp.zeros((count,) + values.shape, values.dtype)
    out = lax.dynamic_update_slice_in_dim(out, values[None], place, 0)
    zeros = (0,) * (values.ndim - 1)
    results = []
    for step in range(1, count):
        up = lax.ppermute(up, axis, ring(axis, 1))
        down = lax.ppermute(down, axis, ring(axis, -1))
        if step <= len(beside) and beside[step - 1]:
            up, down, result = lax.optimization_barrier((up, down, beside[step - 1]()))
            results.append(result)
        out = lax.dynamic_update_slice(out, up[None], ((place - step) % count, 0) + zeros)
        out = lax.dynamic_update_slice(out, down[None], ((place + step) % count, half) + zeros)
    return (out, results) if beside else out


def ring_terms(blocks, axis, beside=(), first=None):
    count, place = lax.axis_size(axis), lax.axis_index(axis)
    half = blocks.shape[1] // 2

    def own(offset, upper):
        block = lax.dynamic_index_in_dim(blocks, (place + offset) % count, 0, keepdims=False)
        return block[half:] if upper else block[:half]

    up, down = first or (own(-1, False), own(1, True))
    state = None
    for step in range(1, count):
        up = lax.ppermute(up, axis, ring(axis, 1))
        down = lax.ppermute(down, axis, ring(axis, -1))
        if step <= len(beside):
            state = beside[step - 1](state)
            up, down, state = lax.optimization_barrier((up, down, state))
        if step < count - 1:
            up = (up.astype(F32) + own(-1 - step, False).astype(F32)).astype(BF16)
            down = (down.astype(F32) + own(1 + step, True).astype(F32)).astype(BF16)
    for other in beside[count - 1 :]:
        state = other(state)
    return (up, down, own(0, False), own(0, True)), state


def swapped(values):
    pairs = [(source, source ^ 1) for source in range(lax.axis_size("seq"))]
    return lax.ppermute(values, "seq", pairs)


def chip_parts(half):
    count = lax.axis_size("seq")
    chips = count // 2
    chip = lax.axis_index("seq") // 2
    blocks = half.reshape(chips, half.shape[0] // chips, half.shape[1])
    total = lax.dynamic_index_in_dim(blocks, chip, 0, keepdims=False)
    parts = [total]
    for step in range(1, chips):
        block = lax.dynamic_index_in_dim(blocks, (chip + step) % chips, 0, keepdims=False)
        parts.append(lax.ppermute(block, "seq", ring("seq", 2 * step)))
    return parts


def owned_direct(values, axis):
    count, place = lax.axis_size(axis), lax.axis_index(axis)
    parts = [lax.dynamic_index_in_dim(values, place, 0, keepdims=False)]
    for step in range(1, count):
        block = lax.dynamic_index_in_dim(values, (place + step) % count, 0, keepdims=False)
        parts.append(lax.ppermute(block, axis, ring(axis, step)))
    return parts


def chip_gather(parts):
    part = sum(part.astype(F32) for part in parts).astype(BF16)
    behind = [lax.ppermute(part, "seq", ring("seq", 2 * step)) for step in range(1, len(parts))]
    return jnp.concatenate([part] + behind, 0)


def spread_direct(values, axis):
    count, place = lax.axis_size(axis), lax.axis_index(axis)
    out = jnp.zeros((count,) + values.shape, values.dtype)
    out = lax.dynamic_update_slice_in_dim(out, values[None], place, 0)
    for step in range(1, count):
        came = lax.ppermute(values, axis, ring(axis, step))
        out = lax.dynamic_update_slice_in_dim(out, came[None], (place - step) % count, 0)
    return out


def core_gather(half):
    core, chip = lax.axis_index("seq") % 2, lax.axis_index("seq") // 2
    chips = lax.axis_size("seq") // 2
    order = (chip - jnp.arange(chips)) % chips

    def sorted_parts(values):
        parts = values.reshape(chips, -1, values.shape[1])
        picked = [lax.dynamic_index_in_dim(parts, order[n], 0) for n in range(chips)]
        return jnp.concatenate(picked, 0).reshape(values.shape)

    half, other = sorted_parts(half), sorted_parts(swapped(half))
    first = jnp.where(core == 0, half, other)
    second = jnp.where(core == 0, other, half)
    return jnp.concatenate([first, second], 0)


def regrouped(values, width):
    count, size, columns = values.shape
    if width == columns:
        return values
    if width > columns:
        merged = values.reshape(-1, width // columns, size, columns).transpose(0, 2, 1, 3)
        return merged.reshape(-1, size, width)
    cut = values.reshape(count, size, columns // width, width).transpose(0, 2, 1, 3)
    return cut.reshape(-1, size, width)


def group_gather(pieces, group):
    if group == 2:
        rank = lax.axis_index("seq") % 2
        other = swapped(pieces)
        return jnp.stack([jnp.where(rank == 0, pieces, other), jnp.where(rank == 0, other, pieces)])
    count = lax.axis_size("seq")
    groups = [[first + i for i in range(group)] for first in range(0, count, group)]
    return lax.all_gather(pieces, "seq", axis_index_groups=groups)


def on_device(
    tokens,
    segment_ids,
    out_grad,
    ln1_gain,
    ln1_bias,
    w_qkv,
    b_qv,
    w_out,
    b_out,
    ln2_gain,
    ln2_bias,
    w_up,
    b_up,
    w_down,
    b_down,
    prefix_embed,
    reparam_in,
    reparam_in_bias,
    reparam_out,
    reparam_out_bias,
):
    rows, features = tokens.shape
    heads = w_qkv.shape[1]
    size = w_qkv.shape[2] // 3
    inner = w_up.shape[1]
    seqs, tensors = lax.axis_size("seq"), lax.axis_size("tensor")
    width = features * tensors
    own_rows = rows // tensors
    group = seqs // heads
    chunk = own_rows // group
    place, slot = lax.axis_index("seq"), lax.axis_index("tensor")
    head, rank = place // group, place % group
    prefix = prefix_embed.shape[0]
    tokens_head = rows // group
    query_width = max(tokens_head, LANES)
    forward_tile = min(512, query_width)
    backward_tile = min(512, query_width)
    forward_keys, backward_keys = 1024, 1024
    both = ("seq", "tensor")
    paired = group == 2 and chunk == LANES

    own_tokens, own_grads = turned(tokens, out_grad)
    numbers = jnp.arange(1, DOCS, dtype=jnp.int32)

    def document_starts():
        before = jnp.sum((segment_ids[None, :] < numbers[:, None]).astype(jnp.int32), 1)
        return spread(jnp.broadcast_to(before[:, None], (DOCS - 1, LANES)), "seq")

    def whole_vectors():
        return spread(
            jnp.stack([ln1_gain, ln1_bias, ln2_gain, ln2_bias, b_out, b_down]), "tensor"
        )

    full_tokens, (vectors, starts) = ring_gather(
        own_tokens, "tensor", (None, whole_vectors, document_starts)
    )
    full_tokens = full_tokens.reshape(width, rows)
    meta = jnp.concatenate([jnp.sum(starts, 0)[:, 0], rank[None].astype(jnp.int32)])
    columns = vectors.transpose(0, 2, 1).reshape(width, 6).astype(F32)
    out_share = w_out.reshape(seqs, heads * size // seqs, width)
    out_share = lax.dynamic_index_in_dim(out_share, place, 0, keepdims=False)
    core = place % 2
    spot = jnp.stack([slot, core, place // 2]).astype(jnp.int32)

    prefix_hidden = jnp.tanh(
        jnp.dot(prefix_embed, reparam_in, preferred_element_type=F32)
        + reparam_in_bias.astype(F32)
    )
    prefix_pair = jnp.einsum(
        "pa,ahe->phe", prefix_hidden, reparam_out.astype(F32), precision=HIGHEST
    )
    prefix_pair = (prefix_pair + reparam_out_bias.astype(F32)).astype(BF16)
    own_pair = lax.dynamic_index_in_dim(prefix_pair, head, 1, keepdims=False)
    own_pair = jnp.pad(own_pair, ((0, LANES - prefix), (0, 0)))
    pre_key, pre_value = own_pair[:, :size], own_pair[:, size:]

    w_flat = w_qkv.reshape(width, heads * 3 * size)
    bias_pair = b_qv.astype(F32)
    bias_three = jnp.stack(
        [bias_pair[:, :size], jnp.zeros((heads, size), F32), bias_pair[:, size:]], 1
    ).reshape(-1, 1)
    if paired:
        full1, sent, stats = project(
            full_tokens, columns, w_flat.T, bias_three, heads, size, own_rows
        )
    else:
        wide = full_tokens.astype(F32)
        mean = jnp.mean(wide, 0, keepdims=True)
        inverse = lax.rsqrt(jnp.mean((wide - mean) ** 2, 0, keepdims=True) + EPS)
        stats = jnp.concatenate([mean, inverse], 0)
        full1 = ((wide - mean) * inverse * columns[:, 0:1] + columns[:, 1:2]).astype(BF16)
        mixed = (contract(w_flat, full1, 0, 0) + bias_three).astype(BF16)
        mixed = mixed.reshape(heads, 3, size, rows)
        query_part = mixed[:, 0].reshape(heads, size, tensors, group, chunk)
        query_part = query_part.transpose(0, 3, 1, 2, 4).reshape(seqs, size, tokens_head)
        pair_part = mixed[:, 1:].transpose(0, 2, 1, 3).reshape(heads, size, group, 2 * tokens_head)
        pair_part = pair_part.transpose(0, 2, 1, 3).reshape(seqs, size, 2 * tokens_head)
        sent = jnp.concatenate([query_part, pair_part], 2)
    out_share = spread_direct(after(out_share, sent), "tensor")
    came = lax.all_to_all(sent, "seq", 0, 0, tiled=True)
    came, out_share = lax.optimization_barrier((came, out_share))
    w_out_full = lax.all_gather(out_share, "seq")
    w_out_full = w_out_full.transpose(1, 0, 2, 3).reshape(width, width)
    if group == 2:
        query, own, other = came, came, swapped(came)
    else:
        query, pair = came[:, :, :tokens_head], came[:, :, tokens_head:]
        query = regrouped(query, query_width)
        pair = group_gather(pair, group).transpose(1, 2, 0, 3).reshape(seqs, size, 2, rows)
        own, other = pair[:, :, 0], pair[:, :, 1]
    full_grad = lax.all_gather(after(own_grads, full_tokens), "tensor", axis=0, tiled=True)
    out_low, out_full, log_total = attend_forward(
        meta, query, own, other, pre_key.T, pre_value.T,
        forward_tile, forward_keys, prefix, chunk, group, rows, query_width,
    )
    out_low, full_grad, late_up, late_down, late_qkv = lax.optimization_barrier(
        (out_low, full_grad, w_up, w_down, w_qkv)
    )
    late_flat = late_qkv.reshape(width, heads * 3 * size)

    came = lax.all_to_all(regrouped(out_low, chunk), both, 0, 0, tiled=True)
    came, up_turned, down_turned, late_flat, w_out_full = lax.optimization_barrier(
        (came, late_up.T, late_down.T, late_flat, w_out_full)
    )
    if paired:
        attended, middle, normed2, inverse2, out2 = enter(
            spot, came, w_out_full, full_tokens, columns, heads
        )
    else:
        came = came.reshape(heads, group, tensors, size, chunk).transpose(2, 0, 3, 1, 4)
        attended = came.reshape(width, own_rows)
        branch = contract(w_out_full, attended, 0, 0)
        own_block = lax.dynamic_slice_in_dim(full_tokens, slot * own_rows, own_rows, 1)
        middle = own_block.astype(F32) + branch + columns[:, 4:5]
        centered = middle - jnp.mean(middle, 0, keepdims=True)
        inverse2 = lax.rsqrt(jnp.mean(centered * centered, 0, keepdims=True) + EPS)
        normed2 = centered * inverse2
        out2 = (normed2 * columns[:, 2:3] + columns[:, 3:4]).astype(BF16)

    full2 = ring_gather(out2, "tensor")
    hidden, grad_pre, part = feed(
        full2, full_grad, up_turned, w_up, w_down, b_up.astype(F32)[:, None]
    )

    def weights_here(_):
        return feed_weights(full2, full_grad, hidden, grad_pre)

    def out_here(state):
        return state, feed_out(spot, hidden, down_turned, middle, columns)

    terms, (weights, mlp_out) = ring_terms(part, "tensor", (weights_here, out_here))
    grad_w_down, grad_w_up, grad_b_up = weights
    feed_sums = lax.psum((grad_w_down, grad_w_up), "seq")

    if paired:
        grad_middle, grad_branch, token_sums, sent = leave(
            spot, terms, normed2, inverse2, full_grad, w_out_full, columns, heads, size
        )
    else:
        up, down, own_up, own_down = [a.astype(F32) for a in terms]
        grad_normed2 = jnp.concatenate([up + own_up, down + own_down], 0)
        scaled = grad_normed2 * columns[:, 2:3]
        first = jnp.mean(scaled, 0, keepdims=True)
        second = jnp.mean(scaled * normed2, 0, keepdims=True)
        own_grad = lax.dynamic_slice_in_dim(full_grad, slot * own_rows, own_rows, 1)
        grad_middle = own_grad.astype(F32) + inverse2 * (scaled - first - normed2 * second)
        grad_branch = grad_middle.astype(BF16)
        token_sums = [grad_normed2 * normed2, grad_normed2, grad_middle]
        token_sums = jnp.stack([jnp.sum(a, 1) for a in token_sums], 1)
        sent = contract(w_out_full, grad_branch, 1, 0).astype(BF16)
        sent = sent.reshape(tensors, heads, size, group, chunk).transpose(1, 3, 0, 2, 4)
        sent = sent.reshape(seqs * tensors, size, chunk)
    came = lax.all_to_all(sent, both, 0, 0, tiled=True)
    grad_out = regrouped(came, LANES)

    grad_w_out = contract(attended, grad_branch, 1, 1).astype(BF16)
    grad_out, mlp_out, grad_w_out = lax.optimization_barrier((grad_out, mlp_out, grad_w_out))
    output_act = lax.all_to_all(mlp_out, "tensor", 0, 0, tiled=True)
    grad_w_out = lax.psum_scatter(grad_w_out, "tensor", scatter_dimension=0, tiled=True)

    levels = log_total.reshape(-1, 1, backward_tile)
    grad_query, grad_keep, grad_send, grad_prefix = attend_backward(
        meta, query, own, other, pre_key[:PAD], pre_value[:PAD], grad_out, out_full, levels,
        backward_tile, backward_keys, prefix, chunk, group, rows, query_width,
    )
    if group == 2:
        grad_share = (grad_keep.astype(F32) + swapped(grad_send).astype(F32)).astype(BF16)
    else:
        grad_pair = jnp.stack([grad_keep, grad_send])
        groups = [[first + i for i in range(group)] for first in range(0, seqs, group)]
        shares = grad_pair.transpose(1, 2, 0, 3).reshape(seqs, size, group, 2 * tokens_head)
        grad_share = lax.psum_scatter(
            shares.transpose(2, 0, 1, 3), "seq", axis_index_groups=groups
        )
    prefix_part = grad_prefix.transpose(2, 0, 1).reshape(size, 2 * PAD).astype(BF16)
    prefix_part = jnp.pad(prefix_part, ((0, 0), (0, LANES - 2 * PAD)))
    prefix_part = jnp.broadcast_to(prefix_part[None], (seqs, size, LANES))
    sent = jnp.concatenate([regrouped(grad_query, tokens_head), grad_share, prefix_part], 2)
    sent, output_act, feed_sums = lax.optimization_barrier((sent, output_act, feed_sums))
    came = lax.all_to_all(sent, "seq", 0, 0, tiled=True)
    output_act = jnp.sum(output_act.astype(F32), 0).astype(BF16)
    output_act = output_act.transpose(0, 2, 1).reshape(rows, features)
    out_w_down = feed_sums[0].astype(F32)
    out_w_up = (feed_sums[1] if inner == width else feed_sums[1].T).astype(F32)
    came, output_act, grad_w_out, out_w_down, out_w_up = lax.optimization_barrier(
        (came, output_act, grad_w_out, out_w_down, out_w_up)
    )
    if paired:
        grad_flat, grad_part, first_up, first_down, head_row, prefix_low, *small = unproject(
            spot, came, late_flat, full_tokens, stats, columns, grad_middle, token_sums,
            reparam_out.reshape(reparam_out.shape[0], -1), heads, size, own_rows,
        )
        first_blocks = first_up, first_down
        mine, other = rest_halves(spot, grad_flat, full1, grad_w_out)
    else:
        query_part = came[:, :, :tokens_head].reshape(heads, group, size, tensors, chunk)
        query_part = query_part.transpose(0, 2, 3, 1, 4).reshape(heads, 1, size, rows)
        pair_part = came[:, :, tokens_head : 3 * tokens_head]
        pair_part = pair_part.reshape(heads, group, size, 2 * tokens_head).transpose(0, 2, 1, 3)
        pair_part = pair_part.reshape(heads, size, 2, rows).transpose(0, 2, 1, 3)
        grad_flat = jnp.concatenate([query_part, pair_part], 1).reshape(heads * 3 * size, rows)
        back = contract(late_flat, grad_flat, 1, 0)
        normed1 = (full_tokens.astype(F32) - stats[0]) * stats[1]
        scaled = back * columns[:, 0:1]
        row_sums = jnp.stack([jnp.sum(scaled, 0), jnp.sum(scaled * normed1, 0)])
        sums1 = jnp.stack([jnp.sum(back * normed1, 1), jnp.sum(back, 1)], 1)
        head_sums = jnp.sum(grad_flat.astype(F32), 1)
        own_inverse = lax.dynamic_slice_in_dim(stats[1:2], slot * own_rows, own_rows, 1)
        own_part = lax.dynamic_slice_in_dim(back, slot * own_rows, own_rows, 1)
        own_part = own_part + grad_middle / (own_inverse * columns[:, 0:1])
        back = lax.dynamic_update_slice_in_dim(back, own_part, slot * own_rows, 1)
        grad_part = back.astype(BF16)
        first_blocks = None
        grad_w_qkv = contract(grad_flat, full1, 1, 1).astype(BF16)
        rest = jnp.concatenate([grad_w_qkv, grad_w_out], 0)
        halves = rest.reshape(2, rest.shape[0] // 2, width)
        mine = lax.dynamic_index_in_dim(halves, core, 0, keepdims=False)
        other = lax.dynamic_index_in_dim(halves, 1 - core, 0, keepdims=False)

    if not paired:
        prefix_low = came[:, :, 3 * tokens_head : 3 * tokens_head + 2 * PAD].astype(F32)
        prefix_low = jnp.sum(prefix_low.reshape(heads, group, size, 2, PAD), 1)
        prefix_low = prefix_low.transpose(3, 0, 2, 1).reshape(PAD, -1).astype(BF16)
        hidden_part = contract(prefix_low, reparam_out.reshape(reparam_out.shape[0], -1), 1, 1)
        owned = jnp.concatenate([sums1.T, token_sums.T], 0)
        owned = owned.reshape(-1, tensors, features).transpose(1, 0, 2).reshape(tensors, -1)
        shared = jnp.concatenate([row_sums.reshape(-1), hidden_part.reshape(-1)])
        shared = jnp.broadcast_to(shared[None], (tensors, shared.shape[0]))
        small = jnp.concatenate([owned, shared], 1)[:, None, :]

    grad_b_down = jnp.sum(out_grad.astype(F32), 0)

    def small_here(_):
        if not paired:
            return swapped(other), owned_direct(small, "tensor")
        pieces = [small[0]]
        for step in range(1, tensors):
            pieces.append(lax.ppermute(small[step], "tensor", ring("tensor", step)))
        return swapped(other), pieces

    def parts_here(state):
        half = (mine.astype(F32) + state[0].astype(F32)).astype(BF16)
        if paired:
            sums = small_totals(
                state[1], grad_b_down[None], grad_b_up, head_row, rows,
                prefix_hidden.shape[1], width,
            )
            return chip_parts(half), sums
        sums = sum(state[1])[0]
        after_rows = 5 * features + 2 * rows
        row_means = sums[5 * features : after_rows].reshape(2, rows) / width
        hidden = sums[after_rows:].reshape(PAD, -1)
        mixed_sums = head_sums.reshape(heads, 3, size)
        late = [sums[: 5 * features], grad_b_down, grad_b_up[0]]
        late += [mixed_sums[:, 0].reshape(-1), mixed_sums[:, 2].reshape(-1)]
        return chip_parts(half), (row_means, hidden, jnp.concatenate(late)[None])

    def gather_here(state):
        return chip_gather(state[0]), state[1], spread(state[1][2], "seq")

    last_terms, (rest_half, (row_means, hidden_grad, _), late) = ring_terms(
        grad_part.reshape(tensors, features, rows),
        "tensor",
        (small_here, parts_here) + (lambda state: state,) * (tensors - 4) + (gather_here,),
        first_blocks,
    )
    input_grad = finish(
        *last_terms, own_tokens, ln1_gain.astype(F32)[:, None], stats, row_means,
    )
    mixed_rows = heads * 3 * size
    if paired:
        out_w_qkv, out_w_out = rest_whole(
            spot, rest_half, swapped(rest_half), mixed_rows, seqs // 2
        )
    else:
        rest = core_gather(rest_half).astype(F32)
        out_w_qkv, out_w_out = rest[:mixed_rows], rest[mixed_rows:]
    out_w_qkv = out_w_qkv.reshape(heads, 3 * size, width).transpose(2, 0, 1)
    out_w_out = out_w_out.reshape(heads, size, width)
    if paired:
        vectors, out_b_up, out_b_qv = late_totals(late, inner, heads, size)
        out_b_up = out_b_up[0]
    else:
        late = jnp.sum(late, 0)[0]
        vectors = late[: 6 * features].reshape(6, features)
        out_b_up = late[6 * features : 6 * features + inner]
        pair_sums = late[6 * features + inner :].reshape(2, heads, size)
        out_b_qv = jnp.concatenate([pair_sums[0], pair_sums[1]], 1)
    out_ln1_gain, out_ln1_bias, out_ln2_gain, out_ln2_bias, out_b_out, out_b_down = [
        vectors[i] for i in range(6)
    ]

    (
        grad_prefix_embed,
        grad_reparam_in,
        grad_reparam_in_bias,
        grad_reparam_out,
        grad_reparam_out_bias,
    ) = prefix_back(hidden_grad, prefix_hidden, prefix_embed, reparam_in, prefix_low, heads)
    return (
        output_act,
        input_grad,
        out_ln1_gain,
        out_ln1_bias,
        out_w_qkv,
        out_b_qv,
        out_w_out,
        out_b_out,
        out_ln2_gain,
        out_ln2_bias,
        out_w_up,
        out_b_up,
        out_w_down,
        out_b_down,
        grad_prefix_embed,
        grad_reparam_in,
        grad_reparam_in_bias,
        grad_reparam_out,
        grad_reparam_out_bias,
    )


def solution(mesh):
    placed = (
        P("seq", "tensor"),
        P("seq"),
        P("seq", "tensor"),
        P("tensor"),
        P("tensor"),
        P(None, "tensor", None),
        P("tensor", None),
        P("tensor", None, None),
        P("tensor"),
        P("tensor"),
        P("tensor"),
        P(None, "tensor"),
        P("tensor"),
        P("tensor", None),
        P("tensor"),
        P(),
        P(),
        P(),
        P(None, "tensor", None),
        P("tensor", None),
    )
    return jax.shard_map(
        on_device,
        mesh=mesh,
        in_specs=placed,
        out_specs=(
            P("seq", "tensor"),
            P("seq", "tensor"),
            P("tensor"),
            P("tensor"),
            P(None, "tensor", None),
            P("tensor", None),
            P("tensor", None, None),
            P("tensor"),
            P("tensor"),
            P("tensor"),
            P(None, "tensor"),
            P("tensor"),
            P("tensor", None),
            P("tensor"),
            P(),
            P(),
            P(),
            P(None, "tensor", None),
            P("tensor", None),
        ),
        check_vma=False,
    )
```

```python
import functools

import jax
import jax.numpy as jnp
from jax import lax
from jax.experimental import pallas as pl
from jax.experimental.pallas import tpu as pltpu
from jax.sharding import PartitionSpec as P

EPS = 1e-05
NEGATIVE = -1e30
HIGHEST = lax.Precision.HIGHEST
F32 = jnp.float32
BF16 = jnp.bfloat16
LANES = 128
PAD = 16
WEAK = 1e-24
DOCS = 5

VM = pl.BlockSpec(memory_space=pltpu.VMEM)
SM = pl.BlockSpec(memory_space=pltpu.SMEM)


def gelu_tanh(values):
    return jax.nn.gelu(values, approximate=True)


def contract(first, second, first_dim, second_dim):
    return lax.dot_general(
        first, second, (((first_dim,), (second_dim,)), ((), ())), preferred_element_type=F32
    )


def work(queries, keys, products):
    pairs = queries * keys // 2
    return pl.CostEstimate(
        flops=2 * 256 * products * pairs, bytes_accessed=8 * 2**20, transcendentals=pairs
    )


def after(values, other):
    return lax.optimization_barrier((values, other))[0]


def document_start(meta, place):
    found = jnp.zeros_like(place) if getattr(place, "shape", ()) else jnp.int32(0)
    for number in range(DOCS - 1):
        begin = meta[number]
        found = jnp.where(place >= begin, jnp.maximum(found, begin), found)
    return found


def query_places(meta, index, base, chunk, group):
    return base + (index // chunk) * (chunk * group) + meta[DOCS - 1] * chunk + index % chunk


def tile_bounds(meta, base, count, chunk, group):
    rank = meta[DOCS - 1]
    first = base + rank * chunk
    last = base + (count // chunk - 1) * (chunk * group) + rank * chunk + chunk - 1
    return document_start(meta, first), document_start(meta, last)


def one_row(rows, columns):
    return lax.broadcasted_iota(jnp.int32, (rows, columns), 0) == 0


def by_rank(meta, group, first, second, work):
    if group != 2:
        work(first, second)
        return

    @pl.when(meta[DOCS - 1] == 0)
    def _():
        work(first, second)

    @pl.when(meta[DOCS - 1] == 1)
    def _():
        work(second, first)


def over_keys(bounds, base, tile, group, keys, block):
    low, low_last = bounds

    def step(number, _):
        clear = number * keys >= low_last

        @pl.when(clear)
        def _():
            block(number * keys, keys, 0, False)

        @pl.when(jnp.logical_not(clear))
        def _():
            block(number * keys, keys, 0, True)

        return 0

    lax.fori_loop(low // keys, base // keys, step, 0)
    for stair in range(tile // LANES):
        block(base + stair * LANES * group, LANES * group, stair * LANES, True)


def allowed(meta, start, count, places):
    key = start + lax.broadcasted_iota(jnp.int32, (count, 1), 0)
    return (key <= places) & (key >= document_start(meta, places))


def forward_kernel(
    meta, query, own, other, pre_key, pre_value,
    out_low, out_full, log_total,
    key_rows, value_ones, accum, peak, norm,
    *, tile, keys, prefix, chunk, group, length, width,
):
    sources, size, whole = own.shape
    blocks = query.shape[0]
    per = width // tile
    scale = size**-0.5
    padded = pre_key.shape[1]
    kept = slice(whole - length, whole)

    def extended(values, count, total):
        ones = jnp.where(one_row(PAD, count), 1.0, 0.0).astype(BF16)
        rest = total - size - PAD
        tail = [jnp.zeros((rest, count), BF16)] if rest else []
        return jnp.concatenate([values, ones] + tail, 0)

    def longest(values):
        wide = values.astype(F32)
        return jnp.max(jnp.sum(wide * wide, 0, keepdims=True), 1, keepdims=True)

    norm[...] = jnp.broadcast_to(longest(pre_key[...]), norm.shape)

    def fill(key, value):
        def prepare(source, _):
            rows = pl.ds(pl.multiple_of(source * length, length), length)
            found = key[source, :, kept]
            key_rows[rows, :] = extended(found, length, LANES).astype(F32).T.astype(BF16)
            value_ones[:, rows] = extended(value[source, :, kept], length, size + PAD)
            norm[...] = jnp.maximum(norm[...], longest(found))
            return 0

        lax.fori_loop(0, sources, prepare, 0)

    by_rank(meta, group, own, other, fill)
    most = jnp.sqrt(norm[0:1, 0:1])
    pre_key_ones = extended(pre_key[...], padded, LANES)
    pre_value_ones = extended(pre_value[...], padded, size + PAD)
    pre_row = lax.broadcasted_iota(jnp.int32, (padded, tile), 0)

    def query_tile(number, _):
        source, part = number // per, number % per
        base = number * tile * group
        columns = pl.ds(pl.multiple_of(part * tile, tile), tile)
        scaled = query[source, :, columns].astype(F32) * scale
        limit = jnp.sqrt(jnp.sum(scaled * scaled, 0, keepdims=True)) * most
        limit = limit.astype(BF16).astype(F32)
        shifted = jnp.concatenate(
            [
                scaled,
                jnp.where(one_row(PAD, tile), -limit, 0.0),
                jnp.zeros((LANES - size - PAD, tile), F32),
            ],
            0,
        ).astype(BF16)
        index = lax.broadcasted_iota(jnp.int32, (1, tile), 1)
        places = query_places(meta, index, base, chunk, group)
        bounds = tile_bounds(meta, base, tile, chunk, group)

        weights = jnp.where(pre_row < prefix, jnp.exp(contract(pre_key_ones, shifted, 0, 0)), 0.0)
        accum[...] = contract(pre_value_ones, weights.astype(BF16), 1, 0)

        def block(start, count, lane, masked):
            rows = pl.ds(pl.multiple_of(start, LANES), count)
            weights = jnp.exp(contract(key_rows[rows, :], shifted[:, lane:], 1, 0))
            if masked:
                weights = jnp.where(allowed(meta, start, count, places[:, lane:]), weights, 0.0)
            accum[:, lane:] += contract(value_ones[:, rows], weights.astype(BF16), 1, 0)

        over_keys(bounds, base, tile, group, keys, block)
        peak[...] = limit

        @pl.when(jnp.min(accum[size : size + 1, :]) < WEAK)
        def _():
            plain = scaled.astype(BF16)

            def fold(scores, mask, values):
                scores = jnp.where(mask, scores, NEGATIVE)
                new = jnp.maximum(peak[...], jnp.max(scores, 0, keepdims=True))
                weights = jnp.where(mask, jnp.exp(scores - new), 0.0).astype(BF16)
                accum[...] = accum[...] * jnp.exp(peak[...] - new) + contract(values, weights, 1, 0)
                peak[...] = new

            peak[...] = jnp.full(peak.shape, NEGATIVE, F32)
            accum[...] = jnp.zeros(accum.shape, F32)
            fold(contract(pre_key[...], plain, 0, 0), pre_row < prefix, pre_value_ones)

            def step(number, _):
                rows = pl.ds(pl.multiple_of(number * keys, keys), keys)
                scores = contract(key_rows[rows, :][:, :size], plain, 1, 0)
                mask = allowed(meta, number * keys, keys, places)
                fold(scores, mask, value_ones[:, rows])
                return 0

            lax.fori_loop(bounds[0] // keys, (base + tile * group - 1) // keys + 1, step, 0)

        total = accum[size : size + 1, :]
        result = accum[:size, :] / total
        log_total[number] = peak[...] + jnp.log(total)
        for part in range(tile // LANES):
            piece = result[:, part * LANES : (part + 1) * LANES]
            out_full[number * (tile // LANES) + part] = piece
            out_low[number * (tile // LANES) + part] = piece.astype(BF16)
        return 0

    lax.fori_loop(0, blocks * per, query_tile, 0)


def attend_forward(
    meta, query, own, other, pre_key, pre_value,
    tile, keys, prefix, chunk, group, length, width,
):
    sources, size, _ = own.shape
    count = query.shape[0] * width
    return pl.pallas_call(
        functools.partial(
            forward_kernel, tile=tile, keys=keys, prefix=prefix, chunk=chunk, group=group,
            length=length, width=width,
        ),
        out_shape=(
            jax.ShapeDtypeStruct((count // LANES, size, LANES), BF16),
            jax.ShapeDtypeStruct((count // LANES, size, LANES), F32),
            jax.ShapeDtypeStruct((count // tile, 1, tile), F32),
        ),
        in_specs=[SM] + [VM] * 5,
        out_specs=(VM, VM, VM),
        scratch_shapes=[
            pltpu.VMEM((sources * length, LANES), BF16),
            pltpu.VMEM((size + PAD, sources * length), BF16),
            pltpu.VMEM((size + PAD, tile), F32),
            pltpu.VMEM((1, tile), F32),
            pltpu.VMEM((8, LANES), F32),
        ],
        compiler_params=pltpu.CompilerParams(vmem_limit_bytes=26 * 2**20),
        cost_estimate=work(count, sources * length, 2),
        name="attend_forward",
    )(meta, query, own, other, pre_key, pre_value)


def in_three(values):
    high = values.astype(BF16).astype(F32)
    middle = (values - high).astype(BF16).astype(F32)
    low = values - high - middle
    row = lax.broadcasted_iota(jnp.int32, (PAD, values.shape[1]), 0)
    return jnp.where(row == 0, high, jnp.where(row == 1, middle, jnp.where(row == 2, low, 0.0)))


def backward_kernel(
    meta, query, own, other, pre_key, pre_value, grad_out, out_full, log_total,
    grad_query, grad_keep, grad_send, grad_prefix,
    key_rows, value_rows, key_columns, sums, query_sum,
    *, tile, keys, prefix, chunk, group, length, width,
):
    sources, size, whole = own.shape
    blocks = query.shape[0]
    kept = slice(whole - length, whole)
    per = width // tile
    scale = size**-0.5
    count = tile // LANES
    rank = meta[DOCS - 1]

    def extended(values):
        ones = jnp.where(
            lax.broadcasted_iota(jnp.int32, (LANES - size, values.shape[1]), 0) < 3, 1.0, 0.0
        )
        return jnp.concatenate([values.astype(F32), ones], 0)

    def fill(key, value):
        def prepare(source, _):
            rows = pl.ds(pl.multiple_of(source * length, length), length)
            found = key[source, :, kept]
            key_rows[rows, :] = extended(found).T.astype(BF16)
            value_rows[rows, :] = extended(value[source, :, kept]).T.astype(BF16)
            key_columns[:, rows] = found
            sums[rows, :] = jnp.zeros((length, LANES), F32)
            return 0

        lax.fori_loop(0, sources, prepare, 0)

    by_rank(meta, group, own, other, fill)
    grad_prefix[...] = jnp.zeros(grad_prefix.shape, F32)
    pre_row = lax.broadcasted_iota(jnp.int32, (pre_key.shape[0], tile), 0)

    def query_tile(number, _):
        source, part = number // per, number % per
        base = number * tile * group
        columns = pl.ds(pl.multiple_of(part * tile, tile), tile)
        scaled = (query[source, :, columns].astype(F32) * scale).astype(BF16)
        pieces = [number * count + piece for piece in range(count)]
        grad = jnp.concatenate([grad_out[piece] for piece in pieces], 1)
        full = jnp.concatenate([out_full[piece] for piece in pieces], 1)
        delta = jnp.sum(grad.astype(F32) * full, 0, keepdims=True)
        level = log_total[number]
        index = lax.broadcasted_iota(jnp.int32, (1, tile), 1)
        places = query_places(meta, index, base, chunk, group)
        bounds = tile_bounds(meta, base, tile, chunk, group)
        rest = jnp.zeros((LANES - size - PAD, tile), BF16)
        scaled_less = jnp.concatenate([scaled, in_three(-level).astype(BF16), rest], 0)
        grad_less = jnp.concatenate([grad, in_three(-delta).astype(BF16), rest], 0)
        none = jnp.zeros((size, tile), BF16)
        pair = jnp.concatenate(
            [jnp.concatenate([grad, none], 1), jnp.concatenate([none, scaled], 1)], 0
        )

        probs = jnp.exp(contract(pre_key[...], scaled, 1, 0) - level)
        probs = jnp.where(pre_row < prefix, probs, 0.0)
        slope = (probs * (contract(pre_value[...], grad, 1, 0) - delta)).astype(BF16)
        grad_prefix[0] += contract(slope, scaled, 1, 1)
        grad_prefix[1] += contract(probs.astype(BF16), grad, 1, 1)
        query_sum[...] = contract(pre_key[...], slope, 0, 0)

        def block(start, count, lane, masked):
            rows = pl.ds(pl.multiple_of(start, LANES), count)
            probs = jnp.exp(contract(key_rows[rows, :], scaled_less[:, lane:], 1, 0))
            if masked:
                probs = jnp.where(allowed(meta, start, count, places[:, lane:]), probs, 0.0)
            slope = probs * contract(value_rows[rows, :], grad_less[:, lane:], 1, 0)
            slope = slope.astype(BF16)
            both = jnp.concatenate([probs.astype(BF16), slope], 1)
            ends = jnp.concatenate([pair[:, lane:tile], pair[:, tile + lane :]], 1) if lane else pair
            sums[rows, :] += contract(both, ends, 1, 1)
            query_sum[:, lane:] += contract(key_columns[:, rows], slope, 1, 0)

        over_keys(bounds, base, tile, group, keys, block)
        grad_query[source, :, columns] = (query_sum[...] * scale).astype(BF16)
        return 0

    lax.fori_loop(0, blocks * per, query_tile, 0)

    def flush(keys_target, values_target):
        def step(source, _):
            rows = pl.ds(pl.multiple_of(source * length, length), length)
            turned = sums[rows, :].T.astype(BF16)
            values_target[source] = turned[:size]
            keys_target[source] = turned[size:]
            return 0

        lax.fori_loop(0, sources, step, 0)

    if group == 2:

        @pl.when(rank == 0)
        def _():
            flush(grad_keep, grad_send)

        @pl.when(rank == 1)
        def _():
            flush(grad_send, grad_keep)

    else:
        flush(grad_keep, grad_send)


def attend_backward(
    meta, query, own, other, pre_key, pre_value, grad_out, out_full, log_total,
    tile, keys, prefix, chunk, group, length, width,
):
    sources, size, _ = own.shape
    pair = jax.ShapeDtypeStruct((sources, size, length), BF16)
    return pl.pallas_call(
        functools.partial(
            backward_kernel, tile=tile, keys=keys, prefix=prefix, chunk=chunk, group=group,
            length=length, width=width,
        ),
        out_shape=(
            jax.ShapeDtypeStruct((query.shape[0], size, width), BF16),
            pair,
            pair,
            jax.ShapeDtypeStruct((2,) + pre_key.shape, F32),
        ),
        in_specs=[SM] + [VM] * 8,
        out_specs=(VM,) * 4,
        scratch_shapes=[
            pltpu.VMEM((sources * length, LANES), BF16),
            pltpu.VMEM((sources * length, LANES), BF16),
            pltpu.VMEM((size, sources * length), BF16),
            pltpu.VMEM((sources * length, LANES), F32),
            pltpu.VMEM((size, tile), F32),
        ],
        compiler_params=pltpu.CompilerParams(vmem_limit_bytes=34 * 2**20),
        cost_estimate=work(query.shape[0] * width, sources * length, 5),
        name="attend_backward",
    )(meta, query, own, other, pre_key, pre_value, grad_out, out_full, log_total)


def as_rows(columns):
    lane = lax.broadcasted_iota(jnp.int32, (columns[0].shape[0], LANES), 1)
    wide = jnp.zeros(lane.shape, F32)
    for number, column in enumerate(columns):
        wide = jnp.where(lane == number, column, wide)
    return wide.T[:8]


def turn_kernel(*refs):
    count = len(refs) // 2
    for source, target in zip(refs[:count], refs[count:]):
        target[...] = source[...].astype(F32).T.astype(BF16)


def turned(*arrays):
    return pl.pallas_call(
        turn_kernel,
        out_shape=tuple(jax.ShapeDtypeStruct(a.shape[::-1], BF16) for a in arrays),
        in_specs=[VM] * len(arrays),
        out_specs=(VM,) * len(arrays),
        compiler_params=pltpu.CompilerParams(vmem_limit_bytes=8 * 2**20),
        name="turned",
    )(*arrays)


def project_kernel(rows, columns, weight, bias, full, sent, stats, *, heads, size, step):
    length = rows.shape[1]
    pieces = length // step
    half = step // 2
    width = length // 2
    for piece in range(pieces):
        lanes = slice(piece * step, (piece + 1) * step)
        values = rows[:, lanes].astype(F32)
        mean = jnp.mean(values, 0, keepdims=True)
        centered = values - mean
        inverse = lax.rsqrt(jnp.mean(centered * centered, 0, keepdims=True) + EPS)
        stats[0:1, lanes] = mean
        stats[1:2, lanes] = inverse
        low = (centered * inverse * columns[:, 0:1] + columns[:, 1:2]).astype(BF16)
        full[:, lanes] = low
        mixed = (contract(weight[...], low, 1, 0) + bias[...]).astype(BF16)
        for head in range(heads):
            part = mixed[head * 3 * size : (head + 1) * 3 * size]
            spot = slice(piece * half, (piece + 1) * half)
            sent[2 * head, :, spot] = part[:size, :half]
            sent[2 * head + 1, :, spot] = part[:size, half:]
            spot = slice(width + piece * step, width + (piece + 1) * step)
            sent[2 * head, :, spot] = part[size : 2 * size]
            sent[2 * head + 1, :, spot] = part[2 * size :]


def project(rows, columns, weight, bias, heads, size, step):
    width, length = rows.shape
    return pl.pallas_call(
        functools.partial(project_kernel, heads=heads, size=size, step=step),
        out_shape=(
            jax.ShapeDtypeStruct((width, length), BF16),
            jax.ShapeDtypeStruct((2 * heads, size, length // 2 * 3), BF16),
            jax.ShapeDtypeStruct((2, length), F32),
        ),
        in_specs=[VM] * 4,
        out_specs=(VM, VM, VM),
        compiler_params=pltpu.CompilerParams(vmem_limit_bytes=20 * 2**20),
        name="project",
    )(rows, columns, weight, bias)


def unproject_kernel(
    spot, came, weight, rows, stats, columns, own_grad, token_rows, reparam,
    flat, part, first_up, first_down, head_row, prefix_low, small, totals,
    *, heads, size, step,
):
    width, length = rows.shape
    half = step // 2
    past = length // 2
    gain = columns[:, 0:1]
    row_sums = []
    sums = [0.0, 0.0, 0.0]
    for piece in range(length // step):
        lanes = slice(piece * step, (piece + 1) * step)
        place = slice(piece * half, (piece + 1) * half)
        pair = slice(past + piece * step, past + (piece + 1) * step)
        pieces = []
        for head in range(heads):
            first, second = 2 * head, 2 * head + 1
            pieces.append(jnp.concatenate([came[first, :, place], came[second, :, place]], 1))
            pieces += [came[first, :, pair], came[second, :, pair]]
        grads = jnp.concatenate(pieces, 0)
        flat[:, lanes] = grads
        back = contract(weight[...], grads, 1, 0)
        part[:, lanes] = back.astype(BF16)

        @pl.when(spot[0] == piece)
        def _():
            part[:, lanes] = (back + own_grad[...] / (stats[1:2, lanes] * gain)).astype(BF16)

        normed = (rows[:, lanes].astype(F32) - stats[0:1, lanes]) * stats[1:2, lanes]
        scaled = back * gain
        row_sums.append(
            [jnp.sum(values, 0, keepdims=True) for values in (scaled, scaled * normed)]
        )
        for number, values in enumerate((back * normed, back, grads.astype(F32))):
            sums[number] += jnp.sum(values, 1, keepdims=True)
    count = first_up.shape[0]
    blocks = width // (2 * count)
    for block in range(blocks):
        row = 2 * count * block

        @pl.when(lax.rem(spot[0] + blocks - 1, blocks) == block)
        def _():
            first_up[...] = part[row : row + count]

        @pl.when(lax.rem(spot[0] + 1, blocks) == block)
        def _():
            first_down[...] = part[row + count : row + 2 * count]

    head_row[...] = as_rows(sums[2:])[:1]
    totals[...] = as_rows(sums[:2])
    found = []
    for head in range(heads):
        both = came[2 * head, :, 3 * past :].astype(F32) + came[2 * head + 1, :, 3 * past :].astype(F32)
        both = both.T
        found += [both[:PAD], both[PAD : 2 * PAD]]
    low = jnp.concatenate(found, 1).astype(BF16)
    prefix_low[...] = low
    each = 2 * size
    hidden = sum(
        contract(low[:, head * each : (head + 1) * each], reparam[:, head, :], 1, 1)
        for head in range(heads)
    )
    features = 2 * count
    for number in range(blocks):
        spread_over = slice(number * features, (number + 1) * features)
        target = small.at[number]
        target[0:2] = totals[0:2, spread_over]
        target[2:5] = token_rows[0:3, spread_over]
        target[5:8] = jnp.zeros((3, features), F32)
        for which in range(2):
            for piece in range(blocks):
                row = 8 + which * blocks + piece
                target[row : row + 1] = row_sums[piece][which]
        for piece in range(hidden.shape[1] // features):
            row = 8 + 2 * blocks + piece * PAD
            target[row : row + PAD] = hidden[:, piece * features : (piece + 1) * features]


def unproject(spot, came, weight, rows, stats, columns, own_grad, token_rows, reparam, heads, size, step):
    width, length = rows.shape
    blocks = length // step
    features = width // blocks
    mixed = 3 * heads * size
    small = 8 + 2 * blocks + reparam.shape[0] // features * PAD
    first = jax.ShapeDtypeStruct((features // 2, length), BF16)
    return pl.pallas_call(
        functools.partial(unproject_kernel, heads=heads, size=size, step=step),
        out_shape=(
            jax.ShapeDtypeStruct((mixed, length), BF16),
            jax.ShapeDtypeStruct((width, length), BF16),
            first,
            first,
            jax.ShapeDtypeStruct((1, mixed), F32),
            jax.ShapeDtypeStruct((PAD, 2 * heads * size), BF16),
            jax.ShapeDtypeStruct((blocks, small, features), F32),
        ),
        in_specs=[SM] + [VM] * 8,
        out_specs=(VM,) * 7,
        scratch_shapes=[pltpu.VMEM((8, width), F32)],
        compiler_params=pltpu.CompilerParams(vmem_limit_bytes=20 * 2**20),
        cost_estimate=pl.CostEstimate(
            flops=4 * mixed * width * length, bytes_accessed=2**23, transcendentals=0
        ),
        name="unproject",
    )(spot, came, weight, rows, stats, columns, own_grad, token_rows, reparam)


def small_kernel(parts, down_row, up_row, head_row, row_sums, hidden, late, *, width):
    blocks = parts.shape[0]
    total = sum(parts[n] for n in range(blocks))
    features = total.shape[1]
    for which in range(2):
        for piece in range(blocks):
            row = 8 + which * blocks + piece
            lanes = slice(piece * features, (piece + 1) * features)
            row_sums[which : which + 1, lanes] = total[row : row + 1] / width
    for piece in range(hidden.shape[1] // features):
        row = 8 + 2 * blocks + piece * PAD
        hidden[:, piece * features : (piece + 1) * features] = total[row : row + PAD]
    late[...] = jnp.zeros(late.shape, F32)
    late[0:5] = total[0:5]
    late[5:6] = down_row[...]
    row = 6
    for source in (up_row, head_row):
        for piece in range(source.shape[1] // features):
            late[row : row + 1] = source[:, piece * features : (piece + 1) * features]
            row += 1


def small_totals(parts, down_row, up_row, head_row, rows, hidden_width, width):
    features = parts.shape[2]
    late = 6 + (up_row.shape[1] + head_row.shape[1]) // features
    return pl.pallas_call(
        functools.partial(small_kernel, width=width),
        out_shape=(
            jax.ShapeDtypeStruct((2, rows), F32),
            jax.ShapeDtypeStruct((PAD, hidden_width), F32),
            jax.ShapeDtypeStruct((-(-late // 8) * 8, features), F32),
        ),
        in_specs=[VM] * 4,
        out_specs=(VM,) * 3,
        compiler_params=pltpu.CompilerParams(vmem_limit_bytes=8 * 2**20),
        name="small_totals",
    )(parts, down_row, up_row, head_row)


def late_kernel(parts, vectors, up, pairs, *, heads, size):
    total = sum(parts[n] for n in range(parts.shape[0]))
    features = total.shape[1]
    vectors[...] = total[:8]
    count = up.shape[1] // features
    up[...] = jnp.concatenate([total[6 + n : 7 + n] for n in range(count)], 1)
    mixed = 3 * heads * size
    row = jnp.concatenate(
        [total[6 + count + n : 7 + count + n] for n in range(mixed // features)], 1
    )
    for head in range(heads):
        start = 3 * size * head
        pairs[head : head + 1] = jnp.concatenate(
            [row[:, start : start + size], row[:, start + 2 * size : start + 3 * size]], 1
        )


def late_totals(parts, inner, heads, size):
    return pl.pallas_call(
        functools.partial(late_kernel, heads=heads, size=size),
        out_shape=(
            jax.ShapeDtypeStruct((8, parts.shape[2]), F32),
            jax.ShapeDtypeStruct((1, inner), F32),
            jax.ShapeDtypeStruct((heads, 2 * size), F32),
        ),
        in_specs=[VM],
        out_specs=(VM,) * 3,
        compiler_params=pltpu.CompilerParams(vmem_limit_bytes=8 * 2**20),
        name="late_totals",
    )(parts)


def finish_kernel(up, down, own_up, own_down, rows, gain, stats, row_sums, grad):
    half = up.shape[0]
    mean, inverse = stats[0:1], stats[1:2]
    first, second = row_sums[0:1], row_sums[1:2]
    for start, came, own in ((0, up, own_up), (half, down, own_down)):
        spot = slice(start, start + half)
        total = came[...].astype(F32) + own[...].astype(F32)
        normed = (rows[spot].astype(F32) - mean) * inverse
        back = inverse * (gain[spot] * total - first - normed * second)
        grad[:, spot] = back.T.astype(BF16)


def finish(up, down, own_up, own_down, rows, gain, stats, row_sums):
    return pl.pallas_call(
        finish_kernel,
        out_shape=jax.ShapeDtypeStruct(rows.shape[::-1], BF16),
        in_specs=[VM] * 8,
        out_specs=VM,
        compiler_params=pltpu.CompilerParams(vmem_limit_bytes=8 * 2**20),
        name="finish",
    )(up, down, own_up, own_down, rows, gain, stats, row_sums)


def ring_lanes(slot, step, blocks, count):
    half = count // 2
    below = lax.rem(slot + blocks - step, blocks) * count
    above = lax.rem(slot + step, blocks) * count + half
    if half % LANES == 0:
        below, above = pl.multiple_of(below, half), pl.multiple_of(above, half)
    return pl.ds(below, half), pl.ds(above, half)


def feed_kernel(
    rows_up, rows_down, given, up_turned, up, down, bias,
    rows, hidden, grad_pre, part_up, part_down,
):
    half = rows_up.shape[1]
    both = jnp.concatenate([rows_up[...], rows_down[...]], 1)
    rows[...] = both
    pre = contract(up_turned[...], both, 1, 0) + bias[...]
    act, pull = jax.vjp(gelu_tanh, pre)
    hidden[...] = act.astype(BF16)
    low = pull(contract(down[...], given[...], 1, 0))[0].astype(BF16)
    grad_pre[...] = low
    part = contract(up[...], low, 1, 0).astype(BF16)
    part_up[...] = part[:, :half]
    part_down[...] = part[:, half:]


def feed(rows_up, rows_down, given, up_turned, up, down, bias):
    width, half = rows_up.shape
    inner = down.shape[0]
    count = 2 * half
    return pl.pallas_call(
        feed_kernel,
        out_shape=(
            jax.ShapeDtypeStruct((width, count), BF16),
            jax.ShapeDtypeStruct((inner, count), BF16),
            jax.ShapeDtypeStruct((inner, count), BF16),
            jax.ShapeDtypeStruct((width, half), BF16),
            jax.ShapeDtypeStruct((width, half), BF16),
        ),
        in_specs=[VM] * 7,
        out_specs=(VM,) * 5,
        compiler_params=pltpu.CompilerParams(vmem_limit_bytes=12 * 2**20),
        cost_estimate=pl.CostEstimate(
            flops=6 * width * inner * count, bytes_accessed=2**22, transcendentals=0
        ),
        name="feed",
    )(rows_up, rows_down, given, up_turned, up, down, bias)


def given_kernel(spot, grads, *given):
    blocks = len(given)
    count = given[0].shape[1]
    for step, target in enumerate(given):
        lanes = ring_lanes(spot[0], step, blocks, count)
        target[...] = jnp.concatenate([grads[:, spread] for spread in lanes], 1)


def given_grads(spot, grads, blocks):
    width, length = grads.shape
    count = length // blocks
    if count // 2 % LANES:
        found = []
        for step in range(blocks):
            below = (spot[0] - step) % blocks * count
            above = (spot[0] + step) % blocks * count + count // 2
            halves = [lax.dynamic_slice_in_dim(grads, at, count // 2, 1) for at in (below, above)]
            found.append(jnp.concatenate(halves, 1))
        return found
    return pl.pallas_call(
        given_kernel,
        out_shape=(jax.ShapeDtypeStruct((width, count), BF16),) * blocks,
        in_specs=[SM, VM],
        out_specs=(VM,) * blocks,
        compiler_params=pltpu.CompilerParams(vmem_limit_bytes=8 * 2**20),
        name="given_grads",
    )(spot, grads)


def feed_weights_kernel(*refs, blocks, square):
    rows, grads, hidden, grad_pre = [refs[n * blocks : (n + 1) * blocks] for n in range(4)]
    grad_down, grad_up, bias = refs[4 * blocks :]

    def weights(target, first, second):
        step = min(256, second[0].shape[0])
        whole = jnp.concatenate([ref[...] for ref in first], 1)
        for start in range(0, second[0].shape[0], step):
            tile = slice(start, start + step)
            turned = jnp.concatenate([ref[tile] for ref in second], 1)
            target[:, tile] = contract(whole, turned, 1, 1).astype(BF16)

    weights(grad_down, hidden, grads)
    if square:
        weights(grad_up, rows, grad_pre)
    else:
        weights(grad_up, grad_pre, rows)
    total = sum(jnp.sum(ref[...].astype(F32), 1, keepdims=True) for ref in grad_pre)
    bias[...] = as_rows([total])[:1]


def feed_weights(rows, grads, hidden, grad_pre):
    blocks = len(rows)
    width, count = rows[0].shape
    inner = hidden[0].shape[0]
    return pl.pallas_call(
        functools.partial(feed_weights_kernel, blocks=blocks, square=inner == width),
        out_shape=(
            jax.ShapeDtypeStruct((inner, width), BF16),
            jax.ShapeDtypeStruct((inner, width), BF16),
            jax.ShapeDtypeStruct((1, inner), F32),
        ),
        in_specs=[VM] * (4 * blocks),
        out_specs=(VM,) * 3,
        compiler_params=pltpu.CompilerParams(vmem_limit_bytes=14 * 2**20),
        cost_estimate=pl.CostEstimate(
            flops=4 * blocks * width * inner * count, bytes_accessed=2**24, transcendentals=0
        ),
        name="feed_weights",
    )(*rows, *grads, *hidden, *grad_pre)


def feed_out_kernel(spot, *refs, blocks):
    hidden = refs[:blocks]
    down_turned, middle, columns, out = refs[blocks:]
    features, half = out.shape[2:]
    for step, source in enumerate(hidden):
        result = contract(down_turned[...], source[...], 1, 0)
        if step == 0:
            result = result + middle[...] + columns[:, 5:6]
        result = result.astype(BF16)
        below = lax.rem(spot[0] + blocks - step, blocks)
        above = lax.rem(spot[0] + step, blocks)
        for block in range(blocks):
            piece = result[block * features : (block + 1) * features]
            out[block, 2 * below] = piece[:, :half]
            out[block, 2 * above + 1] = piece[:, half:]


def feed_out(spot, hidden, down_turned, middle, columns):
    blocks = len(hidden)
    inner, count = hidden[0].shape
    width = middle.shape[0]
    return pl.pallas_call(
        functools.partial(feed_out_kernel, blocks=blocks),
        out_shape=jax.ShapeDtypeStruct((blocks, 2 * blocks, width // blocks, count // 2), BF16),
        in_specs=[SM] + [VM] * (blocks + 3),
        out_specs=VM,
        compiler_params=pltpu.CompilerParams(vmem_limit_bytes=8 * 2**20),
        cost_estimate=pl.CostEstimate(
            flops=2 * blocks * width * inner * count, bytes_accessed=2**23, transcendentals=0
        ),
        name="feed_out",
    )(spot, *hidden, down_turned, middle, columns)


def enter_kernel(
    spot, came, weight, tokens, columns,
    attended, middle, normed, inverse, low_up, low_down,
    *, heads,
):
    size, half = came.shape[1:]
    count = 2 * half
    tensors = came.shape[0] // (2 * heads)
    for block in range(tensors):
        for head in range(heads):
            row = (block * heads + head) * size
            for rank in range(2):
                attended[row : row + size, rank * half : (rank + 1) * half] = came[
                    (2 * head + rank) * tensors + block
                ]
    branch = contract(attended[...], weight[...], 0, 0).T
    lanes = pl.ds(pl.multiple_of(spot[0] * count, count), count)
    values = tokens[:, lanes].astype(F32) + branch + columns[:, 4:5]
    middle[...] = values
    centered = values - jnp.mean(values, 0, keepdims=True)
    scale = lax.rsqrt(jnp.mean(centered * centered, 0, keepdims=True) + EPS)
    inverse[...] = scale
    centered = centered * scale
    normed[...] = centered
    low = (centered * columns[:, 2:3] + columns[:, 3:4]).astype(BF16)
    low_up[...] = low[:, :half]
    low_down[...] = low[:, half:]


def enter(spot, came, weight, tokens, columns, heads):
    width, count = tokens.shape[0], 2 * came.shape[2]
    return pl.pallas_call(
        functools.partial(enter_kernel, heads=heads),
        out_shape=(
            jax.ShapeDtypeStruct((width, count), BF16),
            jax.ShapeDtypeStruct((width, count), F32),
            jax.ShapeDtypeStruct((width, count), F32),
            jax.ShapeDtypeStruct((1, count), F32),
            jax.ShapeDtypeStruct((width, count // 2), BF16),
            jax.ShapeDtypeStruct((width, count // 2), BF16),
        ),
        in_specs=[SM] + [VM] * 4,
        out_specs=(VM,) * 6,
        compiler_params=pltpu.CompilerParams(vmem_limit_bytes=12 * 2**20),
        name="enter",
    )(spot, came, weight, tokens, columns)


def leave_kernel(
    spot, up, down, own_up, own_down, normed, inverse, grads, weight, columns,
    middle, branch, sums, sent,
    *, heads,
):
    size, half = sent.shape[1:]
    count = 2 * half
    tensors = sent.shape[0] // (2 * heads)
    total = jnp.concatenate(
        [
            up[...].astype(F32) + own_up[...].astype(F32),
            down[...].astype(F32) + own_down[...].astype(F32),
        ],
        1,
    )
    scaled = total * columns[:, 2:3]
    first = jnp.mean(scaled, 0, keepdims=True)
    second = jnp.mean(scaled * normed[...], 0, keepdims=True)
    lanes = pl.ds(pl.multiple_of(spot[0] * count, count), count)
    result = grads[:, lanes].astype(F32) + inverse[...] * (
        scaled - first - normed[...] * second
    )
    middle[...] = result
    low = result.astype(BF16)
    branch[...] = low
    back = contract(weight[...], low, 1, 0).astype(BF16)
    for block in range(tensors):
        for head in range(heads):
            row = (block * heads + head) * size
            for rank in range(2):
                sent[(2 * head + rank) * tensors + block] = back[
                    row : row + size, rank * half : (rank + 1) * half
                ]
    sums[...] = as_rows(
        [jnp.sum(values, 1, keepdims=True) for values in (total * normed[...], total, result)]
    )


def leave(spot, terms, normed, inverse, grads, weight, columns, heads, size):
    width, count = normed.shape
    blocks = width // size
    return pl.pallas_call(
        functools.partial(leave_kernel, heads=heads),
        out_shape=(
            jax.ShapeDtypeStruct((width, count), F32),
            jax.ShapeDtypeStruct((width, count), BF16),
            jax.ShapeDtypeStruct((8, width), F32),
            jax.ShapeDtypeStruct((2 * blocks, size, count // 2), BF16),
        ),
        in_specs=[SM] + [VM] * 9,
        out_specs=(VM,) * 4,
        compiler_params=pltpu.CompilerParams(vmem_limit_bytes=12 * 2**20),
        name="leave",
    )(spot, *terms, normed, inverse, grads, weight, columns)


def rest_kernel(spot, flat, full, out, mine, other):
    width = full.shape[0]
    split = mine.shape[0]
    step = min(256, width)
    for start in range(0, width, step):
        tile = slice(start, start + step)
        result = contract(flat[...], full[tile], 1, 1).astype(BF16)
        first = result[:split]
        second = jnp.concatenate([result[split:], out[:, tile]], 0)

        @pl.when(spot[1] == 0)
        def _():
            mine[:, tile] = first
            other[:, tile] = second

        @pl.when(spot[1] == 1)
        def _():
            mine[:, tile] = second
            other[:, tile] = first


def rest_halves(spot, flat, full, out):
    half = (flat.shape[0] + out.shape[0]) // 2
    return pl.pallas_call(
        rest_kernel,
        out_shape=(jax.ShapeDtypeStruct((half, full.shape[0]), BF16),) * 2,
        in_specs=[SM] + [VM] * 3,
        out_specs=(VM, VM),
        compiler_params=pltpu.CompilerParams(vmem_limit_bytes=8 * 2**20),
        cost_estimate=pl.CostEstimate(
            flops=2 * flat.shape[0] * full.size, bytes_accessed=2**23, transcendentals=0
        ),
        name="rest_halves",
    )(spot, flat, full, out)


def rest_whole_kernel(spot, half, other, mixed, out, *, chips):
    step = half.shape[0] // chips
    edge = mixed.shape[0] // step
    for piece in range(chips):
        owner = lax.rem(spot[2] + chips - piece, chips)
        rows = slice(piece * step, (piece + 1) * step)
        for source, core in ((half, spot[1]), (other, 1 - spot[1])):
            block = core * chips + owner
            values = source[rows].astype(F32)

            @pl.when(block < edge)
            def _():
                mixed[pl.ds(pl.multiple_of(jnp.minimum(block, edge - 1) * step, step), step)] = values

            @pl.when(block >= edge)
            def _():
                out[pl.ds(pl.multiple_of(jnp.maximum(block - edge, 0) * step, step), step)] = values


def rest_whole(spot, half, other, rows, chips):
    width = half.shape[1]
    return pl.pallas_call(
        functools.partial(rest_whole_kernel, chips=chips),
        out_shape=(
            jax.ShapeDtypeStruct((rows, width), F32),
            jax.ShapeDtypeStruct((2 * half.shape[0] - rows, width), F32),
        ),
        in_specs=[SM, VM, VM],
        out_specs=(VM, VM),
        compiler_params=pltpu.CompilerParams(vmem_limit_bytes=8 * 2**20),
        name="rest_whole",
    )(spot, half, other)


def prefix_kernel(
    total, hidden, embed, weight, low, grad_embed, grad_weight, grad_bias, grad_out, grad_out_bias
):
    pre = total[...] * (1.0 - hidden[...] * hidden[...])
    grad_bias[...] = jnp.sum(pre, 0, keepdims=True)

    def exact(first, second, dims):
        return lax.dot_general(
            first, second, ((dims[:1], dims[1:]), ((), ())),
            preferred_element_type=F32, precision=HIGHEST,
        )

    grad_weight[...] = exact(embed[...].astype(F32), pre, (0, 0))
    grad_embed[...] = exact(pre, weight[...].astype(F32), (1, 1))
    wide = low[...].astype(F32)
    result = exact(hidden[...], wide, (0, 0))
    sums = jnp.sum(wide, 0, keepdims=True)
    each = grad_out.shape[2]
    for head in range(grad_out.shape[1]):
        lanes = slice(head * each, (head + 1) * each)
        grad_out[:, head, :] = result[:, lanes]
        grad_out_bias[head : head + 1] = sums[:, lanes]


def prefix_back(total, hidden, embed, weight, low, heads):
    rows, width = embed.shape
    extra = PAD - rows
    hidden = jnp.pad(hidden, ((0, extra), (0, 0)))
    embed = jnp.pad(embed, ((0, extra), (0, 0)))
    inner = weight.shape[1]
    each = low.shape[1] // heads
    grad_embed, grad_weight, grad_bias, grad_out, grad_out_bias = pl.pallas_call(
        prefix_kernel,
        out_shape=(
            jax.ShapeDtypeStruct((PAD, width), F32),
            jax.ShapeDtypeStruct(weight.shape, F32),
            jax.ShapeDtypeStruct((1, inner), F32),
            jax.ShapeDtypeStruct((inner, heads, each), F32),
            jax.ShapeDtypeStruct((heads, each), F32),
        ),
        in_specs=[VM] * 5,
        out_specs=(VM,) * 5,
        compiler_params=pltpu.CompilerParams(vmem_limit_bytes=16 * 2**20),
        cost_estimate=pl.CostEstimate(flops=2**31, bytes_accessed=2**22, transcendentals=0),
        name="prefix_back",
    )(total, hidden, embed, weight, low)
    return grad_embed[:rows], grad_weight, grad_bias[0], grad_out, grad_out_bias


def spread(values, axis):
    count = lax.axis_size(axis)
    copies = jnp.broadcast_to(values[None], (count,) + values.shape)
    return lax.all_to_all(copies, axis, 0, 0, tiled=True)


def small_sum(values, axis):
    return jnp.sum(spread(values, axis), 0)


def ring(axis, by):
    count = lax.axis_size(axis)
    return [(source, (source + by) % count) for source in range(count)]


def ring_gather(values, axis, beside=()):
    count, place = lax.axis_size(axis), lax.axis_index(axis)
    half = values.shape[0] // 2
    up, down = values[:half], values[half:]
    out = jnp.zeros((count,) + values.shape, values.dtype)
    out = lax.dynamic_update_slice_in_dim(out, values[None], place, 0)
    zeros = (0,) * (values.ndim - 1)
    results = []
    for step in range(1, count):
        up = lax.ppermute(up, axis, ring(axis, 1))
        down = lax.ppermute(down, axis, ring(axis, -1))
        if step <= len(beside) and beside[step - 1]:
            up, down, result = lax.optimization_barrier((up, down, beside[step - 1]()))
            results.append(result)
        out = lax.dynamic_update_slice(out, up[None], ((place - step) % count, 0) + zeros)
        out = lax.dynamic_update_slice(out, down[None], ((place + step) % count, half) + zeros)
    return (out, results) if beside else out


def half_blocks(blocks, axis):
    count, place = lax.axis_size(axis), lax.axis_index(axis)
    half = blocks.shape[1] // 2

    def own(step, upper):
        at = place + step if upper else place - step
        block = lax.dynamic_index_in_dim(blocks, at % count, 0, keepdims=False)
        return block[half:] if upper else block[:half]

    return own


def ring_terms(own, axis, beside=(), first=None):
    count = lax.axis_size(axis)
    up, down = first or (own(1, False), own(1, True))
    state = None
    for step in range(1, count):
        up = lax.ppermute(up, axis, ring(axis, 1))
        down = lax.ppermute(down, axis, ring(axis, -1))
        if step <= len(beside):
            state = beside[step - 1](state)
            up, down, state = lax.optimization_barrier((up, down, state))
        if step < count - 1:
            up = (up.astype(F32) + own(step + 1, False).astype(F32)).astype(BF16)
            down = (down.astype(F32) + own(step + 1, True).astype(F32)).astype(BF16)
    for other in beside[count - 1 :]:
        state = other(state)
    return (up, down, own(0, False), own(0, True)), state


def swapped(values):
    pairs = [(source, source ^ 1) for source in range(lax.axis_size("seq"))]
    return lax.ppermute(values, "seq", pairs)


def chip_parts(half):
    count = lax.axis_size("seq")
    chips = count // 2
    chip = lax.axis_index("seq") // 2
    blocks = half.reshape(chips, half.shape[0] // chips, half.shape[1])
    total = lax.dynamic_index_in_dim(blocks, chip, 0, keepdims=False)
    parts = [total]
    for step in range(1, chips):
        block = lax.dynamic_index_in_dim(blocks, (chip + step) % chips, 0, keepdims=False)
        parts.append(lax.ppermute(block, "seq", ring("seq", 2 * step)))
    return parts


def chip_gather(parts):
    part = sum(part.astype(F32) for part in parts).astype(BF16)
    behind = [lax.ppermute(part, "seq", ring("seq", 2 * step)) for step in range(1, len(parts))]
    return jnp.concatenate([part] + behind, 0)


def spread_direct(values, axis):
    count, place = lax.axis_size(axis), lax.axis_index(axis)
    out = jnp.zeros((count,) + values.shape, values.dtype)
    out = lax.dynamic_update_slice_in_dim(out, values[None], place, 0)
    for step in range(1, count):
        came = lax.ppermute(values, axis, ring(axis, step))
        out = lax.dynamic_update_slice_in_dim(out, came[None], (place - step) % count, 0)
    return out


def core_gather(half):
    core, chip = lax.axis_index("seq") % 2, lax.axis_index("seq") // 2
    chips = lax.axis_size("seq") // 2
    order = (chip - jnp.arange(chips)) % chips

    def sorted_parts(values):
        parts = values.reshape(chips, -1, values.shape[1])
        picked = [lax.dynamic_index_in_dim(parts, order[n], 0) for n in range(chips)]
        return jnp.concatenate(picked, 0).reshape(values.shape)

    half, other = sorted_parts(half), sorted_parts(swapped(half))
    first = jnp.where(core == 0, half, other)
    second = jnp.where(core == 0, other, half)
    return jnp.concatenate([first, second], 0)


def regrouped(values, width):
    count, size, columns = values.shape
    if width == columns:
        return values
    if width > columns:
        merged = values.reshape(-1, width // columns, size, columns).transpose(0, 2, 1, 3)
        return merged.reshape(-1, size, width)
    cut = values.reshape(count, size, columns // width, width).transpose(0, 2, 1, 3)
    return cut.reshape(-1, size, width)


def group_gather(pieces, group):
    if group == 2:
        rank = lax.axis_index("seq") % 2
        other = swapped(pieces)
        return jnp.stack([jnp.where(rank == 0, pieces, other), jnp.where(rank == 0, other, pieces)])
    count = lax.axis_size("seq")
    groups = [[first + i for i in range(group)] for first in range(0, count, group)]
    return lax.all_gather(pieces, "seq", axis_index_groups=groups)


def on_device(
    tokens,
    segment_ids,
    out_grad,
    ln1_gain,
    ln1_bias,
    w_qkv,
    b_qv,
    w_out,
    b_out,
    ln2_gain,
    ln2_bias,
    w_up,
    b_up,
    w_down,
    b_down,
    prefix_embed,
    reparam_in,
    reparam_in_bias,
    reparam_out,
    reparam_out_bias,
):
    rows, features = tokens.shape
    heads = w_qkv.shape[1]
    size = w_qkv.shape[2] // 3
    inner = w_up.shape[1]
    seqs, tensors = lax.axis_size("seq"), lax.axis_size("tensor")
    width = features * tensors
    own_rows = rows // tensors
    group = seqs // heads
    chunk = own_rows // group
    place, slot = lax.axis_index("seq"), lax.axis_index("tensor")
    head, rank = place // group, place % group
    prefix = prefix_embed.shape[0]
    tokens_head = rows // group
    query_width = max(tokens_head, LANES)
    forward_tile = min(512, query_width)
    backward_tile = min(512, query_width)
    forward_keys, backward_keys = 1024, 1024
    both = ("seq", "tensor")
    paired = group == 2 and chunk == LANES

    own_tokens, own_grads = turned(tokens, out_grad)
    numbers = jnp.arange(1, DOCS, dtype=jnp.int32)

    def document_starts():
        before = jnp.sum((segment_ids[None, :] < numbers[:, None]).astype(jnp.int32), 1)
        return spread(jnp.broadcast_to(before[:, None], (DOCS - 1, LANES)), "seq")

    def whole_vectors():
        return spread(
            jnp.stack([ln1_gain, ln1_bias, ln2_gain, ln2_bias, b_out, b_down]), "tensor"
        )

    full_tokens, (vectors, starts) = ring_gather(
        own_tokens, "tensor", (None, whole_vectors, document_starts)
    )
    full_tokens = full_tokens.reshape(width, rows)
    meta = jnp.concatenate([jnp.sum(starts, 0)[:, 0], rank[None].astype(jnp.int32)])
    columns = vectors.transpose(0, 2, 1).reshape(width, 6).astype(F32)
    out_share = w_out.reshape(seqs, heads * size // seqs, width)
    out_share = lax.dynamic_index_in_dim(out_share, place, 0, keepdims=False)
    core = place % 2
    spot = jnp.stack([slot, core, place // 2]).astype(jnp.int32)

    prefix_hidden = jnp.tanh(
        jnp.dot(prefix_embed, reparam_in, preferred_element_type=F32)
        + reparam_in_bias.astype(F32)
    )
    prefix_pair = jnp.einsum(
        "pa,ahe->phe", prefix_hidden, reparam_out.astype(F32), precision=HIGHEST
    )
    prefix_pair = (prefix_pair + reparam_out_bias.astype(F32)).astype(BF16)
    own_pair = lax.dynamic_index_in_dim(prefix_pair, head, 1, keepdims=False)
    own_pair = jnp.pad(own_pair, ((0, LANES - prefix), (0, 0)))
    pre_key, pre_value = own_pair[:, :size], own_pair[:, size:]

    w_flat = w_qkv.reshape(width, heads * 3 * size)
    bias_pair = b_qv.astype(F32)
    bias_three = jnp.stack(
        [bias_pair[:, :size], jnp.zeros((heads, size), F32), bias_pair[:, size:]], 1
    ).reshape(-1, 1)
    if paired:
        full1, sent, stats = project(
            full_tokens, columns, w_flat.T, bias_three, heads, size, own_rows
        )
    else:
        wide = full_tokens.astype(F32)
        mean = jnp.mean(wide, 0, keepdims=True)
        inverse = lax.rsqrt(jnp.mean((wide - mean) ** 2, 0, keepdims=True) + EPS)
        stats = jnp.concatenate([mean, inverse], 0)
        full1 = ((wide - mean) * inverse * columns[:, 0:1] + columns[:, 1:2]).astype(BF16)
        mixed = (contract(w_flat, full1, 0, 0) + bias_three).astype(BF16)
        mixed = mixed.reshape(heads, 3, size, rows)
        query_part = mixed[:, 0].reshape(heads, size, tensors, group, chunk)
        query_part = query_part.transpose(0, 3, 1, 2, 4).reshape(seqs, size, tokens_head)
        pair_part = mixed[:, 1:].transpose(0, 2, 1, 3).reshape(heads, size, group, 2 * tokens_head)
        pair_part = pair_part.transpose(0, 2, 1, 3).reshape(seqs, size, 2 * tokens_head)
        sent = jnp.concatenate([query_part, pair_part], 2)
    out_share = spread_direct(after(out_share, sent), "tensor")
    came = lax.all_to_all(sent, "seq", 0, 0, tiled=True)
    came, out_share = lax.optimization_barrier((came, out_share))
    w_out_full = lax.all_gather(out_share, "seq")
    w_out_full = w_out_full.transpose(1, 0, 2, 3).reshape(width, width)
    if group == 2:
        query, own, other = came, came, swapped(came)
    else:
        query, pair = came[:, :, :tokens_head], came[:, :, tokens_head:]
        query = regrouped(query, query_width)
        pair = group_gather(pair, group).transpose(1, 2, 0, 3).reshape(seqs, size, 2, rows)
        own, other = pair[:, :, 0], pair[:, :, 1]
    full_grad = lax.all_gather(after(own_grads, full_tokens), "tensor", axis=0, tiled=True)
    out_low, out_full, log_total = attend_forward(
        meta, query, own, other, pre_key.T, pre_value.T,
        forward_tile, forward_keys, prefix, chunk, group, rows, query_width,
    )
    out_low, full_grad, late_up, late_down, late_qkv = lax.optimization_barrier(
        (out_low, full_grad, w_up, w_down, w_qkv)
    )
    late_qkv = late_qkv.transpose(1, 2, 0).reshape(heads * 3 * size, width)
    up_turned, down_turned, late_flat = turned(late_up, late_down, late_qkv)

    came = lax.all_to_all(regrouped(out_low, chunk), both, 0, 0, tiled=True)
    came, up_turned, down_turned, late_flat, w_out_full = lax.optimization_barrier(
        (came, up_turned, down_turned, late_flat, w_out_full)
    )
    if paired:
        attended, middle, normed2, inverse2, ring_up, ring_down = enter(
            spot, came, w_out_full, full_tokens, columns, heads
        )
    else:
        came = came.reshape(heads, group, tensors, size, chunk).transpose(2, 0, 3, 1, 4)
        attended = came.reshape(width, own_rows)
        branch = contract(w_out_full, attended, 0, 0)
        own_block = lax.dynamic_slice_in_dim(full_tokens, slot * own_rows, own_rows, 1)
        middle = own_block.astype(F32) + branch + columns[:, 4:5]
        centered = middle - jnp.mean(middle, 0, keepdims=True)
        inverse2 = lax.rsqrt(jnp.mean(centered * centered, 0, keepdims=True) + EPS)
        normed2 = centered * inverse2
        out2 = (normed2 * columns[:, 2:3] + columns[:, 3:4]).astype(BF16)
        ring_up, ring_down = out2[:, : own_rows // 2], out2[:, own_rows // 2 :]

    bias_up = b_up.astype(F32)[:, None]
    given = given_grads(spot, full_grad, tensors)
    results = []
    for step in range(tensors):
        def block(up=ring_up, down=ring_down, step=step):
            return feed(up, down, given[step], up_turned, w_up, w_down, bias_up)

        if step < tensors - 1:
            ring_up = lax.ppermute(ring_up, "tensor", ring("tensor", 1))
            ring_down = lax.ppermute(ring_down, "tensor", ring("tensor", -1))
            ring_up, ring_down, result = lax.optimization_barrier((ring_up, ring_down, block()))
        else:
            result = block()
        results.append(result)
    blocks, hidden, grad_pre, parts_up, parts_down = zip(*results)

    def weights_here(_):
        return feed_weights(blocks, given, hidden, grad_pre)

    def out_here(state):
        return state, feed_out(spot, hidden, down_turned, middle, columns)

    terms, (weights, mlp_out) = ring_terms(
        lambda step, upper: (parts_down if upper else parts_up)[step],
        "tensor",
        (weights_here, out_here),
    )
    grad_w_down, grad_w_up, grad_b_up = weights
    feed_sums = lax.psum((grad_w_down, grad_w_up), "seq")

    if paired:
        grad_middle, grad_branch, token_sums, sent = leave(
            spot, terms, normed2, inverse2, full_grad, w_out_full, columns, heads, size
        )
    else:
        up, down, own_up, own_down = [a.astype(F32) for a in terms]
        grad_normed2 = jnp.concatenate([up + own_up, down + own_down], 1)
        scaled = grad_normed2 * columns[:, 2:3]
        first = jnp.mean(scaled, 0, keepdims=True)
        second = jnp.mean(scaled * normed2, 0, keepdims=True)
        own_grad = lax.dynamic_slice_in_dim(full_grad, slot * own_rows, own_rows, 1)
        grad_middle = own_grad.astype(F32) + inverse2 * (scaled - first - normed2 * second)
        grad_branch = grad_middle.astype(BF16)
        token_sums = [grad_normed2 * normed2, grad_normed2, grad_middle]
        token_sums = jnp.stack([jnp.sum(a, 1) for a in token_sums], 1)
        sent = contract(w_out_full, grad_branch, 1, 0).astype(BF16)
        sent = sent.reshape(tensors, heads, size, group, chunk).transpose(1, 3, 0, 2, 4)
        sent = sent.reshape(seqs * tensors, size, chunk)
    came = lax.all_to_all(sent, both, 0, 0, tiled=True)
    grad_out = regrouped(came, LANES)

    grad_w_out = contract(attended, grad_branch, 1, 1).astype(BF16)
    grad_out, mlp_out, grad_w_out = lax.optimization_barrier((grad_out, mlp_out, grad_w_out))
    output_act = lax.all_to_all(mlp_out, "tensor", 0, 0, tiled=True)
    grad_w_out = lax.psum_scatter(grad_w_out, "tensor", scatter_dimension=0, tiled=True)

    levels = log_total.reshape(-1, 1, backward_tile)
    grad_query, grad_keep, grad_send, grad_prefix = attend_backward(
        meta, query, own, other, pre_key[:PAD], pre_value[:PAD], grad_out, out_full, levels,
        backward_tile, backward_keys, prefix, chunk, group, rows, query_width,
    )
    if group == 2:
        grad_share = (grad_keep.astype(F32) + swapped(grad_send).astype(F32)).astype(BF16)
    else:
        grad_pair = jnp.stack([grad_keep, grad_send])
        groups = [[first + i for i in range(group)] for first in range(0, seqs, group)]
        shares = grad_pair.transpose(1, 2, 0, 3).reshape(seqs, size, group, 2 * tokens_head)
        grad_share = lax.psum_scatter(
            shares.transpose(2, 0, 1, 3), "seq", axis_index_groups=groups
        )
    prefix_part = grad_prefix.transpose(2, 0, 1).reshape(size, 2 * PAD).astype(BF16)
    prefix_part = jnp.pad(prefix_part, ((0, 0), (0, LANES - 2 * PAD)))
    prefix_part = jnp.broadcast_to(prefix_part[None], (seqs, size, LANES))
    sent = jnp.concatenate([regrouped(grad_query, tokens_head), grad_share, prefix_part], 2)
    sent, output_act, feed_sums = lax.optimization_barrier((sent, output_act, feed_sums))
    came = lax.all_to_all(sent, "seq", 0, 0, tiled=True)
    output_act = jnp.sum(output_act.astype(F32), 0).astype(BF16)
    output_act = output_act.transpose(0, 2, 1).reshape(rows, features)
    out_w_down = feed_sums[0].astype(F32)
    out_w_up = (feed_sums[1] if inner == width else feed_sums[1].T).astype(F32)
    came, output_act, grad_w_out, out_w_down, out_w_up = lax.optimization_barrier(
        (came, output_act, grad_w_out, out_w_down, out_w_up)
    )
    if paired:
        grad_flat, grad_part, first_up, first_down, head_row, prefix_low, small = unproject(
            spot, came, late_flat, full_tokens, stats, columns, grad_middle, token_sums,
            reparam_out, heads, size, own_rows,
        )
        first_blocks = first_up, first_down
        mine, other = rest_halves(spot, grad_flat, full1, grad_w_out)
    else:
        query_part = came[:, :, :tokens_head].reshape(heads, group, size, tensors, chunk)
        query_part = query_part.transpose(0, 2, 3, 1, 4).reshape(heads, 1, size, rows)
        pair_part = came[:, :, tokens_head : 3 * tokens_head]
        pair_part = pair_part.reshape(heads, group, size, 2 * tokens_head).transpose(0, 2, 1, 3)
        pair_part = pair_part.reshape(heads, size, 2, rows).transpose(0, 2, 1, 3)
        grad_flat = jnp.concatenate([query_part, pair_part], 1).reshape(heads * 3 * size, rows)
        back = contract(late_flat, grad_flat, 1, 0)
        normed1 = (full_tokens.astype(F32) - stats[0]) * stats[1]
        scaled = back * columns[:, 0:1]
        row_sums = jnp.stack([jnp.sum(scaled, 0), jnp.sum(scaled * normed1, 0)])
        sums1 = jnp.stack([jnp.sum(back * normed1, 1), jnp.sum(back, 1)], 1)
        head_sums = jnp.sum(grad_flat.astype(F32), 1)
        own_inverse = lax.dynamic_slice_in_dim(stats[1:2], slot * own_rows, own_rows, 1)
        own_part = lax.dynamic_slice_in_dim(back, slot * own_rows, own_rows, 1)
        own_part = own_part + grad_middle / (own_inverse * columns[:, 0:1])
        back = lax.dynamic_update_slice_in_dim(back, own_part, slot * own_rows, 1)
        grad_part = back.astype(BF16)
        first_blocks = None
        grad_w_qkv = contract(grad_flat, full1, 1, 1).astype(BF16)
        rest = jnp.concatenate([grad_w_qkv, grad_w_out], 0)
        halves = rest.reshape(2, rest.shape[0] // 2, width)
        mine = lax.dynamic_index_in_dim(halves, core, 0, keepdims=False)
        other = lax.dynamic_index_in_dim(halves, 1 - core, 0, keepdims=False)

    if not paired:
        prefix_low = came[:, :, 3 * tokens_head : 3 * tokens_head + 2 * PAD].astype(F32)
        prefix_low = jnp.sum(prefix_low.reshape(heads, group, size, 2, PAD), 1)
        prefix_low = prefix_low.transpose(3, 0, 2, 1).reshape(PAD, -1).astype(BF16)
        hidden_part = contract(prefix_low, reparam_out.reshape(reparam_out.shape[0], -1), 1, 1)
        owned = jnp.concatenate([sums1.T, token_sums.T], 0)
        owned = owned.reshape(-1, tensors, features).transpose(1, 0, 2).reshape(tensors, -1)
        shared = jnp.concatenate([row_sums.reshape(-1), hidden_part.reshape(-1)])
        shared = jnp.broadcast_to(shared[None], (tensors, shared.shape[0]))
        small = jnp.concatenate([owned, shared], 1)[:, None, :]

    grad_b_down = jnp.sum(out_grad.astype(F32), 0)

    def halves_here(_):
        return (mine.astype(F32) + swapped(other).astype(F32)).astype(BF16)

    def parts_here(half):
        return chip_parts(half), lax.all_to_all(small, "tensor", 0, 0, tiled=True)

    def totals(parts):
        if paired:
            return small_totals(
                parts, grad_b_down[None], grad_b_up, head_row, rows, prefix_hidden.shape[1], width
            )
        sums = jnp.sum(parts, 0)[0]
        after_rows = 5 * features + 2 * rows
        row_means = sums[5 * features : after_rows].reshape(2, rows) / width
        hidden = sums[after_rows:].reshape(PAD, -1)
        mixed_sums = head_sums.reshape(heads, 3, size)
        late = [sums[: 5 * features], grad_b_down, grad_b_up[0]]
        late += [mixed_sums[:, 0].reshape(-1), mixed_sums[:, 2].reshape(-1)]
        return row_means, hidden, jnp.concatenate(late)[None]

    def gather_here(state):
        row_means, hidden_grad, late = totals(state[1])
        prefix_grads = prefix_back(
            hidden_grad, prefix_hidden, prefix_embed, reparam_in, prefix_low, heads
        )
        return chip_gather(state[0]), row_means, spread(late, "seq"), prefix_grads

    last_terms, (rest_half, row_means, late, prefix_grads) = ring_terms(
        half_blocks(grad_part.reshape(tensors, features, rows), "tensor"),
        "tensor",
        (halves_here, parts_here) + (lambda state: state,) * (tensors - 4) + (gather_here,),
        first_blocks,
    )
    input_grad = finish(
        *last_terms, own_tokens, ln1_gain.astype(F32)[:, None], stats, row_means,
    )
    mixed_rows = heads * 3 * size
    if paired:
        out_w_qkv, out_w_out = rest_whole(
            spot, rest_half, swapped(rest_half), mixed_rows, seqs // 2
        )
    else:
        rest = core_gather(rest_half).astype(F32)
        out_w_qkv, out_w_out = rest[:mixed_rows], rest[mixed_rows:]
    out_w_qkv = out_w_qkv.reshape(heads, 3 * size, width).transpose(2, 0, 1)
    out_w_out = out_w_out.reshape(heads, size, width)
    if paired:
        vectors, out_b_up, out_b_qv = late_totals(late, inner, heads, size)
        out_b_up = out_b_up[0]
    else:
        late = jnp.sum(late, 0)[0]
        vectors = late[: 6 * features].reshape(6, features)
        out_b_up = late[6 * features : 6 * features + inner]
        pair_sums = late[6 * features + inner :].reshape(2, heads, size)
        out_b_qv = jnp.concatenate([pair_sums[0], pair_sums[1]], 1)
    out_ln1_gain, out_ln1_bias, out_ln2_gain, out_ln2_bias, out_b_out, out_b_down = [
        vectors[i] for i in range(6)
    ]

    return (
        output_act,
        input_grad,
        out_ln1_gain,
        out_ln1_bias,
        out_w_qkv,
        out_b_qv,
        out_w_out,
        out_b_out,
        out_ln2_gain,
        out_ln2_bias,
        out_w_up,
        out_b_up,
        out_w_down,
        out_b_down,
        *prefix_grads,
    )


def solution(mesh):
    placed = (
        P("seq", "tensor"),
        P("seq"),
        P("seq", "tensor"),
        P("tensor"),
        P("tensor"),
        P(None, "tensor", None),
        P("tensor", None),
        P("tensor", None, None),
        P("tensor"),
        P("tensor"),
        P("tensor"),
        P(None, "tensor"),
        P("tensor"),
        P("tensor", None),
        P("tensor"),
        P(),
        P(),
        P(),
        P(None, "tensor", None),
        P("tensor", None),
    )
    return jax.shard_map(
        on_device,
        mesh=mesh,
        in_specs=placed,
        out_specs=(
            P("seq", "tensor"),
            P("seq", "tensor"),
            P("tensor"),
            P("tensor"),
            P(None, "tensor", None),
            P("tensor", None),
            P("tensor", None, None),
            P("tensor"),
            P("tensor"),
            P("tensor"),
            P(None, "tensor"),
            P("tensor"),
            P("tensor", None),
            P("tensor"),
            P(),
            P(),
            P(),
            P(None, "tensor", None),
            P("tensor", None),
        ),
        check_vma=False,
    )
```

```python
import functools

import jax
import jax.numpy as jnp
from jax import lax
from jax.experimental import pallas as pl
from jax.experimental.pallas import tpu as pltpu
from jax.sharding import PartitionSpec as P

EPS = 1e-05
NEGATIVE = -1e30
HIGHEST = lax.Precision.HIGHEST
F32 = jnp.float32
BF16 = jnp.bfloat16
LANES = 128
PAD = 16
WEAK = 1e-24
DOCS = 5
CLEAR, EARLIER, AMONG = range(3)

VM = pl.BlockSpec(memory_space=pltpu.VMEM)
SM = pl.BlockSpec(memory_space=pltpu.SMEM)


def gelu_tanh(values):
    return jax.nn.gelu(values, approximate=True)


def contract(first, second, first_dim, second_dim):
    return lax.dot_general(
        first, second, (((first_dim,), (second_dim,)), ((), ())), preferred_element_type=F32
    )


def work(queries, keys, products):
    pairs = queries * keys // 2
    return pl.CostEstimate(
        flops=2 * 256 * products * pairs, bytes_accessed=8 * 2**20, transcendentals=pairs
    )


def after(values, other):
    return lax.optimization_barrier((values, other))[0]


def document_start(meta, place):
    found = jnp.zeros_like(place) if getattr(place, "shape", ()) else jnp.int32(0)
    for number in range(DOCS - 1):
        begin = meta[number]
        found = jnp.where(place >= begin, jnp.maximum(found, begin), found)
    return found


def query_places(meta, index, base, chunk, group):
    return base + (index // chunk) * (chunk * group) + meta[DOCS - 1] * chunk + index % chunk


def tile_bounds(meta, base, count, chunk, group):
    rank = meta[DOCS - 1]
    first = base + rank * chunk
    last = base + (count // chunk - 1) * (chunk * group) + rank * chunk + chunk - 1
    return document_start(meta, first), document_start(meta, last)


def one_row(rows, columns):
    return lax.broadcasted_iota(jnp.int32, (rows, columns), 0) == 0


def by_rank(meta, group, first, second, work):
    if group != 2:
        work(first, second)
        return

    @pl.when(meta[DOCS - 1] == 0)
    def _():
        work(first, second)

    @pl.when(meta[DOCS - 1] == 1)
    def _():
        work(second, first)


def over_keys(bounds, base, tile, group, keys, block):
    low, low_last = bounds
    first, last = low // keys, base // keys
    clear = jnp.clip((low_last + keys - 1) // keys, first, jnp.maximum(first, last))

    def masked(number, _):
        block(number * keys, keys, 0, EARLIER)
        return 0

    def pair(number, _):
        block((clear + 2 * number) * keys, 2 * keys, 0, CLEAR)
        return 0

    lax.fori_loop(first, jnp.minimum(clear, last), masked, 0)
    left = jnp.maximum(last - clear, 0)
    lax.fori_loop(0, left // 2, pair, 0)

    @pl.when(left % 2 == 1)
    def _():
        block((last - 1) * keys, keys, 0, CLEAR)

    for stair in range(tile // LANES):
        block(base + stair * LANES * group, LANES * group, stair * LANES, AMONG)


def allowed(meta, start, count, places, kind=AMONG):
    key = start + lax.broadcasted_iota(jnp.int32, (count, 1), 0)
    inside = key >= document_start(meta, places)
    return inside if kind == EARLIER else (key <= places) & inside


def forward_kernel(
    meta, query, own, other, pre_key, pre_value,
    out_low, out_full, log_total,
    key_rows, value_ones, accum, peak, norm,
    *, tile, keys, prefix, chunk, group, length, width,
):
    sources, size, whole = own.shape
    blocks = query.shape[0]
    per = width // tile
    scale = size**-0.5
    padded = pre_key.shape[1]
    kept = slice(whole - length, whole)

    def extended(values, count, total):
        ones = jnp.where(one_row(PAD, count), 1.0, 0.0).astype(BF16)
        rest = total - size - PAD
        tail = [jnp.zeros((rest, count), BF16)] if rest else []
        return jnp.concatenate([values, ones] + tail, 0)

    def longest(values):
        wide = values.astype(F32)
        return jnp.max(jnp.sum(wide * wide, 0, keepdims=True), 1, keepdims=True)

    norm[...] = jnp.broadcast_to(longest(pre_key[...]), norm.shape)

    def fill(key, value):
        def prepare(source, _):
            rows = pl.ds(pl.multiple_of(source * length, length), length)
            found = key[source, :, kept]
            key_rows[rows, :] = extended(found, length, LANES).astype(F32).T.astype(BF16)
            value_ones[:, rows] = extended(value[source, :, kept], length, size + PAD)
            norm[...] = jnp.maximum(norm[...], longest(found))
            return 0

        lax.fori_loop(0, sources, prepare, 0)

    by_rank(meta, group, own, other, fill)
    most = jnp.sqrt(norm[0:1, 0:1])
    pre_key_ones = extended(pre_key[...], padded, LANES)
    pre_value_ones = extended(pre_value[...], padded, size + PAD)
    pre_row = lax.broadcasted_iota(jnp.int32, (padded, tile), 0)

    def query_tile(number, _):
        source, part = number // per, number % per
        base = number * tile * group
        columns = pl.ds(pl.multiple_of(part * tile, tile), tile)
        scaled = query[source, :, columns].astype(F32) * scale
        limit = jnp.sqrt(jnp.sum(scaled * scaled, 0, keepdims=True)) * most
        limit = limit.astype(BF16).astype(F32)
        shifted = jnp.concatenate(
            [
                scaled,
                jnp.where(one_row(PAD, tile), -limit, 0.0),
                jnp.zeros((LANES - size - PAD, tile), F32),
            ],
            0,
        ).astype(BF16)
        index = lax.broadcasted_iota(jnp.int32, (1, tile), 1)
        places = query_places(meta, index, base, chunk, group)
        bounds = tile_bounds(meta, base, tile, chunk, group)

        weights = jnp.where(pre_row < prefix, jnp.exp(contract(pre_key_ones, shifted, 0, 0)), 0.0)
        accum[...] = contract(pre_value_ones, weights.astype(BF16), 1, 0)

        def block(start, count, lane, masked):
            rows = pl.ds(pl.multiple_of(start, LANES), count)
            weights = jnp.exp(contract(key_rows[rows, :], shifted[:, lane:], 1, 0))
            if masked:
                mask = allowed(meta, start, count, places[:, lane:], masked)
                weights = jnp.where(mask, weights, 0.0)
            accum[:, lane:] += contract(value_ones[:, rows], weights.astype(BF16), 1, 0)

        over_keys(bounds, base, tile, group, keys, block)
        peak[...] = limit

        @pl.when(jnp.min(accum[size : size + 1, :]) < WEAK)
        def _():
            plain = scaled.astype(BF16)

            def fold(scores, mask, values):
                scores = jnp.where(mask, scores, NEGATIVE)
                new = jnp.maximum(peak[...], jnp.max(scores, 0, keepdims=True))
                weights = jnp.where(mask, jnp.exp(scores - new), 0.0).astype(BF16)
                accum[...] = accum[...] * jnp.exp(peak[...] - new) + contract(values, weights, 1, 0)
                peak[...] = new

            peak[...] = jnp.full(peak.shape, NEGATIVE, F32)
            accum[...] = jnp.zeros(accum.shape, F32)
            fold(contract(pre_key[...], plain, 0, 0), pre_row < prefix, pre_value_ones)

            def step(number, _):
                rows = pl.ds(pl.multiple_of(number * keys, keys), keys)
                scores = contract(key_rows[rows, :][:, :size], plain, 1, 0)
                mask = allowed(meta, number * keys, keys, places)
                fold(scores, mask, value_ones[:, rows])
                return 0

            lax.fori_loop(bounds[0] // keys, (base + tile * group - 1) // keys + 1, step, 0)

        total = accum[size : size + 1, :]
        result = accum[:size, :] / total
        log_total[number] = peak[...] + jnp.log(total)
        for part in range(tile // LANES):
            piece = result[:, part * LANES : (part + 1) * LANES]
            out_full[number * (tile // LANES) + part] = piece
            out_low[number * (tile // LANES) + part] = piece.astype(BF16)
        return 0

    lax.fori_loop(0, blocks * per, query_tile, 0)


def attend_forward(
    meta, query, own, other, pre_key, pre_value,
    tile, keys, prefix, chunk, group, length, width,
):
    sources, size, _ = own.shape
    count = query.shape[0] * width
    return pl.pallas_call(
        functools.partial(
            forward_kernel, tile=tile, keys=keys, prefix=prefix, chunk=chunk, group=group,
            length=length, width=width,
        ),
        out_shape=(
            jax.ShapeDtypeStruct((count // LANES, size, LANES), BF16),
            jax.ShapeDtypeStruct((count // LANES, size, LANES), F32),
            jax.ShapeDtypeStruct((count // tile, 1, tile), F32),
        ),
        in_specs=[SM] + [VM] * 5,
        out_specs=(VM, VM, VM),
        scratch_shapes=[
            pltpu.VMEM((sources * length, LANES), BF16),
            pltpu.VMEM((size + PAD, sources * length), BF16),
            pltpu.VMEM((size + PAD, tile), F32),
            pltpu.VMEM((1, tile), F32),
            pltpu.VMEM((8, LANES), F32),
        ],
        compiler_params=pltpu.CompilerParams(vmem_limit_bytes=36 * 2**20),
        cost_estimate=work(count, sources * length, 2),
        name="attend_forward",
    )(meta, query, own, other, pre_key, pre_value)


def in_three(values):
    high = values.astype(BF16).astype(F32)
    middle = (values - high).astype(BF16).astype(F32)
    low = values - high - middle
    row = lax.broadcasted_iota(jnp.int32, (PAD, values.shape[1]), 0)
    return jnp.where(row == 0, high, jnp.where(row == 1, middle, jnp.where(row == 2, low, 0.0)))


def backward_kernel(
    meta, query, own, other, pre_key, pre_value, grad_out, out_full, log_total,
    grad_query, grad_keep, grad_send, grad_prefix,
    key_rows, value_rows, key_columns, sums, query_sum,
    *, tile, keys, prefix, chunk, group, length, width,
):
    sources, size, whole = own.shape
    blocks = query.shape[0]
    kept = slice(whole - length, whole)
    per = width // tile
    scale = size**-0.5
    count = tile // LANES
    rank = meta[DOCS - 1]

    def extended(values):
        ones = jnp.where(
            lax.broadcasted_iota(jnp.int32, (LANES - size, values.shape[1]), 0) < 3, 1.0, 0.0
        )
        return jnp.concatenate([values.astype(F32), ones], 0)

    def fill(key, value):
        def prepare(source, _):
            rows = pl.ds(pl.multiple_of(source * length, length), length)
            found = key[source, :, kept]
            key_rows[rows, :] = extended(found).T.astype(BF16)
            value_rows[rows, :] = extended(value[source, :, kept]).T.astype(BF16)
            key_columns[:, rows] = found
            sums[rows, :] = jnp.zeros((length, LANES), F32)
            return 0

        lax.fori_loop(0, sources, prepare, 0)

    by_rank(meta, group, own, other, fill)
    grad_prefix[...] = jnp.zeros(grad_prefix.shape, F32)
    pre_row = lax.broadcasted_iota(jnp.int32, (pre_key.shape[0], tile), 0)

    def query_tile(number, _):
        source, part = number // per, number % per
        base = number * tile * group
        columns = pl.ds(pl.multiple_of(part * tile, tile), tile)
        scaled = (query[source, :, columns].astype(F32) * scale).astype(BF16)
        pieces = [number * count + piece for piece in range(count)]
        grad = jnp.concatenate([grad_out[piece] for piece in pieces], 1)
        full = jnp.concatenate([out_full[piece] for piece in pieces], 1)
        delta = jnp.sum(grad.astype(F32) * full, 0, keepdims=True)
        level = log_total[number]
        index = lax.broadcasted_iota(jnp.int32, (1, tile), 1)
        places = query_places(meta, index, base, chunk, group)
        bounds = tile_bounds(meta, base, tile, chunk, group)
        rest = jnp.zeros((LANES - size - PAD, tile), BF16)
        scaled_less = jnp.concatenate([scaled, in_three(-level).astype(BF16), rest], 0)
        grad_less = jnp.concatenate([grad, in_three(-delta).astype(BF16), rest], 0)
        none = jnp.zeros((size, tile), BF16)
        pair = jnp.concatenate(
            [jnp.concatenate([grad, none], 1), jnp.concatenate([none, scaled], 1)], 0
        )

        probs = jnp.exp(contract(pre_key[...], scaled, 1, 0) - level)
        probs = jnp.where(pre_row < prefix, probs, 0.0)
        slope = (probs * (contract(pre_value[...], grad, 1, 0) - delta)).astype(BF16)
        grad_prefix[0] += contract(slope, scaled, 1, 1)
        grad_prefix[1] += contract(probs.astype(BF16), grad, 1, 1)
        query_sum[...] = contract(pre_key[...], slope, 0, 0)

        def block(start, count, lane, masked):
            rows = pl.ds(pl.multiple_of(start, LANES), count)
            probs = jnp.exp(contract(key_rows[rows, :], scaled_less[:, lane:], 1, 0))
            if masked:
                mask = allowed(meta, start, count, places[:, lane:], masked)
                probs = jnp.where(mask, probs, 0.0)
            slope = probs * contract(value_rows[rows, :], grad_less[:, lane:], 1, 0)
            slope = slope.astype(BF16)
            both = jnp.concatenate([probs.astype(BF16), slope], 1)
            ends = jnp.concatenate([pair[:, lane:tile], pair[:, tile + lane :]], 1) if lane else pair
            sums[rows, :] += contract(both, ends, 1, 1)
            query_sum[:, lane:] += contract(key_columns[:, rows], slope, 1, 0)

        over_keys(bounds, base, tile, group, keys, block)
        grad_query[source, :, columns] = (query_sum[...] * scale).astype(BF16)
        return 0

    lax.fori_loop(0, blocks * per, query_tile, 0)

    def flush(keys_target, values_target):
        def step(source, _):
            rows = pl.ds(pl.multiple_of(source * length, length), length)
            turned = sums[rows, :].T.astype(BF16)
            values_target[source] = turned[:size]
            keys_target[source] = turned[size:]
            return 0

        lax.fori_loop(0, sources, step, 0)

    if group == 2:

        @pl.when(rank == 0)
        def _():
            flush(grad_keep, grad_send)

        @pl.when(rank == 1)
        def _():
            flush(grad_send, grad_keep)

    else:
        flush(grad_keep, grad_send)


def attend_backward(
    meta, query, own, other, pre_key, pre_value, grad_out, out_full, log_total,
    tile, keys, prefix, chunk, group, length, width,
):
    sources, size, _ = own.shape
    pair = jax.ShapeDtypeStruct((sources, size, length), BF16)
    return pl.pallas_call(
        functools.partial(
            backward_kernel, tile=tile, keys=keys, prefix=prefix, chunk=chunk, group=group,
            length=length, width=width,
        ),
        out_shape=(
            jax.ShapeDtypeStruct((query.shape[0], size, width), BF16),
            pair,
            pair,
            jax.ShapeDtypeStruct((2,) + pre_key.shape, F32),
        ),
        in_specs=[SM] + [VM] * 8,
        out_specs=(VM,) * 4,
        scratch_shapes=[
            pltpu.VMEM((sources * length, LANES), BF16),
            pltpu.VMEM((sources * length, LANES), BF16),
            pltpu.VMEM((size, sources * length), BF16),
            pltpu.VMEM((sources * length, LANES), F32),
            pltpu.VMEM((size, tile), F32),
        ],
        compiler_params=pltpu.CompilerParams(vmem_limit_bytes=44 * 2**20),
        cost_estimate=work(query.shape[0] * width, sources * length, 5),
        name="attend_backward",
    )(meta, query, own, other, pre_key, pre_value, grad_out, out_full, log_total)


def as_rows(columns):
    lane = lax.broadcasted_iota(jnp.int32, (columns[0].shape[0], LANES), 1)
    wide = jnp.zeros(lane.shape, F32)
    for number, column in enumerate(columns):
        wide = jnp.where(lane == number, column, wide)
    return wide.T[:8]


def turn_kernel(*refs):
    count = len(refs) // 2
    for source, target in zip(refs[:count], refs[count:]):
        target[...] = source[...].astype(F32).T.astype(BF16)


def turned(*arrays):
    return pl.pallas_call(
        turn_kernel,
        out_shape=tuple(jax.ShapeDtypeStruct(a.shape[::-1], BF16) for a in arrays),
        in_specs=[VM] * len(arrays),
        out_specs=(VM,) * len(arrays),
        compiler_params=pltpu.CompilerParams(vmem_limit_bytes=8 * 2**20),
        name="turned",
    )(*arrays)


def project_kernel(rows, columns, weight, bias, full, sent, stats, *, heads, size, step):
    length = rows.shape[1]
    pieces = length // step
    half = step // 2
    width = length // 2
    for piece in range(pieces):
        lanes = slice(piece * step, (piece + 1) * step)
        values = rows[:, lanes].astype(F32)
        mean = jnp.mean(values, 0, keepdims=True)
        centered = values - mean
        inverse = lax.rsqrt(jnp.mean(centered * centered, 0, keepdims=True) + EPS)
        stats[0:1, lanes] = mean
        stats[1:2, lanes] = inverse
        low = (centered * inverse * columns[:, 0:1] + columns[:, 1:2]).astype(BF16)
        full[:, lanes] = low
        mixed = (contract(weight[...], low, 1, 0) + bias[...]).astype(BF16)
        for head in range(heads):
            part = mixed[head * 3 * size : (head + 1) * 3 * size]
            spot = slice(piece * half, (piece + 1) * half)
            sent[2 * head, :, spot] = part[:size, :half]
            sent[2 * head + 1, :, spot] = part[:size, half:]
            spot = slice(width + piece * step, width + (piece + 1) * step)
            sent[2 * head, :, spot] = part[size : 2 * size]
            sent[2 * head + 1, :, spot] = part[2 * size :]


def project(rows, columns, weight, bias, heads, size, step):
    width, length = rows.shape
    return pl.pallas_call(
        functools.partial(project_kernel, heads=heads, size=size, step=step),
        out_shape=(
            jax.ShapeDtypeStruct((width, length), BF16),
            jax.ShapeDtypeStruct((2 * heads, size, length // 2 * 3), BF16),
            jax.ShapeDtypeStruct((2, length), F32),
        ),
        in_specs=[VM] * 4,
        out_specs=(VM, VM, VM),
        compiler_params=pltpu.CompilerParams(vmem_limit_bytes=20 * 2**20),
        name="project",
    )(rows, columns, weight, bias)


def unproject_kernel(
    spot, came, weight, rows, stats, columns, own_grad, token_rows, reparam,
    flat, part, first_block, head_row, prefix_low, small, totals,
    *, heads, size, step,
):
    width, length = rows.shape
    half = step // 2
    past = length // 2
    gain = columns[:, 0:1]
    row_sums = []
    sums = [0.0, 0.0, 0.0]
    for piece in range(length // step):
        lanes = slice(piece * step, (piece + 1) * step)
        place = slice(piece * half, (piece + 1) * half)
        pair = slice(past + piece * step, past + (piece + 1) * step)
        pieces = []
        for head in range(heads):
            first, second = 2 * head, 2 * head + 1
            pieces.append(jnp.concatenate([came[first, :, place], came[second, :, place]], 1))
            pieces += [came[first, :, pair], came[second, :, pair]]
        grads = jnp.concatenate(pieces, 0)
        flat[:, lanes] = grads
        back = contract(weight[...], grads, 1, 0)
        part[:, lanes] = back.astype(BF16)

        @pl.when(spot[0] == piece)
        def _():
            part[:, lanes] = (back + own_grad[...] / (stats[1:2, lanes] * gain)).astype(BF16)

        normed = (rows[:, lanes].astype(F32) - stats[0:1, lanes]) * stats[1:2, lanes]
        scaled = back * gain
        row_sums.append(
            [jnp.sum(values, 0, keepdims=True) for values in (scaled, scaled * normed)]
        )
        for number, values in enumerate((back * normed, back, grads.astype(F32))):
            sums[number] += jnp.sum(values, 1, keepdims=True)
    features = first_block.shape[0]
    blocks = width // features
    for block in range(blocks):

        @pl.when(lax.rem(spot[0] + blocks - 1, blocks) == block)
        def _():
            first_block[...] = part[block * features : (block + 1) * features]

    head_row[...] = as_rows(sums[2:])[:1]
    totals[...] = as_rows(sums[:2])
    found = []
    for head in range(heads):
        both = came[2 * head, :, 3 * past :].astype(F32) + came[2 * head + 1, :, 3 * past :].astype(F32)
        both = both.T
        found += [both[:PAD], both[PAD : 2 * PAD]]
    low = jnp.concatenate(found, 1).astype(BF16)
    prefix_low[...] = low
    each = 2 * size
    hidden = sum(
        contract(low[:, head * each : (head + 1) * each], reparam[:, head, :], 1, 1)
        for head in range(heads)
    )
    for number in range(blocks):
        spread_over = slice(number * features, (number + 1) * features)
        target = small.at[number]
        target[0:2] = totals[0:2, spread_over]
        target[2:5] = token_rows[0:3, spread_over]
        target[5:8] = jnp.zeros((3, features), F32)
        for which in range(2):
            for piece in range(blocks):
                row = 8 + which * blocks + piece
                target[row : row + 1] = row_sums[piece][which]
        for piece in range(hidden.shape[1] // features):
            row = 8 + 2 * blocks + piece * PAD
            target[row : row + PAD] = hidden[:, piece * features : (piece + 1) * features]


def unproject(spot, came, weight, rows, stats, columns, own_grad, token_rows, reparam, heads, size, step):
    width, length = rows.shape
    blocks = length // step
    features = width // blocks
    mixed = 3 * heads * size
    small = 8 + 2 * blocks + reparam.shape[0] // features * PAD
    return pl.pallas_call(
        functools.partial(unproject_kernel, heads=heads, size=size, step=step),
        out_shape=(
            jax.ShapeDtypeStruct((mixed, length), BF16),
            jax.ShapeDtypeStruct((width, length), BF16),
            jax.ShapeDtypeStruct((features, length), BF16),
            jax.ShapeDtypeStruct((1, mixed), F32),
            jax.ShapeDtypeStruct((PAD, 2 * heads * size), BF16),
            jax.ShapeDtypeStruct((blocks, small, features), F32),
        ),
        in_specs=[SM] + [VM] * 8,
        out_specs=(VM,) * 6,
        scratch_shapes=[pltpu.VMEM((8, width), F32)],
        compiler_params=pltpu.CompilerParams(vmem_limit_bytes=20 * 2**20),
        cost_estimate=pl.CostEstimate(
            flops=4 * mixed * width * length, bytes_accessed=2**23, transcendentals=0
        ),
        name="unproject",
    )(spot, came, weight, rows, stats, columns, own_grad, token_rows, reparam)


def small_kernel(parts, down_row, up_row, head_row, row_sums, hidden, late, *, width):
    blocks = parts.shape[0]
    total = sum(parts[n] for n in range(blocks))
    features = total.shape[1]
    for which in range(2):
        for piece in range(blocks):
            row = 8 + which * blocks + piece
            lanes = slice(piece * features, (piece + 1) * features)
            row_sums[which : which + 1, lanes] = total[row : row + 1] / width
    for piece in range(hidden.shape[1] // features):
        row = 8 + 2 * blocks + piece * PAD
        hidden[:, piece * features : (piece + 1) * features] = total[row : row + PAD]
    late[...] = jnp.zeros(late.shape, F32)
    late[0:5] = total[0:5]
    late[5:6] = down_row[...]
    row = 6
    for source in (up_row, head_row):
        for piece in range(source.shape[1] // features):
            late[row : row + 1] = source[:, piece * features : (piece + 1) * features]
            row += 1


def small_totals(parts, down_row, up_row, head_row, rows, hidden_width, width):
    features = parts.shape[2]
    late = 6 + (up_row.shape[1] + head_row.shape[1]) // features
    return pl.pallas_call(
        functools.partial(small_kernel, width=width),
        out_shape=(
            jax.ShapeDtypeStruct((2, rows), F32),
            jax.ShapeDtypeStruct((PAD, hidden_width), F32),
            jax.ShapeDtypeStruct((-(-late // 8) * 8, features), F32),
        ),
        in_specs=[VM] * 4,
        out_specs=(VM,) * 3,
        compiler_params=pltpu.CompilerParams(vmem_limit_bytes=8 * 2**20),
        name="small_totals",
    )(parts, down_row, up_row, head_row)


def late_kernel(parts, vectors, up, pairs, *, heads, size):
    total = sum(parts[n] for n in range(parts.shape[0]))
    features = total.shape[1]
    vectors[...] = total[:8]
    count = up.shape[1] // features
    up[...] = jnp.concatenate([total[6 + n : 7 + n] for n in range(count)], 1)
    mixed = 3 * heads * size
    row = jnp.concatenate(
        [total[6 + count + n : 7 + count + n] for n in range(mixed // features)], 1
    )
    for head in range(heads):
        start = 3 * size * head
        pairs[head : head + 1] = jnp.concatenate(
            [row[:, start : start + size], row[:, start + 2 * size : start + 3 * size]], 1
        )


def late_totals(parts, inner, heads, size):
    return pl.pallas_call(
        functools.partial(late_kernel, heads=heads, size=size),
        out_shape=(
            jax.ShapeDtypeStruct((8, parts.shape[2]), F32),
            jax.ShapeDtypeStruct((1, inner), F32),
            jax.ShapeDtypeStruct((heads, 2 * size), F32),
        ),
        in_specs=[VM],
        out_specs=(VM,) * 3,
        compiler_params=pltpu.CompilerParams(vmem_limit_bytes=8 * 2**20),
        name="late_totals",
    )(parts)


def finish_kernel(came, own, rows, gain, stats, row_means, grad):
    total = came[...].astype(F32) + own[...].astype(F32)
    normed = (rows[...].astype(F32) - stats[0:1]) * stats[1:2]
    back = gain[...] * total - row_means[0:1] - normed * row_means[1:2]
    grad[...] = (stats[1:2] * back).T.astype(BF16)


def finish(came, own, rows, gain, stats, row_means):
    return pl.pallas_call(
        finish_kernel,
        out_shape=jax.ShapeDtypeStruct(rows.shape[::-1], BF16),
        in_specs=[VM] * 6,
        out_specs=VM,
        compiler_params=pltpu.CompilerParams(vmem_limit_bytes=10 * 2**20),
        name="finish",
    )(came, own, rows, gain, stats, row_means)


def ring_lanes(slot, step, blocks, count):
    half = count // 2
    below = lax.rem(slot + blocks - step, blocks) * count
    above = lax.rem(slot + step, blocks) * count + half
    if half % LANES == 0:
        below, above = pl.multiple_of(below, half), pl.multiple_of(above, half)
    return pl.ds(below, half), pl.ds(above, half)


def feed_kernel(
    rows_up, rows_down, given, up_turned, up, down, bias,
    rows, hidden, grad_pre, part_up, part_down,
):
    half = rows_up.shape[1]
    both = jnp.concatenate([rows_up[...], rows_down[...]], 1)
    rows[...] = both
    pre = contract(up_turned[...], both, 1, 0) + bias[...]
    act, pull = jax.vjp(gelu_tanh, pre)
    hidden[...] = act.astype(BF16)
    low = pull(contract(down[...], given[...], 1, 0))[0].astype(BF16)
    grad_pre[...] = low
    part = contract(up[...], low, 1, 0).astype(BF16)
    part_up[...] = part[:, :half]
    part_down[...] = part[:, half:]


def feed(rows_up, rows_down, given, up_turned, up, down, bias):
    width, half = rows_up.shape
    inner = down.shape[0]
    count = 2 * half
    return pl.pallas_call(
        feed_kernel,
        out_shape=(
            jax.ShapeDtypeStruct((width, count), BF16),
            jax.ShapeDtypeStruct((inner, count), BF16),
            jax.ShapeDtypeStruct((inner, count), BF16),
            jax.ShapeDtypeStruct((width, half), BF16),
            jax.ShapeDtypeStruct((width, half), BF16),
        ),
        in_specs=[VM] * 7,
        out_specs=(VM,) * 5,
        compiler_params=pltpu.CompilerParams(vmem_limit_bytes=12 * 2**20),
        cost_estimate=pl.CostEstimate(
            flops=6 * width * inner * count, bytes_accessed=2**22, transcendentals=0
        ),
        name="feed",
    )(rows_up, rows_down, given, up_turned, up, down, bias)


def given_kernel(spot, grads, *given):
    blocks = len(given)
    count = given[0].shape[1]
    for step, target in enumerate(given):
        lanes = ring_lanes(spot[0], step, blocks, count)
        target[...] = jnp.concatenate([grads[:, spread] for spread in lanes], 1)


def given_grads(spot, grads, blocks):
    width, length = grads.shape
    count = length // blocks
    if count // 2 % LANES:
        found = []
        for step in range(blocks):
            below = (spot[0] - step) % blocks * count
            above = (spot[0] + step) % blocks * count + count // 2
            halves = [lax.dynamic_slice_in_dim(grads, at, count // 2, 1) for at in (below, above)]
            found.append(jnp.concatenate(halves, 1))
        return found
    return pl.pallas_call(
        given_kernel,
        out_shape=(jax.ShapeDtypeStruct((width, count), BF16),) * blocks,
        in_specs=[SM, VM],
        out_specs=(VM,) * blocks,
        compiler_params=pltpu.CompilerParams(vmem_limit_bytes=8 * 2**20),
        name="given_grads",
    )(spot, grads)


def feed_weights_kernel(*refs, blocks, square):
    rows, grads, hidden, grad_pre = [refs[n * blocks : (n + 1) * blocks] for n in range(4)]
    grad_down, grad_up, bias = refs[4 * blocks :]

    def weights(target, first, second):
        step = min(256, second[0].shape[0])
        whole = jnp.concatenate([ref[...] for ref in first], 1)
        for start in range(0, second[0].shape[0], step):
            tile = slice(start, start + step)
            turned = jnp.concatenate([ref[tile] for ref in second], 1)
            target[:, tile] = contract(whole, turned, 1, 1).astype(BF16)

    weights(grad_down, hidden, grads)
    if square:
        weights(grad_up, rows, grad_pre)
    else:
        weights(grad_up, grad_pre, rows)
    total = sum(jnp.sum(ref[...].astype(F32), 1, keepdims=True) for ref in grad_pre)
    bias[...] = as_rows([total])[:1]


def feed_weights(rows, grads, hidden, grad_pre):
    blocks = len(rows)
    width, count = rows[0].shape
    inner = hidden[0].shape[0]
    return pl.pallas_call(
        functools.partial(feed_weights_kernel, blocks=blocks, square=inner == width),
        out_shape=(
            jax.ShapeDtypeStruct((inner, width), BF16),
            jax.ShapeDtypeStruct((inner, width), BF16),
            jax.ShapeDtypeStruct((1, inner), F32),
        ),
        in_specs=[VM] * (4 * blocks),
        out_specs=(VM,) * 3,
        compiler_params=pltpu.CompilerParams(vmem_limit_bytes=14 * 2**20),
        cost_estimate=pl.CostEstimate(
            flops=4 * blocks * width * inner * count, bytes_accessed=2**24, transcendentals=0
        ),
        name="feed_weights",
    )(*rows, *grads, *hidden, *grad_pre)


def feed_out_kernel(spot, *refs, blocks):
    hidden = refs[:blocks]
    down_turned, middle, columns, out = refs[blocks:]
    features, half = out.shape[2:]
    for step, source in enumerate(hidden):
        result = contract(down_turned[...], source[...], 1, 0)
        if step == 0:
            result = result + middle[...] + columns[:, 5:6]
        result = result.astype(BF16)
        below = lax.rem(spot[0] + blocks - step, blocks)
        above = lax.rem(spot[0] + step, blocks)
        for block in range(blocks):
            piece = result[block * features : (block + 1) * features]
            out[block, 2 * below] = piece[:, :half]
            out[block, 2 * above + 1] = piece[:, half:]


def feed_out(spot, hidden, down_turned, middle, columns):
    blocks = len(hidden)
    inner, count = hidden[0].shape
    width = middle.shape[0]
    return pl.pallas_call(
        functools.partial(feed_out_kernel, blocks=blocks),
        out_shape=jax.ShapeDtypeStruct((blocks, 2 * blocks, width // blocks, count // 2), BF16),
        in_specs=[SM] + [VM] * (blocks + 3),
        out_specs=VM,
        compiler_params=pltpu.CompilerParams(vmem_limit_bytes=8 * 2**20),
        cost_estimate=pl.CostEstimate(
            flops=2 * blocks * width * inner * count, bytes_accessed=2**23, transcendentals=0
        ),
        name="feed_out",
    )(spot, *hidden, down_turned, middle, columns)


def enter_kernel(
    spot, came, weight, tokens, columns,
    attended, middle, normed, inverse, low_up, low_down,
    *, heads,
):
    size, half = came.shape[1:]
    count = 2 * half
    tensors = came.shape[0] // (2 * heads)
    for block in range(tensors):
        for head in range(heads):
            row = (block * heads + head) * size
            for rank in range(2):
                attended[row : row + size, rank * half : (rank + 1) * half] = came[
                    (2 * head + rank) * tensors + block
                ]
    branch = contract(attended[...], weight[...], 0, 0).T
    lanes = pl.ds(pl.multiple_of(spot[0] * count, count), count)
    values = tokens[:, lanes].astype(F32) + branch + columns[:, 4:5]
    middle[...] = values
    centered = values - jnp.mean(values, 0, keepdims=True)
    scale = lax.rsqrt(jnp.mean(centered * centered, 0, keepdims=True) + EPS)
    inverse[...] = scale
    centered = centered * scale
    normed[...] = centered
    low = (centered * columns[:, 2:3] + columns[:, 3:4]).astype(BF16)
    low_up[...] = low[:, :half]
    low_down[...] = low[:, half:]


def enter(spot, came, weight, tokens, columns, heads):
    width, count = tokens.shape[0], 2 * came.shape[2]
    return pl.pallas_call(
        functools.partial(enter_kernel, heads=heads),
        out_shape=(
            jax.ShapeDtypeStruct((width, count), BF16),
            jax.ShapeDtypeStruct((width, count), F32),
            jax.ShapeDtypeStruct((width, count), F32),
            jax.ShapeDtypeStruct((1, count), F32),
            jax.ShapeDtypeStruct((width, count // 2), BF16),
            jax.ShapeDtypeStruct((width, count // 2), BF16),
        ),
        in_specs=[SM] + [VM] * 4,
        out_specs=(VM,) * 6,
        compiler_params=pltpu.CompilerParams(vmem_limit_bytes=12 * 2**20),
        name="enter",
    )(spot, came, weight, tokens, columns)


def leave_kernel(
    spot, up, down, own_up, own_down, normed, inverse, grads, weight, columns,
    middle, branch, sums, sent,
    *, heads,
):
    size, half = sent.shape[1:]
    count = 2 * half
    tensors = sent.shape[0] // (2 * heads)
    total = jnp.concatenate(
        [
            up[...].astype(F32) + own_up[...].astype(F32),
            down[...].astype(F32) + own_down[...].astype(F32),
        ],
        1,
    )
    scaled = total * columns[:, 2:3]
    first = jnp.mean(scaled, 0, keepdims=True)
    second = jnp.mean(scaled * normed[...], 0, keepdims=True)
    lanes = pl.ds(pl.multiple_of(spot[0] * count, count), count)
    result = grads[:, lanes].astype(F32) + inverse[...] * (
        scaled - first - normed[...] * second
    )
    middle[...] = result
    low = result.astype(BF16)
    branch[...] = low
    back = contract(weight[...], low, 1, 0).astype(BF16)
    for block in range(tensors):
        for head in range(heads):
            row = (block * heads + head) * size
            for rank in range(2):
                sent[(2 * head + rank) * tensors + block] = back[
                    row : row + size, rank * half : (rank + 1) * half
                ]
    sums[...] = as_rows(
        [jnp.sum(values, 1, keepdims=True) for values in (total * normed[...], total, result)]
    )


def leave(spot, terms, normed, inverse, grads, weight, columns, heads, size):
    width, count = normed.shape
    blocks = width // size
    return pl.pallas_call(
        functools.partial(leave_kernel, heads=heads),
        out_shape=(
            jax.ShapeDtypeStruct((width, count), F32),
            jax.ShapeDtypeStruct((width, count), BF16),
            jax.ShapeDtypeStruct((8, width), F32),
            jax.ShapeDtypeStruct((2 * blocks, size, count // 2), BF16),
        ),
        in_specs=[SM] + [VM] * 9,
        out_specs=(VM,) * 4,
        compiler_params=pltpu.CompilerParams(vmem_limit_bytes=12 * 2**20),
        name="leave",
    )(spot, *terms, normed, inverse, grads, weight, columns)


def rest_kernel(spot, flat, full, out, mine, other):
    width = full.shape[0]
    split = mine.shape[0]
    step = min(256, width)
    for start in range(0, width, step):
        tile = slice(start, start + step)
        result = contract(flat[...], full[tile], 1, 1).astype(BF16)
        first = result[:split]
        second = jnp.concatenate([result[split:], out[:, tile]], 0)

        @pl.when(spot[1] == 0)
        def _():
            mine[:, tile] = first
            other[:, tile] = second

        @pl.when(spot[1] == 1)
        def _():
            mine[:, tile] = second
            other[:, tile] = first


def rest_halves(spot, flat, full, out):
    half = (flat.shape[0] + out.shape[0]) // 2
    return pl.pallas_call(
        rest_kernel,
        out_shape=(jax.ShapeDtypeStruct((half, full.shape[0]), BF16),) * 2,
        in_specs=[SM] + [VM] * 3,
        out_specs=(VM, VM),
        compiler_params=pltpu.CompilerParams(vmem_limit_bytes=8 * 2**20),
        cost_estimate=pl.CostEstimate(
            flops=2 * flat.shape[0] * full.size, bytes_accessed=2**23, transcendentals=0
        ),
        name="rest_halves",
    )(spot, flat, full, out)


def rest_whole_kernel(spot, half, other, mixed, out, *, chips):
    step = half.shape[0] // chips
    edge = mixed.shape[0] // step
    for piece in range(chips):
        owner = lax.rem(spot[2] + chips - piece, chips)
        rows = slice(piece * step, (piece + 1) * step)
        for source, core in ((half, spot[1]), (other, 1 - spot[1])):
            block = core * chips + owner
            values = source[rows].astype(F32)

            @pl.when(block < edge)
            def _():
                mixed[pl.ds(pl.multiple_of(jnp.minimum(block, edge - 1) * step, step), step)] = values

            @pl.when(block >= edge)
            def _():
                out[pl.ds(pl.multiple_of(jnp.maximum(block - edge, 0) * step, step), step)] = values


def rest_whole(spot, half, other, rows, chips):
    width = half.shape[1]
    return pl.pallas_call(
        functools.partial(rest_whole_kernel, chips=chips),
        out_shape=(
            jax.ShapeDtypeStruct((rows, width), F32),
            jax.ShapeDtypeStruct((2 * half.shape[0] - rows, width), F32),
        ),
        in_specs=[SM, VM, VM],
        out_specs=(VM, VM),
        compiler_params=pltpu.CompilerParams(vmem_limit_bytes=8 * 2**20),
        name="rest_whole",
    )(spot, half, other)


def prefix_kernel(
    total, hidden, embed, weight, low, grad_embed, grad_weight, grad_bias, grad_out, grad_out_bias
):
    pre = total[...] * (1.0 - hidden[...] * hidden[...])
    grad_bias[...] = jnp.sum(pre, 0, keepdims=True)

    def exact(first, second, dims):
        return lax.dot_general(
            first, second, ((dims[:1], dims[1:]), ((), ())),
            preferred_element_type=F32, precision=HIGHEST,
        )

    grad_weight[...] = exact(embed[...].astype(F32), pre, (0, 0))
    grad_embed[...] = exact(pre, weight[...].astype(F32), (1, 1))
    wide = low[...].astype(F32)
    result = exact(hidden[...], wide, (0, 0))
    sums = jnp.sum(wide, 0, keepdims=True)
    each = grad_out.shape[2]
    for head in range(grad_out.shape[1]):
        lanes = slice(head * each, (head + 1) * each)
        grad_out[:, head, :] = result[:, lanes]
        grad_out_bias[head : head + 1] = sums[:, lanes]


def prefix_back(total, hidden, embed, weight, low, heads):
    rows, width = embed.shape
    extra = PAD - rows
    hidden = jnp.pad(hidden, ((0, extra), (0, 0)))
    embed = jnp.pad(embed, ((0, extra), (0, 0)))
    inner = weight.shape[1]
    each = low.shape[1] // heads
    grad_embed, grad_weight, grad_bias, grad_out, grad_out_bias = pl.pallas_call(
        prefix_kernel,
        out_shape=(
            jax.ShapeDtypeStruct((PAD, width), F32),
            jax.ShapeDtypeStruct(weight.shape, F32),
            jax.ShapeDtypeStruct((1, inner), F32),
            jax.ShapeDtypeStruct((inner, heads, each), F32),
            jax.ShapeDtypeStruct((heads, each), F32),
        ),
        in_specs=[VM] * 5,
        out_specs=(VM,) * 5,
        compiler_params=pltpu.CompilerParams(vmem_limit_bytes=16 * 2**20),
        cost_estimate=pl.CostEstimate(flops=2**31, bytes_accessed=2**22, transcendentals=0),
        name="prefix_back",
    )(total, hidden, embed, weight, low)
    return grad_embed[:rows], grad_weight, grad_bias[0], grad_out, grad_out_bias


def spread(values, axis):
    count = lax.axis_size(axis)
    copies = jnp.broadcast_to(values[None], (count,) + values.shape)
    return lax.all_to_all(copies, axis, 0, 0, tiled=True)


def small_sum(values, axis):
    return jnp.sum(spread(values, axis), 0)


def ring(axis, by):
    count = lax.axis_size(axis)
    return [(source, (source + by) % count) for source in range(count)]


def ring_gather(values, axis, beside=()):
    count, place = lax.axis_size(axis), lax.axis_index(axis)
    half = values.shape[0] // 2
    up, down = values[:half], values[half:]
    out = jnp.zeros((count,) + values.shape, values.dtype)
    out = lax.dynamic_update_slice_in_dim(out, values[None], place, 0)
    zeros = (0,) * (values.ndim - 1)
    results = []
    for step in range(1, count):
        up = lax.ppermute(up, axis, ring(axis, 1))
        down = lax.ppermute(down, axis, ring(axis, -1))
        if step <= len(beside) and beside[step - 1]:
            up, down, result = lax.optimization_barrier((up, down, beside[step - 1]()))
            results.append(result)
        out = lax.dynamic_update_slice(out, up[None], ((place - step) % count, 0) + zeros)
        out = lax.dynamic_update_slice(out, down[None], ((place + step) % count, half) + zeros)
    return (out, results) if beside else out


def ring_terms(own, axis, beside=(), first=None):
    count = lax.axis_size(axis)
    up, down = first or (own(1, False), own(1, True))
    state = None
    for step in range(1, count):
        up = lax.ppermute(up, axis, ring(axis, 1))
        down = lax.ppermute(down, axis, ring(axis, -1))
        if step <= len(beside):
            state = beside[step - 1](state)
            up, down, state = lax.optimization_barrier((up, down, state))
        if step < count - 1:
            up = (up.astype(F32) + own(step + 1, False).astype(F32)).astype(BF16)
            down = (down.astype(F32) + own(step + 1, True).astype(F32)).astype(BF16)
    for other in beside[count - 1 :]:
        state = other(state)
    return (up, down, own(0, False), own(0, True)), state


def one_way_terms(own, axis, beside, first):
    count = lax.axis_size(axis)
    moving, state = first, None
    for step in range(1, count):
        moving = lax.ppermute(moving, axis, ring(axis, 1))
        if step <= len(beside):
            state = beside[step - 1](state)
            moving, state = lax.optimization_barrier((moving, state))
        if step < count - 1:
            moving = (moving.astype(F32) + own(step + 1).astype(F32)).astype(BF16)
    return (moving, own(0)), state


def swapped(values):
    pairs = [(source, source ^ 1) for source in range(lax.axis_size("seq"))]
    return lax.ppermute(values, "seq", pairs)


def chip_parts(half):
    count = lax.axis_size("seq")
    chips = count // 2
    chip = lax.axis_index("seq") // 2
    blocks = half.reshape(chips, half.shape[0] // chips, half.shape[1])
    total = lax.dynamic_index_in_dim(blocks, chip, 0, keepdims=False)
    parts = [total]
    for step in range(1, chips):
        block = lax.dynamic_index_in_dim(blocks, (chip + step) % chips, 0, keepdims=False)
        parts.append(lax.ppermute(block, "seq", ring("seq", 2 * step)))
    return parts


def chip_gather(parts):
    part = sum(part.astype(F32) for part in parts).astype(BF16)
    behind = [lax.ppermute(part, "seq", ring("seq", 2 * step)) for step in range(1, len(parts))]
    return jnp.concatenate([part] + behind, 0)


def spread_direct(values, axis):
    count, place = lax.axis_size(axis), lax.axis_index(axis)
    out = jnp.zeros((count,) + values.shape, values.dtype)
    out = lax.dynamic_update_slice_in_dim(out, values[None], place, 0)
    for step in range(1, count):
        came = lax.ppermute(values, axis, ring(axis, step))
        out = lax.dynamic_update_slice_in_dim(out, came[None], (place - step) % count, 0)
    return out


def core_gather(half):
    core, chip = lax.axis_index("seq") % 2, lax.axis_index("seq") // 2
    chips = lax.axis_size("seq") // 2
    order = (chip - jnp.arange(chips)) % chips

    def sorted_parts(values):
        parts = values.reshape(chips, -1, values.shape[1])
        picked = [lax.dynamic_index_in_dim(parts, order[n], 0) for n in range(chips)]
        return jnp.concatenate(picked, 0).reshape(values.shape)

    half, other = sorted_parts(half), sorted_parts(swapped(half))
    first = jnp.where(core == 0, half, other)
    second = jnp.where(core == 0, other, half)
    return jnp.concatenate([first, second], 0)


def regrouped(values, width):
    count, size, columns = values.shape
    if width == columns:
        return values
    if width > columns:
        merged = values.reshape(-1, width // columns, size, columns).transpose(0, 2, 1, 3)
        return merged.reshape(-1, size, width)
    cut = values.reshape(count, size, columns // width, width).transpose(0, 2, 1, 3)
    return cut.reshape(-1, size, width)


def group_gather(pieces, group):
    if group == 2:
        rank = lax.axis_index("seq") % 2
        other = swapped(pieces)
        return jnp.stack([jnp.where(rank == 0, pieces, other), jnp.where(rank == 0, other, pieces)])
    count = lax.axis_size("seq")
    groups = [[first + i for i in range(group)] for first in range(0, count, group)]
    return lax.all_gather(pieces, "seq", axis_index_groups=groups)


def on_device(
    tokens,
    segment_ids,
    out_grad,
    ln1_gain,
    ln1_bias,
    w_qkv,
    b_qv,
    w_out,
    b_out,
    ln2_gain,
    ln2_bias,
    w_up,
    b_up,
    w_down,
    b_down,
    prefix_embed,
    reparam_in,
    reparam_in_bias,
    reparam_out,
    reparam_out_bias,
):
    rows, features = tokens.shape
    heads = w_qkv.shape[1]
    size = w_qkv.shape[2] // 3
    inner = w_up.shape[1]
    seqs, tensors = lax.axis_size("seq"), lax.axis_size("tensor")
    width = features * tensors
    own_rows = rows // tensors
    group = seqs // heads
    chunk = own_rows // group
    place, slot = lax.axis_index("seq"), lax.axis_index("tensor")
    head, rank = place // group, place % group
    prefix = prefix_embed.shape[0]
    tokens_head = rows // group
    query_width = max(tokens_head, LANES)
    forward_tile = min(512, query_width)
    backward_tile = min(512, query_width)
    forward_keys, backward_keys = 1024, 1024
    both = ("seq", "tensor")
    paired = group == 2 and chunk == LANES

    own_tokens, own_grads = turned(tokens, out_grad)
    numbers = jnp.arange(1, DOCS, dtype=jnp.int32)

    def document_starts():
        before = jnp.sum((segment_ids[None, :] < numbers[:, None]).astype(jnp.int32), 1)
        return spread(jnp.broadcast_to(before[:, None], (DOCS - 1, LANES)), "seq")

    def whole_vectors():
        return spread(
            jnp.stack([ln1_gain, ln1_bias, ln2_gain, ln2_bias, b_out, b_down]), "tensor"
        )

    full_tokens, (vectors, starts) = ring_gather(
        own_tokens, "tensor", (None, whole_vectors, document_starts)
    )
    full_tokens = full_tokens.reshape(width, rows)
    meta = jnp.concatenate([jnp.sum(starts, 0)[:, 0], rank[None].astype(jnp.int32)])
    columns = vectors.transpose(0, 2, 1).reshape(width, 6).astype(F32)
    out_share = w_out.reshape(seqs, heads * size // seqs, width)
    out_share = lax.dynamic_index_in_dim(out_share, place, 0, keepdims=False)
    core = place % 2
    spot = jnp.stack([slot, core, place // 2]).astype(jnp.int32)

    prefix_hidden = jnp.tanh(
        jnp.dot(prefix_embed, reparam_in, preferred_element_type=F32)
        + reparam_in_bias.astype(F32)
    )
    prefix_pair = jnp.einsum(
        "pa,ahe->phe", prefix_hidden, reparam_out.astype(F32), precision=HIGHEST
    )
    prefix_pair = (prefix_pair + reparam_out_bias.astype(F32)).astype(BF16)
    own_pair = lax.dynamic_index_in_dim(prefix_pair, head, 1, keepdims=False)
    own_pair = jnp.pad(own_pair, ((0, LANES - prefix), (0, 0)))
    pre_key, pre_value = own_pair[:, :size], own_pair[:, size:]

    w_flat = w_qkv.reshape(width, heads * 3 * size)
    bias_pair = b_qv.astype(F32)
    bias_three = jnp.stack(
        [bias_pair[:, :size], jnp.zeros((heads, size), F32), bias_pair[:, size:]], 1
    ).reshape(-1, 1)
    if paired:
        full1, sent, stats = project(
            full_tokens, columns, w_flat.T, bias_three, heads, size, own_rows
        )
    else:
        wide = full_tokens.astype(F32)
        mean = jnp.mean(wide, 0, keepdims=True)
        inverse = lax.rsqrt(jnp.mean((wide - mean) ** 2, 0, keepdims=True) + EPS)
        stats = jnp.concatenate([mean, inverse], 0)
        full1 = ((wide - mean) * inverse * columns[:, 0:1] + columns[:, 1:2]).astype(BF16)
        mixed = (contract(w_flat, full1, 0, 0) + bias_three).astype(BF16)
        mixed = mixed.reshape(heads, 3, size, rows)
        query_part = mixed[:, 0].reshape(heads, size, tensors, group, chunk)
        query_part = query_part.transpose(0, 3, 1, 2, 4).reshape(seqs, size, tokens_head)
        pair_part = mixed[:, 1:].transpose(0, 2, 1, 3).reshape(heads, size, group, 2 * tokens_head)
        pair_part = pair_part.transpose(0, 2, 1, 3).reshape(seqs, size, 2 * tokens_head)
        sent = jnp.concatenate([query_part, pair_part], 2)
    out_share = spread_direct(after(out_share, sent), "tensor")
    came = lax.all_to_all(sent, "seq", 0, 0, tiled=True)
    came, out_share = lax.optimization_barrier((came, out_share))
    w_out_full = lax.all_gather(out_share, "seq")
    w_out_full = w_out_full.transpose(1, 0, 2, 3).reshape(width, width)
    if group == 2:
        query, own, other = came, came, swapped(came)
    else:
        query, pair = came[:, :, :tokens_head], came[:, :, tokens_head:]
        query = regrouped(query, query_width)
        pair = group_gather(pair, group).transpose(1, 2, 0, 3).reshape(seqs, size, 2, rows)
        own, other = pair[:, :, 0], pair[:, :, 1]
    full_grad = lax.all_gather(after(own_grads, full_tokens), "tensor", axis=0, tiled=True)
    out_low, out_full, log_total = attend_forward(
        meta, query, own, other, pre_key.T, pre_value.T,
        forward_tile, forward_keys, prefix, chunk, group, rows, query_width,
    )
    out_low, full_grad, late_up, late_down, late_qkv = lax.optimization_barrier(
        (out_low, full_grad, w_up, w_down, w_qkv)
    )
    late_qkv = late_qkv.transpose(1, 2, 0).reshape(heads * 3 * size, width)
    up_turned, down_turned, late_flat = turned(late_up, late_down, late_qkv)

    came = lax.all_to_all(regrouped(out_low, chunk), both, 0, 0, tiled=True)
    came, up_turned, down_turned, late_flat, w_out_full = lax.optimization_barrier(
        (came, up_turned, down_turned, late_flat, w_out_full)
    )
    if paired:
        attended, middle, normed2, inverse2, ring_up, ring_down = enter(
            spot, came, w_out_full, full_tokens, columns, heads
        )
    else:
        came = came.reshape(heads, group, tensors, size, chunk).transpose(2, 0, 3, 1, 4)
        attended = came.reshape(width, own_rows)
        branch = contract(w_out_full, attended, 0, 0)
        own_block = lax.dynamic_slice_in_dim(full_tokens, slot * own_rows, own_rows, 1)
        middle = own_block.astype(F32) + branch + columns[:, 4:5]
        centered = middle - jnp.mean(middle, 0, keepdims=True)
        inverse2 = lax.rsqrt(jnp.mean(centered * centered, 0, keepdims=True) + EPS)
        normed2 = centered * inverse2
        out2 = (normed2 * columns[:, 2:3] + columns[:, 3:4]).astype(BF16)
        ring_up, ring_down = out2[:, : own_rows // 2], out2[:, own_rows // 2 :]

    bias_up = b_up.astype(F32)[:, None]
    given = given_grads(spot, full_grad, tensors)
    results = []
    for step in range(tensors):
        def block(up=ring_up, down=ring_down, step=step):
            return feed(up, down, given[step], up_turned, w_up, w_down, bias_up)

        if step < tensors - 1:
            ring_up = lax.ppermute(ring_up, "tensor", ring("tensor", 1))
            ring_down = lax.ppermute(ring_down, "tensor", ring("tensor", -1))
            ring_up, ring_down, result = lax.optimization_barrier((ring_up, ring_down, block()))
        else:
            result = block()
        results.append(result)
    blocks, hidden, grad_pre, parts_up, parts_down = zip(*results)

    def weights_here(_):
        return feed_weights(blocks, given, hidden, grad_pre)

    def out_here(state):
        return state, feed_out(spot, hidden, down_turned, middle, columns)

    terms, (weights, mlp_out) = ring_terms(
        lambda step, upper: (parts_down if upper else parts_up)[step],
        "tensor",
        (weights_here, out_here),
    )
    grad_w_down, grad_w_up, grad_b_up = weights
    feed_sums = lax.psum((grad_w_down, grad_w_up), "seq")

    if paired:
        grad_middle, grad_branch, token_sums, sent = leave(
            spot, terms, normed2, inverse2, full_grad, w_out_full, columns, heads, size
        )
    else:
        up, down, own_up, own_down = [a.astype(F32) for a in terms]
        grad_normed2 = jnp.concatenate([up + own_up, down + own_down], 1)
        scaled = grad_normed2 * columns[:, 2:3]
        first = jnp.mean(scaled, 0, keepdims=True)
        second = jnp.mean(scaled * normed2, 0, keepdims=True)
        own_grad = lax.dynamic_slice_in_dim(full_grad, slot * own_rows, own_rows, 1)
        grad_middle = own_grad.astype(F32) + inverse2 * (scaled - first - normed2 * second)
        grad_branch = grad_middle.astype(BF16)
        token_sums = [grad_normed2 * normed2, grad_normed2, grad_middle]
        token_sums = jnp.stack([jnp.sum(a, 1) for a in token_sums], 1)
        sent = contract(w_out_full, grad_branch, 1, 0).astype(BF16)
        sent = sent.reshape(tensors, heads, size, group, chunk).transpose(1, 3, 0, 2, 4)
        sent = sent.reshape(seqs * tensors, size, chunk)
    came = lax.all_to_all(sent, both, 0, 0, tiled=True)
    grad_out = regrouped(came, LANES)

    grad_w_out = contract(attended, grad_branch, 1, 1).astype(BF16)
    grad_out, mlp_out, grad_w_out = lax.optimization_barrier((grad_out, mlp_out, grad_w_out))
    output_act = lax.all_to_all(mlp_out, "tensor", 0, 0, tiled=True)
    grad_w_out = lax.psum_scatter(grad_w_out, "tensor", scatter_dimension=0, tiled=True)

    levels = log_total.reshape(-1, 1, backward_tile)
    grad_query, grad_keep, grad_send, grad_prefix = attend_backward(
        meta, query, own, other, pre_key[:PAD], pre_value[:PAD], grad_out, out_full, levels,
        backward_tile, backward_keys, prefix, chunk, group, rows, query_width,
    )
    if group == 2:
        grad_share = (grad_keep.astype(F32) + swapped(grad_send).astype(F32)).astype(BF16)
    else:
        grad_pair = jnp.stack([grad_keep, grad_send])
        groups = [[first + i for i in range(group)] for first in range(0, seqs, group)]
        shares = grad_pair.transpose(1, 2, 0, 3).reshape(seqs, size, group, 2 * tokens_head)
        grad_share = lax.psum_scatter(
            shares.transpose(2, 0, 1, 3), "seq", axis_index_groups=groups
        )
    prefix_part = grad_prefix.transpose(2, 0, 1).reshape(size, 2 * PAD).astype(BF16)
    prefix_part = jnp.pad(prefix_part, ((0, 0), (0, LANES - 2 * PAD)))
    prefix_part = jnp.broadcast_to(prefix_part[None], (seqs, size, LANES))
    sent = jnp.concatenate([regrouped(grad_query, tokens_head), grad_share, prefix_part], 2)
    sent, output_act, feed_sums = lax.optimization_barrier((sent, output_act, feed_sums))
    came = lax.all_to_all(sent, "seq", 0, 0, tiled=True)
    output_act = jnp.sum(output_act.astype(F32), 0).astype(BF16)
    output_act = output_act.transpose(0, 2, 1).reshape(rows, features)
    out_w_down = feed_sums[0].astype(F32)
    out_w_up = (feed_sums[1] if inner == width else feed_sums[1].T).astype(F32)
    came, output_act, grad_w_out, out_w_down, out_w_up = lax.optimization_barrier(
        (came, output_act, grad_w_out, out_w_down, out_w_up)
    )
    if paired:
        grad_flat, grad_part, first_block, head_row, prefix_low, small = unproject(
            spot, came, late_flat, full_tokens, stats, columns, grad_middle, token_sums,
            reparam_out, heads, size, own_rows,
        )
        mine, other = rest_halves(spot, grad_flat, full1, grad_w_out)
    else:
        query_part = came[:, :, :tokens_head].reshape(heads, group, size, tensors, chunk)
        query_part = query_part.transpose(0, 2, 3, 1, 4).reshape(heads, 1, size, rows)
        pair_part = came[:, :, tokens_head : 3 * tokens_head]
        pair_part = pair_part.reshape(heads, group, size, 2 * tokens_head).transpose(0, 2, 1, 3)
        pair_part = pair_part.reshape(heads, size, 2, rows).transpose(0, 2, 1, 3)
        grad_flat = jnp.concatenate([query_part, pair_part], 1).reshape(heads * 3 * size, rows)
        back = contract(late_flat, grad_flat, 1, 0)
        normed1 = (full_tokens.astype(F32) - stats[0]) * stats[1]
        scaled = back * columns[:, 0:1]
        row_sums = jnp.stack([jnp.sum(scaled, 0), jnp.sum(scaled * normed1, 0)])
        sums1 = jnp.stack([jnp.sum(back * normed1, 1), jnp.sum(back, 1)], 1)
        head_sums = jnp.sum(grad_flat.astype(F32), 1)
        own_inverse = lax.dynamic_slice_in_dim(stats[1:2], slot * own_rows, own_rows, 1)
        own_part = lax.dynamic_slice_in_dim(back, slot * own_rows, own_rows, 1)
        own_part = own_part + grad_middle / (own_inverse * columns[:, 0:1])
        back = lax.dynamic_update_slice_in_dim(back, own_part, slot * own_rows, 1)
        grad_part = back.astype(BF16)
        below = (slot - 1) % tensors * features
        first_block = lax.dynamic_slice_in_dim(grad_part, below, features, 0)
        grad_w_qkv = contract(grad_flat, full1, 1, 1).astype(BF16)
        rest = jnp.concatenate([grad_w_qkv, grad_w_out], 0)
        halves = rest.reshape(2, rest.shape[0] // 2, width)
        mine = lax.dynamic_index_in_dim(halves, core, 0, keepdims=False)
        other = lax.dynamic_index_in_dim(halves, 1 - core, 0, keepdims=False)

    if not paired:
        prefix_low = came[:, :, 3 * tokens_head : 3 * tokens_head + 2 * PAD].astype(F32)
        prefix_low = jnp.sum(prefix_low.reshape(heads, group, size, 2, PAD), 1)
        prefix_low = prefix_low.transpose(3, 0, 2, 1).reshape(PAD, -1).astype(BF16)
        hidden_part = contract(prefix_low, reparam_out.reshape(reparam_out.shape[0], -1), 1, 1)
        owned = jnp.concatenate([sums1.T, token_sums.T], 0)
        owned = owned.reshape(-1, tensors, features).transpose(1, 0, 2).reshape(tensors, -1)
        shared = jnp.concatenate([row_sums.reshape(-1), hidden_part.reshape(-1)])
        shared = jnp.broadcast_to(shared[None], (tensors, shared.shape[0]))
        small = jnp.concatenate([owned, shared], 1)[:, None, :]

    grad_b_down = jnp.sum(out_grad.astype(F32), 0)

    def halves_here(_):
        return (mine.astype(F32) + swapped(other).astype(F32)).astype(BF16)

    def parts_here(half):
        return chip_parts(half), lax.all_to_all(small, "tensor", 0, 0, tiled=True)

    def totals(parts):
        if paired:
            return small_totals(
                parts, grad_b_down[None], grad_b_up, head_row, rows, prefix_hidden.shape[1], width
            )
        sums = jnp.sum(parts, 0)[0]
        after_rows = 5 * features + 2 * rows
        row_means = sums[5 * features : after_rows].reshape(2, rows) / width
        hidden = sums[after_rows:].reshape(PAD, -1)
        mixed_sums = head_sums.reshape(heads, 3, size)
        late = [sums[: 5 * features], grad_b_down, grad_b_up[0]]
        late += [mixed_sums[:, 0].reshape(-1), mixed_sums[:, 2].reshape(-1)]
        return row_means, hidden, jnp.concatenate(late)[None]

    def gather_here(state):
        row_means, hidden_grad, late = totals(state[1])
        prefix_grads = prefix_back(
            hidden_grad, prefix_hidden, prefix_embed, reparam_in, prefix_low, heads
        )
        return chip_gather(state[0]), row_means, spread(late, "seq"), prefix_grads

    def own_part(step):
        return lax.dynamic_slice_in_dim(grad_part, (slot - step) % tensors * features, features, 0)

    last_terms, (rest_half, row_means, late, prefix_grads) = one_way_terms(
        own_part,
        "tensor",
        (halves_here, parts_here) + (lambda state: state,) * (tensors - 4) + (gather_here,),
        first_block,
    )
    input_grad = finish(
        *last_terms, own_tokens, ln1_gain.astype(F32)[:, None], stats, row_means,
    )
    mixed_rows = heads * 3 * size
    if paired:
        out_w_qkv, out_w_out = rest_whole(
            spot, rest_half, swapped(rest_half), mixed_rows, seqs // 2
        )
    else:
        rest = core_gather(rest_half).astype(F32)
        out_w_qkv, out_w_out = rest[:mixed_rows], rest[mixed_rows:]
    out_w_qkv = out_w_qkv.reshape(heads, 3 * size, width).transpose(2, 0, 1)
    out_w_out = out_w_out.reshape(heads, size, width)
    if paired:
        vectors, out_b_up, out_b_qv = late_totals(late, inner, heads, size)
        out_b_up = out_b_up[0]
    else:
        late = jnp.sum(late, 0)[0]
        vectors = late[: 6 * features].reshape(6, features)
        out_b_up = late[6 * features : 6 * features + inner]
        pair_sums = late[6 * features + inner :].reshape(2, heads, size)
        out_b_qv = jnp.concatenate([pair_sums[0], pair_sums[1]], 1)
    out_ln1_gain, out_ln1_bias, out_ln2_gain, out_ln2_bias, out_b_out, out_b_down = [
        vectors[i] for i in range(6)
    ]

    return (
        output_act,
        input_grad,
        out_ln1_gain,
        out_ln1_bias,
        out_w_qkv,
        out_b_qv,
        out_w_out,
        out_b_out,
        out_ln2_gain,
        out_ln2_bias,
        out_w_up,
        out_b_up,
        out_w_down,
        out_b_down,
        *prefix_grads,
    )


def solution(mesh):
    placed = (
        P("seq", "tensor"),
        P("seq"),
        P("seq", "tensor"),
        P("tensor"),
        P("tensor"),
        P(None, "tensor", None),
        P("tensor", None),
        P("tensor", None, None),
        P("tensor"),
        P("tensor"),
        P("tensor"),
        P(None, "tensor"),
        P("tensor"),
        P("tensor", None),
        P("tensor"),
        P(),
        P(),
        P(),
        P(None, "tensor", None),
        P("tensor", None),
    )
    return jax.shard_map(
        on_device,
        mesh=mesh,
        in_specs=placed,
        out_specs=(
            P("seq", "tensor"),
            P("seq", "tensor"),
            P("tensor"),
            P("tensor"),
            P(None, "tensor", None),
            P("tensor", None),
            P("tensor", None, None),
            P("tensor"),
            P("tensor"),
            P("tensor"),
            P(None, "tensor"),
            P("tensor"),
            P("tensor", None),
            P("tensor"),
            P(),
            P(),
            P(),
            P(None, "tensor", None),
            P("tensor", None),
        ),
        check_vma=False,
    )
```

```python
import functools

import jax
import jax.numpy as jnp
from jax import lax
from jax.experimental import pallas as pl
from jax.experimental.pallas import tpu as pltpu
from jax.sharding import PartitionSpec as P

EPS = 1e-05
NEGATIVE = -1e30
HIGHEST = lax.Precision.HIGHEST
F32 = jnp.float32
BF16 = jnp.bfloat16
LANES = 128
PAD = 16
WEAK = 1e-24
DOCS = 5
CLEAR, EARLIER, AMONG = range(3)

VM = pl.BlockSpec(memory_space=pltpu.VMEM)
SM = pl.BlockSpec(memory_space=pltpu.SMEM)


def gelu_tanh(values):
    return jax.nn.gelu(values, approximate=True)


def contract(first, second, first_dim, second_dim):
    return lax.dot_general(
        first, second, (((first_dim,), (second_dim,)), ((), ())), preferred_element_type=F32
    )


def work(queries, keys, products):
    pairs = queries * keys // 2
    return pl.CostEstimate(
        flops=2 * 256 * products * pairs, bytes_accessed=8 * 2**20, transcendentals=pairs
    )


def after(values, other):
    return lax.optimization_barrier((values, other))[0]


def document_start(meta, place):
    found = jnp.zeros_like(place) if getattr(place, "shape", ()) else jnp.int32(0)
    for number in range(DOCS - 1):
        begin = meta[number]
        found = jnp.where(place >= begin, jnp.maximum(found, begin), found)
    return found


def query_places(meta, index, base, chunk, group):
    return base + (index // chunk) * (chunk * group) + meta[DOCS - 1] * chunk + index % chunk


def tile_bounds(meta, base, count, chunk, group):
    rank = meta[DOCS - 1]
    first = base + rank * chunk
    last = base + (count // chunk - 1) * (chunk * group) + rank * chunk + chunk - 1
    return document_start(meta, first), document_start(meta, last)


def one_row(rows, columns):
    return lax.broadcasted_iota(jnp.int32, (rows, columns), 0) == 0


def by_rank(meta, group, first, second, work):
    if group != 2:
        work(first, second)
        return

    @pl.when(meta[DOCS - 1] == 0)
    def _():
        work(first, second)

    @pl.when(meta[DOCS - 1] == 1)
    def _():
        work(second, first)


def over_keys(bounds, base, tile, group, keys, block):
    low, low_last = bounds
    first, last = low // keys, base // keys
    clear = jnp.clip((low_last + keys - 1) // keys, first, jnp.maximum(first, last))

    def masked(number, _):
        block(number * keys, keys, 0, EARLIER)
        return 0

    def pair(number, _):
        block((clear + 2 * number) * keys, 2 * keys, 0, CLEAR)
        return 0

    lax.fori_loop(first, jnp.minimum(clear, last), masked, 0)
    left = jnp.maximum(last - clear, 0)
    lax.fori_loop(0, left // 2, pair, 0)

    @pl.when(left % 2 == 1)
    def _():
        block((last - 1) * keys, keys, 0, CLEAR)

    for stair in range(tile // LANES):
        block(base + stair * LANES * group, LANES * group, stair * LANES, AMONG)


def allowed(meta, start, count, places, kind=AMONG):
    key = start + lax.broadcasted_iota(jnp.int32, (count, 1), 0)
    inside = key >= document_start(meta, places)
    return inside if kind == EARLIER else (key <= places) & inside


def forward_kernel(
    meta, query, own, other, pre_key, pre_value,
    out_low, out_full, log_total,
    key_rows, value_ones, accum, peak, norm,
    *, tile, keys, prefix, chunk, group, length, width,
):
    sources, size, whole = own.shape
    blocks = query.shape[0]
    per = width // tile
    scale = size**-0.5
    padded = pre_key.shape[1]
    kept = slice(whole - length, whole)

    def extended(values, count, total):
        ones = jnp.where(one_row(PAD, count), 1.0, 0.0).astype(BF16)
        rest = total - size - PAD
        tail = [jnp.zeros((rest, count), BF16)] if rest else []
        return jnp.concatenate([values, ones] + tail, 0)

    def longest(values):
        wide = values.astype(F32)
        return jnp.max(jnp.sum(wide * wide, 0, keepdims=True), 1, keepdims=True)

    norm[...] = jnp.broadcast_to(longest(pre_key[...]), norm.shape)

    def fill(key, value):
        def prepare(source, _):
            rows = pl.ds(pl.multiple_of(source * length, length), length)
            found = key[source, :, kept]
            key_rows[rows, :] = extended(found, length, LANES).astype(F32).T.astype(BF16)
            value_ones[:, rows] = extended(value[source, :, kept], length, size + PAD)
            norm[...] = jnp.maximum(norm[...], longest(found))
            return 0

        lax.fori_loop(0, sources, prepare, 0)

    by_rank(meta, group, own, other, fill)
    most = jnp.sqrt(norm[0:1, 0:1])
    pre_key_ones = extended(pre_key[...], padded, LANES)
    pre_value_ones = extended(pre_value[...], padded, size + PAD)
    pre_row = lax.broadcasted_iota(jnp.int32, (padded, tile), 0)

    def query_tile(number, _):
        source, part = number // per, number % per
        base = number * tile * group
        columns = pl.ds(pl.multiple_of(part * tile, tile), tile)
        scaled = query[source, :, columns].astype(F32) * scale
        limit = jnp.sqrt(jnp.sum(scaled * scaled, 0, keepdims=True)) * most
        limit = limit.astype(BF16).astype(F32)
        shifted = jnp.concatenate(
            [
                scaled,
                jnp.where(one_row(PAD, tile), -limit, 0.0),
                jnp.zeros((LANES - size - PAD, tile), F32),
            ],
            0,
        ).astype(BF16)
        index = lax.broadcasted_iota(jnp.int32, (1, tile), 1)
        places = query_places(meta, index, base, chunk, group)
        bounds = tile_bounds(meta, base, tile, chunk, group)

        weights = jnp.where(pre_row < prefix, jnp.exp(contract(pre_key_ones, shifted, 0, 0)), 0.0)
        accum[...] = contract(pre_value_ones, weights.astype(BF16), 1, 0)

        def block(start, count, lane, masked):
            rows = pl.ds(pl.multiple_of(start, LANES), count)
            weights = jnp.exp(contract(key_rows[rows, :], shifted[:, lane:], 1, 0))
            if masked:
                mask = allowed(meta, start, count, places[:, lane:], masked)
                weights = jnp.where(mask, weights, 0.0)
            accum[:, lane:] += contract(value_ones[:, rows], weights.astype(BF16), 1, 0)

        over_keys(bounds, base, tile, group, keys, block)
        peak[...] = limit

        @pl.when(jnp.min(accum[size : size + 1, :]) < WEAK)
        def _():
            plain = scaled.astype(BF16)

            def fold(scores, mask, values):
                scores = jnp.where(mask, scores, NEGATIVE)
                new = jnp.maximum(peak[...], jnp.max(scores, 0, keepdims=True))
                weights = jnp.where(mask, jnp.exp(scores - new), 0.0).astype(BF16)
                accum[...] = accum[...] * jnp.exp(peak[...] - new) + contract(values, weights, 1, 0)
                peak[...] = new

            peak[...] = jnp.full(peak.shape, NEGATIVE, F32)
            accum[...] = jnp.zeros(accum.shape, F32)
            fold(contract(pre_key[...], plain, 0, 0), pre_row < prefix, pre_value_ones)

            def step(number, _):
                rows = pl.ds(pl.multiple_of(number * keys, keys), keys)
                scores = contract(key_rows[rows, :][:, :size], plain, 1, 0)
                mask = allowed(meta, number * keys, keys, places)
                fold(scores, mask, value_ones[:, rows])
                return 0

            lax.fori_loop(bounds[0] // keys, (base + tile * group - 1) // keys + 1, step, 0)

        total = accum[size : size + 1, :]
        result = accum[:size, :] / total
        log_total[number] = peak[...] + jnp.log(total)
        for part in range(tile // LANES):
            piece = result[:, part * LANES : (part + 1) * LANES]
            out_full[number * (tile // LANES) + part] = piece
            out_low[number * (tile // LANES) + part] = piece.astype(BF16)
        return 0

    lax.fori_loop(0, blocks * per, query_tile, 0)


def attend_forward(
    meta, query, own, other, pre_key, pre_value,
    tile, keys, prefix, chunk, group, length, width,
):
    sources, size, _ = own.shape
    count = query.shape[0] * width
    return pl.pallas_call(
        functools.partial(
            forward_kernel, tile=tile, keys=keys, prefix=prefix, chunk=chunk, group=group,
            length=length, width=width,
        ),
        out_shape=(
            jax.ShapeDtypeStruct((count // LANES, size, LANES), BF16),
            jax.ShapeDtypeStruct((count // LANES, size, LANES), F32),
            jax.ShapeDtypeStruct((count // tile, 1, tile), F32),
        ),
        in_specs=[SM] + [VM] * 5,
        out_specs=(VM, VM, VM),
        scratch_shapes=[
            pltpu.VMEM((sources * length, LANES), BF16),
            pltpu.VMEM((size + PAD, sources * length), BF16),
            pltpu.VMEM((size + PAD, tile), F32),
            pltpu.VMEM((1, tile), F32),
            pltpu.VMEM((8, LANES), F32),
        ],
        compiler_params=pltpu.CompilerParams(vmem_limit_bytes=36 * 2**20),
        cost_estimate=work(count, sources * length, 2),
        name="attend_forward",
    )(meta, query, own, other, pre_key, pre_value)


def in_three(values):
    high = values.astype(BF16).astype(F32)
    middle = (values - high).astype(BF16).astype(F32)
    low = values - high - middle
    row = lax.broadcasted_iota(jnp.int32, (PAD, values.shape[1]), 0)
    return jnp.where(row == 0, high, jnp.where(row == 1, middle, jnp.where(row == 2, low, 0.0)))


def backward_kernel(
    meta, query, own, other, pre_key, pre_value, grad_out, out_full, log_total,
    grad_query, grad_keep, grad_send, grad_prefix,
    key_rows, value_rows, key_columns, sums, query_sum,
    *, tile, keys, prefix, chunk, group, length, width,
):
    sources, size, whole = own.shape
    blocks = query.shape[0]
    kept = slice(whole - length, whole)
    per = width // tile
    scale = size**-0.5
    count = tile // LANES
    rank = meta[DOCS - 1]

    def extended(values):
        ones = jnp.where(
            lax.broadcasted_iota(jnp.int32, (LANES - size, values.shape[1]), 0) < 3, 1.0, 0.0
        )
        return jnp.concatenate([values.astype(F32), ones], 0)

    def fill(key, value):
        def prepare(source, _):
            rows = pl.ds(pl.multiple_of(source * length, length), length)
            found = key[source, :, kept]
            key_rows[rows, :] = extended(found).T.astype(BF16)
            value_rows[rows, :] = extended(value[source, :, kept]).T.astype(BF16)
            key_columns[:, rows] = found
            sums[rows, :] = jnp.zeros((length, LANES), F32)
            return 0

        lax.fori_loop(0, sources, prepare, 0)

    by_rank(meta, group, own, other, fill)
    grad_prefix[...] = jnp.zeros(grad_prefix.shape, F32)
    pre_row = lax.broadcasted_iota(jnp.int32, (pre_key.shape[0], tile), 0)

    def query_tile(number, _):
        source, part = number // per, number % per
        base = number * tile * group
        columns = pl.ds(pl.multiple_of(part * tile, tile), tile)
        scaled = (query[source, :, columns].astype(F32) * scale).astype(BF16)
        pieces = [number * count + piece for piece in range(count)]
        grad = jnp.concatenate([grad_out[piece] for piece in pieces], 1)
        full = jnp.concatenate([out_full[piece] for piece in pieces], 1)
        delta = jnp.sum(grad.astype(F32) * full, 0, keepdims=True)
        level = log_total[number]
        index = lax.broadcasted_iota(jnp.int32, (1, tile), 1)
        places = query_places(meta, index, base, chunk, group)
        bounds = tile_bounds(meta, base, tile, chunk, group)
        rest = jnp.zeros((LANES - size - PAD, tile), BF16)
        scaled_less = jnp.concatenate([scaled, in_three(-level).astype(BF16), rest], 0)
        grad_less = jnp.concatenate([grad, in_three(-delta).astype(BF16), rest], 0)
        none = jnp.zeros((size, tile), BF16)
        pair = jnp.concatenate(
            [jnp.concatenate([grad, none], 1), jnp.concatenate([none, scaled], 1)], 0
        )

        probs = jnp.exp(contract(pre_key[...], scaled, 1, 0) - level)
        probs = jnp.where(pre_row < prefix, probs, 0.0)
        slope = (probs * (contract(pre_value[...], grad, 1, 0) - delta)).astype(BF16)
        grad_prefix[0] += contract(slope, scaled, 1, 1)
        grad_prefix[1] += contract(probs.astype(BF16), grad, 1, 1)
        query_sum[...] = contract(pre_key[...], slope, 0, 0)

        def block(start, count, lane, masked):
            rows = pl.ds(pl.multiple_of(start, LANES), count)
            probs = jnp.exp(contract(key_rows[rows, :], scaled_less[:, lane:], 1, 0))
            if masked:
                mask = allowed(meta, start, count, places[:, lane:], masked)
                probs = jnp.where(mask, probs, 0.0)
            slope = probs * contract(value_rows[rows, :], grad_less[:, lane:], 1, 0)
            slope = slope.astype(BF16)
            both = jnp.concatenate([probs.astype(BF16), slope], 1)
            ends = jnp.concatenate([pair[:, lane:tile], pair[:, tile + lane :]], 1) if lane else pair
            sums[rows, :] += contract(both, ends, 1, 1)
            query_sum[:, lane:] += contract(key_columns[:, rows], slope, 1, 0)

        over_keys(bounds, base, tile, group, keys, block)
        grad_query[source, :, columns] = (query_sum[...] * scale).astype(BF16)
        return 0

    lax.fori_loop(0, blocks * per, query_tile, 0)

    def flush(keys_target, values_target):
        def step(source, _):
            rows = pl.ds(pl.multiple_of(source * length, length), length)
            turned = sums[rows, :].T.astype(BF16)
            values_target[source] = turned[:size]
            keys_target[source] = turned[size:]
            return 0

        lax.fori_loop(0, sources, step, 0)

    if group == 2:

        @pl.when(rank == 0)
        def _():
            flush(grad_keep, grad_send)

        @pl.when(rank == 1)
        def _():
            flush(grad_send, grad_keep)

    else:
        flush(grad_keep, grad_send)


def attend_backward(
    meta, query, own, other, pre_key, pre_value, grad_out, out_full, log_total,
    tile, keys, prefix, chunk, group, length, width,
):
    sources, size, _ = own.shape
    pair = jax.ShapeDtypeStruct((sources, size, length), BF16)
    return pl.pallas_call(
        functools.partial(
            backward_kernel, tile=tile, keys=keys, prefix=prefix, chunk=chunk, group=group,
            length=length, width=width,
        ),
        out_shape=(
            jax.ShapeDtypeStruct((query.shape[0], size, width), BF16),
            pair,
            pair,
            jax.ShapeDtypeStruct((2,) + pre_key.shape, F32),
        ),
        in_specs=[SM] + [VM] * 8,
        out_specs=(VM,) * 4,
        scratch_shapes=[
            pltpu.VMEM((sources * length, LANES), BF16),
            pltpu.VMEM((sources * length, LANES), BF16),
            pltpu.VMEM((size, sources * length), BF16),
            pltpu.VMEM((sources * length, LANES), F32),
            pltpu.VMEM((size, tile), F32),
        ],
        compiler_params=pltpu.CompilerParams(vmem_limit_bytes=44 * 2**20),
        cost_estimate=work(query.shape[0] * width, sources * length, 5),
        name="attend_backward",
    )(meta, query, own, other, pre_key, pre_value, grad_out, out_full, log_total)


def as_rows(columns):
    lane = lax.broadcasted_iota(jnp.int32, (columns[0].shape[0], LANES), 1)
    wide = jnp.zeros(lane.shape, F32)
    for number, column in enumerate(columns):
        wide = jnp.where(lane == number, column, wide)
    return wide.T[:8]


def turn_kernel(*refs):
    count = len(refs) // 2
    for source, target in zip(refs[:count], refs[count:]):
        target[...] = source[...].astype(F32).T.astype(BF16)


def turned(*arrays):
    return pl.pallas_call(
        turn_kernel,
        out_shape=tuple(jax.ShapeDtypeStruct(a.shape[::-1], BF16) for a in arrays),
        in_specs=[VM] * len(arrays),
        out_specs=(VM,) * len(arrays),
        compiler_params=pltpu.CompilerParams(vmem_limit_bytes=8 * 2**20),
        name="turned",
    )(*arrays)


def project_kernel(rows, columns, weight, bias, full, sent, stats, *, heads, size, step):
    length = rows.shape[1]
    pieces = length // step
    half = step // 2
    width = length // 2
    for piece in range(pieces):
        lanes = slice(piece * step, (piece + 1) * step)
        values = rows[:, lanes].astype(F32)
        mean = jnp.mean(values, 0, keepdims=True)
        centered = values - mean
        inverse = lax.rsqrt(jnp.mean(centered * centered, 0, keepdims=True) + EPS)
        stats[0:1, lanes] = mean
        stats[1:2, lanes] = inverse
        low = (centered * inverse * columns[:, 0:1] + columns[:, 1:2]).astype(BF16)
        full[:, lanes] = low
        mixed = (contract(weight[...], low, 1, 0) + bias[...]).astype(BF16)
        for head in range(heads):
            part = mixed[head * 3 * size : (head + 1) * 3 * size]
            spot = slice(piece * half, (piece + 1) * half)
            sent[2 * head, :, spot] = part[:size, :half]
            sent[2 * head + 1, :, spot] = part[:size, half:]
            spot = slice(width + piece * step, width + (piece + 1) * step)
            sent[2 * head, :, spot] = part[size : 2 * size]
            sent[2 * head + 1, :, spot] = part[2 * size :]


def project(rows, columns, weight, bias, heads, size, step):
    width, length = rows.shape
    return pl.pallas_call(
        functools.partial(project_kernel, heads=heads, size=size, step=step),
        out_shape=(
            jax.ShapeDtypeStruct((width, length), BF16),
            jax.ShapeDtypeStruct((2 * heads, size, length // 2 * 3), BF16),
            jax.ShapeDtypeStruct((2, length), F32),
        ),
        in_specs=[VM] * 4,
        out_specs=(VM, VM, VM),
        compiler_params=pltpu.CompilerParams(vmem_limit_bytes=20 * 2**20),
        name="project",
    )(rows, columns, weight, bias)


def unproject_kernel(
    spot, came, weight, rows, stats, columns, own_grad, token_rows, reparam,
    flat, part, first_block, last_block, head_row, prefix_low, small, totals,
    *, heads, size, step,
):
    width, length = rows.shape
    half = step // 2
    past = length // 2
    gain = columns[:, 0:1]
    row_sums = []
    sums = [0.0, 0.0, 0.0]
    for piece in range(length // step):
        lanes = slice(piece * step, (piece + 1) * step)
        place = slice(piece * half, (piece + 1) * half)
        pair = slice(past + piece * step, past + (piece + 1) * step)
        pieces = []
        for head in range(heads):
            first, second = 2 * head, 2 * head + 1
            pieces.append(jnp.concatenate([came[first, :, place], came[second, :, place]], 1))
            pieces += [came[first, :, pair], came[second, :, pair]]
        grads = jnp.concatenate(pieces, 0)
        flat[:, lanes] = grads
        back = contract(weight[...], grads, 1, 0)
        part[:, lanes] = back.astype(BF16)

        @pl.when(spot[0] == piece)
        def _():
            part[:, lanes] = (back + own_grad[...] / (stats[1:2, lanes] * gain)).astype(BF16)

        normed = (rows[:, lanes].astype(F32) - stats[0:1, lanes]) * stats[1:2, lanes]
        scaled = back * gain
        row_sums.append(
            [jnp.sum(values, 0, keepdims=True) for values in (scaled, scaled * normed)]
        )
        for number, values in enumerate((back * normed, back, grads.astype(F32))):
            sums[number] += jnp.sum(values, 1, keepdims=True)
    features = first_block.shape[0]
    blocks = width // features
    for block in range(blocks):

        @pl.when(lax.rem(spot[0] + blocks - 1, blocks) == block)
        def _():
            first_block[...] = part[block * features : (block + 1) * features]

        @pl.when(spot[0] == block)
        def _():
            last_block[...] = part[block * features : (block + 1) * features]

    head_row[...] = as_rows(sums[2:])[:1]
    totals[...] = as_rows(sums[:2])
    found = []
    for head in range(heads):
        both = came[2 * head, :, 3 * past :].astype(F32) + came[2 * head + 1, :, 3 * past :].astype(F32)
        both = both.T
        found += [both[:PAD], both[PAD : 2 * PAD]]
    low = jnp.concatenate(found, 1).astype(BF16)
    prefix_low[...] = low
    each = 2 * size
    hidden = sum(
        contract(low[:, head * each : (head + 1) * each], reparam[:, head, :], 1, 1)
        for head in range(heads)
    )
    for number in range(blocks):
        spread_over = slice(number * features, (number + 1) * features)
        target = small.at[number]
        target[0:2] = totals[0:2, spread_over]
        target[2:5] = token_rows[0:3, spread_over]
        target[5:8] = jnp.zeros((3, features), F32)
        for which in range(2):
            for piece in range(blocks):
                row = 8 + which * blocks + piece
                target[row : row + 1] = row_sums[piece][which]
        for piece in range(hidden.shape[1] // features):
            row = 8 + 2 * blocks + piece * PAD
            target[row : row + PAD] = hidden[:, piece * features : (piece + 1) * features]


def unproject(spot, came, weight, rows, stats, columns, own_grad, token_rows, reparam, heads, size, step):
    width, length = rows.shape
    blocks = length // step
    features = width // blocks
    mixed = 3 * heads * size
    small = 8 + 2 * blocks + reparam.shape[0] // features * PAD
    return pl.pallas_call(
        functools.partial(unproject_kernel, heads=heads, size=size, step=step),
        out_shape=(
            jax.ShapeDtypeStruct((mixed, length), BF16),
            jax.ShapeDtypeStruct((width, length), BF16),
            jax.ShapeDtypeStruct((features, length), BF16),
            jax.ShapeDtypeStruct((features, length), BF16),
            jax.ShapeDtypeStruct((1, mixed), F32),
            jax.ShapeDtypeStruct((PAD, 2 * heads * size), BF16),
            jax.ShapeDtypeStruct((blocks, small, features), F32),
        ),
        in_specs=[SM] + [VM] * 8,
        out_specs=(VM,) * 7,
        scratch_shapes=[pltpu.VMEM((8, width), F32)],
        compiler_params=pltpu.CompilerParams(vmem_limit_bytes=20 * 2**20),
        cost_estimate=pl.CostEstimate(
            flops=4 * mixed * width * length, bytes_accessed=2**23, transcendentals=0
        ),
        name="unproject",
    )(spot, came, weight, rows, stats, columns, own_grad, token_rows, reparam)


def small_kernel(parts, down_row, up_row, head_row, row_sums, hidden, late, *, width):
    blocks = parts.shape[0]
    total = sum(parts[n] for n in range(blocks))
    features = total.shape[1]
    for which in range(2):
        for piece in range(blocks):
            row = 8 + which * blocks + piece
            lanes = slice(piece * features, (piece + 1) * features)
            row_sums[which : which + 1, lanes] = total[row : row + 1] / width
    for piece in range(hidden.shape[1] // features):
        row = 8 + 2 * blocks + piece * PAD
        hidden[:, piece * features : (piece + 1) * features] = total[row : row + PAD]
    late[...] = jnp.zeros(late.shape, F32)
    late[0:5] = total[0:5]
    late[5:6] = down_row[...]
    row = 6
    for source in (up_row, head_row):
        for piece in range(source.shape[1] // features):
            late[row : row + 1] = source[:, piece * features : (piece + 1) * features]
            row += 1


def small_totals(parts, down_row, up_row, head_row, rows, hidden_width, width):
    features = parts.shape[2]
    late = 6 + (up_row.shape[1] + head_row.shape[1]) // features
    return pl.pallas_call(
        functools.partial(small_kernel, width=width),
        out_shape=(
            jax.ShapeDtypeStruct((2, rows), F32),
            jax.ShapeDtypeStruct((PAD, hidden_width), F32),
            jax.ShapeDtypeStruct((-(-late // 8) * 8, features), F32),
        ),
        in_specs=[VM] * 4,
        out_specs=(VM,) * 3,
        compiler_params=pltpu.CompilerParams(vmem_limit_bytes=8 * 2**20),
        name="small_totals",
    )(parts, down_row, up_row, head_row)


def late_kernel(parts, vectors, up, pairs, *, heads, size):
    total = sum(parts[n] for n in range(parts.shape[0]))
    features = total.shape[1]
    vectors[...] = total[:8]
    count = up.shape[1] // features
    up[...] = jnp.concatenate([total[6 + n : 7 + n] for n in range(count)], 1)
    mixed = 3 * heads * size
    row = jnp.concatenate(
        [total[6 + count + n : 7 + count + n] for n in range(mixed // features)], 1
    )
    for head in range(heads):
        start = 3 * size * head
        pairs[head : head + 1] = jnp.concatenate(
            [row[:, start : start + size], row[:, start + 2 * size : start + 3 * size]], 1
        )


def late_totals(parts, inner, heads, size):
    return pl.pallas_call(
        functools.partial(late_kernel, heads=heads, size=size),
        out_shape=(
            jax.ShapeDtypeStruct((8, parts.shape[2]), F32),
            jax.ShapeDtypeStruct((1, inner), F32),
            jax.ShapeDtypeStruct((heads, 2 * size), F32),
        ),
        in_specs=[VM],
        out_specs=(VM,) * 3,
        compiler_params=pltpu.CompilerParams(vmem_limit_bytes=8 * 2**20),
        name="late_totals",
    )(parts)


def finish_kernel(came, own, rows, gain, stats, row_means, grad):
    total = came[...].astype(F32) + own[...].astype(F32)
    normed = (rows[...].astype(F32) - stats[0:1]) * stats[1:2]
    back = gain[...] * total - row_means[0:1] - normed * row_means[1:2]
    grad[...] = (stats[1:2] * back).T.astype(BF16)


def finish(came, own, rows, gain, stats, row_means):
    return pl.pallas_call(
        finish_kernel,
        out_shape=jax.ShapeDtypeStruct(rows.shape[::-1], BF16),
        in_specs=[VM] * 6,
        out_specs=VM,
        compiler_params=pltpu.CompilerParams(vmem_limit_bytes=10 * 2**20),
        name="finish",
    )(came, own, rows, gain, stats, row_means)


def ring_lanes(slot, step, blocks, count):
    half = count // 2
    below = lax.rem(slot + blocks - step, blocks) * count
    above = lax.rem(slot + step, blocks) * count + half
    if half % LANES == 0:
        below, above = pl.multiple_of(below, half), pl.multiple_of(above, half)
    return pl.ds(below, half), pl.ds(above, half)


def feed_kernel(
    rows_up, rows_down, given, up_turned, up, down, bias,
    rows, hidden, grad_pre, part_up, part_down,
):
    half = rows_up.shape[1]
    both = jnp.concatenate([rows_up[...], rows_down[...]], 1)
    rows[...] = both
    pre = contract(up_turned[...], both, 1, 0) + bias[...]
    act, pull = jax.vjp(gelu_tanh, pre)
    hidden[...] = act.astype(BF16)
    low = pull(contract(down[...], given[...], 1, 0))[0].astype(BF16)
    grad_pre[...] = low
    part = contract(up[...], low, 1, 0).astype(BF16)
    part_up[...] = part[:, :half]
    part_down[...] = part[:, half:]


def feed(rows_up, rows_down, given, up_turned, up, down, bias):
    width, half = rows_up.shape
    inner = down.shape[0]
    count = 2 * half
    return pl.pallas_call(
        feed_kernel,
        out_shape=(
            jax.ShapeDtypeStruct((width, count), BF16),
            jax.ShapeDtypeStruct((inner, count), BF16),
            jax.ShapeDtypeStruct((inner, count), BF16),
            jax.ShapeDtypeStruct((width, half), BF16),
            jax.ShapeDtypeStruct((width, half), BF16),
        ),
        in_specs=[VM] * 7,
        out_specs=(VM,) * 5,
        compiler_params=pltpu.CompilerParams(vmem_limit_bytes=12 * 2**20),
        cost_estimate=pl.CostEstimate(
            flops=6 * width * inner * count, bytes_accessed=2**22, transcendentals=0
        ),
        name="feed",
    )(rows_up, rows_down, given, up_turned, up, down, bias)


def given_kernel(spot, grads, *given):
    blocks = len(given)
    count = given[0].shape[1]
    for step, target in enumerate(given):
        lanes = ring_lanes(spot[0], step, blocks, count)
        target[...] = jnp.concatenate([grads[:, spread] for spread in lanes], 1)


def given_grads(spot, grads, blocks):
    width, length = grads.shape
    count = length // blocks
    if count // 2 % LANES:
        found = []
        for step in range(blocks):
            below = (spot[0] - step) % blocks * count
            above = (spot[0] + step) % blocks * count + count // 2
            halves = [lax.dynamic_slice_in_dim(grads, at, count // 2, 1) for at in (below, above)]
            found.append(jnp.concatenate(halves, 1))
        return found
    return pl.pallas_call(
        given_kernel,
        out_shape=(jax.ShapeDtypeStruct((width, count), BF16),) * blocks,
        in_specs=[SM, VM],
        out_specs=(VM,) * blocks,
        compiler_params=pltpu.CompilerParams(vmem_limit_bytes=8 * 2**20),
        name="given_grads",
    )(spot, grads)


def feed_weights_kernel(*refs, blocks, square):
    rows, grads, hidden, grad_pre = [refs[n * blocks : (n + 1) * blocks] for n in range(4)]
    grad_down, grad_up, bias = refs[4 * blocks :]

    def weights(target, first, second):
        step = min(256, second[0].shape[0])
        whole = jnp.concatenate([ref[...] for ref in first], 1)
        for start in range(0, second[0].shape[0], step):
            tile = slice(start, start + step)
            turned = jnp.concatenate([ref[tile] for ref in second], 1)
            target[:, tile] = contract(whole, turned, 1, 1).astype(BF16)

    weights(grad_down, hidden, grads)
    if square:
        weights(grad_up, rows, grad_pre)
    else:
        weights(grad_up, grad_pre, rows)
    total = sum(jnp.sum(ref[...].astype(F32), 1, keepdims=True) for ref in grad_pre)
    bias[...] = as_rows([total])[:1]


def feed_weights(rows, grads, hidden, grad_pre):
    blocks = len(rows)
    width, count = rows[0].shape
    inner = hidden[0].shape[0]
    return pl.pallas_call(
        functools.partial(feed_weights_kernel, blocks=blocks, square=inner == width),
        out_shape=(
            jax.ShapeDtypeStruct((inner, width), BF16),
            jax.ShapeDtypeStruct((inner, width), BF16),
            jax.ShapeDtypeStruct((1, inner), F32),
        ),
        in_specs=[VM] * (4 * blocks),
        out_specs=(VM,) * 3,
        compiler_params=pltpu.CompilerParams(vmem_limit_bytes=14 * 2**20),
        cost_estimate=pl.CostEstimate(
            flops=4 * blocks * width * inner * count, bytes_accessed=2**24, transcendentals=0
        ),
        name="feed_weights",
    )(*rows, *grads, *hidden, *grad_pre)


def feed_out_kernel(spot, *refs, blocks):
    hidden = refs[:blocks]
    down_turned, middle, columns, out = refs[blocks:]
    features, half = out.shape[2:]
    for step, source in enumerate(hidden):
        result = contract(down_turned[...], source[...], 1, 0)
        if step == 0:
            result = result + middle[...] + columns[:, 5:6]
        result = result.astype(BF16)
        below = lax.rem(spot[0] + blocks - step, blocks)
        above = lax.rem(spot[0] + step, blocks)
        for block in range(blocks):
            piece = result[block * features : (block + 1) * features]
            out[block, 2 * below] = piece[:, :half]
            out[block, 2 * above + 1] = piece[:, half:]


def feed_out(spot, hidden, down_turned, middle, columns):
    blocks = len(hidden)
    inner, count = hidden[0].shape
    width = middle.shape[0]
    return pl.pallas_call(
        functools.partial(feed_out_kernel, blocks=blocks),
        out_shape=jax.ShapeDtypeStruct((blocks, 2 * blocks, width // blocks, count // 2), BF16),
        in_specs=[SM] + [VM] * (blocks + 3),
        out_specs=VM,
        compiler_params=pltpu.CompilerParams(vmem_limit_bytes=8 * 2**20),
        cost_estimate=pl.CostEstimate(
            flops=2 * blocks * width * inner * count, bytes_accessed=2**23, transcendentals=0
        ),
        name="feed_out",
    )(spot, *hidden, down_turned, middle, columns)


def enter_kernel(
    came, weight, tokens, columns,
    attended, middle, normed, inverse, low_up, low_down,
    *, heads,
):
    size, half = came.shape[1:]
    count = 2 * half
    tensors = came.shape[0] // (2 * heads)
    for block in range(tensors):
        for head in range(heads):
            row = (block * heads + head) * size
            for rank in range(2):
                attended[row : row + size, rank * half : (rank + 1) * half] = came[
                    (2 * head + rank) * tensors + block
                ]
    branch = contract(attended[...], weight[...], 0, 0).T
    values = tokens[...].astype(F32) + branch + columns[:, 4:5]
    middle[...] = values
    centered = values - jnp.mean(values, 0, keepdims=True)
    scale = lax.rsqrt(jnp.mean(centered * centered, 0, keepdims=True) + EPS)
    inverse[...] = scale
    centered = centered * scale
    normed[...] = centered
    low = (centered * columns[:, 2:3] + columns[:, 3:4]).astype(BF16)
    low_up[...] = low[:, :half]
    low_down[...] = low[:, half:]


def enter(came, weight, tokens, columns, heads):
    width, count = tokens.shape[0], 2 * came.shape[2]
    return pl.pallas_call(
        functools.partial(enter_kernel, heads=heads),
        out_shape=(
            jax.ShapeDtypeStruct((width, count), BF16),
            jax.ShapeDtypeStruct((width, count), F32),
            jax.ShapeDtypeStruct((width, count), F32),
            jax.ShapeDtypeStruct((1, count), F32),
            jax.ShapeDtypeStruct((width, count // 2), BF16),
            jax.ShapeDtypeStruct((width, count // 2), BF16),
        ),
        in_specs=[VM] * 4,
        out_specs=(VM,) * 6,
        compiler_params=pltpu.CompilerParams(vmem_limit_bytes=12 * 2**20),
        name="enter",
    )(came, weight, tokens, columns)


def leave_kernel(
    up, down, own_up, own_down, normed, inverse, grads, weight, columns,
    middle, branch, sums, sent,
    *, heads,
):
    size, half = sent.shape[1:]
    count = 2 * half
    tensors = sent.shape[0] // (2 * heads)
    total = jnp.concatenate(
        [
            up[...].astype(F32) + own_up[...].astype(F32),
            down[...].astype(F32) + own_down[...].astype(F32),
        ],
        1,
    )
    scaled = total * columns[:, 2:3]
    first = jnp.mean(scaled, 0, keepdims=True)
    second = jnp.mean(scaled * normed[...], 0, keepdims=True)
    result = grads[...].astype(F32) + inverse[...] * (
        scaled - first - normed[...] * second
    )
    middle[...] = result
    low = result.astype(BF16)
    branch[...] = low
    back = contract(weight[...], low, 1, 0).astype(BF16)
    for block in range(tensors):
        for head in range(heads):
            row = (block * heads + head) * size
            for rank in range(2):
                sent[(2 * head + rank) * tensors + block] = back[
                    row : row + size, rank * half : (rank + 1) * half
                ]
    sums[...] = as_rows(
        [jnp.sum(values, 1, keepdims=True) for values in (total * normed[...], total, result)]
    )


def leave(terms, normed, inverse, grads, weight, columns, heads, size):
    width, count = normed.shape
    blocks = width // size
    return pl.pallas_call(
        functools.partial(leave_kernel, heads=heads),
        out_shape=(
            jax.ShapeDtypeStruct((width, count), F32),
            jax.ShapeDtypeStruct((width, count), BF16),
            jax.ShapeDtypeStruct((8, width), F32),
            jax.ShapeDtypeStruct((2 * blocks, size, count // 2), BF16),
        ),
        in_specs=[VM] * 9,
        out_specs=(VM,) * 4,
        compiler_params=pltpu.CompilerParams(vmem_limit_bytes=12 * 2**20),
        name="leave",
    )(*terms, normed, inverse, grads, weight, columns)


def rest_kernel(spot, flat, full, out, mine, other):
    width = full.shape[0]
    split = mine.shape[0]
    step = min(256, width)
    for start in range(0, width, step):
        tile = slice(start, start + step)
        result = contract(flat[...], full[tile], 1, 1).astype(BF16)
        first = result[:split]
        second = jnp.concatenate([result[split:], out[:, tile]], 0)

        @pl.when(spot[1] == 0)
        def _():
            mine[:, tile] = first
            other[:, tile] = second

        @pl.when(spot[1] == 1)
        def _():
            mine[:, tile] = second
            other[:, tile] = first


def rest_halves(spot, flat, full, out):
    half = (flat.shape[0] + out.shape[0]) // 2
    return pl.pallas_call(
        rest_kernel,
        out_shape=(jax.ShapeDtypeStruct((half, full.shape[0]), BF16),) * 2,
        in_specs=[SM] + [VM] * 3,
        out_specs=(VM, VM),
        compiler_params=pltpu.CompilerParams(vmem_limit_bytes=8 * 2**20),
        cost_estimate=pl.CostEstimate(
            flops=2 * flat.shape[0] * full.size, bytes_accessed=2**23, transcendentals=0
        ),
        name="rest_halves",
    )(spot, flat, full, out)


def rest_whole_kernel(spot, half, other, mixed, out, *, chips):
    step = half.shape[0] // chips
    edge = mixed.shape[0] // step
    for piece in range(chips):
        owner = lax.rem(spot[2] + chips - piece, chips)
        rows = slice(piece * step, (piece + 1) * step)
        for source, core in ((half, spot[1]), (other, 1 - spot[1])):
            block = core * chips + owner
            values = source[rows].astype(F32)

            @pl.when(block < edge)
            def _():
                mixed[pl.ds(pl.multiple_of(jnp.minimum(block, edge - 1) * step, step), step)] = values

            @pl.when(block >= edge)
            def _():
                out[pl.ds(pl.multiple_of(jnp.maximum(block - edge, 0) * step, step), step)] = values


def rest_whole(spot, half, other, rows, chips):
    width = half.shape[1]
    return pl.pallas_call(
        functools.partial(rest_whole_kernel, chips=chips),
        out_shape=(
            jax.ShapeDtypeStruct((rows, width), F32),
            jax.ShapeDtypeStruct((2 * half.shape[0] - rows, width), F32),
        ),
        in_specs=[SM, VM, VM],
        out_specs=(VM, VM),
        compiler_params=pltpu.CompilerParams(vmem_limit_bytes=8 * 2**20),
        name="rest_whole",
    )(spot, half, other)


def prefix_kernel(
    total, hidden, embed, weight, low, grad_embed, grad_weight, grad_bias, grad_out, grad_out_bias
):
    pre = total[...] * (1.0 - hidden[...] * hidden[...])
    grad_bias[...] = jnp.sum(pre, 0, keepdims=True)

    def exact(first, second, dims):
        return lax.dot_general(
            first, second, ((dims[:1], dims[1:]), ((), ())),
            preferred_element_type=F32, precision=HIGHEST,
        )

    grad_weight[...] = exact(embed[...].astype(F32), pre, (0, 0))
    grad_embed[...] = exact(pre, weight[...].astype(F32), (1, 1))
    wide = low[...].astype(F32)
    result = exact(hidden[...], wide, (0, 0))
    sums = jnp.sum(wide, 0, keepdims=True)
    each = grad_out.shape[2]
    for head in range(grad_out.shape[1]):
        lanes = slice(head * each, (head + 1) * each)
        grad_out[:, head, :] = result[:, lanes]
        grad_out_bias[head : head + 1] = sums[:, lanes]


def prefix_back(total, hidden, embed, weight, low, heads):
    rows, width = embed.shape
    extra = PAD - rows
    hidden = jnp.pad(hidden, ((0, extra), (0, 0)))
    embed = jnp.pad(embed, ((0, extra), (0, 0)))
    inner = weight.shape[1]
    each = low.shape[1] // heads
    grad_embed, grad_weight, grad_bias, grad_out, grad_out_bias = pl.pallas_call(
        prefix_kernel,
        out_shape=(
            jax.ShapeDtypeStruct((PAD, width), F32),
            jax.ShapeDtypeStruct(weight.shape, F32),
            jax.ShapeDtypeStruct((1, inner), F32),
            jax.ShapeDtypeStruct((inner, heads, each), F32),
            jax.ShapeDtypeStruct((heads, each), F32),
        ),
        in_specs=[VM] * 5,
        out_specs=(VM,) * 5,
        compiler_params=pltpu.CompilerParams(vmem_limit_bytes=16 * 2**20),
        cost_estimate=pl.CostEstimate(flops=2**31, bytes_accessed=2**22, transcendentals=0),
        name="prefix_back",
    )(total, hidden, embed, weight, low)
    return grad_embed[:rows], grad_weight, grad_bias[0], grad_out, grad_out_bias


def spread(values, axis):
    count = lax.axis_size(axis)
    copies = jnp.broadcast_to(values[None], (count,) + values.shape)
    return lax.all_to_all(copies, axis, 0, 0, tiled=True)


def small_sum(values, axis):
    return jnp.sum(spread(values, axis), 0)


def ring(axis, by):
    count = lax.axis_size(axis)
    return [(source, (source + by) % count) for source in range(count)]


def ring_gather(values, axis, beside=()):
    count, place = lax.axis_size(axis), lax.axis_index(axis)
    half = values.shape[0] // 2
    up, down = values[:half], values[half:]
    out = jnp.zeros((count,) + values.shape, values.dtype)
    out = lax.dynamic_update_slice_in_dim(out, values[None], place, 0)
    zeros = (0,) * (values.ndim - 1)
    results = []
    for step in range(1, count):
        up = lax.ppermute(up, axis, ring(axis, 1))
        down = lax.ppermute(down, axis, ring(axis, -1))
        if step <= len(beside) and beside[step - 1]:
            up, down, result = lax.optimization_barrier((up, down, beside[step - 1]()))
            results.append(result)
        out = lax.dynamic_update_slice(out, up[None], ((place - step) % count, 0) + zeros)
        out = lax.dynamic_update_slice(out, down[None], ((place + step) % count, half) + zeros)
    return (out, results) if beside else out


def ring_terms(own, axis, beside=(), first=None):
    count = lax.axis_size(axis)
    up, down = first or (own(1, False), own(1, True))
    state = None
    for step in range(1, count):
        up = lax.ppermute(up, axis, ring(axis, 1))
        down = lax.ppermute(down, axis, ring(axis, -1))
        if step <= len(beside):
            state = beside[step - 1](state)
            up, down, state = lax.optimization_barrier((up, down, state))
        if step < count - 1:
            up = (up.astype(F32) + own(step + 1, False).astype(F32)).astype(BF16)
            down = (down.astype(F32) + own(step + 1, True).astype(F32)).astype(BF16)
    for other in beside[count - 1 :]:
        state = other(state)
    return (up, down, own(0, False), own(0, True)), state


def one_way_terms(own, axis, beside, first):
    count = lax.axis_size(axis)
    moving, state = first, None
    for step in range(1, count):
        moving = lax.ppermute(moving, axis, ring(axis, 1))
        if step <= len(beside):
            state = beside[step - 1](state)
            moving, state = lax.optimization_barrier((moving, state))
        if step < count - 1:
            moving = (moving.astype(F32) + own(step + 1).astype(F32)).astype(BF16)
    return moving, state


def swapped(values):
    pairs = [(source, source ^ 1) for source in range(lax.axis_size("seq"))]
    return lax.ppermute(values, "seq", pairs)


def chip_parts(half):
    count = lax.axis_size("seq")
    chips = count // 2
    chip = lax.axis_index("seq") // 2
    blocks = half.reshape(chips, half.shape[0] // chips, half.shape[1])
    total = lax.dynamic_index_in_dim(blocks, chip, 0, keepdims=False)
    parts = [total]
    for step in range(1, chips):
        block = lax.dynamic_index_in_dim(blocks, (chip + step) % chips, 0, keepdims=False)
        parts.append(lax.ppermute(block, "seq", ring("seq", 2 * step)))
    return parts


def chip_gather(parts):
    part = sum(part.astype(F32) for part in parts).astype(BF16)
    behind = [lax.ppermute(part, "seq", ring("seq", 2 * step)) for step in range(1, len(parts))]
    return jnp.concatenate([part] + behind, 0)


def spread_direct(values, axis):
    count, place = lax.axis_size(axis), lax.axis_index(axis)
    out = jnp.zeros((count,) + values.shape, values.dtype)
    out = lax.dynamic_update_slice_in_dim(out, values[None], place, 0)
    for step in range(1, count):
        came = lax.ppermute(values, axis, ring(axis, step))
        out = lax.dynamic_update_slice_in_dim(out, came[None], (place - step) % count, 0)
    return out


def core_gather(half):
    core, chip = lax.axis_index("seq") % 2, lax.axis_index("seq") // 2
    chips = lax.axis_size("seq") // 2
    order = (chip - jnp.arange(chips)) % chips

    def sorted_parts(values):
        parts = values.reshape(chips, -1, values.shape[1])
        picked = [lax.dynamic_index_in_dim(parts, order[n], 0) for n in range(chips)]
        return jnp.concatenate(picked, 0).reshape(values.shape)

    half, other = sorted_parts(half), sorted_parts(swapped(half))
    first = jnp.where(core == 0, half, other)
    second = jnp.where(core == 0, other, half)
    return jnp.concatenate([first, second], 0)


def regrouped(values, width):
    count, size, columns = values.shape
    if width == columns:
        return values
    if width > columns:
        merged = values.reshape(-1, width // columns, size, columns).transpose(0, 2, 1, 3)
        return merged.reshape(-1, size, width)
    cut = values.reshape(count, size, columns // width, width).transpose(0, 2, 1, 3)
    return cut.reshape(-1, size, width)


def group_gather(pieces, group):
    if group == 2:
        rank = lax.axis_index("seq") % 2
        other = swapped(pieces)
        return jnp.stack([jnp.where(rank == 0, pieces, other), jnp.where(rank == 0, other, pieces)])
    count = lax.axis_size("seq")
    groups = [[first + i for i in range(group)] for first in range(0, count, group)]
    return lax.all_gather(pieces, "seq", axis_index_groups=groups)


def on_device(
    tokens,
    segment_ids,
    out_grad,
    ln1_gain,
    ln1_bias,
    w_qkv,
    b_qv,
    w_out,
    b_out,
    ln2_gain,
    ln2_bias,
    w_up,
    b_up,
    w_down,
    b_down,
    prefix_embed,
    reparam_in,
    reparam_in_bias,
    reparam_out,
    reparam_out_bias,
):
    rows, features = tokens.shape
    heads = w_qkv.shape[1]
    size = w_qkv.shape[2] // 3
    inner = w_up.shape[1]
    seqs, tensors = lax.axis_size("seq"), lax.axis_size("tensor")
    width = features * tensors
    own_rows = rows // tensors
    group = seqs // heads
    chunk = own_rows // group
    place, slot = lax.axis_index("seq"), lax.axis_index("tensor")
    head, rank = place // group, place % group
    prefix = prefix_embed.shape[0]
    tokens_head = rows // group
    query_width = max(tokens_head, LANES)
    forward_tile = min(512, query_width)
    backward_tile = min(512, query_width)
    forward_keys, backward_keys = 1024, 1024
    both = ("seq", "tensor")
    paired = group == 2 and chunk == LANES

    own_tokens, own_grads = turned(tokens, out_grad)
    numbers = jnp.arange(1, DOCS, dtype=jnp.int32)

    def document_starts():
        before = jnp.sum((segment_ids[None, :] < numbers[:, None]).astype(jnp.int32), 1)
        return spread(jnp.broadcast_to(before[:, None], (DOCS - 1, LANES)), "seq")

    def whole_vectors():
        return spread(
            jnp.stack([ln1_gain, ln1_bias, ln2_gain, ln2_bias, b_out, b_down]), "tensor"
        )

    def prefix_network():
        prefix_hidden = jnp.tanh(
            jnp.dot(prefix_embed, reparam_in, preferred_element_type=F32)
            + reparam_in_bias.astype(F32)
        )
        prefix_pair = jnp.einsum(
            "pa,ahe->phe", prefix_hidden, reparam_out.astype(F32), precision=HIGHEST
        )
        prefix_pair = (prefix_pair + reparam_out_bias.astype(F32)).astype(BF16)
        own_pair = lax.dynamic_index_in_dim(prefix_pair, head, 1, keepdims=False)
        own_pair = jnp.pad(own_pair, ((0, LANES - prefix), (0, 0)))
        pre_key, pre_value = own_pair[:, :size], own_pair[:, size:]
        return prefix_hidden, pre_key, pre_value

    full_tokens, (vectors, starts) = ring_gather(
        own_tokens, "tensor", (None, whole_vectors, document_starts)
    )
    prefix_hidden, pre_key, pre_value = prefix_network()
    full_tokens = full_tokens.reshape(width, rows)
    meta = jnp.concatenate([jnp.sum(starts, 0)[:, 0], rank[None].astype(jnp.int32)])
    columns = vectors.transpose(0, 2, 1).reshape(width, 6).astype(F32)
    out_share = w_out.reshape(seqs, heads * size // seqs, width)
    out_share = lax.dynamic_index_in_dim(out_share, place, 0, keepdims=False)
    core = place % 2
    spot = jnp.stack([slot, core, place // 2]).astype(jnp.int32)

    w_flat = w_qkv.reshape(width, heads * 3 * size)
    bias_pair = b_qv.astype(F32)
    bias_three = jnp.stack(
        [bias_pair[:, :size], jnp.zeros((heads, size), F32), bias_pair[:, size:]], 1
    ).reshape(-1, 1)
    if paired:
        full1, sent, stats = project(
            full_tokens, columns, w_flat.T, bias_three, heads, size, own_rows
        )
    else:
        wide = full_tokens.astype(F32)
        mean = jnp.mean(wide, 0, keepdims=True)
        inverse = lax.rsqrt(jnp.mean((wide - mean) ** 2, 0, keepdims=True) + EPS)
        stats = jnp.concatenate([mean, inverse], 0)
        full1 = ((wide - mean) * inverse * columns[:, 0:1] + columns[:, 1:2]).astype(BF16)
        mixed = (contract(w_flat, full1, 0, 0) + bias_three).astype(BF16)
        mixed = mixed.reshape(heads, 3, size, rows)
        query_part = mixed[:, 0].reshape(heads, size, tensors, group, chunk)
        query_part = query_part.transpose(0, 3, 1, 2, 4).reshape(seqs, size, tokens_head)
        pair_part = mixed[:, 1:].transpose(0, 2, 1, 3).reshape(heads, size, group, 2 * tokens_head)
        pair_part = pair_part.transpose(0, 2, 1, 3).reshape(seqs, size, 2 * tokens_head)
        sent = jnp.concatenate([query_part, pair_part], 2)
    out_share = spread_direct(after(out_share, sent), "tensor")
    came = lax.all_to_all(sent, "seq", 0, 0, tiled=True)
    came, out_share = lax.optimization_barrier((came, out_share))
    w_out_full = lax.all_gather(out_share, "seq")
    w_out_full = w_out_full.transpose(1, 0, 2, 3).reshape(width, width)
    if group == 2:
        query, own, other = came, came, swapped(came)
    else:
        query, pair = came[:, :, :tokens_head], came[:, :, tokens_head:]
        query = regrouped(query, query_width)
        pair = group_gather(pair, group).transpose(1, 2, 0, 3).reshape(seqs, size, 2, rows)
        own, other = pair[:, :, 0], pair[:, :, 1]
    full_grad = lax.all_gather(after(own_grads, full_tokens), "tensor", axis=0, tiled=True)
    out_low, out_full, log_total = attend_forward(
        meta, query, own, other, pre_key.T, pre_value.T,
        forward_tile, forward_keys, prefix, chunk, group, rows, query_width,
    )
    out_low, full_grad, late_up, late_down, late_qkv, late_tokens = lax.optimization_barrier(
        (out_low, full_grad, w_up, w_down, w_qkv, full_tokens)
    )
    late_qkv = late_qkv.transpose(1, 2, 0).reshape(heads * 3 * size, width)
    up_turned, down_turned, late_flat = turned(late_up, late_down, late_qkv)

    came = lax.all_to_all(regrouped(out_low, chunk), both, 0, 0, tiled=True)
    own_block = lax.dynamic_slice_in_dim(late_tokens, slot * own_rows, own_rows, 1)
    came, up_turned, down_turned, late_flat, w_out_full, own_block = lax.optimization_barrier(
        (came, up_turned, down_turned, late_flat, w_out_full, own_block)
    )
    if paired:
        attended, middle, normed2, inverse2, ring_up, ring_down = enter(
            came, w_out_full, own_block, columns, heads
        )
    else:
        came = came.reshape(heads, group, tensors, size, chunk).transpose(2, 0, 3, 1, 4)
        attended = came.reshape(width, own_rows)
        branch = contract(w_out_full, attended, 0, 0)
        middle = own_block.astype(F32) + branch + columns[:, 4:5]
        centered = middle - jnp.mean(middle, 0, keepdims=True)
        inverse2 = lax.rsqrt(jnp.mean(centered * centered, 0, keepdims=True) + EPS)
        normed2 = centered * inverse2
        out2 = (normed2 * columns[:, 2:3] + columns[:, 3:4]).astype(BF16)
        ring_up, ring_down = out2[:, : own_rows // 2], out2[:, own_rows // 2 :]

    bias_up = b_up.astype(F32)[:, None]
    given = given_grads(spot, full_grad, tensors)
    results = []
    for step in range(tensors):
        def block(up=ring_up, down=ring_down, step=step):
            return feed(up, down, given[step], up_turned, w_up, w_down, bias_up)

        if step < tensors - 1:
            ring_up = lax.ppermute(ring_up, "tensor", ring("tensor", 1))
            ring_down = lax.ppermute(ring_down, "tensor", ring("tensor", -1))
            ring_up, ring_down, result = lax.optimization_barrier((ring_up, ring_down, block()))
        else:
            result = block()
        results.append(result)
    blocks, hidden, grad_pre, parts_up, parts_down = zip(*results)

    def weights_here(_):
        return feed_weights(blocks, given, hidden, grad_pre)

    def out_here(state):
        return state, feed_out(spot, hidden, down_turned, middle, columns)

    terms, (weights, mlp_out) = ring_terms(
        lambda step, upper: (parts_down if upper else parts_up)[step],
        "tensor",
        (weights_here, out_here),
    )
    grad_w_down, grad_w_up, grad_b_up = weights
    feed_sums = lax.psum((grad_w_down, grad_w_up), "seq")

    if paired:
        grad_middle, grad_branch, token_sums, sent = leave(
            terms, normed2, inverse2, given[0], w_out_full, columns, heads, size
        )
    else:
        up, down, own_up, own_down = [a.astype(F32) for a in terms]
        grad_normed2 = jnp.concatenate([up + own_up, down + own_down], 1)
        scaled = grad_normed2 * columns[:, 2:3]
        first = jnp.mean(scaled, 0, keepdims=True)
        second = jnp.mean(scaled * normed2, 0, keepdims=True)
        own_grad = lax.dynamic_slice_in_dim(full_grad, slot * own_rows, own_rows, 1)
        grad_middle = own_grad.astype(F32) + inverse2 * (scaled - first - normed2 * second)
        grad_branch = grad_middle.astype(BF16)
        token_sums = [grad_normed2 * normed2, grad_normed2, grad_middle]
        token_sums = jnp.stack([jnp.sum(a, 1) for a in token_sums], 1)
        sent = contract(w_out_full, grad_branch, 1, 0).astype(BF16)
        sent = sent.reshape(tensors, heads, size, group, chunk).transpose(1, 3, 0, 2, 4)
        sent = sent.reshape(seqs * tensors, size, chunk)
    came = lax.all_to_all(sent, both, 0, 0, tiled=True)
    grad_out = regrouped(came, LANES)

    grad_w_out = contract(attended, grad_branch, 1, 1).astype(BF16)
    grad_out, mlp_out, grad_w_out = lax.optimization_barrier((grad_out, mlp_out, grad_w_out))
    output_act = lax.all_to_all(mlp_out, "tensor", 0, 0, tiled=True)
    grad_w_out = lax.psum_scatter(grad_w_out, "tensor", scatter_dimension=0, tiled=True)

    levels = log_total.reshape(-1, 1, backward_tile)
    grad_query, grad_keep, grad_send, grad_prefix = attend_backward(
        meta, query, own, other, pre_key[:PAD], pre_value[:PAD], grad_out, out_full, levels,
        backward_tile, backward_keys, prefix, chunk, group, rows, query_width,
    )
    if group == 2:
        grad_share = (grad_keep.astype(F32) + swapped(grad_send).astype(F32)).astype(BF16)
    else:
        grad_pair = jnp.stack([grad_keep, grad_send])
        groups = [[first + i for i in range(group)] for first in range(0, seqs, group)]
        shares = grad_pair.transpose(1, 2, 0, 3).reshape(seqs, size, group, 2 * tokens_head)
        grad_share = lax.psum_scatter(
            shares.transpose(2, 0, 1, 3), "seq", axis_index_groups=groups
        )
    prefix_part = grad_prefix.transpose(2, 0, 1).reshape(size, 2 * PAD).astype(BF16)
    prefix_part = jnp.pad(prefix_part, ((0, 0), (0, LANES - 2 * PAD)))
    prefix_part = jnp.broadcast_to(prefix_part[None], (seqs, size, LANES))
    sent = jnp.concatenate([regrouped(grad_query, tokens_head), grad_share, prefix_part], 2)
    sent, output_act, feed_sums = lax.optimization_barrier((sent, output_act, feed_sums))
    came = lax.all_to_all(sent, "seq", 0, 0, tiled=True)
    output_act = jnp.sum(output_act.astype(F32), 0).astype(BF16)
    output_act = output_act.transpose(0, 2, 1).reshape(rows, features)
    out_w_down = feed_sums[0].astype(F32)
    out_w_up = (feed_sums[1] if inner == width else feed_sums[1].T).astype(F32)
    came, output_act, grad_w_out, out_w_down, out_w_up = lax.optimization_barrier(
        (came, output_act, grad_w_out, out_w_down, out_w_up)
    )
    if paired:
        grad_flat, grad_part, first_block, last_block, head_row, prefix_low, small = unproject(
            spot, came, late_flat, full_tokens, stats, columns, grad_middle, token_sums,
            reparam_out, heads, size, own_rows,
        )
        mine, other = rest_halves(spot, grad_flat, full1, grad_w_out)
    else:
        query_part = came[:, :, :tokens_head].reshape(heads, group, size, tensors, chunk)
        query_part = query_part.transpose(0, 2, 3, 1, 4).reshape(heads, 1, size, rows)
        pair_part = came[:, :, tokens_head : 3 * tokens_head]
        pair_part = pair_part.reshape(heads, group, size, 2 * tokens_head).transpose(0, 2, 1, 3)
        pair_part = pair_part.reshape(heads, size, 2, rows).transpose(0, 2, 1, 3)
        grad_flat = jnp.concatenate([query_part, pair_part], 1).reshape(heads * 3 * size, rows)
        back = contract(late_flat, grad_flat, 1, 0)
        normed1 = (full_tokens.astype(F32) - stats[0]) * stats[1]
        scaled = back * columns[:, 0:1]
        row_sums = jnp.stack([jnp.sum(scaled, 0), jnp.sum(scaled * normed1, 0)])
        sums1 = jnp.stack([jnp.sum(back * normed1, 1), jnp.sum(back, 1)], 1)
        head_sums = jnp.sum(grad_flat.astype(F32), 1)
        own_inverse = lax.dynamic_slice_in_dim(stats[1:2], slot * own_rows, own_rows, 1)
        own_part = lax.dynamic_slice_in_dim(back, slot * own_rows, own_rows, 1)
        own_part = own_part + grad_middle / (own_inverse * columns[:, 0:1])
        back = lax.dynamic_update_slice_in_dim(back, own_part, slot * own_rows, 1)
        grad_part = back.astype(BF16)
        below = (slot - 1) % tensors * features
        first_block = lax.dynamic_slice_in_dim(grad_part, below, features, 0)
        last_block = lax.dynamic_slice_in_dim(grad_part, slot * features, features, 0)
        grad_w_qkv = contract(grad_flat, full1, 1, 1).astype(BF16)
        rest = jnp.concatenate([grad_w_qkv, grad_w_out], 0)
        halves = rest.reshape(2, rest.shape[0] // 2, width)
        mine = lax.dynamic_index_in_dim(halves, core, 0, keepdims=False)
        other = lax.dynamic_index_in_dim(halves, 1 - core, 0, keepdims=False)

    if not paired:
        prefix_low = came[:, :, 3 * tokens_head : 3 * tokens_head + 2 * PAD].astype(F32)
        prefix_low = jnp.sum(prefix_low.reshape(heads, group, size, 2, PAD), 1)
        prefix_low = prefix_low.transpose(3, 0, 2, 1).reshape(PAD, -1).astype(BF16)
        hidden_part = contract(prefix_low, reparam_out.reshape(reparam_out.shape[0], -1), 1, 1)
        owned = jnp.concatenate([sums1.T, token_sums.T], 0)
        owned = owned.reshape(-1, tensors, features).transpose(1, 0, 2).reshape(tensors, -1)
        shared = jnp.concatenate([row_sums.reshape(-1), hidden_part.reshape(-1)])
        shared = jnp.broadcast_to(shared[None], (tensors, shared.shape[0]))
        small = jnp.concatenate([owned, shared], 1)[:, None, :]

    grad_b_down = jnp.sum(out_grad.astype(F32), 0)

    def halves_here(_):
        return (mine.astype(F32) + swapped(other).astype(F32)).astype(BF16)

    def parts_here(half):
        return chip_parts(half), lax.all_to_all(small, "tensor", 0, 0, tiled=True)

    def totals(parts):
        if paired:
            return small_totals(
                parts, grad_b_down[None], grad_b_up, head_row, rows, prefix_hidden.shape[1], width
            )
        sums = jnp.sum(parts, 0)[0]
        after_rows = 5 * features + 2 * rows
        row_means = sums[5 * features : after_rows].reshape(2, rows) / width
        hidden = sums[after_rows:].reshape(PAD, -1)
        mixed_sums = head_sums.reshape(heads, 3, size)
        late = [sums[: 5 * features], grad_b_down, grad_b_up[0]]
        late += [mixed_sums[:, 0].reshape(-1), mixed_sums[:, 2].reshape(-1)]
        return row_means, hidden, jnp.concatenate(late)[None]

    def gather_here(state):
        row_means, hidden_grad, late = totals(state[1])
        prefix_grads = prefix_back(
            hidden_grad, prefix_hidden, prefix_embed, reparam_in, prefix_low, heads
        )
        return chip_gather(state[0]), row_means, spread(late, "seq"), prefix_grads

    def own_part(step):
        return lax.dynamic_slice_in_dim(grad_part, (slot - step) % tensors * features, features, 0)

    moved, (rest_half, row_means, late, prefix_grads) = one_way_terms(
        own_part,
        "tensor",
        (halves_here, parts_here) + (lambda state: state,) * (tensors - 4) + (gather_here,),
        first_block,
    )
    input_grad = finish(
        moved, last_block, own_tokens, ln1_gain.astype(F32)[:, None], stats, row_means,
    )
    mixed_rows = heads * 3 * size
    if paired:
        out_w_qkv, out_w_out = rest_whole(
            spot, rest_half, swapped(rest_half), mixed_rows, seqs // 2
        )
    else:
        rest = core_gather(rest_half).astype(F32)
        out_w_qkv, out_w_out = rest[:mixed_rows], rest[mixed_rows:]
    out_w_qkv = out_w_qkv.reshape(heads, 3 * size, width).transpose(2, 0, 1)
    out_w_out = out_w_out.reshape(heads, size, width)
    if paired:
        vectors, out_b_up, out_b_qv = late_totals(late, inner, heads, size)
        out_b_up = out_b_up[0]
    else:
        late = jnp.sum(late, 0)[0]
        vectors = late[: 6 * features].reshape(6, features)
        out_b_up = late[6 * features : 6 * features + inner]
        pair_sums = late[6 * features + inner :].reshape(2, heads, size)
        out_b_qv = jnp.concatenate([pair_sums[0], pair_sums[1]], 1)
    out_ln1_gain, out_ln1_bias, out_ln2_gain, out_ln2_bias, out_b_out, out_b_down = [
        vectors[i] for i in range(6)
    ]

    return (
        output_act,
        input_grad,
        out_ln1_gain,
        out_ln1_bias,
        out_w_qkv,
        out_b_qv,
        out_w_out,
        out_b_out,
        out_ln2_gain,
        out_ln2_bias,
        out_w_up,
        out_b_up,
        out_w_down,
        out_b_down,
        *prefix_grads,
    )


def solution(mesh):
    placed = (
        P("seq", "tensor"),
        P("seq"),
        P("seq", "tensor"),
        P("tensor"),
        P("tensor"),
        P(None, "tensor", None),
        P("tensor", None),
        P("tensor", None, None),
        P("tensor"),
        P("tensor"),
        P("tensor"),
        P(None, "tensor"),
        P("tensor"),
        P("tensor", None),
        P("tensor"),
        P(),
        P(),
        P(),
        P(None, "tensor", None),
        P("tensor", None),
    )
    return jax.shard_map(
        on_device,
        mesh=mesh,
        in_specs=placed,
        out_specs=(
            P("seq", "tensor"),
            P("seq", "tensor"),
            P("tensor"),
            P("tensor"),
            P(None, "tensor", None),
            P("tensor", None),
            P("tensor", None, None),
            P("tensor"),
            P("tensor"),
            P("tensor"),
            P(None, "tensor"),
            P("tensor"),
            P("tensor", None),
            P("tensor"),
            P(),
            P(),
            P(),
            P(None, "tensor", None),
            P("tensor", None),
        ),
        check_vma=False,
    )
```

```python
import functools

import jax
import jax.numpy as jnp
from jax import lax
from jax.experimental import pallas as pl
from jax.experimental.pallas import tpu as pltpu
from jax.sharding import PartitionSpec as P

EPS = 1e-05
NEGATIVE = -1e30
HIGHEST = lax.Precision.HIGHEST
F32 = jnp.float32
BF16 = jnp.bfloat16
LANES = 128
PAD = 16
WEAK = 1e-24
DOCS = 5
CLEAR, EARLIER, AMONG = range(3)

VM = pl.BlockSpec(memory_space=pltpu.VMEM)
SM = pl.BlockSpec(memory_space=pltpu.SMEM)


def gelu_tanh(values):
    return jax.nn.gelu(values, approximate=True)


def contract(first, second, first_dim, second_dim):
    return lax.dot_general(
        first, second, (((first_dim,), (second_dim,)), ((), ())), preferred_element_type=F32
    )


def work(queries, keys, products):
    pairs = queries * keys // 2
    return pl.CostEstimate(
        flops=2 * 256 * products * pairs, bytes_accessed=8 * 2**20, transcendentals=pairs
    )


def after(values, other):
    return lax.optimization_barrier((values, other))[0]


def document_start(meta, place):
    found = jnp.zeros_like(place) if getattr(place, "shape", ()) else jnp.int32(0)
    for number in range(DOCS - 1):
        begin = meta[number]
        found = jnp.where(place >= begin, jnp.maximum(found, begin), found)
    return found


def query_places(meta, index, base, chunk, group):
    return base + (index // chunk) * (chunk * group) + meta[DOCS - 1] * chunk + index % chunk


def tile_bounds(meta, base, count, chunk, group):
    rank = meta[DOCS - 1]
    first = base + rank * chunk
    last = base + (count // chunk - 1) * (chunk * group) + rank * chunk + chunk - 1
    return document_start(meta, first), document_start(meta, last)


def one_row(rows, columns):
    return lax.broadcasted_iota(jnp.int32, (rows, columns), 0) == 0


def by_rank(meta, group, first, second, work):
    if group != 2:
        work(first, second)
        return

    @pl.when(meta[DOCS - 1] == 0)
    def _():
        work(first, second)

    @pl.when(meta[DOCS - 1] == 1)
    def _():
        work(second, first)


def over_keys(bounds, base, tile, group, keys, block):
    low, low_last = bounds
    first, last = low // keys, base // keys
    clear = jnp.clip((low_last + keys - 1) // keys, first, jnp.maximum(first, last))

    def masked(number, _):
        block(number * keys, keys, 0, EARLIER)
        return 0

    def pair(number, _):
        block((clear + 2 * number) * keys, 2 * keys, 0, CLEAR)
        return 0

    lax.fori_loop(first, jnp.minimum(clear, last), masked, 0)
    left = jnp.maximum(last - clear, 0)
    lax.fori_loop(0, left // 2, pair, 0)

    @pl.when(left % 2 == 1)
    def _():
        block((last - 1) * keys, keys, 0, CLEAR)

    for stair in range(tile // LANES):
        block(base + stair * LANES * group, LANES * group, stair * LANES, AMONG)


def allowed(meta, start, count, places, kind=AMONG):
    key = start + lax.broadcasted_iota(jnp.int32, (count, 1), 0)
    inside = key >= document_start(meta, places)
    return inside if kind == EARLIER else (key <= places) & inside


def forward_kernel(
    meta, query, own, other, pre_key, pre_value,
    out_low, out_full, log_total,
    key_rows, value_ones, accum, peak, norm,
    *, tile, keys, prefix, chunk, group, length, width,
):
    sources, size, whole = own.shape
    blocks = query.shape[0]
    per = width // tile
    scale = size**-0.5
    padded = pre_key.shape[1]
    kept = slice(whole - length, whole)

    def extended(values, count, total):
        ones = jnp.where(one_row(PAD, count), 1.0, 0.0).astype(BF16)
        rest = total - size - PAD
        tail = [jnp.zeros((rest, count), BF16)] if rest else []
        return jnp.concatenate([values, ones] + tail, 0)

    def longest(values):
        wide = values.astype(F32)
        return jnp.max(jnp.sum(wide * wide, 0, keepdims=True), 1, keepdims=True)

    norm[...] = jnp.broadcast_to(longest(pre_key[...]), norm.shape)

    def fill(key, value):
        def prepare(source, _):
            rows = pl.ds(pl.multiple_of(source * length, length), length)
            found = key[source, :, kept]
            key_rows[rows, :] = extended(found, length, LANES).astype(F32).T.astype(BF16)
            value_ones[:, rows] = extended(value[source, :, kept], length, size + PAD)
            norm[...] = jnp.maximum(norm[...], longest(found))
            return 0

        lax.fori_loop(0, sources, prepare, 0)

    by_rank(meta, group, own, other, fill)
    most = jnp.sqrt(norm[0:1, 0:1])
    pre_key_ones = extended(pre_key[...], padded, LANES)
    pre_value_ones = extended(pre_value[...], padded, size + PAD)
    pre_row = lax.broadcasted_iota(jnp.int32, (padded, tile), 0)

    def query_tile(number, _):
        source, part = number // per, number % per
        base = number * tile * group
        columns = pl.ds(pl.multiple_of(part * tile, tile), tile)
        scaled = query[source, :, columns].astype(F32) * scale
        limit = jnp.sqrt(jnp.sum(scaled * scaled, 0, keepdims=True)) * most
        limit = limit.astype(BF16).astype(F32)
        shifted = jnp.concatenate(
            [
                scaled,
                jnp.where(one_row(PAD, tile), -limit, 0.0),
                jnp.zeros((LANES - size - PAD, tile), F32),
            ],
            0,
        ).astype(BF16)
        index = lax.broadcasted_iota(jnp.int32, (1, tile), 1)
        places = query_places(meta, index, base, chunk, group)
        bounds = tile_bounds(meta, base, tile, chunk, group)

        weights = jnp.where(pre_row < prefix, jnp.exp(contract(pre_key_ones, shifted, 0, 0)), 0.0)
        accum[...] = contract(pre_value_ones, weights.astype(BF16), 1, 0)

        def block(start, count, lane, masked):
            rows = pl.ds(pl.multiple_of(start, LANES), count)
            weights = jnp.exp(contract(key_rows[rows, :], shifted[:, lane:], 1, 0))
            if masked:
                mask = allowed(meta, start, count, places[:, lane:], masked)
                weights = jnp.where(mask, weights, 0.0)
            accum[:, lane:] += contract(value_ones[:, rows], weights.astype(BF16), 1, 0)

        over_keys(bounds, base, tile, group, keys, block)
        peak[...] = limit

        @pl.when(jnp.min(accum[size : size + 1, :]) < WEAK)
        def _():
            plain = scaled.astype(BF16)

            def fold(scores, mask, values):
                scores = jnp.where(mask, scores, NEGATIVE)
                new = jnp.maximum(peak[...], jnp.max(scores, 0, keepdims=True))
                weights = jnp.where(mask, jnp.exp(scores - new), 0.0).astype(BF16)
                accum[...] = accum[...] * jnp.exp(peak[...] - new) + contract(values, weights, 1, 0)
                peak[...] = new

            peak[...] = jnp.full(peak.shape, NEGATIVE, F32)
            accum[...] = jnp.zeros(accum.shape, F32)
            fold(contract(pre_key[...], plain, 0, 0), pre_row < prefix, pre_value_ones)

            def step(number, _):
                rows = pl.ds(pl.multiple_of(number * keys, keys), keys)
                scores = contract(key_rows[rows, :][:, :size], plain, 1, 0)
                mask = allowed(meta, number * keys, keys, places)
                fold(scores, mask, value_ones[:, rows])
                return 0

            lax.fori_loop(bounds[0] // keys, (base + tile * group - 1) // keys + 1, step, 0)

        total = accum[size : size + 1, :]
        result = accum[:size, :] / total
        log_total[number] = peak[...] + jnp.log(total)
        for part in range(tile // LANES):
            piece = result[:, part * LANES : (part + 1) * LANES]
            out_full[number * (tile // LANES) + part] = piece
            out_low[number * (tile // LANES) + part] = piece.astype(BF16)
        return 0

    lax.fori_loop(0, blocks * per, query_tile, 0)


def attend_forward(
    meta, query, own, other, pre_key, pre_value,
    tile, keys, prefix, chunk, group, length, width,
):
    sources, size, _ = own.shape
    count = query.shape[0] * width
    return pl.pallas_call(
        functools.partial(
            forward_kernel, tile=tile, keys=keys, prefix=prefix, chunk=chunk, group=group,
            length=length, width=width,
        ),
        out_shape=(
            jax.ShapeDtypeStruct((count // LANES, size, LANES), BF16),
            jax.ShapeDtypeStruct((count // LANES, size, LANES), F32),
            jax.ShapeDtypeStruct((count // tile, 1, tile), F32),
        ),
        in_specs=[SM] + [VM] * 5,
        out_specs=(VM, VM, VM),
        scratch_shapes=[
            pltpu.VMEM((sources * length, LANES), BF16),
            pltpu.VMEM((size + PAD, sources * length), BF16),
            pltpu.VMEM((size + PAD, tile), F32),
            pltpu.VMEM((1, tile), F32),
            pltpu.VMEM((8, LANES), F32),
        ],
        compiler_params=pltpu.CompilerParams(vmem_limit_bytes=36 * 2**20),
        cost_estimate=work(count, sources * length, 2),
        name="attend_forward",
    )(meta, query, own, other, pre_key, pre_value)


def in_three(values):
    high = values.astype(BF16).astype(F32)
    middle = (values - high).astype(BF16).astype(F32)
    low = values - high - middle
    row = lax.broadcasted_iota(jnp.int32, (PAD, values.shape[1]), 0)
    return jnp.where(row == 0, high, jnp.where(row == 1, middle, jnp.where(row == 2, low, 0.0)))


def backward_kernel(
    meta, query, own, other, pre_key, pre_value, grad_out, out_full, log_total,
    grad_query, grad_keep, grad_send, grad_prefix,
    key_rows, value_rows, key_columns, sums, query_sum,
    *, tile, keys, prefix, chunk, group, length, width,
):
    sources, size, whole = own.shape
    blocks = query.shape[0]
    kept = slice(whole - length, whole)
    per = width // tile
    scale = size**-0.5
    count = tile // LANES
    rank = meta[DOCS - 1]

    def extended(values):
        ones = jnp.where(
            lax.broadcasted_iota(jnp.int32, (LANES - size, values.shape[1]), 0) < 3, 1.0, 0.0
        )
        return jnp.concatenate([values.astype(F32), ones], 0)

    def fill(key, value):
        def prepare(source, _):
            rows = pl.ds(pl.multiple_of(source * length, length), length)
            found = key[source, :, kept]
            key_rows[rows, :] = extended(found).T.astype(BF16)
            value_rows[rows, :] = extended(value[source, :, kept]).T.astype(BF16)
            key_columns[:, rows] = found
            sums[rows, :] = jnp.zeros((length, LANES), F32)
            return 0

        lax.fori_loop(0, sources, prepare, 0)

    by_rank(meta, group, own, other, fill)
    grad_prefix[...] = jnp.zeros(grad_prefix.shape, F32)
    pre_row = lax.broadcasted_iota(jnp.int32, (pre_key.shape[0], tile), 0)

    def query_tile(number, _):
        source, part = number // per, number % per
        base = number * tile * group
        columns = pl.ds(pl.multiple_of(part * tile, tile), tile)
        scaled = (query[source, :, columns].astype(F32) * scale).astype(BF16)
        pieces = [number * count + piece for piece in range(count)]
        grad = jnp.concatenate([grad_out[piece] for piece in pieces], 1)
        full = jnp.concatenate([out_full[piece] for piece in pieces], 1)
        delta = jnp.sum(grad.astype(F32) * full, 0, keepdims=True)
        level = log_total[number]
        index = lax.broadcasted_iota(jnp.int32, (1, tile), 1)
        places = query_places(meta, index, base, chunk, group)
        bounds = tile_bounds(meta, base, tile, chunk, group)
        rest = jnp.zeros((LANES - size - PAD, tile), BF16)
        scaled_less = jnp.concatenate([scaled, in_three(-level).astype(BF16), rest], 0)
        grad_less = jnp.concatenate([grad, in_three(-delta).astype(BF16), rest], 0)
        none = jnp.zeros((size, tile), BF16)
        pair = jnp.concatenate(
            [jnp.concatenate([grad, none], 1), jnp.concatenate([none, scaled], 1)], 0
        )

        probs = jnp.exp(contract(pre_key[...], scaled, 1, 0) - level)
        probs = jnp.where(pre_row < prefix, probs, 0.0)
        slope = (probs * (contract(pre_value[...], grad, 1, 0) - delta)).astype(BF16)
        grad_prefix[0] += contract(slope, scaled, 1, 1)
        grad_prefix[1] += contract(probs.astype(BF16), grad, 1, 1)
        query_sum[...] = contract(pre_key[...], slope, 0, 0)

        def block(start, count, lane, masked):
            rows = pl.ds(pl.multiple_of(start, LANES), count)
            probs = jnp.exp(contract(key_rows[rows, :], scaled_less[:, lane:], 1, 0))
            if masked:
                mask = allowed(meta, start, count, places[:, lane:], masked)
                probs = jnp.where(mask, probs, 0.0)
            slope = probs * contract(value_rows[rows, :], grad_less[:, lane:], 1, 0)
            slope = slope.astype(BF16)
            both = jnp.concatenate([probs.astype(BF16), slope], 1)
            ends = jnp.concatenate([pair[:, lane:tile], pair[:, tile + lane :]], 1) if lane else pair
            sums[rows, :] += contract(both, ends, 1, 1)
            query_sum[:, lane:] += contract(key_columns[:, rows], slope, 1, 0)

        over_keys(bounds, base, tile, group, keys, block)
        grad_query[source, :, columns] = (query_sum[...] * scale).astype(BF16)
        return 0

    lax.fori_loop(0, blocks * per, query_tile, 0)

    def flush(keys_target, values_target):
        def step(source, _):
            rows = pl.ds(pl.multiple_of(source * length, length), length)
            turned = sums[rows, :].T.astype(BF16)
            values_target[source] = turned[:size]
            keys_target[source] = turned[size:]
            return 0

        lax.fori_loop(0, sources, step, 0)

    if group == 2:

        @pl.when(rank == 0)
        def _():
            flush(grad_keep, grad_send)

        @pl.when(rank == 1)
        def _():
            flush(grad_send, grad_keep)

    else:
        flush(grad_keep, grad_send)


def attend_backward(
    meta, query, own, other, pre_key, pre_value, grad_out, out_full, log_total,
    tile, keys, prefix, chunk, group, length, width,
):
    sources, size, _ = own.shape
    pair = jax.ShapeDtypeStruct((sources, size, length), BF16)
    return pl.pallas_call(
        functools.partial(
            backward_kernel, tile=tile, keys=keys, prefix=prefix, chunk=chunk, group=group,
            length=length, width=width,
        ),
        out_shape=(
            jax.ShapeDtypeStruct((query.shape[0], size, width), BF16),
            pair,
            pair,
            jax.ShapeDtypeStruct((2,) + pre_key.shape, F32),
        ),
        in_specs=[SM] + [VM] * 8,
        out_specs=(VM,) * 4,
        scratch_shapes=[
            pltpu.VMEM((sources * length, LANES), BF16),
            pltpu.VMEM((sources * length, LANES), BF16),
            pltpu.VMEM((size, sources * length), BF16),
            pltpu.VMEM((sources * length, LANES), F32),
            pltpu.VMEM((size, tile), F32),
        ],
        compiler_params=pltpu.CompilerParams(vmem_limit_bytes=44 * 2**20),
        cost_estimate=work(query.shape[0] * width, sources * length, 5),
        name="attend_backward",
    )(meta, query, own, other, pre_key, pre_value, grad_out, out_full, log_total)


def as_rows(columns):
    lane = lax.broadcasted_iota(jnp.int32, (columns[0].shape[0], LANES), 1)
    wide = jnp.zeros(lane.shape, F32)
    for number, column in enumerate(columns):
        wide = jnp.where(lane == number, column, wide)
    return wide.T[:8]


def turn_kernel(*refs):
    count = len(refs) // 2
    for source, target in zip(refs[:count], refs[count:]):
        target[...] = source[...].astype(F32).T.astype(BF16)


def turned(*arrays):
    return pl.pallas_call(
        turn_kernel,
        out_shape=tuple(jax.ShapeDtypeStruct(a.shape[::-1], BF16) for a in arrays),
        in_specs=[VM] * len(arrays),
        out_specs=(VM,) * len(arrays),
        compiler_params=pltpu.CompilerParams(vmem_limit_bytes=8 * 2**20),
        name="turned",
    )(*arrays)


def project_kernel(rows, columns, weight, bias, full, sent, stats, *, heads, size, step):
    length = rows.shape[1]
    pieces = length // step
    half = step // 2
    width = length // 2
    for piece in range(pieces):
        lanes = slice(piece * step, (piece + 1) * step)
        values = rows[:, lanes].astype(F32)
        mean = jnp.mean(values, 0, keepdims=True)
        centered = values - mean
        inverse = lax.rsqrt(jnp.mean(centered * centered, 0, keepdims=True) + EPS)
        stats[0:1, lanes] = mean
        stats[1:2, lanes] = inverse
        low = (centered * inverse * columns[:, 0:1] + columns[:, 1:2]).astype(BF16)
        full[:, lanes] = low
        mixed = (contract(weight[...], low, 1, 0) + bias[...]).astype(BF16)
        for head in range(heads):
            part = mixed[head * 3 * size : (head + 1) * 3 * size]
            spot = slice(piece * half, (piece + 1) * half)
            sent[2 * head, :, spot] = part[:size, :half]
            sent[2 * head + 1, :, spot] = part[:size, half:]
            spot = slice(width + piece * step, width + (piece + 1) * step)
            sent[2 * head, :, spot] = part[size : 2 * size]
            sent[2 * head + 1, :, spot] = part[2 * size :]


def project(rows, columns, weight, bias, heads, size, step):
    width, length = rows.shape
    return pl.pallas_call(
        functools.partial(project_kernel, heads=heads, size=size, step=step),
        out_shape=(
            jax.ShapeDtypeStruct((width, length), BF16),
            jax.ShapeDtypeStruct((2 * heads, size, length // 2 * 3), BF16),
            jax.ShapeDtypeStruct((2, length), F32),
        ),
        in_specs=[VM] * 4,
        out_specs=(VM, VM, VM),
        compiler_params=pltpu.CompilerParams(vmem_limit_bytes=20 * 2**20),
        name="project",
    )(rows, columns, weight, bias)


def unproject_kernel(
    spot, came, weight, rows, stats, columns, own_grad, token_rows, reparam,
    flat, part, first_block, last_block, head_row, prefix_low, small, totals,
    *, heads, size, step,
):
    width, length = rows.shape
    half = step // 2
    past = length // 2
    gain = columns[:, 0:1]
    row_sums = []
    sums = [0.0, 0.0, 0.0]
    for piece in range(length // step):
        lanes = slice(piece * step, (piece + 1) * step)
        place = slice(piece * half, (piece + 1) * half)
        pair = slice(past + piece * step, past + (piece + 1) * step)
        pieces = []
        for head in range(heads):
            first, second = 2 * head, 2 * head + 1
            pieces.append(jnp.concatenate([came[first, :, place], came[second, :, place]], 1))
            pieces += [came[first, :, pair], came[second, :, pair]]
        grads = jnp.concatenate(pieces, 0)
        flat[:, lanes] = grads
        back = contract(weight[...], grads, 1, 0)
        part[:, lanes] = back.astype(BF16)

        @pl.when(spot[0] == piece)
        def _():
            part[:, lanes] = (back + own_grad[...] / (stats[1:2, lanes] * gain)).astype(BF16)

        normed = (rows[:, lanes].astype(F32) - stats[0:1, lanes]) * stats[1:2, lanes]
        scaled = back * gain
        row_sums.append(
            [jnp.sum(values, 0, keepdims=True) for values in (scaled, scaled * normed)]
        )
        for number, values in enumerate((back * normed, back, grads.astype(F32))):
            sums[number] += jnp.sum(values, 1, keepdims=True)
    features = first_block.shape[0]
    blocks = width // features
    for block in range(blocks):

        @pl.when(lax.rem(spot[0] + blocks - 1, blocks) == block)
        def _():
            first_block[...] = part[block * features : (block + 1) * features]

        @pl.when(spot[0] == block)
        def _():
            last_block[...] = part[block * features : (block + 1) * features]

    head_row[...] = as_rows(sums[2:])[:1]
    totals[...] = as_rows(sums[:2])
    found = []
    for head in range(heads):
        both = came[2 * head, :, 3 * past :].astype(F32) + came[2 * head + 1, :, 3 * past :].astype(F32)
        both = both.T
        found += [both[:PAD], both[PAD : 2 * PAD]]
    low = jnp.concatenate(found, 1).astype(BF16)
    prefix_low[...] = low
    each = 2 * size
    hidden = sum(
        contract(low[:, head * each : (head + 1) * each], reparam[:, head, :], 1, 1)
        for head in range(heads)
    )
    for number in range(blocks):
        spread_over = slice(number * features, (number + 1) * features)
        target = small.at[number]
        target[0:2] = totals[0:2, spread_over]
        target[2:5] = token_rows[0:3, spread_over]
        target[5:8] = jnp.zeros((3, features), F32)
        for which in range(2):
            for piece in range(blocks):
                row = 8 + which * blocks + piece
                target[row : row + 1] = row_sums[piece][which]
        for piece in range(hidden.shape[1] // features):
            row = 8 + 2 * blocks + piece * PAD
            target[row : row + PAD] = hidden[:, piece * features : (piece + 1) * features]


def unproject(spot, came, weight, rows, stats, columns, own_grad, token_rows, reparam, heads, size, step):
    width, length = rows.shape
    blocks = length // step
    features = width // blocks
    mixed = 3 * heads * size
    small = 8 + 2 * blocks + reparam.shape[0] // features * PAD
    return pl.pallas_call(
        functools.partial(unproject_kernel, heads=heads, size=size, step=step),
        out_shape=(
            jax.ShapeDtypeStruct((mixed, length), BF16),
            jax.ShapeDtypeStruct((width, length), BF16),
            jax.ShapeDtypeStruct((features, length), BF16),
            jax.ShapeDtypeStruct((features, length), BF16),
            jax.ShapeDtypeStruct((1, mixed), F32),
            jax.ShapeDtypeStruct((PAD, 2 * heads * size), BF16),
            jax.ShapeDtypeStruct((blocks, small, features), F32),
        ),
        in_specs=[SM] + [VM] * 8,
        out_specs=(VM,) * 7,
        scratch_shapes=[pltpu.VMEM((8, width), F32)],
        compiler_params=pltpu.CompilerParams(vmem_limit_bytes=20 * 2**20),
        cost_estimate=pl.CostEstimate(
            flops=4 * mixed * width * length, bytes_accessed=2**23, transcendentals=0
        ),
        name="unproject",
    )(spot, came, weight, rows, stats, columns, own_grad, token_rows, reparam)


def small_kernel(parts, down_row, up_row, head_row, row_sums, hidden, late, *, width):
    blocks = parts.shape[0]
    total = sum(parts[n] for n in range(blocks))
    features = total.shape[1]
    for which in range(2):
        for piece in range(blocks):
            row = 8 + which * blocks + piece
            lanes = slice(piece * features, (piece + 1) * features)
            row_sums[which : which + 1, lanes] = total[row : row + 1] / width
    for piece in range(hidden.shape[1] // features):
        row = 8 + 2 * blocks + piece * PAD
        hidden[:, piece * features : (piece + 1) * features] = total[row : row + PAD]
    late[...] = jnp.zeros(late.shape, F32)
    late[0:5] = total[0:5]
    late[5:6] = down_row[...]
    row = 6
    for source in (up_row, head_row):
        for piece in range(source.shape[1] // features):
            late[row : row + 1] = source[:, piece * features : (piece + 1) * features]
            row += 1


def small_totals(parts, down_row, up_row, head_row, rows, hidden_width, width):
    features = parts.shape[2]
    late = 6 + (up_row.shape[1] + head_row.shape[1]) // features
    return pl.pallas_call(
        functools.partial(small_kernel, width=width),
        out_shape=(
            jax.ShapeDtypeStruct((2, rows), F32),
            jax.ShapeDtypeStruct((PAD, hidden_width), F32),
            jax.ShapeDtypeStruct((-(-late // 8) * 8, features), F32),
        ),
        in_specs=[VM] * 4,
        out_specs=(VM,) * 3,
        compiler_params=pltpu.CompilerParams(vmem_limit_bytes=8 * 2**20),
        name="small_totals",
    )(parts, down_row, up_row, head_row)


def late_kernel(parts, vectors, up, pairs, *, heads, size):
    total = sum(parts[n] for n in range(parts.shape[0]))
    features = total.shape[1]
    vectors[...] = total[:8]
    count = up.shape[1] // features
    up[...] = jnp.concatenate([total[6 + n : 7 + n] for n in range(count)], 1)
    mixed = 3 * heads * size
    row = jnp.concatenate(
        [total[6 + count + n : 7 + count + n] for n in range(mixed // features)], 1
    )
    for head in range(heads):
        start = 3 * size * head
        pairs[head : head + 1] = jnp.concatenate(
            [row[:, start : start + size], row[:, start + 2 * size : start + 3 * size]], 1
        )


def late_totals(parts, inner, heads, size):
    return pl.pallas_call(
        functools.partial(late_kernel, heads=heads, size=size),
        out_shape=(
            jax.ShapeDtypeStruct((8, parts.shape[2]), F32),
            jax.ShapeDtypeStruct((1, inner), F32),
            jax.ShapeDtypeStruct((heads, 2 * size), F32),
        ),
        in_specs=[VM],
        out_specs=(VM,) * 3,
        compiler_params=pltpu.CompilerParams(vmem_limit_bytes=8 * 2**20),
        name="late_totals",
    )(parts)


def finish_kernel(came, own, rows, gain, stats, row_means, grad):
    total = came[...].astype(F32) + own[...].astype(F32)
    normed = (rows[...].astype(F32) - stats[0:1]) * stats[1:2]
    back = gain[...] * total - row_means[0:1] - normed * row_means[1:2]
    grad[...] = (stats[1:2] * back).T.astype(BF16)


def finish(came, own, rows, gain, stats, row_means):
    return pl.pallas_call(
        finish_kernel,
        out_shape=jax.ShapeDtypeStruct(rows.shape[::-1], BF16),
        in_specs=[VM] * 6,
        out_specs=VM,
        compiler_params=pltpu.CompilerParams(vmem_limit_bytes=10 * 2**20),
        name="finish",
    )(came, own, rows, gain, stats, row_means)


def ring_lanes(slot, step, blocks, count):
    half = count // 2
    below = lax.rem(slot + blocks - step, blocks) * count
    above = lax.rem(slot + step, blocks) * count + half
    if half % LANES == 0:
        below, above = pl.multiple_of(below, half), pl.multiple_of(above, half)
    return pl.ds(below, half), pl.ds(above, half)


def feed_kernel(
    rows_up, rows_down, given, up_turned, up, down, bias,
    rows, hidden, grad_pre, part_up, part_down,
):
    half = rows_up.shape[1]
    both = jnp.concatenate([rows_up[...], rows_down[...]], 1)
    rows[...] = both
    pre = contract(up_turned[...], both, 1, 0) + bias[...]
    act, pull = jax.vjp(gelu_tanh, pre)
    hidden[...] = act.astype(BF16)
    low = pull(contract(down[...], given[...], 1, 0))[0].astype(BF16)
    grad_pre[...] = low
    part = contract(up[...], low, 1, 0).astype(BF16)
    part_up[...] = part[:, :half]
    part_down[...] = part[:, half:]


def feed(rows_up, rows_down, given, up_turned, up, down, bias):
    width, half = rows_up.shape
    inner = down.shape[0]
    count = 2 * half
    return pl.pallas_call(
        feed_kernel,
        out_shape=(
            jax.ShapeDtypeStruct((width, count), BF16),
            jax.ShapeDtypeStruct((inner, count), BF16),
            jax.ShapeDtypeStruct((inner, count), BF16),
            jax.ShapeDtypeStruct((width, half), BF16),
            jax.ShapeDtypeStruct((width, half), BF16),
        ),
        in_specs=[VM] * 7,
        out_specs=(VM,) * 5,
        compiler_params=pltpu.CompilerParams(vmem_limit_bytes=12 * 2**20),
        cost_estimate=pl.CostEstimate(
            flops=6 * width * inner * count, bytes_accessed=2**22, transcendentals=0
        ),
        name="feed",
    )(rows_up, rows_down, given, up_turned, up, down, bias)


def given_kernel(spot, grads, *given):
    blocks = len(given)
    count = given[0].shape[1]
    for step, target in enumerate(given):
        lanes = ring_lanes(spot[0], step, blocks, count)
        target[...] = jnp.concatenate([grads[:, spread] for spread in lanes], 1)


def given_grads(spot, grads, blocks):
    width, length = grads.shape
    count = length // blocks
    if count // 2 % LANES:
        found = []
        for step in range(blocks):
            below = (spot[0] - step) % blocks * count
            above = (spot[0] + step) % blocks * count + count // 2
            halves = [lax.dynamic_slice_in_dim(grads, at, count // 2, 1) for at in (below, above)]
            found.append(jnp.concatenate(halves, 1))
        return found
    return pl.pallas_call(
        given_kernel,
        out_shape=(jax.ShapeDtypeStruct((width, count), BF16),) * blocks,
        in_specs=[SM, VM],
        out_specs=(VM,) * blocks,
        compiler_params=pltpu.CompilerParams(vmem_limit_bytes=8 * 2**20),
        name="given_grads",
    )(spot, grads)


def feed_weights_kernel(*refs, blocks, square):
    rows, grads, hidden, grad_pre = [refs[n * blocks : (n + 1) * blocks] for n in range(4)]
    grad_down, grad_up, bias = refs[4 * blocks :]

    def weights(target, first, second):
        step = min(256, second[0].shape[0])
        whole = jnp.concatenate([ref[...] for ref in first], 1)
        for start in range(0, second[0].shape[0], step):
            tile = slice(start, start + step)
            turned = jnp.concatenate([ref[tile] for ref in second], 1)
            target[:, tile] = contract(whole, turned, 1, 1).astype(BF16)

    weights(grad_down, hidden, grads)
    if square:
        weights(grad_up, rows, grad_pre)
    else:
        weights(grad_up, grad_pre, rows)
    total = sum(jnp.sum(ref[...].astype(F32), 1, keepdims=True) for ref in grad_pre)
    bias[...] = as_rows([total])[:1]


def feed_weights(rows, grads, hidden, grad_pre):
    blocks = len(rows)
    width, count = rows[0].shape
    inner = hidden[0].shape[0]
    return pl.pallas_call(
        functools.partial(feed_weights_kernel, blocks=blocks, square=inner == width),
        out_shape=(
            jax.ShapeDtypeStruct((inner, width), BF16),
            jax.ShapeDtypeStruct((inner, width), BF16),
            jax.ShapeDtypeStruct((1, inner), F32),
        ),
        in_specs=[VM] * (4 * blocks),
        out_specs=(VM,) * 3,
        compiler_params=pltpu.CompilerParams(vmem_limit_bytes=14 * 2**20),
        cost_estimate=pl.CostEstimate(
            flops=4 * blocks * width * inner * count, bytes_accessed=2**24, transcendentals=0
        ),
        name="feed_weights",
    )(*rows, *grads, *hidden, *grad_pre)


def feed_out_kernel(spot, *refs, blocks):
    hidden = refs[:blocks]
    down_turned, middle, columns, out = refs[blocks:]
    features, half = out.shape[2:]
    for step, source in enumerate(hidden):
        result = contract(down_turned[...], source[...], 1, 0)
        if step == 0:
            result = result + middle[...] + columns[:, 5:6]
        result = result.astype(BF16)
        below = lax.rem(spot[0] + blocks - step, blocks)
        above = lax.rem(spot[0] + step, blocks)
        for block in range(blocks):
            piece = result[block * features : (block + 1) * features]
            out[block, 2 * below] = piece[:, :half]
            out[block, 2 * above + 1] = piece[:, half:]


def feed_out(spot, hidden, down_turned, middle, columns):
    blocks = len(hidden)
    inner, count = hidden[0].shape
    width = middle.shape[0]
    return pl.pallas_call(
        functools.partial(feed_out_kernel, blocks=blocks),
        out_shape=jax.ShapeDtypeStruct((blocks, 2 * blocks, width // blocks, count // 2), BF16),
        in_specs=[SM] + [VM] * (blocks + 3),
        out_specs=VM,
        compiler_params=pltpu.CompilerParams(vmem_limit_bytes=8 * 2**20),
        cost_estimate=pl.CostEstimate(
            flops=2 * blocks * width * inner * count, bytes_accessed=2**23, transcendentals=0
        ),
        name="feed_out",
    )(spot, *hidden, down_turned, middle, columns)


def enter_kernel(
    came, weight, tokens, columns,
    attended, middle, normed, inverse, low_up, low_down,
    *, heads,
):
    size, half = came.shape[1:]
    count = 2 * half
    tensors = came.shape[0] // (2 * heads)
    for block in range(tensors):
        for head in range(heads):
            row = (block * heads + head) * size
            for rank in range(2):
                attended[row : row + size, rank * half : (rank + 1) * half] = came[
                    (2 * head + rank) * tensors + block
                ]
    branch = contract(attended[...], weight[...], 0, 0).T
    values = tokens[...].astype(F32) + branch + columns[:, 4:5]
    middle[...] = values
    centered = values - jnp.mean(values, 0, keepdims=True)
    scale = lax.rsqrt(jnp.mean(centered * centered, 0, keepdims=True) + EPS)
    inverse[...] = scale
    centered = centered * scale
    normed[...] = centered
    low = (centered * columns[:, 2:3] + columns[:, 3:4]).astype(BF16)
    low_up[...] = low[:, :half]
    low_down[...] = low[:, half:]


def enter(came, weight, tokens, columns, heads):
    width, count = tokens.shape[0], 2 * came.shape[2]
    return pl.pallas_call(
        functools.partial(enter_kernel, heads=heads),
        out_shape=(
            jax.ShapeDtypeStruct((width, count), BF16),
            jax.ShapeDtypeStruct((width, count), F32),
            jax.ShapeDtypeStruct((width, count), F32),
            jax.ShapeDtypeStruct((1, count), F32),
            jax.ShapeDtypeStruct((width, count // 2), BF16),
            jax.ShapeDtypeStruct((width, count // 2), BF16),
        ),
        in_specs=[VM] * 4,
        out_specs=(VM,) * 6,
        compiler_params=pltpu.CompilerParams(vmem_limit_bytes=12 * 2**20),
        name="enter",
    )(came, weight, tokens, columns)


def leave_kernel(
    up, down, own_up, own_down, normed, inverse, grads, weight, columns,
    middle, branch, sums, sent,
    *, heads,
):
    size, half = sent.shape[1:]
    count = 2 * half
    tensors = sent.shape[0] // (2 * heads)
    total = jnp.concatenate(
        [
            up[...].astype(F32) + own_up[...].astype(F32),
            down[...].astype(F32) + own_down[...].astype(F32),
        ],
        1,
    )
    scaled = total * columns[:, 2:3]
    first = jnp.mean(scaled, 0, keepdims=True)
    second = jnp.mean(scaled * normed[...], 0, keepdims=True)
    result = grads[...].astype(F32) + inverse[...] * (
        scaled - first - normed[...] * second
    )
    middle[...] = result
    low = result.astype(BF16)
    branch[...] = low
    back = contract(weight[...], low, 1, 0).astype(BF16)
    for block in range(tensors):
        for head in range(heads):
            row = (block * heads + head) * size
            for rank in range(2):
                sent[(2 * head + rank) * tensors + block] = back[
                    row : row + size, rank * half : (rank + 1) * half
                ]
    sums[...] = as_rows(
        [jnp.sum(values, 1, keepdims=True) for values in (total * normed[...], total, result)]
    )


def leave(terms, normed, inverse, grads, weight, columns, heads, size):
    width, count = normed.shape
    blocks = width // size
    return pl.pallas_call(
        functools.partial(leave_kernel, heads=heads),
        out_shape=(
            jax.ShapeDtypeStruct((width, count), F32),
            jax.ShapeDtypeStruct((width, count), BF16),
            jax.ShapeDtypeStruct((8, width), F32),
            jax.ShapeDtypeStruct((2 * blocks, size, count // 2), BF16),
        ),
        in_specs=[VM] * 9,
        out_specs=(VM,) * 4,
        compiler_params=pltpu.CompilerParams(vmem_limit_bytes=12 * 2**20),
        name="leave",
    )(*terms, normed, inverse, grads, weight, columns)


def rest_kernel(spot, flat, full, out, mine, other):
    width = full.shape[0]
    split = mine.shape[0]
    step = min(256, width)
    for start in range(0, width, step):
        tile = slice(start, start + step)
        result = contract(flat[...], full[tile], 1, 1).astype(BF16)
        first = result[:split]
        second = jnp.concatenate([result[split:], out[:, tile]], 0)

        @pl.when(spot[1] == 0)
        def _():
            mine[:, tile] = first
            other[:, tile] = second

        @pl.when(spot[1] == 1)
        def _():
            mine[:, tile] = second
            other[:, tile] = first


def rest_halves(spot, flat, full, out):
    half = (flat.shape[0] + out.shape[0]) // 2
    return pl.pallas_call(
        rest_kernel,
        out_shape=(jax.ShapeDtypeStruct((half, full.shape[0]), BF16),) * 2,
        in_specs=[SM] + [VM] * 3,
        out_specs=(VM, VM),
        compiler_params=pltpu.CompilerParams(vmem_limit_bytes=8 * 2**20),
        cost_estimate=pl.CostEstimate(
            flops=2 * flat.shape[0] * full.size, bytes_accessed=2**23, transcendentals=0
        ),
        name="rest_halves",
    )(spot, flat, full, out)


def rest_whole_kernel(spot, half, other, mixed, out, *, chips):
    step = half.shape[0] // chips
    edge = mixed.shape[0] // step
    for piece in range(chips):
        owner = lax.rem(spot[2] + chips - piece, chips)
        rows = slice(piece * step, (piece + 1) * step)
        for source, core in ((half, spot[1]), (other, 1 - spot[1])):
            block = core * chips + owner
            values = source[rows].astype(F32)

            @pl.when(block < edge)
            def _():
                mixed[pl.ds(pl.multiple_of(jnp.minimum(block, edge - 1) * step, step), step)] = values

            @pl.when(block >= edge)
            def _():
                out[pl.ds(pl.multiple_of(jnp.maximum(block - edge, 0) * step, step), step)] = values


def rest_whole(spot, half, other, rows, chips):
    width = half.shape[1]
    return pl.pallas_call(
        functools.partial(rest_whole_kernel, chips=chips),
        out_shape=(
            jax.ShapeDtypeStruct((rows, width), F32),
            jax.ShapeDtypeStruct((2 * half.shape[0] - rows, width), F32),
        ),
        in_specs=[SM, VM, VM],
        out_specs=(VM, VM),
        compiler_params=pltpu.CompilerParams(vmem_limit_bytes=8 * 2**20),
        name="rest_whole",
    )(spot, half, other)


def prefix_kernel(
    total, hidden, embed, weight, low, grad_embed, grad_weight, grad_bias, grad_out, grad_out_bias
):
    pre = total[...] * (1.0 - hidden[...] * hidden[...])
    grad_bias[...] = jnp.sum(pre, 0, keepdims=True)

    def exact(first, second, dims):
        return lax.dot_general(
            first, second, ((dims[:1], dims[1:]), ((), ())),
            preferred_element_type=F32, precision=HIGHEST,
        )

    grad_weight[...] = exact(embed[...].astype(F32), pre, (0, 0))
    grad_embed[...] = exact(pre, weight[...].astype(F32), (1, 1))
    wide = low[...].astype(F32)
    result = exact(hidden[...], wide, (0, 0))
    sums = jnp.sum(wide, 0, keepdims=True)
    each = grad_out.shape[2]
    for head in range(grad_out.shape[1]):
        lanes = slice(head * each, (head + 1) * each)
        grad_out[:, head, :] = result[:, lanes]
        grad_out_bias[head : head + 1] = sums[:, lanes]


def prefix_back(total, hidden, embed, weight, low, heads):
    rows, width = embed.shape
    extra = PAD - rows
    hidden = jnp.pad(hidden, ((0, extra), (0, 0)))
    embed = jnp.pad(embed, ((0, extra), (0, 0)))
    inner = weight.shape[1]
    each = low.shape[1] // heads
    grad_embed, grad_weight, grad_bias, grad_out, grad_out_bias = pl.pallas_call(
        prefix_kernel,
        out_shape=(
            jax.ShapeDtypeStruct((PAD, width), F32),
            jax.ShapeDtypeStruct(weight.shape, F32),
            jax.ShapeDtypeStruct((1, inner), F32),
            jax.ShapeDtypeStruct((inner, heads, each), F32),
            jax.ShapeDtypeStruct((heads, each), F32),
        ),
        in_specs=[VM] * 5,
        out_specs=(VM,) * 5,
        compiler_params=pltpu.CompilerParams(vmem_limit_bytes=16 * 2**20),
        cost_estimate=pl.CostEstimate(flops=2**31, bytes_accessed=2**22, transcendentals=0),
        name="prefix_back",
    )(total, hidden, embed, weight, low)
    return grad_embed[:rows], grad_weight, grad_bias[0], grad_out, grad_out_bias


def spread(values, axis):
    count = lax.axis_size(axis)
    copies = jnp.broadcast_to(values[None], (count,) + values.shape)
    return lax.all_to_all(copies, axis, 0, 0, tiled=True)


def small_sum(values, axis):
    return jnp.sum(spread(values, axis), 0)


def ring(axis, by):
    count = lax.axis_size(axis)
    return [(source, (source + by) % count) for source in range(count)]


def ring_gather(values, axis, beside=()):
    count, place = lax.axis_size(axis), lax.axis_index(axis)
    half = values.shape[0] // 2
    up, down = values[:half], values[half:]
    out = jnp.zeros((count,) + values.shape, values.dtype)
    out = lax.dynamic_update_slice_in_dim(out, values[None], place, 0)
    zeros = (0,) * (values.ndim - 1)
    results = []
    for step in range(1, count):
        up = lax.ppermute(up, axis, ring(axis, 1))
        down = lax.ppermute(down, axis, ring(axis, -1))
        if step <= len(beside) and beside[step - 1]:
            up, down, result = lax.optimization_barrier((up, down, beside[step - 1]()))
            results.append(result)
        out = lax.dynamic_update_slice(out, up[None], ((place - step) % count, 0) + zeros)
        out = lax.dynamic_update_slice(out, down[None], ((place + step) % count, half) + zeros)
    return (out, results) if beside else out


def ring_terms(own, axis, beside=(), first=None):
    count = lax.axis_size(axis)
    up, down = first or (own(1, False), own(1, True))
    state = None
    for step in range(1, count):
        up = lax.ppermute(up, axis, ring(axis, 1))
        down = lax.ppermute(down, axis, ring(axis, -1))
        if step <= len(beside):
            state = beside[step - 1](state)
            up, down, state = lax.optimization_barrier((up, down, state))
        if step < count - 1:
            up = (up.astype(F32) + own(step + 1, False).astype(F32)).astype(BF16)
            down = (down.astype(F32) + own(step + 1, True).astype(F32)).astype(BF16)
    for other in beside[count - 1 :]:
        state = other(state)
    return (up, down, own(0, False), own(0, True)), state


def one_way_terms(own, axis, beside, first):
    count = lax.axis_size(axis)
    moving, state = first, None
    for step in range(1, count):
        moving = lax.ppermute(moving, axis, ring(axis, 1))
        if step <= len(beside):
            state = beside[step - 1](state)
            moving, state = lax.optimization_barrier((moving, state))
        if step < count - 1:
            moving = (moving.astype(F32) + own(step + 1).astype(F32)).astype(BF16)
    return moving, state


def swapped(values):
    pairs = [(source, source ^ 1) for source in range(lax.axis_size("seq"))]
    return lax.ppermute(values, "seq", pairs)


def chip_parts(half):
    count = lax.axis_size("seq")
    chips = count // 2
    chip = lax.axis_index("seq") // 2
    blocks = half.reshape(chips, half.shape[0] // chips, half.shape[1])
    total = lax.dynamic_index_in_dim(blocks, chip, 0, keepdims=False)
    parts = [total]
    for step in range(1, chips):
        block = lax.dynamic_index_in_dim(blocks, (chip + step) % chips, 0, keepdims=False)
        parts.append(lax.ppermute(block, "seq", ring("seq", 2 * step)))
    return parts


def chip_gather(parts):
    part = sum(part.astype(F32) for part in parts).astype(BF16)
    behind = [lax.ppermute(part, "seq", ring("seq", 2 * step)) for step in range(1, len(parts))]
    return jnp.concatenate([part] + behind, 0)


def spread_direct(values, axis):
    count, place = lax.axis_size(axis), lax.axis_index(axis)
    out = jnp.zeros((count,) + values.shape, values.dtype)
    out = lax.dynamic_update_slice_in_dim(out, values[None], place, 0)
    for step in range(1, count):
        came = lax.ppermute(values, axis, ring(axis, step))
        out = lax.dynamic_update_slice_in_dim(out, came[None], (place - step) % count, 0)
    return out


def core_gather(half):
    core, chip = lax.axis_index("seq") % 2, lax.axis_index("seq") // 2
    chips = lax.axis_size("seq") // 2
    order = (chip - jnp.arange(chips)) % chips

    def sorted_parts(values):
        parts = values.reshape(chips, -1, values.shape[1])
        picked = [lax.dynamic_index_in_dim(parts, order[n], 0) for n in range(chips)]
        return jnp.concatenate(picked, 0).reshape(values.shape)

    half, other = sorted_parts(half), sorted_parts(swapped(half))
    first = jnp.where(core == 0, half, other)
    second = jnp.where(core == 0, other, half)
    return jnp.concatenate([first, second], 0)


def regrouped(values, width):
    count, size, columns = values.shape
    if width == columns:
        return values
    if width > columns:
        merged = values.reshape(-1, width // columns, size, columns).transpose(0, 2, 1, 3)
        return merged.reshape(-1, size, width)
    cut = values.reshape(count, size, columns // width, width).transpose(0, 2, 1, 3)
    return cut.reshape(-1, size, width)


def group_gather(pieces, group):
    if group == 2:
        rank = lax.axis_index("seq") % 2
        other = swapped(pieces)
        return jnp.stack([jnp.where(rank == 0, pieces, other), jnp.where(rank == 0, other, pieces)])
    count = lax.axis_size("seq")
    groups = [[first + i for i in range(group)] for first in range(0, count, group)]
    return lax.all_gather(pieces, "seq", axis_index_groups=groups)


def on_device(
    tokens,
    segment_ids,
    out_grad,
    ln1_gain,
    ln1_bias,
    w_qkv,
    b_qv,
    w_out,
    b_out,
    ln2_gain,
    ln2_bias,
    w_up,
    b_up,
    w_down,
    b_down,
    prefix_embed,
    reparam_in,
    reparam_in_bias,
    reparam_out,
    reparam_out_bias,
):
    rows, features = tokens.shape
    heads = w_qkv.shape[1]
    size = w_qkv.shape[2] // 3
    inner = w_up.shape[1]
    seqs, tensors = lax.axis_size("seq"), lax.axis_size("tensor")
    width = features * tensors
    own_rows = rows // tensors
    group = seqs // heads
    chunk = own_rows // group
    place, slot = lax.axis_index("seq"), lax.axis_index("tensor")
    head, rank = place // group, place % group
    prefix = prefix_embed.shape[0]
    tokens_head = rows // group
    query_width = max(tokens_head, LANES)
    forward_tile = min(512, query_width)
    backward_tile = min(512, query_width)
    forward_keys, backward_keys = 1024, 1024
    both = ("seq", "tensor")
    paired = group == 2 and chunk == LANES

    own_tokens, own_grads = turned(tokens, out_grad)
    numbers = jnp.arange(1, DOCS, dtype=jnp.int32)

    def document_starts():
        before = jnp.sum((segment_ids[None, :] < numbers[:, None]).astype(jnp.int32), 1)
        return spread(jnp.broadcast_to(before[:, None], (DOCS - 1, LANES)), "seq")

    def whole_vectors():
        return spread(
            jnp.stack([ln1_gain, ln1_bias, ln2_gain, ln2_bias, b_out, b_down]), "tensor"
        )

    def prefix_network():
        prefix_hidden = jnp.tanh(
            jnp.dot(prefix_embed, reparam_in, preferred_element_type=F32)
            + reparam_in_bias.astype(F32)
        )
        prefix_pair = jnp.einsum(
            "pa,ahe->phe", prefix_hidden, reparam_out.astype(F32), precision=HIGHEST
        )
        prefix_pair = (prefix_pair + reparam_out_bias.astype(F32)).astype(BF16)
        own_pair = lax.dynamic_index_in_dim(prefix_pair, head, 1, keepdims=False)
        own_pair = jnp.pad(own_pair, ((0, LANES - prefix), (0, 0)))
        pre_key, pre_value = own_pair[:, :size], own_pair[:, size:]
        return prefix_hidden, pre_key, pre_value

    full_tokens, (vectors, starts) = ring_gather(
        own_tokens, "tensor", (None, whole_vectors, document_starts)
    )
    prefix_hidden, pre_key, pre_value = prefix_network()
    full_tokens = full_tokens.reshape(width, rows)
    meta = jnp.concatenate([jnp.sum(starts, 0)[:, 0], rank[None].astype(jnp.int32)])
    columns = vectors.transpose(0, 2, 1).reshape(width, 6).astype(F32)
    out_share = w_out.reshape(seqs, heads * size // seqs, width)
    out_share = lax.dynamic_index_in_dim(out_share, place, 0, keepdims=False)
    core = place % 2
    spot = jnp.stack([slot, core, place // 2]).astype(jnp.int32)

    w_flat = w_qkv.reshape(width, heads * 3 * size)
    bias_pair = b_qv.astype(F32)
    bias_three = jnp.stack(
        [bias_pair[:, :size], jnp.zeros((heads, size), F32), bias_pair[:, size:]], 1
    ).reshape(-1, 1)
    if paired:
        full1, sent, stats = project(
            full_tokens, columns, w_flat.T, bias_three, heads, size, own_rows
        )
    else:
        wide = full_tokens.astype(F32)
        mean = jnp.mean(wide, 0, keepdims=True)
        inverse = lax.rsqrt(jnp.mean((wide - mean) ** 2, 0, keepdims=True) + EPS)
        stats = jnp.concatenate([mean, inverse], 0)
        full1 = ((wide - mean) * inverse * columns[:, 0:1] + columns[:, 1:2]).astype(BF16)
        mixed = (contract(w_flat, full1, 0, 0) + bias_three).astype(BF16)
        mixed = mixed.reshape(heads, 3, size, rows)
        query_part = mixed[:, 0].reshape(heads, size, tensors, group, chunk)
        query_part = query_part.transpose(0, 3, 1, 2, 4).reshape(seqs, size, tokens_head)
        pair_part = mixed[:, 1:].transpose(0, 2, 1, 3).reshape(heads, size, group, 2 * tokens_head)
        pair_part = pair_part.transpose(0, 2, 1, 3).reshape(seqs, size, 2 * tokens_head)
        sent = jnp.concatenate([query_part, pair_part], 2)
    out_share = spread_direct(after(out_share, sent), "tensor")
    came = lax.all_to_all(sent, "seq", 0, 0, tiled=True)
    came, out_share = lax.optimization_barrier((came, out_share))
    w_out_full = lax.all_gather(out_share, "seq")
    w_out_full = w_out_full.transpose(1, 0, 2, 3).reshape(width, width)
    if group == 2:
        query, own, other = came, came, swapped(came)
    else:
        query, pair = came[:, :, :tokens_head], came[:, :, tokens_head:]
        query = regrouped(query, query_width)
        pair = group_gather(pair, group).transpose(1, 2, 0, 3).reshape(seqs, size, 2, rows)
        own, other = pair[:, :, 0], pair[:, :, 1]
    full_grad = lax.all_gather(after(own_grads, full_tokens), "tensor", axis=0, tiled=True)
    out_low, out_full, log_total = attend_forward(
        meta, query, own, other, pre_key.T, pre_value.T,
        forward_tile, forward_keys, prefix, chunk, group, rows, query_width,
    )
    out_low, full_grad, late_up, late_down, late_qkv, late_tokens = lax.optimization_barrier(
        (out_low, full_grad, w_up, w_down, w_qkv, full_tokens)
    )
    late_qkv = late_qkv.transpose(1, 2, 0).reshape(heads * 3 * size, width)
    up_turned, down_turned, late_flat = turned(late_up, late_down, late_qkv)

    came = lax.all_to_all(regrouped(out_low, chunk), both, 0, 0, tiled=True)
    own_block = lax.dynamic_slice_in_dim(late_tokens, slot * own_rows, own_rows, 1)
    came, up_turned, down_turned, late_flat, w_out_full, own_block = lax.optimization_barrier(
        (came, up_turned, down_turned, late_flat, w_out_full, own_block)
    )
    if paired:
        attended, middle, normed2, inverse2, ring_up, ring_down = enter(
            came, w_out_full, own_block, columns, heads
        )
    else:
        came = came.reshape(heads, group, tensors, size, chunk).transpose(2, 0, 3, 1, 4)
        attended = came.reshape(width, own_rows)
        branch = contract(w_out_full, attended, 0, 0)
        middle = own_block.astype(F32) + branch + columns[:, 4:5]
        centered = middle - jnp.mean(middle, 0, keepdims=True)
        inverse2 = lax.rsqrt(jnp.mean(centered * centered, 0, keepdims=True) + EPS)
        normed2 = centered * inverse2
        out2 = (normed2 * columns[:, 2:3] + columns[:, 3:4]).astype(BF16)
        ring_up, ring_down = out2[:, : own_rows // 2], out2[:, own_rows // 2 :]

    bias_up = b_up.astype(F32)[:, None]
    given = given_grads(spot, full_grad, tensors)
    results = []
    for step in range(tensors):
        def block(up=ring_up, down=ring_down, step=step):
            return feed(up, down, given[step], up_turned, w_up, w_down, bias_up)

        if step < tensors - 1:
            ring_up = lax.ppermute(ring_up, "tensor", ring("tensor", 1))
            ring_down = lax.ppermute(ring_down, "tensor", ring("tensor", -1))
            ring_up, ring_down, result = lax.optimization_barrier((ring_up, ring_down, block()))
        else:
            result = block()
        results.append(result)
    blocks, hidden, grad_pre, parts_up, parts_down = zip(*results)

    def weights_here(_):
        return feed_weights(blocks, given, hidden, grad_pre)

    def out_here(state):
        return state, feed_out(spot, hidden, down_turned, middle, columns)

    terms, (weights, mlp_out) = ring_terms(
        lambda step, upper: (parts_down if upper else parts_up)[step],
        "tensor",
        (weights_here, out_here),
    )
    grad_w_down, grad_w_up, grad_b_up = weights
    feed_sums = lax.psum((grad_w_down, grad_w_up), "seq")

    if paired:
        grad_middle, grad_branch, token_sums, sent = leave(
            terms, normed2, inverse2, given[0], w_out_full, columns, heads, size
        )
    else:
        up, down, own_up, own_down = [a.astype(F32) for a in terms]
        grad_normed2 = jnp.concatenate([up + own_up, down + own_down], 1)
        scaled = grad_normed2 * columns[:, 2:3]
        first = jnp.mean(scaled, 0, keepdims=True)
        second = jnp.mean(scaled * normed2, 0, keepdims=True)
        own_grad = lax.dynamic_slice_in_dim(full_grad, slot * own_rows, own_rows, 1)
        grad_middle = own_grad.astype(F32) + inverse2 * (scaled - first - normed2 * second)
        grad_branch = grad_middle.astype(BF16)
        token_sums = [grad_normed2 * normed2, grad_normed2, grad_middle]
        token_sums = jnp.stack([jnp.sum(a, 1) for a in token_sums], 1)
        sent = contract(w_out_full, grad_branch, 1, 0).astype(BF16)
        sent = sent.reshape(tensors, heads, size, group, chunk).transpose(1, 3, 0, 2, 4)
        sent = sent.reshape(seqs * tensors, size, chunk)
    came = lax.all_to_all(sent, both, 0, 0, tiled=True)
    grad_out = regrouped(came, LANES)

    grad_w_out = contract(attended, grad_branch, 1, 1).astype(BF16)
    grad_out, mlp_out, grad_w_out = lax.optimization_barrier((grad_out, mlp_out, grad_w_out))
    output_act = lax.all_to_all(mlp_out, "tensor", 0, 0, tiled=True)
    grad_w_out = lax.psum_scatter(grad_w_out, "tensor", scatter_dimension=0, tiled=True)

    levels = log_total.reshape(-1, 1, backward_tile)
    grad_query, grad_keep, grad_send, grad_prefix = attend_backward(
        meta, query, own, other, pre_key[:PAD], pre_value[:PAD], grad_out, out_full, levels,
        backward_tile, backward_keys, prefix, chunk, group, rows, query_width,
    )
    if group == 2:
        grad_share = (grad_keep.astype(F32) + swapped(grad_send).astype(F32)).astype(BF16)
    else:
        grad_pair = jnp.stack([grad_keep, grad_send])
        groups = [[first + i for i in range(group)] for first in range(0, seqs, group)]
        shares = grad_pair.transpose(1, 2, 0, 3).reshape(seqs, size, group, 2 * tokens_head)
        grad_share = lax.psum_scatter(
            shares.transpose(2, 0, 1, 3), "seq", axis_index_groups=groups
        )
    prefix_part = grad_prefix.transpose(2, 0, 1).reshape(size, 2 * PAD).astype(BF16)
    prefix_part = jnp.pad(prefix_part, ((0, 0), (0, LANES - 2 * PAD)))
    prefix_part = jnp.broadcast_to(prefix_part[None], (seqs, size, LANES))
    sent = jnp.concatenate([regrouped(grad_query, tokens_head), grad_share, prefix_part], 2)
    sent, output_act, feed_sums = lax.optimization_barrier((sent, output_act, feed_sums))
    came = lax.all_to_all(sent, "seq", 0, 0, tiled=True)
    output_act = jnp.sum(output_act.astype(F32), 0).astype(BF16)
    output_act = output_act.transpose(0, 2, 1).reshape(rows, features)
    out_w_down = feed_sums[0].astype(F32)
    out_w_up = (feed_sums[1] if inner == width else feed_sums[1].T).astype(F32)
    came, output_act, grad_w_out, out_w_down, out_w_up = lax.optimization_barrier(
        (came, output_act, grad_w_out, out_w_down, out_w_up)
    )
    if paired:
        grad_flat, grad_part, first_block, last_block, head_row, prefix_low, small = unproject(
            spot, came, late_flat, full_tokens, stats, columns, grad_middle, token_sums,
            reparam_out, heads, size, own_rows,
        )
        mine, other = rest_halves(spot, grad_flat, full1, grad_w_out)
    else:
        query_part = came[:, :, :tokens_head].reshape(heads, group, size, tensors, chunk)
        query_part = query_part.transpose(0, 2, 3, 1, 4).reshape(heads, 1, size, rows)
        pair_part = came[:, :, tokens_head : 3 * tokens_head]
        pair_part = pair_part.reshape(heads, group, size, 2 * tokens_head).transpose(0, 2, 1, 3)
        pair_part = pair_part.reshape(heads, size, 2, rows).transpose(0, 2, 1, 3)
        grad_flat = jnp.concatenate([query_part, pair_part], 1).reshape(heads * 3 * size, rows)
        back = contract(late_flat, grad_flat, 1, 0)
        normed1 = (full_tokens.astype(F32) - stats[0]) * stats[1]
        scaled = back * columns[:, 0:1]
        row_sums = jnp.stack([jnp.sum(scaled, 0), jnp.sum(scaled * normed1, 0)])
        sums1 = jnp.stack([jnp.sum(back * normed1, 1), jnp.sum(back, 1)], 1)
        head_sums = jnp.sum(grad_flat.astype(F32), 1)
        own_inverse = lax.dynamic_slice_in_dim(stats[1:2], slot * own_rows, own_rows, 1)
        own_part = lax.dynamic_slice_in_dim(back, slot * own_rows, own_rows, 1)
        own_part = own_part + grad_middle / (own_inverse * columns[:, 0:1])
        back = lax.dynamic_update_slice_in_dim(back, own_part, slot * own_rows, 1)
        grad_part = back.astype(BF16)
        below = (slot - 1) % tensors * features
        first_block = lax.dynamic_slice_in_dim(grad_part, below, features, 0)
        last_block = lax.dynamic_slice_in_dim(grad_part, slot * features, features, 0)
        grad_w_qkv = contract(grad_flat, full1, 1, 1).astype(BF16)
        rest = jnp.concatenate([grad_w_qkv, grad_w_out], 0)
        halves = rest.reshape(2, rest.shape[0] // 2, width)
        mine = lax.dynamic_index_in_dim(halves, core, 0, keepdims=False)
        other = lax.dynamic_index_in_dim(halves, 1 - core, 0, keepdims=False)

    if not paired:
        prefix_low = came[:, :, 3 * tokens_head : 3 * tokens_head + 2 * PAD].astype(F32)
        prefix_low = jnp.sum(prefix_low.reshape(heads, group, size, 2, PAD), 1)
        prefix_low = prefix_low.transpose(3, 0, 2, 1).reshape(PAD, -1).astype(BF16)
        hidden_part = contract(prefix_low, reparam_out.reshape(reparam_out.shape[0], -1), 1, 1)
        owned = jnp.concatenate([sums1.T, token_sums.T], 0)
        owned = owned.reshape(-1, tensors, features).transpose(1, 0, 2).reshape(tensors, -1)
        shared = jnp.concatenate([row_sums.reshape(-1), hidden_part.reshape(-1)])
        shared = jnp.broadcast_to(shared[None], (tensors, shared.shape[0]))
        small = jnp.concatenate([owned, shared], 1)[:, None, :]

    grad_b_down = jnp.sum(out_grad.astype(F32), 0)

    def halves_here(_):
        half = (mine.astype(F32) + swapped(other).astype(F32)).astype(BF16)
        return half, lax.all_to_all(small, "tensor", 0, 0, tiled=True)


    def totals(parts):
        if paired:
            return small_totals(
                parts, grad_b_down[None], grad_b_up, head_row, rows, prefix_hidden.shape[1], width
            )
        sums = jnp.sum(parts, 0)[0]
        after_rows = 5 * features + 2 * rows
        row_means = sums[5 * features : after_rows].reshape(2, rows) / width
        hidden = sums[after_rows:].reshape(PAD, -1)
        mixed_sums = head_sums.reshape(heads, 3, size)
        late = [sums[: 5 * features], grad_b_down, grad_b_up[0]]
        late += [mixed_sums[:, 0].reshape(-1), mixed_sums[:, 2].reshape(-1)]
        return row_means, hidden, jnp.concatenate(late)[None]

    def parts_here(state):
        row_means, hidden_grad, late = totals(state[1])
        return chip_parts(state[0]), row_means, hidden_grad, spread(late, "seq")

    def gather_here(state):
        parts, row_means, hidden_grad, late = state
        prefix_grads = prefix_back(
            hidden_grad, prefix_hidden, prefix_embed, reparam_in, prefix_low, heads
        )
        return chip_gather(parts), row_means, late, prefix_grads

    def own_part(step):
        return lax.dynamic_slice_in_dim(grad_part, (slot - step) % tensors * features, features, 0)

    moved, (rest_half, row_means, late, prefix_grads) = one_way_terms(
        own_part,
        "tensor",
        (halves_here, parts_here) + (lambda state: state,) * (tensors - 4) + (gather_here,),
        first_block,
    )
    input_grad = finish(
        moved, last_block, own_tokens, ln1_gain.astype(F32)[:, None], stats, row_means,
    )
    mixed_rows = heads * 3 * size
    if paired:
        out_w_qkv, out_w_out = rest_whole(
            spot, rest_half, swapped(rest_half), mixed_rows, seqs // 2
        )
    else:
        rest = core_gather(rest_half).astype(F32)
        out_w_qkv, out_w_out = rest[:mixed_rows], rest[mixed_rows:]
    out_w_qkv = out_w_qkv.reshape(heads, 3 * size, width).transpose(2, 0, 1)
    out_w_out = out_w_out.reshape(heads, size, width)
    if paired:
        vectors, out_b_up, out_b_qv = late_totals(late, inner, heads, size)
        out_b_up = out_b_up[0]
    else:
        late = jnp.sum(late, 0)[0]
        vectors = late[: 6 * features].reshape(6, features)
        out_b_up = late[6 * features : 6 * features + inner]
        pair_sums = late[6 * features + inner :].reshape(2, heads, size)
        out_b_qv = jnp.concatenate([pair_sums[0], pair_sums[1]], 1)
    out_ln1_gain, out_ln1_bias, out_ln2_gain, out_ln2_bias, out_b_out, out_b_down = [
        vectors[i] for i in range(6)
    ]

    return (
        output_act,
        input_grad,
        out_ln1_gain,
        out_ln1_bias,
        out_w_qkv,
        out_b_qv,
        out_w_out,
        out_b_out,
        out_ln2_gain,
        out_ln2_bias,
        out_w_up,
        out_b_up,
        out_w_down,
        out_b_down,
        *prefix_grads,
    )


def solution(mesh):
    placed = (
        P("seq", "tensor"),
        P("seq"),
        P("seq", "tensor"),
        P("tensor"),
        P("tensor"),
        P(None, "tensor", None),
        P("tensor", None),
        P("tensor", None, None),
        P("tensor"),
        P("tensor"),
        P("tensor"),
        P(None, "tensor"),
        P("tensor"),
        P("tensor", None),
        P("tensor"),
        P(),
        P(),
        P(),
        P(None, "tensor", None),
        P("tensor", None),
    )
    return jax.shard_map(
        on_device,
        mesh=mesh,
        in_specs=placed,
        out_specs=(
            P("seq", "tensor"),
            P("seq", "tensor"),
            P("tensor"),
            P("tensor"),
            P(None, "tensor", None),
            P("tensor", None),
            P("tensor", None, None),
            P("tensor"),
            P("tensor"),
            P("tensor"),
            P(None, "tensor"),
            P("tensor"),
            P("tensor", None),
            P("tensor"),
            P(),
            P(),
            P(),
            P(None, "tensor", None),
            P("tensor", None),
        ),
        check_vma=False,
    )
```

```python
import functools

import jax
import jax.numpy as jnp
from jax import lax
from jax.experimental import pallas as pl
from jax.experimental.pallas import tpu as pltpu
from jax.sharding import PartitionSpec as P

EPS = 1e-05
NEGATIVE = -1e30
HIGHEST = lax.Precision.HIGHEST
F32 = jnp.float32
BF16 = jnp.bfloat16
LANES = 128
PAD = 16
WEAK = 1e-24
DOCS = 5
CLEAR, EARLIER, AMONG = range(3)

VM = pl.BlockSpec(memory_space=pltpu.VMEM)
SM = pl.BlockSpec(memory_space=pltpu.SMEM)


def gelu_tanh(values):
    return jax.nn.gelu(values, approximate=True)


def contract(first, second, first_dim, second_dim):
    return lax.dot_general(
        first, second, (((first_dim,), (second_dim,)), ((), ())), preferred_element_type=F32
    )


def work(queries, keys, products):
    pairs = queries * keys // 2
    return pl.CostEstimate(
        flops=2 * 256 * products * pairs, bytes_accessed=8 * 2**20, transcendentals=pairs
    )


def after(values, other):
    return lax.optimization_barrier((values, other))[0]


def document_start(meta, place):
    found = jnp.zeros_like(place) if getattr(place, "shape", ()) else jnp.int32(0)
    for number in range(DOCS - 1):
        begin = meta[number]
        found = jnp.where(place >= begin, jnp.maximum(found, begin), found)
    return found


def query_places(meta, index, base, chunk, group):
    return base + (index // chunk) * (chunk * group) + meta[DOCS - 1] * chunk + index % chunk


def tile_bounds(meta, base, count, chunk, group):
    rank = meta[DOCS - 1]
    first = base + rank * chunk
    last = base + (count // chunk - 1) * (chunk * group) + rank * chunk + chunk - 1
    return document_start(meta, first), document_start(meta, last)


def one_row(rows, columns):
    return lax.broadcasted_iota(jnp.int32, (rows, columns), 0) == 0


def by_rank(meta, group, first, second, work):
    if group != 2:
        work(first, second)
        return

    @pl.when(meta[DOCS - 1] == 0)
    def _():
        work(first, second)

    @pl.when(meta[DOCS - 1] == 1)
    def _():
        work(second, first)


def over_keys(bounds, base, tile, group, keys, block):
    low, low_last = bounds
    first, last = low // keys, base // keys
    clear = jnp.clip((low_last + keys - 1) // keys, first, jnp.maximum(first, last))

    def masked(number, _):
        block(number * keys, keys, 0, EARLIER)
        return 0

    def pair(number, _):
        block((clear + 2 * number) * keys, 2 * keys, 0, CLEAR)
        return 0

    lax.fori_loop(first, jnp.minimum(clear, last), masked, 0)
    left = jnp.maximum(last - clear, 0)
    lax.fori_loop(0, left // 2, pair, 0)

    @pl.when(left % 2 == 1)
    def _():
        block((last - 1) * keys, keys, 0, CLEAR)

    for stair in range(tile // LANES):
        block(base + stair * LANES * group, LANES * group, stair * LANES, AMONG)


def allowed(meta, start, count, places, kind=AMONG):
    key = start + lax.broadcasted_iota(jnp.int32, (count, 1), 0)
    inside = key >= document_start(meta, places)
    return inside if kind == EARLIER else (key <= places) & inside


def forward_kernel(
    meta, query, own, other, pre_key, pre_value,
    out_low, out_full, log_total,
    key_rows, value_ones, accum, peak, norm,
    *, tile, keys, prefix, chunk, group, length, width,
):
    sources, size, whole = own.shape
    blocks = query.shape[0]
    per = width // tile
    scale = size**-0.5
    padded = pre_key.shape[1]
    kept = slice(whole - length, whole)

    def extended(values, count, total):
        ones = jnp.where(one_row(PAD, count), 1.0, 0.0).astype(BF16)
        rest = total - size - PAD
        tail = [jnp.zeros((rest, count), BF16)] if rest else []
        return jnp.concatenate([values, ones] + tail, 0)

    def longest(values):
        wide = values.astype(F32)
        return jnp.max(jnp.sum(wide * wide, 0, keepdims=True), 1, keepdims=True)

    norm[...] = jnp.broadcast_to(longest(pre_key[...]), norm.shape)

    def fill(key, value):
        def prepare(source, _):
            rows = pl.ds(pl.multiple_of(source * length, length), length)
            found = key[source, :, kept]
            key_rows[rows, :] = extended(found, length, LANES).astype(F32).T.astype(BF16)
            value_ones[:, rows] = extended(value[source, :, kept], length, size + PAD)
            norm[...] = jnp.maximum(norm[...], longest(found))
            return 0

        lax.fori_loop(0, sources, prepare, 0)

    by_rank(meta, group, own, other, fill)
    most = jnp.sqrt(norm[0:1, 0:1])
    pre_key_ones = extended(pre_key[...], padded, LANES)
    pre_value_ones = extended(pre_value[...], padded, size + PAD)
    pre_row = lax.broadcasted_iota(jnp.int32, (padded, tile), 0)

    def query_tile(number, _):
        source, part = number // per, number % per
        base = number * tile * group
        columns = pl.ds(pl.multiple_of(part * tile, tile), tile)
        scaled = query[source, :, columns].astype(F32) * scale
        limit = jnp.sqrt(jnp.sum(scaled * scaled, 0, keepdims=True)) * most
        limit = limit.astype(BF16).astype(F32)
        shifted = jnp.concatenate(
            [
                scaled,
                jnp.where(one_row(PAD, tile), -limit, 0.0),
                jnp.zeros((LANES - size - PAD, tile), F32),
            ],
            0,
        ).astype(BF16)
        index = lax.broadcasted_iota(jnp.int32, (1, tile), 1)
        places = query_places(meta, index, base, chunk, group)
        bounds = tile_bounds(meta, base, tile, chunk, group)

        weights = jnp.where(pre_row < prefix, jnp.exp(contract(pre_key_ones, shifted, 0, 0)), 0.0)
        accum[...] = contract(pre_value_ones, weights.astype(BF16), 1, 0)

        def block(start, count, lane, masked):
            rows = pl.ds(pl.multiple_of(start, LANES), count)
            weights = jnp.exp(contract(key_rows[rows, :], shifted[:, lane:], 1, 0))
            if masked:
                mask = allowed(meta, start, count, places[:, lane:], masked)
                weights = jnp.where(mask, weights, 0.0)
            accum[:, lane:] += contract(value_ones[:, rows], weights.astype(BF16), 1, 0)

        over_keys(bounds, base, tile, group, keys, block)
        peak[...] = limit

        @pl.when(jnp.min(accum[size : size + 1, :]) < WEAK)
        def _():
            plain = scaled.astype(BF16)

            def fold(scores, mask, values):
                scores = jnp.where(mask, scores, NEGATIVE)
                new = jnp.maximum(peak[...], jnp.max(scores, 0, keepdims=True))
                weights = jnp.where(mask, jnp.exp(scores - new), 0.0).astype(BF16)
                accum[...] = accum[...] * jnp.exp(peak[...] - new) + contract(values, weights, 1, 0)
                peak[...] = new

            peak[...] = jnp.full(peak.shape, NEGATIVE, F32)
            accum[...] = jnp.zeros(accum.shape, F32)
            fold(contract(pre_key[...], plain, 0, 0), pre_row < prefix, pre_value_ones)

            def step(number, _):
                rows = pl.ds(pl.multiple_of(number * keys, keys), keys)
                scores = contract(key_rows[rows, :][:, :size], plain, 1, 0)
                mask = allowed(meta, number * keys, keys, places)
                fold(scores, mask, value_ones[:, rows])
                return 0

            lax.fori_loop(bounds[0] // keys, (base + tile * group - 1) // keys + 1, step, 0)

        total = accum[size : size + 1, :]
        result = accum[:size, :] / total
        log_total[number] = peak[...] + jnp.log(total)
        for part in range(tile // LANES):
            piece = result[:, part * LANES : (part + 1) * LANES]
            out_full[number * (tile // LANES) + part] = piece
            out_low[number * (tile // LANES) + part] = piece.astype(BF16)
        return 0

    lax.fori_loop(0, blocks * per, query_tile, 0)


def attend_forward(
    meta, query, own, other, pre_key, pre_value,
    tile, keys, prefix, chunk, group, length, width,
):
    sources, size, _ = own.shape
    count = query.shape[0] * width
    return pl.pallas_call(
        functools.partial(
            forward_kernel, tile=tile, keys=keys, prefix=prefix, chunk=chunk, group=group,
            length=length, width=width,
        ),
        out_shape=(
            jax.ShapeDtypeStruct((count // LANES, size, LANES), BF16),
            jax.ShapeDtypeStruct((count // LANES, size, LANES), F32),
            jax.ShapeDtypeStruct((count // tile, 1, tile), F32),
        ),
        in_specs=[SM] + [VM] * 5,
        out_specs=(VM, VM, VM),
        scratch_shapes=[
            pltpu.VMEM((sources * length, LANES), BF16),
            pltpu.VMEM((size + PAD, sources * length), BF16),
            pltpu.VMEM((size + PAD, tile), F32),
            pltpu.VMEM((1, tile), F32),
            pltpu.VMEM((8, LANES), F32),
        ],
        compiler_params=pltpu.CompilerParams(vmem_limit_bytes=36 * 2**20),
        cost_estimate=work(count, sources * length, 2),
        name="attend_forward",
    )(meta, query, own, other, pre_key, pre_value)


def in_three(values):
    high = values.astype(BF16).astype(F32)
    middle = (values - high).astype(BF16).astype(F32)
    low = values - high - middle
    row = lax.broadcasted_iota(jnp.int32, (PAD, values.shape[1]), 0)
    return jnp.where(row == 0, high, jnp.where(row == 1, middle, jnp.where(row == 2, low, 0.0)))


def backward_kernel(
    meta, query, own, other, pre_key, pre_value, grad_out, out_full, log_total,
    grad_query, grad_keep, grad_send, grad_prefix,
    key_rows, value_rows, key_columns, sums, query_sum,
    *, tile, keys, prefix, chunk, group, length, width,
):
    sources, size, whole = own.shape
    blocks = query.shape[0]
    kept = slice(whole - length, whole)
    per = width // tile
    scale = size**-0.5
    count = tile // LANES
    rank = meta[DOCS - 1]

    def extended(values):
        ones = jnp.where(
            lax.broadcasted_iota(jnp.int32, (LANES - size, values.shape[1]), 0) < 3, 1.0, 0.0
        )
        return jnp.concatenate([values.astype(F32), ones], 0)

    def fill(key, value):
        def prepare(source, _):
            rows = pl.ds(pl.multiple_of(source * length, length), length)
            found = key[source, :, kept]
            key_rows[rows, :] = extended(found).T.astype(BF16)
            value_rows[rows, :] = extended(value[source, :, kept]).T.astype(BF16)
            key_columns[:, rows] = found
            sums[rows, :] = jnp.zeros((length, LANES), F32)
            return 0

        lax.fori_loop(0, sources, prepare, 0)

    by_rank(meta, group, own, other, fill)
    grad_prefix[...] = jnp.zeros(grad_prefix.shape, F32)
    pre_row = lax.broadcasted_iota(jnp.int32, (pre_key.shape[0], tile), 0)

    def query_tile(number, _):
        source, part = number // per, number % per
        base = number * tile * group
        columns = pl.ds(pl.multiple_of(part * tile, tile), tile)
        scaled = (query[source, :, columns].astype(F32) * scale).astype(BF16)
        pieces = [number * count + piece for piece in range(count)]
        grad = jnp.concatenate([grad_out[piece] for piece in pieces], 1)
        full = jnp.concatenate([out_full[piece] for piece in pieces], 1)
        delta = jnp.sum(grad.astype(F32) * full, 0, keepdims=True)
        level = log_total[number]
        index = lax.broadcasted_iota(jnp.int32, (1, tile), 1)
        places = query_places(meta, index, base, chunk, group)
        bounds = tile_bounds(meta, base, tile, chunk, group)
        rest = jnp.zeros((LANES - size - PAD, tile), BF16)
        scaled_less = jnp.concatenate([scaled, in_three(-level).astype(BF16), rest], 0)
        grad_less = jnp.concatenate([grad, in_three(-delta).astype(BF16), rest], 0)
        none = jnp.zeros((size, tile), BF16)
        pair = jnp.concatenate(
            [jnp.concatenate([grad, none], 1), jnp.concatenate([none, scaled], 1)], 0
        )

        probs = jnp.exp(contract(pre_key[...], scaled, 1, 0) - level)
        probs = jnp.where(pre_row < prefix, probs, 0.0)
        slope = (probs * (contract(pre_value[...], grad, 1, 0) - delta)).astype(BF16)
        grad_prefix[0] += contract(slope, scaled, 1, 1)
        grad_prefix[1] += contract(probs.astype(BF16), grad, 1, 1)
        query_sum[...] = contract(pre_key[...], slope, 0, 0)

        def block(start, count, lane, masked):
            rows = pl.ds(pl.multiple_of(start, LANES), count)
            probs = jnp.exp(contract(key_rows[rows, :], scaled_less[:, lane:], 1, 0))
            if masked:
                mask = allowed(meta, start, count, places[:, lane:], masked)
                probs = jnp.where(mask, probs, 0.0)
            slope = probs * contract(value_rows[rows, :], grad_less[:, lane:], 1, 0)
            slope = slope.astype(BF16)
            both = jnp.concatenate([probs.astype(BF16), slope], 1)
            ends = jnp.concatenate([pair[:, lane:tile], pair[:, tile + lane :]], 1) if lane else pair
            sums[rows, :] += contract(both, ends, 1, 1)
            query_sum[:, lane:] += contract(key_columns[:, rows], slope, 1, 0)

        over_keys(bounds, base, tile, group, keys, block)
        grad_query[source, :, columns] = (query_sum[...] * scale).astype(BF16)
        return 0

    lax.fori_loop(0, blocks * per, query_tile, 0)

    def flush(keys_target, values_target):
        def step(source, _):
            rows = pl.ds(pl.multiple_of(source * length, length), length)
            turned = sums[rows, :].T.astype(BF16)
            values_target[source] = turned[:size]
            keys_target[source] = turned[size:]
            return 0

        lax.fori_loop(0, sources, step, 0)

    if group == 2:

        @pl.when(rank == 0)
        def _():
            flush(grad_keep, grad_send)

        @pl.when(rank == 1)
        def _():
            flush(grad_send, grad_keep)

    else:
        flush(grad_keep, grad_send)


def attend_backward(
    meta, query, own, other, pre_key, pre_value, grad_out, out_full, log_total,
    tile, keys, prefix, chunk, group, length, width,
):
    sources, size, _ = own.shape
    pair = jax.ShapeDtypeStruct((sources, size, length), BF16)
    return pl.pallas_call(
        functools.partial(
            backward_kernel, tile=tile, keys=keys, prefix=prefix, chunk=chunk, group=group,
            length=length, width=width,
        ),
        out_shape=(
            jax.ShapeDtypeStruct((query.shape[0], size, width), BF16),
            pair,
            pair,
            jax.ShapeDtypeStruct((2,) + pre_key.shape, F32),
        ),
        in_specs=[SM] + [VM] * 8,
        out_specs=(VM,) * 4,
        scratch_shapes=[
            pltpu.VMEM((sources * length, LANES), BF16),
            pltpu.VMEM((sources * length, LANES), BF16),
            pltpu.VMEM((size, sources * length), BF16),
            pltpu.VMEM((sources * length, LANES), F32),
            pltpu.VMEM((size, tile), F32),
        ],
        compiler_params=pltpu.CompilerParams(vmem_limit_bytes=44 * 2**20),
        cost_estimate=work(query.shape[0] * width, sources * length, 5),
        name="attend_backward",
    )(meta, query, own, other, pre_key, pre_value, grad_out, out_full, log_total)


def as_rows(columns):
    lane = lax.broadcasted_iota(jnp.int32, (columns[0].shape[0], LANES), 1)
    wide = jnp.zeros(lane.shape, F32)
    for number, column in enumerate(columns):
        wide = jnp.where(lane == number, column, wide)
    return wide.T[:8]


def turn_kernel(*refs):
    count = len(refs) // 2
    for source, target in zip(refs[:count], refs[count:]):
        target[...] = source[...].astype(F32).T.astype(BF16)


def turned(*arrays):
    return pl.pallas_call(
        turn_kernel,
        out_shape=tuple(jax.ShapeDtypeStruct(a.shape[::-1], BF16) for a in arrays),
        in_specs=[VM] * len(arrays),
        out_specs=(VM,) * len(arrays),
        compiler_params=pltpu.CompilerParams(vmem_limit_bytes=8 * 2**20),
        name="turned",
    )(*arrays)


def project_kernel(rows, columns, weight, bias, full, sent, stats, *, heads, size, step):
    length = rows.shape[1]
    pieces = length // step
    half = step // 2
    width = length // 2
    for piece in range(pieces):
        lanes = slice(piece * step, (piece + 1) * step)
        values = rows[:, lanes].astype(F32)
        mean = jnp.mean(values, 0, keepdims=True)
        centered = values - mean
        inverse = lax.rsqrt(jnp.mean(centered * centered, 0, keepdims=True) + EPS)
        stats[0:1, lanes] = mean
        stats[1:2, lanes] = inverse
        low = (centered * inverse * columns[:, 0:1] + columns[:, 1:2]).astype(BF16)
        full[:, lanes] = low
        mixed = (contract(weight[...], low, 1, 0) + bias[...]).astype(BF16)
        for head in range(heads):
            part = mixed[head * 3 * size : (head + 1) * 3 * size]
            spot = slice(piece * half, (piece + 1) * half)
            sent[2 * head, :, spot] = part[:size, :half]
            sent[2 * head + 1, :, spot] = part[:size, half:]
            spot = slice(width + piece * step, width + (piece + 1) * step)
            sent[2 * head, :, spot] = part[size : 2 * size]
            sent[2 * head + 1, :, spot] = part[2 * size :]


def project(rows, columns, weight, bias, heads, size, step):
    width, length = rows.shape
    return pl.pallas_call(
        functools.partial(project_kernel, heads=heads, size=size, step=step),
        out_shape=(
            jax.ShapeDtypeStruct((width, length), BF16),
            jax.ShapeDtypeStruct((2 * heads, size, length // 2 * 3), BF16),
            jax.ShapeDtypeStruct((2, length), F32),
        ),
        in_specs=[VM] * 4,
        out_specs=(VM, VM, VM),
        compiler_params=pltpu.CompilerParams(vmem_limit_bytes=20 * 2**20),
        name="project",
    )(rows, columns, weight, bias)


def unproject_kernel(
    spot, came, weight, rows, stats, columns, own_grad, token_rows, reparam,
    flat, part, first_block, last_block, head_row, prefix_low, small, totals,
    *, heads, size, step,
):
    width, length = rows.shape
    half = step // 2
    past = length // 2
    gain = columns[:, 0:1]
    row_sums = []
    sums = [0.0, 0.0, 0.0]
    for piece in range(length // step):
        lanes = slice(piece * step, (piece + 1) * step)
        place = slice(piece * half, (piece + 1) * half)
        pair = slice(past + piece * step, past + (piece + 1) * step)
        pieces = []
        for head in range(heads):
            first, second = 2 * head, 2 * head + 1
            pieces.append(jnp.concatenate([came[first, :, place], came[second, :, place]], 1))
            pieces += [came[first, :, pair], came[second, :, pair]]
        grads = jnp.concatenate(pieces, 0)
        flat[:, lanes] = grads
        back = contract(weight[...], grads, 1, 0)
        part[:, lanes] = back.astype(BF16)

        @pl.when(spot[0] == piece)
        def _():
            part[:, lanes] = (back + own_grad[...].astype(F32) / (stats[1:2, lanes] * gain)).astype(BF16)

        normed = (rows[:, lanes].astype(F32) - stats[0:1, lanes]) * stats[1:2, lanes]
        scaled = back * gain
        row_sums.append(
            [jnp.sum(values, 0, keepdims=True) for values in (scaled, scaled * normed)]
        )
        for number, values in enumerate((back * normed, back, grads.astype(F32))):
            sums[number] += jnp.sum(values, 1, keepdims=True)
    features = first_block.shape[0]
    blocks = width // features
    for block in range(blocks):

        @pl.when(lax.rem(spot[0] + blocks - 1, blocks) == block)
        def _():
            first_block[...] = part[block * features : (block + 1) * features]

        @pl.when(spot[0] == block)
        def _():
            last_block[...] = part[block * features : (block + 1) * features]

    head_row[...] = as_rows(sums[2:])[:1]
    totals[...] = as_rows(sums[:2])
    found = []
    for head in range(heads):
        both = came[2 * head, :, 3 * past :].astype(F32) + came[2 * head + 1, :, 3 * past :].astype(F32)
        both = both.T
        found += [both[:PAD], both[PAD : 2 * PAD]]
    low = jnp.concatenate(found, 1).astype(BF16)
    prefix_low[...] = low
    each = 2 * size
    hidden = sum(
        contract(low[:, head * each : (head + 1) * each], reparam[:, head, :], 1, 1)
        for head in range(heads)
    )
    for number in range(blocks):
        spread_over = slice(number * features, (number + 1) * features)
        target = small.at[number]
        target[0:2] = totals[0:2, spread_over]
        target[2:5] = token_rows[0:3, spread_over]
        target[5:8] = jnp.zeros((3, features), F32)
        for which in range(2):
            for piece in range(blocks):
                row = 8 + which * blocks + piece
                target[row : row + 1] = row_sums[piece][which]
        for piece in range(hidden.shape[1] // features):
            row = 8 + 2 * blocks + piece * PAD
            target[row : row + PAD] = hidden[:, piece * features : (piece + 1) * features]


def unproject(spot, came, weight, rows, stats, columns, own_grad, token_rows, reparam, heads, size, step):
    width, length = rows.shape
    blocks = length // step
    features = width // blocks
    mixed = 3 * heads * size
    small = 8 + 2 * blocks + reparam.shape[0] // features * PAD
    return pl.pallas_call(
        functools.partial(unproject_kernel, heads=heads, size=size, step=step),
        out_shape=(
            jax.ShapeDtypeStruct((mixed, length), BF16),
            jax.ShapeDtypeStruct((width, length), BF16),
            jax.ShapeDtypeStruct((features, length), BF16),
            jax.ShapeDtypeStruct((features, length), BF16),
            jax.ShapeDtypeStruct((1, mixed), F32),
            jax.ShapeDtypeStruct((PAD, 2 * heads * size), BF16),
            jax.ShapeDtypeStruct((blocks, small, features), F32),
        ),
        in_specs=[SM] + [VM] * 8,
        out_specs=(VM,) * 7,
        scratch_shapes=[pltpu.VMEM((8, width), F32)],
        compiler_params=pltpu.CompilerParams(vmem_limit_bytes=20 * 2**20),
        cost_estimate=pl.CostEstimate(
            flops=4 * mixed * width * length, bytes_accessed=2**23, transcendentals=0
        ),
        name="unproject",
    )(spot, came, weight, rows, stats, columns, own_grad, token_rows, reparam)


def small_kernel(parts, down_row, up_row, head_row, row_sums, hidden, late, *, width):
    blocks = parts.shape[0]
    total = sum(parts[n] for n in range(blocks))
    features = total.shape[1]
    for which in range(2):
        for piece in range(blocks):
            row = 8 + which * blocks + piece
            lanes = slice(piece * features, (piece + 1) * features)
            row_sums[which : which + 1, lanes] = total[row : row + 1] / width
    for piece in range(hidden.shape[1] // features):
        row = 8 + 2 * blocks + piece * PAD
        hidden[:, piece * features : (piece + 1) * features] = total[row : row + PAD]
    late[...] = jnp.zeros(late.shape, F32)
    late[0:5] = total[0:5]
    late[5:6] = down_row[...]
    row = 6
    for source in (up_row, head_row):
        for piece in range(source.shape[1] // features):
            late[row : row + 1] = source[:, piece * features : (piece + 1) * features]
            row += 1


def small_totals(parts, down_row, up_row, head_row, rows, hidden_width, width):
    features = parts.shape[2]
    late = 6 + (up_row.shape[1] + head_row.shape[1]) // features
    return pl.pallas_call(
        functools.partial(small_kernel, width=width),
        out_shape=(
            jax.ShapeDtypeStruct((2, rows), F32),
            jax.ShapeDtypeStruct((PAD, hidden_width), F32),
            jax.ShapeDtypeStruct((-(-late // 8) * 8, features), F32),
        ),
        in_specs=[VM] * 4,
        out_specs=(VM,) * 3,
        compiler_params=pltpu.CompilerParams(vmem_limit_bytes=8 * 2**20),
        name="small_totals",
    )(parts, down_row, up_row, head_row)


def late_kernel(parts, vectors, up, pairs, *, heads, size):
    total = sum(parts[n] for n in range(parts.shape[0]))
    features = total.shape[1]
    vectors[...] = total[:8]
    count = up.shape[1] // features
    up[...] = jnp.concatenate([total[6 + n : 7 + n] for n in range(count)], 1)
    mixed = 3 * heads * size
    row = jnp.concatenate(
        [total[6 + count + n : 7 + count + n] for n in range(mixed // features)], 1
    )
    for head in range(heads):
        start = 3 * size * head
        pairs[head : head + 1] = jnp.concatenate(
            [row[:, start : start + size], row[:, start + 2 * size : start + 3 * size]], 1
        )


def late_totals(parts, inner, heads, size):
    return pl.pallas_call(
        functools.partial(late_kernel, heads=heads, size=size),
        out_shape=(
            jax.ShapeDtypeStruct((8, parts.shape[2]), F32),
            jax.ShapeDtypeStruct((1, inner), F32),
            jax.ShapeDtypeStruct((heads, 2 * size), F32),
        ),
        in_specs=[VM],
        out_specs=(VM,) * 3,
        compiler_params=pltpu.CompilerParams(vmem_limit_bytes=8 * 2**20),
        name="late_totals",
    )(parts)


def finish_kernel(came, own, rows, gain, stats, row_means, grad):
    total = came[...].astype(F32) + own[...].astype(F32)
    normed = (rows[...].astype(F32) - stats[0:1]) * stats[1:2]
    back = gain[...] * total - row_means[0:1] - normed * row_means[1:2]
    grad[...] = (stats[1:2] * back).T.astype(BF16)


def finish(came, own, rows, gain, stats, row_means):
    return pl.pallas_call(
        finish_kernel,
        out_shape=jax.ShapeDtypeStruct(rows.shape[::-1], BF16),
        in_specs=[VM] * 6,
        out_specs=VM,
        compiler_params=pltpu.CompilerParams(vmem_limit_bytes=10 * 2**20),
        name="finish",
    )(came, own, rows, gain, stats, row_means)


def ring_lanes(slot, step, blocks, count):
    half = count // 2
    below = lax.rem(slot + blocks - step, blocks) * count
    above = lax.rem(slot + step, blocks) * count + half
    if half % LANES == 0:
        below, above = pl.multiple_of(below, half), pl.multiple_of(above, half)
    return pl.ds(below, half), pl.ds(above, half)


def feed_kernel(
    rows_up, rows_down, given, up_turned, up, down, bias,
    rows, hidden, grad_pre, part_up, part_down,
):
    half = rows_up.shape[1]
    both = jnp.concatenate([rows_up[...], rows_down[...]], 1)
    rows[...] = both
    pre = contract(up_turned[...], both, 1, 0) + bias[...]
    act, pull = jax.vjp(gelu_tanh, pre)
    hidden[...] = act.astype(BF16)
    low = pull(contract(down[...], given[...], 1, 0))[0].astype(BF16)
    grad_pre[...] = low
    part = contract(up[...], low, 1, 0).astype(BF16)
    part_up[...] = part[:, :half]
    part_down[...] = part[:, half:]


def feed(rows_up, rows_down, given, up_turned, up, down, bias):
    width, half = rows_up.shape
    inner = down.shape[0]
    count = 2 * half
    return pl.pallas_call(
        feed_kernel,
        out_shape=(
            jax.ShapeDtypeStruct((width, count), BF16),
            jax.ShapeDtypeStruct((inner, count), BF16),
            jax.ShapeDtypeStruct((inner, count), BF16),
            jax.ShapeDtypeStruct((width, half), BF16),
            jax.ShapeDtypeStruct((width, half), BF16),
        ),
        in_specs=[VM] * 7,
        out_specs=(VM,) * 5,
        compiler_params=pltpu.CompilerParams(vmem_limit_bytes=12 * 2**20),
        cost_estimate=pl.CostEstimate(
            flops=6 * width * inner * count, bytes_accessed=2**22, transcendentals=0
        ),
        name="feed",
    )(rows_up, rows_down, given, up_turned, up, down, bias)


def given_kernel(spot, grads, *given):
    blocks = len(given)
    count = given[0].shape[1]
    for step, target in enumerate(given):
        lanes = ring_lanes(spot[0], step, blocks, count)
        target[...] = jnp.concatenate([grads[:, spread] for spread in lanes], 1)


def given_grads(spot, grads, blocks):
    width, length = grads.shape
    count = length // blocks
    if count // 2 % LANES:
        found = []
        for step in range(blocks):
            below = (spot[0] - step) % blocks * count
            above = (spot[0] + step) % blocks * count + count // 2
            halves = [lax.dynamic_slice_in_dim(grads, at, count // 2, 1) for at in (below, above)]
            found.append(jnp.concatenate(halves, 1))
        return found
    return pl.pallas_call(
        given_kernel,
        out_shape=(jax.ShapeDtypeStruct((width, count), BF16),) * blocks,
        in_specs=[SM, VM],
        out_specs=(VM,) * blocks,
        compiler_params=pltpu.CompilerParams(vmem_limit_bytes=8 * 2**20),
        name="given_grads",
    )(spot, grads)


def feed_weights_kernel(*refs, blocks, square):
    rows, grads, hidden, grad_pre = [refs[n * blocks : (n + 1) * blocks] for n in range(4)]
    grad_down, grad_up, bias = refs[4 * blocks :]

    def weights(target, first, second):
        step = min(256, second[0].shape[0])
        whole = jnp.concatenate([ref[...] for ref in first], 1)
        for start in range(0, second[0].shape[0], step):
            tile = slice(start, start + step)
            turned = jnp.concatenate([ref[tile] for ref in second], 1)
            target[:, tile] = contract(whole, turned, 1, 1).astype(BF16)

    weights(grad_down, hidden, grads)
    if square:
        weights(grad_up, rows, grad_pre)
    else:
        weights(grad_up, grad_pre, rows)
    total = sum(jnp.sum(ref[...].astype(F32), 1, keepdims=True) for ref in grad_pre)
    bias[...] = as_rows([total])[:1]


def feed_weights(rows, grads, hidden, grad_pre):
    blocks = len(rows)
    width, count = rows[0].shape
    inner = hidden[0].shape[0]
    return pl.pallas_call(
        functools.partial(feed_weights_kernel, blocks=blocks, square=inner == width),
        out_shape=(
            jax.ShapeDtypeStruct((inner, width), BF16),
            jax.ShapeDtypeStruct((inner, width), BF16),
            jax.ShapeDtypeStruct((1, inner), F32),
        ),
        in_specs=[VM] * (4 * blocks),
        out_specs=(VM,) * 3,
        compiler_params=pltpu.CompilerParams(vmem_limit_bytes=14 * 2**20),
        cost_estimate=pl.CostEstimate(
            flops=4 * blocks * width * inner * count, bytes_accessed=2**24, transcendentals=0
        ),
        name="feed_weights",
    )(*rows, *grads, *hidden, *grad_pre)


def feed_out_kernel(spot, *refs, blocks):
    hidden = refs[:blocks]
    down_turned, middle, columns, out = refs[blocks:]
    features, half = out.shape[2:]
    for step, source in enumerate(hidden):
        result = contract(down_turned[...], source[...], 1, 0)
        if step == 0:
            result = result + middle[...] + columns[:, 5:6]
        result = result.astype(BF16)
        below = lax.rem(spot[0] + blocks - step, blocks)
        above = lax.rem(spot[0] + step, blocks)
        for block in range(blocks):
            piece = result[block * features : (block + 1) * features]
            out[block, 2 * below] = piece[:, :half]
            out[block, 2 * above + 1] = piece[:, half:]


def feed_out(spot, hidden, down_turned, middle, columns):
    blocks = len(hidden)
    inner, count = hidden[0].shape
    width = middle.shape[0]
    return pl.pallas_call(
        functools.partial(feed_out_kernel, blocks=blocks),
        out_shape=jax.ShapeDtypeStruct((blocks, 2 * blocks, width // blocks, count // 2), BF16),
        in_specs=[SM] + [VM] * (blocks + 3),
        out_specs=VM,
        compiler_params=pltpu.CompilerParams(vmem_limit_bytes=8 * 2**20),
        cost_estimate=pl.CostEstimate(
            flops=2 * blocks * width * inner * count, bytes_accessed=2**23, transcendentals=0
        ),
        name="feed_out",
    )(spot, *hidden, down_turned, middle, columns)


def enter_kernel(
    came, weight, tokens, columns,
    attended, middle, normed, inverse, low_up, low_down,
    *, heads,
):
    size, half = came.shape[1:]
    count = 2 * half
    tensors = came.shape[0] // (2 * heads)
    for block in range(tensors):
        for head in range(heads):
            row = (block * heads + head) * size
            for rank in range(2):
                attended[row : row + size, rank * half : (rank + 1) * half] = came[
                    (2 * head + rank) * tensors + block
                ]
    branch = contract(attended[...], weight[...], 0, 0).T
    values = tokens[...].astype(F32) + branch + columns[:, 4:5]
    middle[...] = values
    centered = values - jnp.mean(values, 0, keepdims=True)
    scale = lax.rsqrt(jnp.mean(centered * centered, 0, keepdims=True) + EPS)
    inverse[...] = scale
    centered = centered * scale
    normed[...] = centered
    low = (centered * columns[:, 2:3] + columns[:, 3:4]).astype(BF16)
    low_up[...] = low[:, :half]
    low_down[...] = low[:, half:]


def enter(came, weight, tokens, columns, heads):
    width, count = tokens.shape[0], 2 * came.shape[2]
    return pl.pallas_call(
        functools.partial(enter_kernel, heads=heads),
        out_shape=(
            jax.ShapeDtypeStruct((width, count), BF16),
            jax.ShapeDtypeStruct((width, count), F32),
            jax.ShapeDtypeStruct((width, count), F32),
            jax.ShapeDtypeStruct((1, count), F32),
            jax.ShapeDtypeStruct((width, count // 2), BF16),
            jax.ShapeDtypeStruct((width, count // 2), BF16),
        ),
        in_specs=[VM] * 4,
        out_specs=(VM,) * 6,
        compiler_params=pltpu.CompilerParams(vmem_limit_bytes=12 * 2**20),
        name="enter",
    )(came, weight, tokens, columns)


def leave_kernel(
    up, down, own_up, own_down, normed, inverse, grads, weight, columns,
    middle, branch, sums, sent,
    *, heads,
):
    size, half = sent.shape[1:]
    count = 2 * half
    tensors = sent.shape[0] // (2 * heads)
    total = jnp.concatenate(
        [
            up[...].astype(F32) + own_up[...].astype(F32),
            down[...].astype(F32) + own_down[...].astype(F32),
        ],
        1,
    )
    scaled = total * columns[:, 2:3]
    first = jnp.mean(scaled, 0, keepdims=True)
    second = jnp.mean(scaled * normed[...], 0, keepdims=True)
    result = grads[...].astype(F32) + inverse[...] * (
        scaled - first - normed[...] * second
    )
    middle[...] = result
    low = result.astype(BF16)
    branch[...] = low
    back = contract(weight[...], low, 1, 0).astype(BF16)
    for block in range(tensors):
        for head in range(heads):
            row = (block * heads + head) * size
            for rank in range(2):
                sent[(2 * head + rank) * tensors + block] = back[
                    row : row + size, rank * half : (rank + 1) * half
                ]
    sums[...] = as_rows(
        [jnp.sum(values, 1, keepdims=True) for values in (total * normed[...], total, result)]
    )


def leave(terms, normed, inverse, grads, weight, columns, heads, size):
    width, count = normed.shape
    blocks = width // size
    return pl.pallas_call(
        functools.partial(leave_kernel, heads=heads),
        out_shape=(
            jax.ShapeDtypeStruct((width, count), F32),
            jax.ShapeDtypeStruct((width, count), BF16),
            jax.ShapeDtypeStruct((8, width), F32),
            jax.ShapeDtypeStruct((2 * blocks, size, count // 2), BF16),
        ),
        in_specs=[VM] * 9,
        out_specs=(VM,) * 4,
        compiler_params=pltpu.CompilerParams(vmem_limit_bytes=12 * 2**20),
        name="leave",
    )(*terms, normed, inverse, grads, weight, columns)


def rest_kernel(spot, flat, full, out, mine, other):
    width = full.shape[0]
    split = mine.shape[0]
    step = min(256, width)
    for start in range(0, width, step):
        tile = slice(start, start + step)
        result = contract(flat[...], full[tile], 1, 1).astype(BF16)
        first = result[:split]
        second = jnp.concatenate([result[split:], out[:, tile]], 0)

        @pl.when(spot[1] == 0)
        def _():
            mine[:, tile] = first
            other[:, tile] = second

        @pl.when(spot[1] == 1)
        def _():
            mine[:, tile] = second
            other[:, tile] = first


def rest_halves(spot, flat, full, out):
    half = (flat.shape[0] + out.shape[0]) // 2
    return pl.pallas_call(
        rest_kernel,
        out_shape=(jax.ShapeDtypeStruct((half, full.shape[0]), BF16),) * 2,
        in_specs=[SM] + [VM] * 3,
        out_specs=(VM, VM),
        compiler_params=pltpu.CompilerParams(vmem_limit_bytes=8 * 2**20),
        cost_estimate=pl.CostEstimate(
            flops=2 * flat.shape[0] * full.size, bytes_accessed=2**23, transcendentals=0
        ),
        name="rest_halves",
    )(spot, flat, full, out)


def rest_whole_kernel(spot, half, other, mixed, out, *, chips):
    step = half.shape[0] // chips
    edge = mixed.shape[0] // step
    for piece in range(chips):
        owner = lax.rem(spot[2] + chips - piece, chips)
        rows = slice(piece * step, (piece + 1) * step)
        for source, core in ((half, spot[1]), (other, 1 - spot[1])):
            block = core * chips + owner
            values = source[rows].astype(F32)

            @pl.when(block < edge)
            def _():
                mixed[pl.ds(pl.multiple_of(jnp.minimum(block, edge - 1) * step, step), step)] = values

            @pl.when(block >= edge)
            def _():
                out[pl.ds(pl.multiple_of(jnp.maximum(block - edge, 0) * step, step), step)] = values


def rest_whole(spot, half, other, rows, chips):
    width = half.shape[1]
    return pl.pallas_call(
        functools.partial(rest_whole_kernel, chips=chips),
        out_shape=(
            jax.ShapeDtypeStruct((rows, width), F32),
            jax.ShapeDtypeStruct((2 * half.shape[0] - rows, width), F32),
        ),
        in_specs=[SM, VM, VM],
        out_specs=(VM, VM),
        compiler_params=pltpu.CompilerParams(vmem_limit_bytes=8 * 2**20),
        name="rest_whole",
    )(spot, half, other)


def prefix_kernel(
    total, hidden, embed, weight, low, grad_embed, grad_weight, grad_bias, grad_out, grad_out_bias
):
    pre = total[...] * (1.0 - hidden[...] * hidden[...])
    grad_bias[...] = jnp.sum(pre, 0, keepdims=True)

    def exact(first, second, dims):
        return lax.dot_general(
            first, second, ((dims[:1], dims[1:]), ((), ())),
            preferred_element_type=F32, precision=HIGHEST,
        )

    grad_weight[...] = exact(embed[...].astype(F32), pre, (0, 0))
    grad_embed[...] = exact(pre, weight[...].astype(F32), (1, 1))
    wide = low[...].astype(F32)
    result = exact(hidden[...], wide, (0, 0))
    sums = jnp.sum(wide, 0, keepdims=True)
    each = grad_out.shape[2]
    for head in range(grad_out.shape[1]):
        lanes = slice(head * each, (head + 1) * each)
        grad_out[:, head, :] = result[:, lanes]
        grad_out_bias[head : head + 1] = sums[:, lanes]


def prefix_back(total, hidden, embed, weight, low, heads):
    rows, width = embed.shape
    extra = PAD - rows
    hidden = jnp.pad(hidden, ((0, extra), (0, 0)))
    embed = jnp.pad(embed, ((0, extra), (0, 0)))
    inner = weight.shape[1]
    each = low.shape[1] // heads
    grad_embed, grad_weight, grad_bias, grad_out, grad_out_bias = pl.pallas_call(
        prefix_kernel,
        out_shape=(
            jax.ShapeDtypeStruct((PAD, width), F32),
            jax.ShapeDtypeStruct(weight.shape, F32),
            jax.ShapeDtypeStruct((1, inner), F32),
            jax.ShapeDtypeStruct((inner, heads, each), F32),
            jax.ShapeDtypeStruct((heads, each), F32),
        ),
        in_specs=[VM] * 5,
        out_specs=(VM,) * 5,
        compiler_params=pltpu.CompilerParams(vmem_limit_bytes=16 * 2**20),
        cost_estimate=pl.CostEstimate(flops=2**31, bytes_accessed=2**22, transcendentals=0),
        name="prefix_back",
    )(total, hidden, embed, weight, low)
    return grad_embed[:rows], grad_weight, grad_bias[0], grad_out, grad_out_bias


def spread(values, axis):
    count = lax.axis_size(axis)
    copies = jnp.broadcast_to(values[None], (count,) + values.shape)
    return lax.all_to_all(copies, axis, 0, 0, tiled=True)


def small_sum(values, axis):
    return jnp.sum(spread(values, axis), 0)


def ring(axis, by):
    count = lax.axis_size(axis)
    return [(source, (source + by) % count) for source in range(count)]


def ring_gather(values, axis, beside=()):
    count, place = lax.axis_size(axis), lax.axis_index(axis)
    half = values.shape[0] // 2
    up, down = values[:half], values[half:]
    out = jnp.zeros((count,) + values.shape, values.dtype)
    out = lax.dynamic_update_slice_in_dim(out, values[None], place, 0)
    zeros = (0,) * (values.ndim - 1)
    results = []
    for step in range(1, count):
        up = lax.ppermute(up, axis, ring(axis, 1))
        down = lax.ppermute(down, axis, ring(axis, -1))
        if step <= len(beside) and beside[step - 1]:
            up, down, result = lax.optimization_barrier((up, down, beside[step - 1]()))
            results.append(result)
        out = lax.dynamic_update_slice(out, up[None], ((place - step) % count, 0) + zeros)
        out = lax.dynamic_update_slice(out, down[None], ((place + step) % count, half) + zeros)
    return (out, results) if beside else out


def ring_terms(own, axis, beside=(), first=None):
    count = lax.axis_size(axis)
    up, down = first or (own(1, False), own(1, True))
    state = None
    for step in range(1, count):
        up = lax.ppermute(up, axis, ring(axis, 1))
        down = lax.ppermute(down, axis, ring(axis, -1))
        if step <= len(beside):
            state = beside[step - 1](state)
            up, down, state = lax.optimization_barrier((up, down, state))
        if step < count - 1:
            up = (up.astype(F32) + own(step + 1, False).astype(F32)).astype(BF16)
            down = (down.astype(F32) + own(step + 1, True).astype(F32)).astype(BF16)
    for other in beside[count - 1 :]:
        state = other(state)
    return (up, down, own(0, False), own(0, True)), state


def one_way_terms(own, axis, beside, first):
    count = lax.axis_size(axis)
    moving, state = first, None
    for step in range(1, count):
        moving = lax.ppermute(moving, axis, ring(axis, 1))
        if step <= len(beside):
            state = beside[step - 1](state)
            moving, state = lax.optimization_barrier((moving, state))
        if step < count - 1:
            moving = (moving.astype(F32) + own(step + 1).astype(F32)).astype(BF16)
    return moving, state


def swapped(values):
    pairs = [(source, source ^ 1) for source in range(lax.axis_size("seq"))]
    return lax.ppermute(values, "seq", pairs)


def chip_parts(half):
    count = lax.axis_size("seq")
    chips = count // 2
    chip = lax.axis_index("seq") // 2
    blocks = half.reshape(chips, half.shape[0] // chips, half.shape[1])
    total = lax.dynamic_index_in_dim(blocks, chip, 0, keepdims=False)
    parts = [total]
    for step in range(1, chips):
        block = lax.dynamic_index_in_dim(blocks, (chip + step) % chips, 0, keepdims=False)
        parts.append(lax.ppermute(block, "seq", ring("seq", 2 * step)))
    return parts


def chip_gather(parts):
    part = sum(part.astype(F32) for part in parts).astype(BF16)
    behind = [lax.ppermute(part, "seq", ring("seq", 2 * step)) for step in range(1, len(parts))]
    return jnp.concatenate([part] + behind, 0)


def spread_direct(values, axis):
    count, place = lax.axis_size(axis), lax.axis_index(axis)
    out = jnp.zeros((count,) + values.shape, values.dtype)
    out = lax.dynamic_update_slice_in_dim(out, values[None], place, 0)
    for step in range(1, count):
        came = lax.ppermute(values, axis, ring(axis, step))
        out = lax.dynamic_update_slice_in_dim(out, came[None], (place - step) % count, 0)
    return out


def core_gather(half):
    core, chip = lax.axis_index("seq") % 2, lax.axis_index("seq") // 2
    chips = lax.axis_size("seq") // 2
    order = (chip - jnp.arange(chips)) % chips

    def sorted_parts(values):
        parts = values.reshape(chips, -1, values.shape[1])
        picked = [lax.dynamic_index_in_dim(parts, order[n], 0) for n in range(chips)]
        return jnp.concatenate(picked, 0).reshape(values.shape)

    half, other = sorted_parts(half), sorted_parts(swapped(half))
    first = jnp.where(core == 0, half, other)
    second = jnp.where(core == 0, other, half)
    return jnp.concatenate([first, second], 0)


def regrouped(values, width):
    count, size, columns = values.shape
    if width == columns:
        return values
    if width > columns:
        merged = values.reshape(-1, width // columns, size, columns).transpose(0, 2, 1, 3)
        return merged.reshape(-1, size, width)
    cut = values.reshape(count, size, columns // width, width).transpose(0, 2, 1, 3)
    return cut.reshape(-1, size, width)


def group_gather(pieces, group):
    if group == 2:
        rank = lax.axis_index("seq") % 2
        other = swapped(pieces)
        return jnp.stack([jnp.where(rank == 0, pieces, other), jnp.where(rank == 0, other, pieces)])
    count = lax.axis_size("seq")
    groups = [[first + i for i in range(group)] for first in range(0, count, group)]
    return lax.all_gather(pieces, "seq", axis_index_groups=groups)


def on_device(
    tokens,
    segment_ids,
    out_grad,
    ln1_gain,
    ln1_bias,
    w_qkv,
    b_qv,
    w_out,
    b_out,
    ln2_gain,
    ln2_bias,
    w_up,
    b_up,
    w_down,
    b_down,
    prefix_embed,
    reparam_in,
    reparam_in_bias,
    reparam_out,
    reparam_out_bias,
):
    rows, features = tokens.shape
    heads = w_qkv.shape[1]
    size = w_qkv.shape[2] // 3
    inner = w_up.shape[1]
    seqs, tensors = lax.axis_size("seq"), lax.axis_size("tensor")
    width = features * tensors
    own_rows = rows // tensors
    group = seqs // heads
    chunk = own_rows // group
    place, slot = lax.axis_index("seq"), lax.axis_index("tensor")
    head, rank = place // group, place % group
    prefix = prefix_embed.shape[0]
    tokens_head = rows // group
    query_width = max(tokens_head, LANES)
    forward_tile = min(512, query_width)
    backward_tile = min(512, query_width)
    forward_keys, backward_keys = 1024, 1024
    both = ("seq", "tensor")
    paired = group == 2 and chunk == LANES

    own_tokens, own_grads = turned(tokens, out_grad)
    numbers = jnp.arange(1, DOCS, dtype=jnp.int32)

    def document_starts():
        before = jnp.sum((segment_ids[None, :] < numbers[:, None]).astype(jnp.int32), 1)
        return spread(jnp.broadcast_to(before[:, None], (DOCS - 1, LANES)), "seq")

    def whole_vectors():
        return spread(
            jnp.stack([ln1_gain, ln1_bias, ln2_gain, ln2_bias, b_out, b_down]), "tensor"
        )

    def prefix_network():
        prefix_hidden = jnp.tanh(
            jnp.dot(prefix_embed, reparam_in, preferred_element_type=F32)
            + reparam_in_bias.astype(F32)
        )
        prefix_pair = jnp.einsum(
            "pa,ahe->phe", prefix_hidden, reparam_out.astype(F32), precision=HIGHEST
        )
        prefix_pair = (prefix_pair + reparam_out_bias.astype(F32)).astype(BF16)
        own_pair = lax.dynamic_index_in_dim(prefix_pair, head, 1, keepdims=False)
        own_pair = jnp.pad(own_pair, ((0, LANES - prefix), (0, 0)))
        pre_key, pre_value = own_pair[:, :size], own_pair[:, size:]
        return prefix_hidden, pre_key, pre_value

    full_tokens, (vectors, starts) = ring_gather(
        own_tokens, "tensor", (None, whole_vectors, document_starts)
    )
    prefix_hidden, pre_key, pre_value = prefix_network()
    full_tokens = full_tokens.reshape(width, rows)
    meta = jnp.concatenate([jnp.sum(starts, 0)[:, 0], rank[None].astype(jnp.int32)])
    columns = vectors.transpose(0, 2, 1).reshape(width, 6).astype(F32)
    out_share = w_out.reshape(seqs, heads * size // seqs, width)
    out_share = lax.dynamic_index_in_dim(out_share, place, 0, keepdims=False)
    core = place % 2
    spot = jnp.stack([slot, core, place // 2]).astype(jnp.int32)

    w_flat = w_qkv.reshape(width, heads * 3 * size)
    bias_pair = b_qv.astype(F32)
    bias_three = jnp.stack(
        [bias_pair[:, :size], jnp.zeros((heads, size), F32), bias_pair[:, size:]], 1
    ).reshape(-1, 1)
    if paired:
        full1, sent, stats = project(
            full_tokens, columns, w_flat.T, bias_three, heads, size, own_rows
        )
    else:
        wide = full_tokens.astype(F32)
        mean = jnp.mean(wide, 0, keepdims=True)
        inverse = lax.rsqrt(jnp.mean((wide - mean) ** 2, 0, keepdims=True) + EPS)
        stats = jnp.concatenate([mean, inverse], 0)
        full1 = ((wide - mean) * inverse * columns[:, 0:1] + columns[:, 1:2]).astype(BF16)
        mixed = (contract(w_flat, full1, 0, 0) + bias_three).astype(BF16)
        mixed = mixed.reshape(heads, 3, size, rows)
        query_part = mixed[:, 0].reshape(heads, size, tensors, group, chunk)
        query_part = query_part.transpose(0, 3, 1, 2, 4).reshape(seqs, size, tokens_head)
        pair_part = mixed[:, 1:].transpose(0, 2, 1, 3).reshape(heads, size, group, 2 * tokens_head)
        pair_part = pair_part.transpose(0, 2, 1, 3).reshape(seqs, size, 2 * tokens_head)
        sent = jnp.concatenate([query_part, pair_part], 2)
    out_share = spread_direct(after(out_share, sent), "tensor")
    came = lax.all_to_all(sent, "seq", 0, 0, tiled=True)
    came, out_share = lax.optimization_barrier((came, out_share))
    w_out_full = lax.all_gather(out_share, "seq")
    w_out_full = w_out_full.transpose(1, 0, 2, 3).reshape(width, width)
    if group == 2:
        query, own, other = came, came, swapped(came)
    else:
        query, pair = came[:, :, :tokens_head], came[:, :, tokens_head:]
        query = regrouped(query, query_width)
        pair = group_gather(pair, group).transpose(1, 2, 0, 3).reshape(seqs, size, 2, rows)
        own, other = pair[:, :, 0], pair[:, :, 1]
    full_grad = lax.all_gather(after(own_grads, full_tokens), "tensor", axis=0, tiled=True)
    out_low, out_full, log_total = attend_forward(
        meta, query, own, other, pre_key.T, pre_value.T,
        forward_tile, forward_keys, prefix, chunk, group, rows, query_width,
    )
    out_low, full_grad, late_up, late_down, late_qkv, late_tokens = lax.optimization_barrier(
        (out_low, full_grad, w_up, w_down, w_qkv, full_tokens)
    )
    late_qkv = late_qkv.transpose(1, 2, 0).reshape(heads * 3 * size, width)
    up_turned, down_turned, late_flat = turned(late_up, late_down, late_qkv)

    came = lax.all_to_all(regrouped(out_low, chunk), both, 0, 0, tiled=True)
    own_block = lax.dynamic_slice_in_dim(late_tokens, slot * own_rows, own_rows, 1)
    came, up_turned, down_turned, late_flat, w_out_full, own_block = lax.optimization_barrier(
        (came, up_turned, down_turned, late_flat, w_out_full, own_block)
    )
    if paired:
        attended, middle, normed2, inverse2, ring_up, ring_down = enter(
            came, w_out_full, own_block, columns, heads
        )
    else:
        came = came.reshape(heads, group, tensors, size, chunk).transpose(2, 0, 3, 1, 4)
        attended = came.reshape(width, own_rows)
        branch = contract(w_out_full, attended, 0, 0)
        middle = own_block.astype(F32) + branch + columns[:, 4:5]
        centered = middle - jnp.mean(middle, 0, keepdims=True)
        inverse2 = lax.rsqrt(jnp.mean(centered * centered, 0, keepdims=True) + EPS)
        normed2 = centered * inverse2
        out2 = (normed2 * columns[:, 2:3] + columns[:, 3:4]).astype(BF16)
        ring_up, ring_down = out2[:, : own_rows // 2], out2[:, own_rows // 2 :]

    bias_up = b_up.astype(F32)[:, None]
    given = given_grads(spot, full_grad, tensors)
    results = []
    for step in range(tensors):
        def block(up=ring_up, down=ring_down, step=step):
            return feed(up, down, given[step], up_turned, w_up, w_down, bias_up)

        if step < tensors - 1:
            ring_up = lax.ppermute(ring_up, "tensor", ring("tensor", 1))
            ring_down = lax.ppermute(ring_down, "tensor", ring("tensor", -1))
            ring_up, ring_down, result = lax.optimization_barrier((ring_up, ring_down, block()))
        else:
            result = block()
        results.append(result)
    blocks, hidden, grad_pre, parts_up, parts_down = zip(*results)

    def weights_here(_):
        return feed_weights(blocks, given, hidden, grad_pre)

    def out_here(state):
        return state, feed_out(spot, hidden, down_turned, middle, columns)

    terms, (weights, mlp_out) = ring_terms(
        lambda step, upper: (parts_down if upper else parts_up)[step],
        "tensor",
        (weights_here, out_here),
    )
    grad_w_down, grad_w_up, grad_b_up = weights
    feed_sums = lax.psum((grad_w_down, grad_w_up), "seq")

    if paired:
        grad_middle, grad_branch, token_sums, sent = leave(
            terms, normed2, inverse2, given[0], w_out_full, columns, heads, size
        )
    else:
        up, down, own_up, own_down = [a.astype(F32) for a in terms]
        grad_normed2 = jnp.concatenate([up + own_up, down + own_down], 1)
        scaled = grad_normed2 * columns[:, 2:3]
        first = jnp.mean(scaled, 0, keepdims=True)
        second = jnp.mean(scaled * normed2, 0, keepdims=True)
        own_grad = lax.dynamic_slice_in_dim(full_grad, slot * own_rows, own_rows, 1)
        grad_middle = own_grad.astype(F32) + inverse2 * (scaled - first - normed2 * second)
        grad_branch = grad_middle.astype(BF16)
        token_sums = [grad_normed2 * normed2, grad_normed2, grad_middle]
        token_sums = jnp.stack([jnp.sum(a, 1) for a in token_sums], 1)
        sent = contract(w_out_full, grad_branch, 1, 0).astype(BF16)
        sent = sent.reshape(tensors, heads, size, group, chunk).transpose(1, 3, 0, 2, 4)
        sent = sent.reshape(seqs * tensors, size, chunk)
    came = lax.all_to_all(sent, both, 0, 0, tiled=True)
    grad_out = regrouped(came, LANES)

    grad_w_out = contract(attended, grad_branch, 1, 1).astype(BF16)
    grad_out, mlp_out, grad_w_out = lax.optimization_barrier((grad_out, mlp_out, grad_w_out))
    output_act = lax.all_to_all(mlp_out, "tensor", 0, 0, tiled=True)
    grad_w_out = lax.psum_scatter(grad_w_out, "tensor", scatter_dimension=0, tiled=True)

    levels = log_total.reshape(-1, 1, backward_tile)
    grad_query, grad_keep, grad_send, grad_prefix = attend_backward(
        meta, query, own, other, pre_key[:PAD], pre_value[:PAD], grad_out, out_full, levels,
        backward_tile, backward_keys, prefix, chunk, group, rows, query_width,
    )
    if group == 2:
        grad_share = (grad_keep.astype(F32) + swapped(grad_send).astype(F32)).astype(BF16)
    else:
        grad_pair = jnp.stack([grad_keep, grad_send])
        groups = [[first + i for i in range(group)] for first in range(0, seqs, group)]
        shares = grad_pair.transpose(1, 2, 0, 3).reshape(seqs, size, group, 2 * tokens_head)
        grad_share = lax.psum_scatter(
            shares.transpose(2, 0, 1, 3), "seq", axis_index_groups=groups
        )
    prefix_part = grad_prefix.transpose(2, 0, 1).reshape(size, 2 * PAD).astype(BF16)
    prefix_part = jnp.pad(prefix_part, ((0, 0), (0, LANES - 2 * PAD)))
    prefix_part = jnp.broadcast_to(prefix_part[None], (seqs, size, LANES))
    sent = jnp.concatenate([regrouped(grad_query, tokens_head), grad_share, prefix_part], 2)
    sent, output_act, feed_sums = lax.optimization_barrier((sent, output_act, feed_sums))
    came = lax.all_to_all(sent, "seq", 0, 0, tiled=True)
    output_act = jnp.sum(output_act.astype(F32), 0).astype(BF16)
    output_act = output_act.transpose(0, 2, 1).reshape(rows, features)
    out_w_down = feed_sums[0].astype(F32)
    out_w_up = (feed_sums[1] if inner == width else feed_sums[1].T).astype(F32)
    came, output_act, grad_w_out, out_w_down, out_w_up = lax.optimization_barrier(
        (came, output_act, grad_w_out, out_w_down, out_w_up)
    )
    if paired:
        grad_flat, grad_part, first_block, last_block, head_row, prefix_low, small = unproject(
            spot, came, late_flat, full_tokens, stats, columns, grad_branch, token_sums,
            reparam_out, heads, size, own_rows,
        )
        mine, other = rest_halves(spot, grad_flat, full1, grad_w_out)
    else:
        query_part = came[:, :, :tokens_head].reshape(heads, group, size, tensors, chunk)
        query_part = query_part.transpose(0, 2, 3, 1, 4).reshape(heads, 1, size, rows)
        pair_part = came[:, :, tokens_head : 3 * tokens_head]
        pair_part = pair_part.reshape(heads, group, size, 2 * tokens_head).transpose(0, 2, 1, 3)
        pair_part = pair_part.reshape(heads, size, 2, rows).transpose(0, 2, 1, 3)
        grad_flat = jnp.concatenate([query_part, pair_part], 1).reshape(heads * 3 * size, rows)
        back = contract(late_flat, grad_flat, 1, 0)
        normed1 = (full_tokens.astype(F32) - stats[0]) * stats[1]
        scaled = back * columns[:, 0:1]
        row_sums = jnp.stack([jnp.sum(scaled, 0), jnp.sum(scaled * normed1, 0)])
        sums1 = jnp.stack([jnp.sum(back * normed1, 1), jnp.sum(back, 1)], 1)
        head_sums = jnp.sum(grad_flat.astype(F32), 1)
        own_inverse = lax.dynamic_slice_in_dim(stats[1:2], slot * own_rows, own_rows, 1)
        own_part = lax.dynamic_slice_in_dim(back, slot * own_rows, own_rows, 1)
        own_part = own_part + grad_middle / (own_inverse * columns[:, 0:1])
        back = lax.dynamic_update_slice_in_dim(back, own_part, slot * own_rows, 1)
        grad_part = back.astype(BF16)
        below = (slot - 1) % tensors * features
        first_block = lax.dynamic_slice_in_dim(grad_part, below, features, 0)
        last_block = lax.dynamic_slice_in_dim(grad_part, slot * features, features, 0)
        grad_w_qkv = contract(grad_flat, full1, 1, 1).astype(BF16)
        rest = jnp.concatenate([grad_w_qkv, grad_w_out], 0)
        halves = rest.reshape(2, rest.shape[0] // 2, width)
        mine = lax.dynamic_index_in_dim(halves, core, 0, keepdims=False)
        other = lax.dynamic_index_in_dim(halves, 1 - core, 0, keepdims=False)

    if not paired:
        prefix_low = came[:, :, 3 * tokens_head : 3 * tokens_head + 2 * PAD].astype(F32)
        prefix_low = jnp.sum(prefix_low.reshape(heads, group, size, 2, PAD), 1)
        prefix_low = prefix_low.transpose(3, 0, 2, 1).reshape(PAD, -1).astype(BF16)
        hidden_part = contract(prefix_low, reparam_out.reshape(reparam_out.shape[0], -1), 1, 1)
        owned = jnp.concatenate([sums1.T, token_sums.T], 0)
        owned = owned.reshape(-1, tensors, features).transpose(1, 0, 2).reshape(tensors, -1)
        shared = jnp.concatenate([row_sums.reshape(-1), hidden_part.reshape(-1)])
        shared = jnp.broadcast_to(shared[None], (tensors, shared.shape[0]))
        small = jnp.concatenate([owned, shared], 1)[:, None, :]

    grad_b_down = jnp.sum(out_grad.astype(F32), 0)

    def halves_here(_):
        half = (mine.astype(F32) + swapped(other).astype(F32)).astype(BF16)
        return half, lax.all_to_all(small, "tensor", 0, 0, tiled=True)


    def totals(parts):
        if paired:
            return small_totals(
                parts, grad_b_down[None], grad_b_up, head_row, rows, prefix_hidden.shape[1], width
            )
        sums = jnp.sum(parts, 0)[0]
        after_rows = 5 * features + 2 * rows
        row_means = sums[5 * features : after_rows].reshape(2, rows) / width
        hidden = sums[after_rows:].reshape(PAD, -1)
        mixed_sums = head_sums.reshape(heads, 3, size)
        late = [sums[: 5 * features], grad_b_down, grad_b_up[0]]
        late += [mixed_sums[:, 0].reshape(-1), mixed_sums[:, 2].reshape(-1)]
        return row_means, hidden, jnp.concatenate(late)[None]

    def parts_here(state):
        row_means, hidden_grad, late = totals(state[1])
        return chip_parts(state[0]), row_means, hidden_grad, spread(late, "seq")

    def gather_here(state):
        parts, row_means, hidden_grad, late = state
        prefix_grads = prefix_back(
            hidden_grad, prefix_hidden, prefix_embed, reparam_in, prefix_low, heads
        )
        return chip_gather(parts), row_means, late, prefix_grads

    def own_part(step):
        return lax.dynamic_slice_in_dim(grad_part, (slot - step) % tensors * features, features, 0)

    moved, (rest_half, row_means, late, prefix_grads) = one_way_terms(
        own_part,
        "tensor",
        (halves_here, parts_here) + (lambda state: state,) * (tensors - 4) + (gather_here,),
        first_block,
    )
    input_grad = finish(
        moved, last_block, own_tokens, ln1_gain.astype(F32)[:, None], stats, row_means,
    )
    mixed_rows = heads * 3 * size
    if paired:
        out_w_qkv, out_w_out = rest_whole(
            spot, rest_half, swapped(rest_half), mixed_rows, seqs // 2
        )
    else:
        rest = core_gather(rest_half).astype(F32)
        out_w_qkv, out_w_out = rest[:mixed_rows], rest[mixed_rows:]
    out_w_qkv = out_w_qkv.reshape(heads, 3 * size, width).transpose(2, 0, 1)
    out_w_out = out_w_out.reshape(heads, size, width)
    if paired:
        vectors, out_b_up, out_b_qv = late_totals(late, inner, heads, size)
        out_b_up = out_b_up[0]
    else:
        late = jnp.sum(late, 0)[0]
        vectors = late[: 6 * features].reshape(6, features)
        out_b_up = late[6 * features : 6 * features + inner]
        pair_sums = late[6 * features + inner :].reshape(2, heads, size)
        out_b_qv = jnp.concatenate([pair_sums[0], pair_sums[1]], 1)
    out_ln1_gain, out_ln1_bias, out_ln2_gain, out_ln2_bias, out_b_out, out_b_down = [
        vectors[i] for i in range(6)
    ]

    return (
        output_act,
        input_grad,
        out_ln1_gain,
        out_ln1_bias,
        out_w_qkv,
        out_b_qv,
        out_w_out,
        out_b_out,
        out_ln2_gain,
        out_ln2_bias,
        out_w_up,
        out_b_up,
        out_w_down,
        out_b_down,
        *prefix_grads,
    )


def solution(mesh):
    placed = (
        P("seq", "tensor"),
        P("seq"),
        P("seq", "tensor"),
        P("tensor"),
        P("tensor"),
        P(None, "tensor", None),
        P("tensor", None),
        P("tensor", None, None),
        P("tensor"),
        P("tensor"),
        P("tensor"),
        P(None, "tensor"),
        P("tensor"),
        P("tensor", None),
        P("tensor"),
        P(),
        P(),
        P(),
        P(None, "tensor", None),
        P("tensor", None),
    )
    return jax.shard_map(
        on_device,
        mesh=mesh,
        in_specs=placed,
        out_specs=(
            P("seq", "tensor"),
            P("seq", "tensor"),
            P("tensor"),
            P("tensor"),
            P(None, "tensor", None),
            P("tensor", None),
            P("tensor", None, None),
            P("tensor"),
            P("tensor"),
            P("tensor"),
            P(None, "tensor"),
            P("tensor"),
            P("tensor", None),
            P("tensor"),
            P(),
            P(),
            P(),
            P(None, "tensor", None),
            P("tensor", None),
        ),
        check_vma=False,
    )
```
